128 devices in a mesh: group: 4 (over z_lo, core), dp: 2 (over z_hi), tensor: 16 (over x, y).
Axes of the slice: x: 4, y: 4, z: 4 (z_hi: 2, z_lo: 2; z = z_hi * 2 + z_lo), core: 2. Of those that a mesh axis runs over, the one named last changes fastest.
Arguments:
- tokens: bfloat16 [2048, 8, 2048], P('tensor', ('group', 'dp')), may hold values from -6 to 6
- cotangent: bfloat16 [2048, 8, 2048], P('tensor', ('group', 'dp')), may hold values from -6 to 6
- lengths: int32 [8], replicated, may hold values from 1 to 2048, 9830 in all
- ln1_gain: float32 [2048], replicated, may hold values from 0.25 to 1.75
- ln1_bias: float32 [2048], replicated, may hold values from -1.75 to 1.75
- w_qkv: bfloat16 [2048, 3, 16, 128], P(None, None, 'tensor'), may hold values from -0.125 to 0.125
- b_qv: float32 [2, 2048], P(None, 'tensor'), may hold values from -1.75 to 1.75
- w_o: bfloat16 [16, 128, 2048], P('tensor'), may hold values from -0.75 to 0.75
- b_o: float32 [2048], replicated, may hold values from -1.75 to 1.75
- ln2_gain: float32 [2048], replicated, may hold values from 0.25 to 1.75
- ln2_bias: float32 [2048], replicated, may hold values from -1.75 to 1.75
- w_in: bfloat16 [2048, 8192], P(None, 'tensor'), may hold values from -0.125 to 0.125
- b_in: float32 [8192], P('tensor'), may hold values from -1.75 to 1.75
- w_out: bfloat16 [8192, 2048], P('tensor'), may hold values from -0.0625 to 0.0625
- b_out: float32 [2048], replicated, may hold values from -1.75 to 1.75
Outputs:
- output: bfloat16 [2048, 8, 2048], P('tensor', ('group', 'dp'))
- input_grad: bfloat16 [2048, 8, 2048], P('tensor', ('group', 'dp'))
- d_ln1_gain: float32 [2048], P(('group', 'dp', 'tensor'))
- d_ln1_bias: float32 [2048], P(('group', 'dp', 'tensor'))
- d_w_qkv: float32 [2048, 3, 16, 128], P(('group', 'dp'), None, 'tensor')
- d_b_qv: float32 [2, 2048], P(None, ('group', 'dp', 'tensor'))
- d_w_o: float32 [16, 128, 2048], P('tensor', None, ('group', 'dp'))
- d_b_o: float32 [2048], P(('group', 'dp', 'tensor'))
- d_ln2_gain: float32 [2048], P(('group', 'dp', 'tensor'))
- d_ln2_bias: float32 [2048], P(('group', 'dp', 'tensor'))
- d_w_in: float32 [2048, 8192], P(('group', 'dp'), 'tensor')
- d_b_in: float32 [8192], P(('group', 'dp', 'tensor'))
- d_w_out: float32 [8192, 2048], P('tensor', ('group', 'dp'))
- d_b_out: float32 [2048], P(('group', 'dp', 'tensor'))
The draws below stay inside these ranges and needn't reach their ends.
Inputs may be any that keep to these rules, and one draw needn't show every extreme that they name: The true lengths of the 8 sequences sum to 9830.
All inputs are finite; a program needn't handle non-finite values.
Results may differ from the reference program's by a relative error of at most 0.02.
Values may be sent and summed in bfloat16 or wider, within the bound.
No kernel may reach another device: no remote copies, remote signals or barrier semaphores. Data moves between devices by JAX's collectives and lax.ppermute only.
A program may use at most 192 MiB of HBM per device.

```python
import math
import jax
import jax.numpy as jnp
import numpy as np
from jax import lax

D = 2048
HEADS = 16
HEAD_DIM = 128
FF = 8192
LEN = 2048
SEQS = 8
N_GROUP = 4


def block_scale(own_key, shape, cuts, least, top_value):
    level = 1.0
    for dim, blocks in cuts:
        draws = jax.random.uniform(jax.random.fold_in(jax.random.fold_in(own_key, 6), dim), (blocks,), jnp.float32, least / len(cuts), top_value / len(cuts))
        level = level * jnp.repeat(jnp.exp(draws), shape[dim] // blocks).reshape((-1,) + (1,) * (len(shape) - 1 - dim))
    return level


def profile(number_of, total, reach, lean):
    portions = [(1 << 20) // math.isqrt(rank ** lean) + 1 for rank in range(2, number_of + 1)]
    spare, holding = total - reach - (number_of - 1), [1] * (number_of - 1)
    while spare > 0:
        movable = [i for i in range(number_of - 1) if holding[i] < reach]
        whole, remaining = sum([portions[i] for i in movable]), spare
        for i in movable:
            addition = min(reach - holding[i], max(1, remaining * portions[i] // whole), spare)
            holding[i] = holding[i] + addition
            spare = spare - addition
    return np.array([reach] + holding)


def uneven_parts(key, count, total, limit, skew):
    if count == 2:
        one = jax.random.randint(key, (), max(1, total - limit), min(limit, total - 1) + 1)
        return jnp.stack([one, total - one])
    sizes = jnp.asarray(profile(count, total, limit, skew), jnp.int32)
    twos = (count - 1) // 2
    donor, taker = sizes[1:1 + 2 * twos:2], sizes[2:2 + 2 * twos:2]
    slack = jnp.minimum(donor - 1, limit - taker)
    moved = jax.random.randint(jax.random.fold_in(key, 1), (twos,), 0, 1 << 20) % (slack + 1)
    sizes = sizes.at[1:1 + 2 * twos:2].set(donor - moved).at[2:2 + 2 * twos:2].set(taker + moved)
    return sizes[jax.random.permutation(jax.random.fold_in(key, 2), count)]


def scatter_about(rng, extent, width, reach, split=(), held_as=jnp.bfloat16):
    level = block_scale(rng, extent, split, -0.22, 0.18) if split else 1.0
    entries = jax.random.normal(rng, extent, jnp.float32) * width * level
    return jnp.minimum(jnp.maximum(entries, -reach), reach).astype(held_as)


def setup_inputs(seed: int = 0) -> dict:
    streams_of = jax.random.split(jax.random.key(seed), 16)
    tokens = scatter_about(streams_of[0], (LEN, SEQS, D), 1.0, 6.0, ((0, 16), (1, 8)))
    cotangent = scatter_about(streams_of[1], (LEN, SEQS, D), 1.0, 6.0, ((0, 16), (1, 8)))
    lengths = uneven_parts(streams_of[2], SEQS, SEQS * LEN * 3 // 5, LEN, 2).astype(jnp.int32)
    ln1_gain = jnp.clip(1.0 + 0.15 * jax.random.normal(streams_of[3], (D,), jnp.float32), 0.25, 1.75)
    ln1_bias = scatter_about(streams_of[4], (D,), 0.3, 1.75, (), jnp.float32)
    w_qkv = scatter_about(streams_of[5], (D, 3, HEADS, HEAD_DIM), D ** -0.5, 0.125, ((2, 16),))
    b_qv = scatter_about(streams_of[6], (2, D), 0.3, 1.75, ((1, 16),), jnp.float32)
    w_o = scatter_about(streams_of[7], (HEADS, HEAD_DIM, D), (D // 32) ** -0.5, 0.75, ((0, 16),))
    b_o = scatter_about(streams_of[8], (D,), 0.3, 1.75, (), jnp.float32)
    ln2_gain = jnp.clip(1.0 + 0.15 * jax.random.normal(streams_of[9], (D,), jnp.float32), 0.25, 1.75)
    ln2_bias = scatter_about(streams_of[10], (D,), 0.3, 1.75, (), jnp.float32)
    w_in = scatter_about(streams_of[11], (D, FF), D ** -0.5, 0.125, ((1, 16),))
    b_in = scatter_about(streams_of[12], (FF,), 0.3, 1.75, ((0, 16),), jnp.float32)
    w_out = scatter_about(streams_of[13], (FF, D), FF ** -0.5, 0.0625, ((0, 16),))
    b_out = scatter_about(streams_of[14], (D,), 0.3, 1.75, (), jnp.float32)
    return {"tokens": tokens, "cotangent": cotangent, "lengths": lengths, "ln1_gain": ln1_gain, "ln1_bias": ln1_bias, "w_qkv": w_qkv, "b_qv": b_qv, "w_o": w_o, "b_o": b_o, "ln2_gain": ln2_gain, "ln2_bias": ln2_bias, "w_in": w_in, "b_in": b_in, "w_out": w_out, "b_out": b_out}


EPS = 1e-05
HIGH = lax.Precision.HIGHEST

@jax.custom_vjp
def low(v):
    return lax.optimization_barrier(v.astype(jnp.bfloat16)).astype(jnp.float32)

@jax.custom_vjp
def low_back(v):
    return v

def low_keep(v):
    return (low(v), None)

def low_pass(kept, grad):
    return (grad,)

def back_keep(v):
    return (v, None)

def back_low(kept, grad):
    return (low(grad),)
low.defvjp(low_keep, low_pass)
low_back.defvjp(back_keep, back_low)

def rounded_both(value):
    return low_back(low(value))

def matmul(left, right):
    return jnp.dot(left, right, precision=HIGH)

def layer_norm(value, gain, shift):
    mean = lax.optimization_barrier(jnp.mean(value, axis=-1, keepdims=True))
    centred = value - mean
    spread = lax.optimization_barrier(jnp.mean(centred * centred, axis=-1, keepdims=True))
    return centred * lax.rsqrt(spread + EPS) * gain + shift

def forward(rows_in, params, length):
    ln1_gain, ln1_bias, w_qkv, b_qv, w_o, b_o, ln2_gain, ln2_bias, w_in, b_in, w_out, b_out = params
    normed = low(layer_norm(rows_in, ln1_gain, ln1_bias))
    projected = matmul(normed, w_qkv.reshape(D, 3 * D))
    query = rounded_both(projected[:, :D] + b_qv[0])
    keys = rounded_both(projected[:, D:2 * D])
    values = rounded_both(projected[:, 2 * D:] + b_qv[1])

    def split_heads(array):
        return jnp.transpose(array.reshape(LEN, HEADS, HEAD_DIM), (1, 0, 2))
    positions = jnp.arange(LEN, dtype=jnp.int32)
    valid = (positions[None, :] <= positions[:, None]) & (positions[None, :] < length)
    score_scale = 1.0 / math.sqrt(HEAD_DIM)

    def one_head(item):
        head_query, head_keys, head_values = item
        scores = low_back(matmul(head_query, head_keys.T) * score_scale)
        scores = jnp.where(valid, scores, -1e+30)
        probs = jax.nn.softmax(scores, axis=-1)
        return rounded_both(matmul(low(probs), head_values))
    heads = lax.map(jax.checkpoint(one_head), (split_heads(query), split_heads(keys), split_heads(values)))
    attended = jnp.transpose(heads, (1, 0, 2)).reshape(LEN, D)
    middle = rows_in + low_back(matmul(attended, w_o.reshape(D, D)) + b_o)
    second = low(layer_norm(middle, ln2_gain, ln2_bias))
    pre = low_back(matmul(second, w_in) + b_in)
    activated = low(jax.nn.gelu(pre, approximate=True))
    return middle + low_back(matmul(activated, w_out) + b_out)

def reference(tokens, cotangent, lengths, ln1_gain, ln1_bias, w_qkv, b_qv, w_o, b_o, ln2_gain, ln2_bias, w_in, b_in, w_out, b_out):
    params = tuple((item.astype(jnp.float32) for item in (ln1_gain, ln1_bias, w_qkv, b_qv, w_o, b_o, ln2_gain, ln2_bias, w_in, b_in, w_out, b_out)))
    group_totals = lax.optimization_barrier(jnp.sum(lengths.reshape(N_GROUP, -1), axis=1)).astype(jnp.float32)
    factors = N_GROUP * group_totals / jnp.sum(group_totals)
    seq_factors = jnp.repeat(factors, SEQS // N_GROUP)
    seq_tokens = jnp.transpose(tokens.astype(jnp.float32), (1, 0, 2))
    seq_upstream = jnp.transpose(cotangent.astype(jnp.float32), (1, 0, 2))
    positions = jnp.arange(LEN, dtype=jnp.int32)

    def step(carry, item):
        rows_in, upstream, length, factor = item
        result, backward = jax.vjp(lambda value, weights: forward(value, weights, length), rows_in, params)
        live = (positions < length)[:, None]
        row_grad, param_grads = backward(jnp.where(live, upstream, 0.0))
        carry = jax.tree.map(lambda acc, part: acc + factor * part, carry, param_grads)
        return (carry, (result, row_grad))
    zeros = jax.tree.map(jnp.zeros_like, params)
    grads, (results, row_grads) = lax.scan(step, zeros, (seq_tokens, seq_upstream, lengths, seq_factors))
    output = jnp.transpose(results, (1, 0, 2)).astype(jnp.bfloat16)
    input_grad = jnp.transpose(row_grads, (1, 0, 2)).astype(jnp.bfloat16)
    return (output, input_grad, grads[0], grads[1], grads[2], grads[3], grads[4], grads[5], grads[6], grads[7], grads[8], grads[9], grads[10], grads[11])
```

```python
from functools import partial
import math

import jax
import jax.numpy as jnp
from jax import lax
from jax.sharding import PartitionSpec as P

EPS = 1e-05
NEGATIVE = -1e30


def layer_norm(value, gain, shift):
    mean = jnp.mean(value, axis=-1, keepdims=True)
    centred = value - mean
    spread = jnp.mean(centred * centred, axis=-1, keepdims=True)
    return centred * lax.rsqrt(spread + EPS) * gain + shift


def gelu_tanh(value):
    return jax.nn.gelu(value, approximate=True)


def block_scores(rows_query, key_rows, first, length, score_scale):
    count = rows_query.shape[0]
    key_pos = jnp.arange(key_rows.shape[0], dtype=jnp.int32)
    query_pos = first + jnp.arange(count, dtype=jnp.int32)
    valid = (key_pos[None, :] <= query_pos[:, None]) & (key_pos[None, :] < length)
    scores = (
        lax.dot_general(
            rows_query, key_rows, (((1,), (1,)), ((), ())), preferred_element_type=jnp.float32
        )
        * score_scale
    )
    return (jnp.where(valid, scores, NEGATIVE), valid)


def attend_forward(item, block_rows, score_scale):
    query, key_rows, value_rows, length = item
    outputs = []
    log_parts = []
    for first in range(0, query.shape[0], block_rows):
        rows_query = query[first : first + block_rows]
        scores, valid = block_scores(rows_query, key_rows, first, length, score_scale)
        peak = jnp.max(scores, axis=-1, keepdims=True)
        expo = jnp.exp(scores - peak)
        weight_sum = jnp.sum(expo, axis=-1, keepdims=True)
        probs = (expo / weight_sum).astype(jnp.bfloat16)
        outputs.append(
            jnp.dot(probs, value_rows, preferred_element_type=jnp.float32).astype(jnp.bfloat16)
        )
        log_parts.append((peak + jnp.log(weight_sum))[:, 0])
    return (jnp.concatenate(outputs, 0), jnp.concatenate(log_parts, 0))


def attend_backward(item, block_rows, score_scale):
    query, key_rows, value_rows, length, grad_out, log_sums = item
    key_grad = jnp.zeros(key_rows.shape, jnp.float32)
    value_grad = jnp.zeros(value_rows.shape, jnp.float32)
    query_parts = []
    for first in range(0, query.shape[0], block_rows):
        rows_query = query[first : first + block_rows]
        scores, valid = block_scores(rows_query, key_rows, first, length, score_scale)
        probs = jnp.where(valid, jnp.exp(scores - log_sums[first : first + block_rows, None]), 0.0)
        grad_rows = grad_out[first : first + block_rows]
        probs_grad = lax.dot_general(
            grad_rows, value_rows, (((1,), (1,)), ((), ())), preferred_element_type=jnp.float32
        )
        inner = jnp.sum(probs * probs_grad, axis=-1, keepdims=True)
        score_grad = (probs * (probs_grad - inner)).astype(jnp.bfloat16)
        query_parts.append(
            jnp.dot(score_grad, key_rows, preferred_element_type=jnp.float32) * score_scale
        )
        key_grad = (
            key_grad
            + lax.dot_general(
                score_grad, rows_query, (((0,), (0,)), ((), ())), preferred_element_type=jnp.float32
            )
            * score_scale
        )
        value_grad = value_grad + lax.dot_general(
            probs.astype(jnp.bfloat16),
            grad_rows,
            (((0,), (0,)), ((), ())),
            preferred_element_type=jnp.float32,
        )
    return (
        jnp.concatenate(query_parts, 0).astype(jnp.bfloat16),
        key_grad.astype(jnp.bfloat16),
        value_grad.astype(jnp.bfloat16),
    )


def shards(
    tokens,
    cotangent,
    lengths,
    ln1_gain,
    ln1_bias,
    w_qkv,
    b_qv,
    w_o,
    b_o,
    ln2_gain,
    ln2_bias,
    w_in,
    b_in,
    w_out,
    b_out,
):
    row_count, seq_count, model_width = tokens.shape
    tensor_count = lax.axis_size("tensor")
    tensor_rank = lax.axis_index("tensor")
    seq_total = row_count * tensor_count
    local_heads = w_qkv.shape[2]
    head_size = w_qkv.shape[3]
    local_width = local_heads * head_size
    hidden = w_in.shape[1]
    block_rows = min(512, seq_total)
    score_scale = 1.0 / math.sqrt(head_size)
    group_count = lax.axis_size("group")
    group_rank = lax.axis_index("group")
    member = group_rank * lax.axis_size("dp") + lax.axis_index("dp")
    seq_lengths = lax.dynamic_slice_in_dim(lengths, member * seq_count, seq_count, 0)
    group_totals = jnp.sum(lengths.reshape(group_count, -1), axis=1).astype(jnp.float32)
    factor = (
        group_count
        * lax.dynamic_index_in_dim(group_totals, group_rank, 0, keepdims=False)
        / jnp.sum(group_totals)
    )
    inputs = tokens.astype(jnp.float32)
    normed_low = layer_norm(inputs, ln1_gain, ln1_bias).astype(jnp.bfloat16)
    normed_full = lax.all_gather(normed_low, "tensor", axis=0, tiled=True)
    joint_weight = w_qkv.reshape(model_width, 3 * local_width)
    projected = jnp.dot(
        normed_full.reshape(seq_total * seq_count, model_width),
        joint_weight,
        preferred_element_type=jnp.float32,
    )
    projected = projected.reshape(seq_total, seq_count, 3, local_width)
    query = (projected[:, :, 0] + b_qv[0]).astype(jnp.bfloat16)
    keys = projected[:, :, 1].astype(jnp.bfloat16)
    values = (projected[:, :, 2] + b_qv[1]).astype(jnp.bfloat16)

    def per_item(array):
        shaped = array.reshape(seq_total, seq_count, local_heads, head_size)
        return jnp.transpose(shaped, (1, 2, 0, 3)).reshape(
            seq_count * local_heads, seq_total, head_size
        )

    def per_row(array):
        shaped = array.reshape(seq_count, local_heads, seq_total, head_size)
        return jnp.transpose(shaped, (2, 0, 1, 3)).reshape(seq_total, seq_count, local_width)

    query_items = per_item(query)
    key_items = per_item(keys)
    value_items = per_item(values)
    item_lengths = jnp.repeat(seq_lengths, local_heads)
    heads_out, log_sums = lax.map(
        partial(attend_forward, block_rows=block_rows, score_scale=score_scale),
        (query_items, key_items, value_items, item_lengths),
    )
    attended = per_row(heads_out)
    out_weight = w_o.reshape(local_width, model_width)
    piece = attended
    attention = (
        lax.psum_scatter(
            jnp.einsum("rse,ed->rsd", piece, out_weight, preferred_element_type=jnp.float32),
            "tensor",
            scatter_dimension=0,
            tiled=True,
        )
        + b_o
    )
    middle = inputs + attention
    second_low = layer_norm(middle, ln2_gain, ln2_bias).astype(jnp.bfloat16)
    second_full = lax.all_gather(second_low, "tensor", axis=0, tiled=True)
    pre_act = (
        jnp.dot(
            second_full.reshape(seq_total * seq_count, model_width),
            w_in,
            preferred_element_type=jnp.float32,
        )
        + b_in
    )
    activated = gelu_tanh(pre_act).astype(jnp.bfloat16).reshape(seq_total, seq_count, hidden)
    piece = activated
    feed = (
        lax.psum_scatter(
            jnp.einsum("rsf,fd->rsd", piece, w_out, preferred_element_type=jnp.float32).astype(
                jnp.bfloat16
            ),
            "tensor",
            scatter_dimension=0,
            tiled=True,
        ).astype(jnp.float32)
        + b_out
    )
    output = (middle + feed).astype(jnp.bfloat16)
    positions = tensor_rank * row_count + jnp.arange(row_count, dtype=jnp.int32)
    live = positions[:, None] < seq_lengths[None, :]
    upstream = jnp.where(live[:, :, None], cotangent, jnp.zeros_like(cotangent))
    piece = lax.all_gather(upstream, "tensor", axis=0, tiled=True)
    weight_grad = jnp.einsum("rsf,rsd->fd", activated, piece, preferred_element_type=jnp.float32)
    part = jnp.einsum("rsd,fd->rsf", piece, w_out, preferred_element_type=jnp.float32)
    act_grad = part
    grad_w_out = weight_grad
    gelu_back = jax.vjp(gelu_tanh, pre_act)[1]
    pre_low = gelu_back(act_grad.reshape(seq_total * seq_count, hidden))[0].astype(jnp.bfloat16)
    grad_b_in = jnp.sum(pre_low, axis=0, dtype=jnp.float32)
    grad_w_in = jnp.einsum(
        "rd,rf->df",
        second_full.reshape(seq_total * seq_count, model_width),
        pre_low,
        preferred_element_type=jnp.float32,
    )
    pre_rows = pre_low.reshape(seq_total, seq_count, hidden)
    piece = pre_rows
    second_grad = lax.psum_scatter(
        jnp.einsum("rsf,df->rsd", piece, w_in, preferred_element_type=jnp.float32),
        "tensor",
        scatter_dimension=0,
        tiled=True,
    )
    norm_two_back = jax.vjp(layer_norm, middle, ln2_gain, ln2_bias)[1]
    middle_part, grad_ln2_gain, grad_ln2_bias = norm_two_back(second_grad)
    middle_grad = upstream.astype(jnp.float32) + middle_part
    branch_low = middle_grad.astype(jnp.bfloat16)
    grad_b_o = jnp.sum(branch_low, axis=(0, 1), dtype=jnp.float32)
    grad_b_out = jnp.sum(upstream, axis=(0, 1), dtype=jnp.float32)
    piece = lax.all_gather(branch_low, "tensor", axis=0, tiled=True)
    weight_grad = jnp.einsum("rse,rsd->ed", attended, piece, preferred_element_type=jnp.float32)
    part = jnp.einsum("rsd,ed->rse", piece, out_weight, preferred_element_type=jnp.float32)
    head_items = per_item(part.astype(jnp.bfloat16))
    grads_query, grads_keys, grads_values = lax.map(
        partial(attend_backward, block_rows=block_rows, score_scale=score_scale),
        (query_items, key_items, value_items, item_lengths, head_items, log_sums),
    )
    joint_grad = jnp.stack(
        (per_row(grads_query), per_row(grads_keys), per_row(grads_values)), axis=2
    )
    grad_b_qv = jnp.sum(joint_grad[:, :, 0::2], axis=(0, 1), dtype=jnp.float32)
    joint_rows = joint_grad.reshape(seq_total, seq_count, 3 * local_width)
    grad_w_qkv = jnp.einsum(
        "rd,rc->dc",
        normed_full.reshape(seq_total * seq_count, model_width),
        joint_rows.reshape(seq_total * seq_count, 3 * local_width),
        preferred_element_type=jnp.float32,
    )
    piece = joint_rows
    normed_grad = lax.psum_scatter(
        jnp.einsum("rsc,dc->rsd", piece, joint_weight, preferred_element_type=jnp.float32).astype(
            jnp.bfloat16
        ),
        "tensor",
        scatter_dimension=0,
        tiled=True,
    ).astype(jnp.float32)
    norm_one_back = jax.vjp(layer_norm, inputs, ln1_gain, ln1_bias)[1]
    input_part, grad_ln1_gain, grad_ln1_bias = norm_one_back(normed_grad)
    input_grad = (middle_grad + input_part).astype(jnp.bfloat16)
    summed = (
        halving_sum(grad_w_qkv.reshape(model_width, 3, local_heads, head_size) * factor, 0),
        halving_sum(weight_grad.reshape(local_heads, head_size, model_width) * factor, 2),
        halving_sum(grad_w_in * factor, 0),
        halving_sum(grad_w_out * factor, 1),
    )
    in_full = lax.dynamic_update_slice_in_dim(
        jnp.zeros((hidden * tensor_count,), jnp.float32), grad_b_in, tensor_rank * hidden, 0
    )
    joint_full = lax.dynamic_update_slice_in_dim(
        jnp.zeros((2, local_width * tensor_count), jnp.float32),
        grad_b_qv,
        tensor_rank * local_width,
        1,
    )
    shard_count = group_count * lax.axis_size("dp")
    vectors = (
        grad_ln1_gain,
        grad_ln1_bias,
        grad_b_o,
        grad_ln2_gain,
        grad_ln2_bias,
        grad_b_out,
        joint_full[0],
        joint_full[1],
        in_full,
    )
    pieces = [
        jnp.transpose(
            (item * factor).reshape(shard_count, tensor_count, -1), (1, 0, 2)
        )
        for item in vectors
    ]
    widths = [piece.shape[2] for piece in pieces]
    packed = jnp.concatenate(pieces, 2)
    packed = halving_steps(packed, 0, [("tensor", tensor_count, 8), ("tensor", tensor_count, 4),
                                       ("tensor", tensor_count, 2), ("tensor", tensor_count, 1)])
    packed = halving_steps(packed, 1, [("group", group_count, 2), ("group", group_count, 1),
                                       ("dp", lax.axis_size("dp"), 1)])
    flat = packed.reshape(-1)
    parts = []
    offset = 0
    for width in widths:
        parts.append(flat[offset : offset + width])
        offset += width
    return (
        output,
        input_grad,
        parts[0],
        parts[1],
        summed[0],
        jnp.stack((parts[6], parts[7])),
        summed[1],
        parts[2],
        parts[3],
        parts[4],
        summed[2],
        parts[8],
        summed[3],
        parts[5],
    )


def halving_steps(value, dim, steps, send_type=None):
    for axis, size, bit in steps:
        half = value.shape[dim] // 2
        low_half = lax.slice_in_dim(value, 0, half, axis=dim)
        high_half = lax.slice_in_dim(value, half, 2 * half, axis=dim)
        upper = (lax.axis_index(axis) // bit) % 2 == 1
        keep = jnp.where(upper, high_half, low_half)
        send = jnp.where(upper, low_half, high_half)
        if send_type is not None:
            send = send.astype(send_type)
        got = lax.ppermute(send, axis, [(i, i ^ bit) for i in range(size)])
        value = keep + got.astype(keep.dtype)
    return value


def halving_sum(value, dim):
    shape = value.shape
    groups = lax.axis_size("group")
    dps = lax.axis_size("dp")
    split = shape[:dim] + (groups * dps, shape[dim] // (groups * dps)) + shape[dim + 1 :]
    value = value.reshape(split)
    value = halving_steps(
        value, dim, [("group", groups, 2), ("group", groups, 1), ("dp", dps, 1)], jnp.bfloat16
    )
    return value.reshape(shape[:dim] + (shape[dim] // (groups * dps),) + shape[dim + 1 :])


def solution(mesh):
    in_specs = (
        P("tensor", ("group", "dp"), None),
        P("tensor", ("group", "dp"), None),
        P(),
        P(),
        P(),
        P(None, None, "tensor", None),
        P(None, "tensor"),
        P("tensor", None, None),
        P(),
        P(),
        P(),
        P(None, "tensor"),
        P("tensor"),
        P("tensor", None),
        P(),
    )
    out_specs = (
        P("tensor", ("group", "dp"), None),
        P("tensor", ("group", "dp"), None),
        P(("group", "dp", "tensor")),
        P(("group", "dp", "tensor")),
        P(("group", "dp"), None, "tensor", None),
        P(None, ("group", "dp", "tensor")),
        P("tensor", None, ("group", "dp")),
        P(("group", "dp", "tensor")),
        P(("group", "dp", "tensor")),
        P(("group", "dp", "tensor")),
        P(("group", "dp"), "tensor"),
        P(("group", "dp", "tensor")),
        P("tensor", ("group", "dp")),
        P(("group", "dp", "tensor")),
    )
    return jax.shard_map(shards, mesh=mesh, in_specs=in_specs, out_specs=out_specs, check_vma=False)
```

```python
from functools import partial
import math

import jax
import jax.numpy as jnp
from jax import lax
from jax.sharding import PartitionSpec as P

EPS = 1e-05
NEGATIVE = -1e30


def layer_norm(value, gain, shift):
    mean = jnp.mean(value, axis=-1, keepdims=True)
    centred = value - mean
    spread = jnp.mean(centred * centred, axis=-1, keepdims=True)
    return centred * lax.rsqrt(spread + EPS) * gain + shift


def gelu_tanh(value):
    return jax.nn.gelu(value, approximate=True)


def block_scores(rows_query, key_rows, first, length, score_scale):
    count = rows_query.shape[0]
    key_pos = jnp.arange(key_rows.shape[0], dtype=jnp.int32)
    query_pos = first + jnp.arange(count, dtype=jnp.int32)
    valid = (key_pos[None, :] <= query_pos[:, None]) & (key_pos[None, :] < length)
    scores = (
        lax.dot_general(
            rows_query, key_rows, (((1,), (1,)), ((), ())), preferred_element_type=jnp.float32
        )
        * score_scale
    )
    return (jnp.where(valid, scores, NEGATIVE), valid)


def attend_forward(item, block_rows, score_scale):
    query, key_rows, value_rows, length = item
    outputs = []
    log_parts = []
    for first in range(0, query.shape[0], block_rows):
        rows_query = query[first : first + block_rows]
        scores, valid = block_scores(rows_query, key_rows, first, length, score_scale)
        peak = jnp.max(scores, axis=-1, keepdims=True)
        expo = jnp.exp(scores - peak)
        weight_sum = jnp.sum(expo, axis=-1, keepdims=True)
        probs = (expo / weight_sum).astype(jnp.bfloat16)
        outputs.append(
            jnp.dot(probs, value_rows, preferred_element_type=jnp.float32).astype(jnp.bfloat16)
        )
        log_parts.append((peak + jnp.log(weight_sum))[:, 0])
    return (jnp.concatenate(outputs, 0), jnp.concatenate(log_parts, 0))


def attend_backward(item, block_rows, score_scale):
    query, key_rows, value_rows, length, grad_out, log_sums = item
    key_grad = jnp.zeros(key_rows.shape, jnp.float32)
    value_grad = jnp.zeros(value_rows.shape, jnp.float32)
    query_parts = []
    for first in range(0, query.shape[0], block_rows):
        rows_query = query[first : first + block_rows]
        scores, valid = block_scores(rows_query, key_rows, first, length, score_scale)
        probs = jnp.where(valid, jnp.exp(scores - log_sums[first : first + block_rows, None]), 0.0)
        grad_rows = grad_out[first : first + block_rows]
        probs_grad = lax.dot_general(
            grad_rows, value_rows, (((1,), (1,)), ((), ())), preferred_element_type=jnp.float32
        )
        inner = jnp.sum(probs * probs_grad, axis=-1, keepdims=True)
        score_grad = (probs * (probs_grad - inner)).astype(jnp.bfloat16)
        query_parts.append(
            jnp.dot(score_grad, key_rows, preferred_element_type=jnp.float32) * score_scale
        )
        key_grad = (
            key_grad
            + lax.dot_general(
                score_grad, rows_query, (((0,), (0,)), ((), ())), preferred_element_type=jnp.float32
            )
            * score_scale
        )
        value_grad = value_grad + lax.dot_general(
            probs.astype(jnp.bfloat16),
            grad_rows,
            (((0,), (0,)), ((), ())),
            preferred_element_type=jnp.float32,
        )
    return (
        jnp.concatenate(query_parts, 0).astype(jnp.bfloat16),
        key_grad.astype(jnp.bfloat16),
        value_grad.astype(jnp.bfloat16),
    )


def shards(
    tokens,
    cotangent,
    lengths,
    ln1_gain,
    ln1_bias,
    w_qkv,
    b_qv,
    w_o,
    b_o,
    ln2_gain,
    ln2_bias,
    w_in,
    b_in,
    w_out,
    b_out,
):
    row_count, seq_count, model_width = tokens.shape
    tensor_count = lax.axis_size("tensor")
    tensor_rank = lax.axis_index("tensor")
    seq_total = row_count * tensor_count
    local_heads = w_qkv.shape[2]
    head_size = w_qkv.shape[3]
    local_width = local_heads * head_size
    hidden = w_in.shape[1]
    block_rows = min(512, seq_total)
    score_scale = 1.0 / math.sqrt(head_size)
    group_count = lax.axis_size("group")
    group_rank = lax.axis_index("group")
    member = group_rank * lax.axis_size("dp") + lax.axis_index("dp")
    seq_lengths = lax.dynamic_slice_in_dim(lengths, member * seq_count, seq_count, 0)
    group_totals = jnp.sum(lengths.reshape(group_count, -1), axis=1).astype(jnp.float32)
    factor = (
        group_count
        * lax.dynamic_index_in_dim(group_totals, group_rank, 0, keepdims=False)
        / jnp.sum(group_totals)
    )
    inputs = tokens.astype(jnp.float32)
    normed_low = layer_norm(inputs, ln1_gain, ln1_bias).astype(jnp.bfloat16)
    normed_full = lax.all_gather(normed_low, "tensor", axis=0, tiled=True)
    joint_weight = w_qkv.reshape(model_width, 3 * local_width)
    projected = jnp.dot(
        normed_full.reshape(seq_total * seq_count, model_width),
        joint_weight,
        preferred_element_type=jnp.float32,
    )
    projected = projected.reshape(seq_total, seq_count, 3, local_width)
    query = (projected[:, :, 0] + b_qv[0]).astype(jnp.bfloat16)
    keys = projected[:, :, 1].astype(jnp.bfloat16)
    values = (projected[:, :, 2] + b_qv[1]).astype(jnp.bfloat16)

    def per_item(array):
        shaped = array.reshape(seq_total, seq_count, local_heads, head_size)
        return jnp.transpose(shaped, (1, 2, 0, 3)).reshape(
            seq_count * local_heads, seq_total, head_size
        )

    def per_row(array):
        shaped = array.reshape(seq_count, local_heads, seq_total, head_size)
        return jnp.transpose(shaped, (2, 0, 1, 3)).reshape(seq_total, seq_count, local_width)

    query_items = per_item(query)
    key_items = per_item(keys)
    value_items = per_item(values)
    item_lengths = jnp.repeat(seq_lengths, local_heads)
    heads_out, log_sums = lax.map(
        partial(attend_forward, block_rows=block_rows, score_scale=score_scale),
        (query_items, key_items, value_items, item_lengths),
    )
    attended = per_row(heads_out)
    out_weight = w_o.reshape(local_width, model_width)
    positions = tensor_rank * row_count + jnp.arange(row_count, dtype=jnp.int32)
    live = positions[:, None] < seq_lengths[None, :]
    upstream = jnp.where(live[:, :, None], cotangent, jnp.zeros_like(cotangent))
    upstream_full = lax.all_gather(upstream, "tensor", axis=0, tiled=True)
    attention_part = jnp.einsum(
        "rse,ed->rsd", attended, out_weight, preferred_element_type=jnp.float32
    ).astype(jnp.bfloat16)
    attention_part, upstream_full = lax.optimization_barrier((attention_part, upstream_full))
    attention = (
        lax.psum_scatter(attention_part, "tensor", scatter_dimension=0, tiled=True).astype(
            jnp.float32
        )
        + b_o
    )
    middle = inputs + attention
    second_low = layer_norm(middle, ln2_gain, ln2_bias).astype(jnp.bfloat16)
    second_full = lax.all_gather(second_low, "tensor", axis=0, tiled=True)
    pre_act = (
        jnp.dot(
            second_full.reshape(seq_total * seq_count, model_width),
            w_in,
            preferred_element_type=jnp.float32,
        )
        + b_in
    )
    activated = gelu_tanh(pre_act).astype(jnp.bfloat16).reshape(seq_total, seq_count, hidden)
    feed_part = jnp.einsum(
        "rsf,fd->rsd", activated, w_out, preferred_element_type=jnp.float32
    ).astype(jnp.bfloat16)
    piece = upstream_full
    weight_grad = jnp.einsum("rsf,rsd->fd", activated, piece, preferred_element_type=jnp.float32)
    part = jnp.einsum("rsd,fd->rsf", piece, w_out, preferred_element_type=jnp.float32)
    act_grad = part
    grad_w_out = weight_grad
    gelu_back = jax.vjp(gelu_tanh, pre_act)[1]
    pre_low = gelu_back(act_grad.reshape(seq_total * seq_count, hidden))[0].astype(jnp.bfloat16)
    grad_b_in = jnp.sum(pre_low, axis=0, dtype=jnp.float32)
    grad_w_in = jnp.einsum(
        "rd,rf->df",
        second_full.reshape(seq_total * seq_count, model_width),
        pre_low,
        preferred_element_type=jnp.float32,
    )
    pre_rows = pre_low.reshape(seq_total, seq_count, hidden)
    piece = pre_rows
    second_grad = lax.psum_scatter(
        jnp.einsum("rsf,df->rsd", piece, w_in, preferred_element_type=jnp.float32).astype(
            jnp.bfloat16
        ),
        "tensor",
        scatter_dimension=0,
        tiled=True,
    ).astype(jnp.float32)
    norm_two_back = jax.vjp(layer_norm, middle, ln2_gain, ln2_bias)[1]
    middle_part, grad_ln2_gain, grad_ln2_bias = norm_two_back(second_grad)
    middle_grad = upstream.astype(jnp.float32) + middle_part
    branch_low = middle_grad.astype(jnp.bfloat16)
    grad_b_o = jnp.sum(branch_low, axis=(0, 1), dtype=jnp.float32)
    grad_b_out = jnp.sum(upstream, axis=(0, 1), dtype=jnp.float32)
    piece = lax.all_gather(branch_low, "tensor", axis=0, tiled=True)
    feed_part, piece = lax.optimization_barrier((feed_part, piece))
    feed = (
        lax.psum_scatter(feed_part, "tensor", scatter_dimension=0, tiled=True).astype(
            jnp.float32
        )
        + b_out
    )
    output = (middle + feed).astype(jnp.bfloat16)
    weight_grad = jnp.einsum("rse,rsd->ed", attended, piece, preferred_element_type=jnp.float32)
    part = jnp.einsum("rsd,ed->rse", piece, out_weight, preferred_element_type=jnp.float32)
    head_items = per_item(part.astype(jnp.bfloat16))
    grads_query, grads_keys, grads_values = lax.map(
        partial(attend_backward, block_rows=block_rows, score_scale=score_scale),
        (query_items, key_items, value_items, item_lengths, head_items, log_sums),
    )
    joint_grad = jnp.stack(
        (per_row(grads_query), per_row(grads_keys), per_row(grads_values)), axis=2
    )
    grad_b_qv = jnp.sum(joint_grad[:, :, 0::2], axis=(0, 1), dtype=jnp.float32)
    joint_rows = joint_grad.reshape(seq_total, seq_count, 3 * local_width)
    grad_w_qkv = jnp.einsum(
        "rd,rc->dc",
        normed_full.reshape(seq_total * seq_count, model_width),
        joint_rows.reshape(seq_total * seq_count, 3 * local_width),
        preferred_element_type=jnp.float32,
    )
    piece = joint_rows
    normed_grad = lax.psum_scatter(
        jnp.einsum("rsc,dc->rsd", piece, joint_weight, preferred_element_type=jnp.float32).astype(
            jnp.bfloat16
        ),
        "tensor",
        scatter_dimension=0,
        tiled=True,
    ).astype(jnp.float32)
    norm_one_back = jax.vjp(layer_norm, inputs, ln1_gain, ln1_bias)[1]
    input_part, grad_ln1_gain, grad_ln1_bias = norm_one_back(normed_grad)
    input_grad = (middle_grad + input_part).astype(jnp.bfloat16)
    summed = (
        halving_sum(grad_w_qkv.reshape(model_width, 3, local_heads, head_size) * factor, 0),
        halving_sum(weight_grad.reshape(local_heads, head_size, model_width) * factor, 2),
        halving_sum(grad_w_in * factor, 0),
        halving_sum(grad_w_out * factor, 1),
    )
    in_full = lax.dynamic_update_slice_in_dim(
        jnp.zeros((hidden * tensor_count,), jnp.float32), grad_b_in, tensor_rank * hidden, 0
    )
    joint_full = lax.dynamic_update_slice_in_dim(
        jnp.zeros((2, local_width * tensor_count), jnp.float32),
        grad_b_qv,
        tensor_rank * local_width,
        1,
    )
    shard_count = group_count * lax.axis_size("dp")
    vectors = (
        grad_ln1_gain,
        grad_ln1_bias,
        grad_b_o,
        grad_ln2_gain,
        grad_ln2_bias,
        grad_b_out,
        joint_full[0],
        joint_full[1],
        in_full,
    )
    pieces = [
        jnp.transpose(
            (item * factor).reshape(shard_count, tensor_count, -1), (1, 0, 2)
        )
        for item in vectors
    ]
    widths = [piece.shape[2] for piece in pieces]
    packed = jnp.concatenate(pieces, 2)
    packed = halving_steps(packed, 0, [("tensor", tensor_count, 8), ("tensor", tensor_count, 4),
                                       ("tensor", tensor_count, 2), ("tensor", tensor_count, 1)])
    packed = halving_steps(packed, 1, [("group", group_count, 2), ("group", group_count, 1),
                                       ("dp", lax.axis_size("dp"), 1)])
    flat = packed.reshape(-1)
    parts = []
    offset = 0
    for width in widths:
        parts.append(flat[offset : offset + width])
        offset += width
    return (
        output,
        input_grad,
        parts[0],
        parts[1],
        summed[0],
        jnp.stack((parts[6], parts[7])),
        summed[1],
        parts[2],
        parts[3],
        parts[4],
        summed[2],
        parts[8],
        summed[3],
        parts[5],
    )


def halving_steps(value, dim, steps, send_type=None):
    for axis, size, bit in steps:
        half = value.shape[dim] // 2
        low_half = lax.slice_in_dim(value, 0, half, axis=dim)
        high_half = lax.slice_in_dim(value, half, 2 * half, axis=dim)
        upper = (lax.axis_index(axis) // bit) % 2 == 1
        keep = jnp.where(upper, high_half, low_half)
        send = jnp.where(upper, low_half, high_half)
        if send_type is not None:
            send = send.astype(send_type)
        got = lax.ppermute(send, axis, [(i, i ^ bit) for i in range(size)])
        value = keep + got.astype(keep.dtype)
    return value


def halving_sum(value, dim):
    shape = value.shape
    groups = lax.axis_size("group")
    dps = lax.axis_size("dp")
    split = shape[:dim] + (groups * dps, shape[dim] // (groups * dps)) + shape[dim + 1 :]
    value = value.reshape(split)
    value = halving_steps(
        value, dim, [("group", groups, 2), ("group", groups, 1), ("dp", dps, 1)], jnp.bfloat16
    )
    return value.reshape(shape[:dim] + (shape[dim] // (groups * dps),) + shape[dim + 1 :])


def solution(mesh):
    in_specs = (
        P("tensor", ("group", "dp"), None),
        P("tensor", ("group", "dp"), None),
        P(),
        P(),
        P(),
        P(None, None, "tensor", None),
        P(None, "tensor"),
        P("tensor", None, None),
        P(),
        P(),
        P(),
        P(None, "tensor"),
        P("tensor"),
        P("tensor", None),
        P(),
    )
    out_specs = (
        P("tensor", ("group", "dp"), None),
        P("tensor", ("group", "dp"), None),
        P(("group", "dp", "tensor")),
        P(("group", "dp", "tensor")),
        P(("group", "dp"), None, "tensor", None),
        P(None, ("group", "dp", "tensor")),
        P("tensor", None, ("group", "dp")),
        P(("group", "dp", "tensor")),
        P(("group", "dp", "tensor")),
        P(("group", "dp", "tensor")),
        P(("group", "dp"), "tensor"),
        P(("group", "dp", "tensor")),
        P("tensor", ("group", "dp")),
        P(("group", "dp", "tensor")),
    )
    return jax.shard_map(shards, mesh=mesh, in_specs=in_specs, out_specs=out_specs, check_vma=False)
```

```python
from functools import partial
import math

import jax
import jax.numpy as jnp
from jax import lax
from jax.experimental import pallas as pl
from jax.experimental.pallas import tpu as pltpu
from jax.sharding import PartitionSpec as P

EPS = 1e-05
NEGATIVE = -1e30


def layer_norm(value, gain, shift):
    mean = jnp.mean(value, axis=-1, keepdims=True)
    centred = value - mean
    spread = jnp.mean(centred * centred, axis=-1, keepdims=True)
    return centred * lax.rsqrt(spread + EPS) * gain + shift


def gelu_tanh(value):
    return jax.nn.gelu(value, approximate=True)


def _valid(first_q, first_k, rows, cols, length):
    q_pos = first_q + lax.broadcasted_iota(jnp.int32, (rows, cols), 0)
    k_pos = first_k + lax.broadcasted_iota(jnp.int32, (rows, cols), 1)
    return (k_pos <= q_pos) & (k_pos < length)


def _key_blocks(i, block_q, block_k, length):
    causal = (i * block_q + block_q + block_k - 1) // block_k
    live = (length + block_k - 1) // block_k
    return jnp.minimum(causal, live)


def _attn_fwd_kernel(len_ref, q_ref, k_ref, v_ref, o_ref, lse_ref, s_buf, *, block_q, block_k, scale):
    i = pl.program_id(0)
    length = len_ref[0]
    count = _key_blocks(i, block_q, block_k, length)
    q = q_ref[...]

    def scores(j, m):
        first = pl.multiple_of(j * block_k, block_k)
        k = k_ref[pl.ds(first, block_k), :]
        s = lax.dot_general(q, k, (((1,), (1,)), ((), ())), preferred_element_type=jnp.float32)
        s = jnp.where(_valid(i * block_q, first, block_q, block_k, length), s * scale, NEGATIVE)
        s_buf[:, pl.ds(first, block_k)] = s
        return jnp.maximum(m, jnp.max(s, axis=1, keepdims=True))

    peak = lax.fori_loop(0, count, scores, jnp.full((block_q, 1), NEGATIVE, jnp.float32))

    def exps(j, total):
        first = pl.multiple_of(j * block_k, block_k)
        e = jnp.exp(s_buf[:, pl.ds(first, block_k)] - peak)
        s_buf[:, pl.ds(first, block_k)] = e
        return total + jnp.sum(e, axis=1, keepdims=True)

    total = lax.fori_loop(0, count, exps, jnp.zeros((block_q, 1), jnp.float32))

    def mix(j, acc):
        first = pl.multiple_of(j * block_k, block_k)
        probs = (s_buf[:, pl.ds(first, block_k)] / total).astype(jnp.bfloat16)
        return acc + jnp.dot(probs, v_ref[pl.ds(first, block_k), :], preferred_element_type=jnp.float32)

    acc = lax.fori_loop(0, count, mix, jnp.zeros(o_ref.shape, jnp.float32))
    o_ref[...] = acc.astype(o_ref.dtype)
    lse_ref[...] = peak + jnp.log(total)


def attention_forward(q, k, v, length, *, block_q=256, block_k=256):
    n, d = q.shape
    scale = 1.0 / math.sqrt(d)
    kernel = partial(_attn_fwd_kernel, block_q=block_q, block_k=block_k, scale=scale)
    pairs = (n // block_q) * (n // block_k + 1) // 2
    return pl.pallas_call(
        kernel,
        out_shape=(jax.ShapeDtypeStruct((n, d), jnp.bfloat16), jax.ShapeDtypeStruct((n, 1), jnp.float32)),
        grid_spec=pltpu.PrefetchScalarGridSpec(
            num_scalar_prefetch=1,
            grid=(n // block_q,),
            in_specs=[
                pl.BlockSpec((block_q, d), lambda i, lens: (i, 0)),
                pl.BlockSpec((n, d), lambda i, lens: (0, 0)),
                pl.BlockSpec((n, d), lambda i, lens: (0, 0)),
            ],
            out_specs=[
                pl.BlockSpec((block_q, d), lambda i, lens: (i, 0)),
                pl.BlockSpec((block_q, 1), lambda i, lens: (i, 0)),
            ],
            scratch_shapes=[pltpu.VMEM((block_q, n), jnp.float32)],
        ),
        compiler_params=pltpu.CompilerParams(dimension_semantics=("arbitrary",)),
        cost_estimate=pl.CostEstimate(
            flops=4 * pairs * block_q * block_k * d,
            transcendentals=pairs * block_q * block_k,
            bytes_accessed=4 * n * d * 2,
        ),
    )(length, q, k, v)


def _attn_bwd_kernel(len_ref, q_ref, k_ref, v_ref, do_ref, lse_ref, dq_ref, dk_ref, dv_ref,
                     p_buf, dp_buf, dk_acc, dv_acc, *, block_q, block_k, scale):
    i = pl.program_id(0)
    length = len_ref[0]

    @pl.when(i == 0)
    def _():
        dk_acc[...] = jnp.zeros_like(dk_acc)
        dv_acc[...] = jnp.zeros_like(dv_acc)

    live = i * block_q < length

    @pl.when(live)
    def _():
        count = _key_blocks(i, block_q, block_k, length)
        q = q_ref[...]
        do = do_ref[...]
        lse = lse_ref[...]

        def first_pass(j, inner):
            first = pl.multiple_of(j * block_k, block_k)
            k = k_ref[pl.ds(first, block_k), :]
            v = v_ref[pl.ds(first, block_k), :]
            s = lax.dot_general(q, k, (((1,), (1,)), ((), ())), preferred_element_type=jnp.float32)
            valid = _valid(i * block_q, first, block_q, block_k, length)
            s = jnp.where(valid, s * scale, NEGATIVE)
            p = jnp.where(valid, jnp.exp(s - lse), 0.0)
            dp = lax.dot_general(do, v, (((1,), (1,)), ((), ())), preferred_element_type=jnp.float32)
            p_buf[:, pl.ds(first, block_k)] = p
            dp_buf[:, pl.ds(first, block_k)] = dp
            return inner + jnp.sum(p * dp, axis=1, keepdims=True)

        inner = lax.fori_loop(0, count, first_pass, jnp.zeros((block_q, 1), jnp.float32))

        def second_pass(j, dq):
            first = pl.multiple_of(j * block_k, block_k)
            p = p_buf[:, pl.ds(first, block_k)]
            dp = dp_buf[:, pl.ds(first, block_k)]
            ds = (p * (dp - inner)).astype(jnp.bfloat16)
            k = k_ref[pl.ds(first, block_k), :]
            dk_acc[pl.ds(first, block_k), :] += lax.dot_general(
                ds, q, (((0,), (0,)), ((), ())), preferred_element_type=jnp.float32)
            dv_acc[pl.ds(first, block_k), :] += lax.dot_general(
                p.astype(jnp.bfloat16), do, (((0,), (0,)), ((), ())), preferred_element_type=jnp.float32)
            return dq + jnp.dot(ds, k, preferred_element_type=jnp.float32)

        dq = lax.fori_loop(0, count, second_pass, jnp.zeros(dq_ref.shape, jnp.float32))
        dq_ref[...] = (dq * scale).astype(dq_ref.dtype)

    @pl.when(jnp.logical_not(live))
    def _():
        dq_ref[...] = jnp.zeros_like(dq_ref)

    @pl.when(i == pl.num_programs(0) - 1)
    def _():
        dk_ref[...] = (dk_acc[...] * scale).astype(dk_ref.dtype)
        dv_ref[...] = dv_acc[...].astype(dv_ref.dtype)


def attention_backward(q, k, v, do, lse, length, *, block_q=256, block_k=256):
    n, d = q.shape
    scale = 1.0 / math.sqrt(d)
    kernel = partial(_attn_bwd_kernel, block_q=block_q, block_k=block_k, scale=scale)
    pairs = (n // block_q) * (n // block_k + 1) // 2
    full = pl.BlockSpec((n, d), lambda i, lens: (0, 0))
    rows = pl.BlockSpec((block_q, d), lambda i, lens: (i, 0))
    return pl.pallas_call(
        kernel,
        out_shape=tuple(jax.ShapeDtypeStruct((n, d), jnp.bfloat16) for _ in range(3)),
        grid_spec=pltpu.PrefetchScalarGridSpec(
            num_scalar_prefetch=1,
            grid=(n // block_q,),
            in_specs=[rows, full, full, rows, pl.BlockSpec((block_q, 1), lambda i, lens: (i, 0))],
            out_specs=[rows, full, full],
            scratch_shapes=[
                pltpu.VMEM((block_q, n), jnp.float32),
                pltpu.VMEM((block_q, n), jnp.float32),
                pltpu.VMEM((n, d), jnp.float32),
                pltpu.VMEM((n, d), jnp.float32),
            ],
        ),
        compiler_params=pltpu.CompilerParams(dimension_semantics=("arbitrary",)),
        cost_estimate=pl.CostEstimate(
            flops=8 * pairs * block_q * block_k * d,
            transcendentals=pairs * block_q * block_k,
            bytes_accessed=8 * n * d * 2,
        ),
    )(length, q, k, v, do, lse)


def shards(
    tokens,
    cotangent,
    lengths,
    ln1_gain,
    ln1_bias,
    w_qkv,
    b_qv,
    w_o,
    b_o,
    ln2_gain,
    ln2_bias,
    w_in,
    b_in,
    w_out,
    b_out,
):
    row_count, seq_count, model_width = tokens.shape
    tensor_count = lax.axis_size("tensor")
    tensor_rank = lax.axis_index("tensor")
    seq_total = row_count * tensor_count
    local_heads = w_qkv.shape[2]
    head_size = w_qkv.shape[3]
    local_width = local_heads * head_size
    hidden = w_in.shape[1]
    group_count = lax.axis_size("group")
    group_rank = lax.axis_index("group")
    member = group_rank * lax.axis_size("dp") + lax.axis_index("dp")
    seq_lengths = lax.dynamic_slice_in_dim(lengths, member * seq_count, seq_count, 0)
    group_totals = jnp.sum(lengths.reshape(group_count, -1), axis=1).astype(jnp.float32)
    factor = (
        group_count
        * lax.dynamic_index_in_dim(group_totals, group_rank, 0, keepdims=False)
        / jnp.sum(group_totals)
    )
    inputs = tokens.astype(jnp.float32)
    normed_low = layer_norm(inputs, ln1_gain, ln1_bias).astype(jnp.bfloat16)
    normed_full = lax.all_gather(normed_low, "tensor", axis=0, tiled=True)
    joint_weight = w_qkv.reshape(model_width, 3 * local_width)
    projected = jnp.dot(
        normed_full.reshape(seq_total * seq_count, model_width),
        joint_weight,
        preferred_element_type=jnp.float32,
    )
    projected = projected.reshape(seq_total, seq_count, 3, local_width)
    query = (projected[:, :, 0] + b_qv[0]).astype(jnp.bfloat16)
    keys = projected[:, :, 1].astype(jnp.bfloat16)
    values = (projected[:, :, 2] + b_qv[1]).astype(jnp.bfloat16)

    def item(array, s, h):
        return array[:, s, h * head_size : (h + 1) * head_size]

    def per_row(items):
        stacked = jnp.stack(items).reshape(seq_count, local_heads, seq_total, head_size)
        return jnp.transpose(stacked, (2, 0, 1, 3)).reshape(seq_total, seq_count, local_width)

    pairs = [(s, h) for s in range(seq_count) for h in range(local_heads)]
    forward_items = [
        attention_forward(
            item(query, s, h), item(keys, s, h), item(values, s, h), seq_lengths[s : s + 1]
        )
        for s, h in pairs
    ]
    attended = per_row([o for o, _ in forward_items])
    out_weight = w_o.reshape(local_width, model_width)
    positions = tensor_rank * row_count + jnp.arange(row_count, dtype=jnp.int32)
    live = positions[:, None] < seq_lengths[None, :]
    upstream = jnp.where(live[:, :, None], cotangent, jnp.zeros_like(cotangent))
    upstream_full = lax.all_gather(upstream, "tensor", axis=0, tiled=True)
    attention_part = jnp.einsum(
        "rse,ed->rsd", attended, out_weight, preferred_element_type=jnp.float32
    ).astype(jnp.bfloat16)
    attention_part, upstream_full = lax.optimization_barrier((attention_part, upstream_full))
    attention = (
        lax.psum_scatter(attention_part, "tensor", scatter_dimension=0, tiled=True).astype(
            jnp.float32
        )
        + b_o
    )
    middle = inputs + attention
    second_low = layer_norm(middle, ln2_gain, ln2_bias).astype(jnp.bfloat16)
    second_full = lax.all_gather(second_low, "tensor", axis=0, tiled=True)
    pre_act = (
        jnp.dot(
            second_full.reshape(seq_total * seq_count, model_width),
            w_in,
            preferred_element_type=jnp.float32,
        )
        + b_in
    )
    activated = gelu_tanh(pre_act).astype(jnp.bfloat16).reshape(seq_total, seq_count, hidden)
    feed_part = jnp.einsum(
        "rsf,fd->rsd", activated, w_out, preferred_element_type=jnp.float32
    ).astype(jnp.bfloat16)
    piece = upstream_full
    weight_grad = jnp.einsum("rsf,rsd->fd", activated, piece, preferred_element_type=jnp.float32)
    part = jnp.einsum("rsd,fd->rsf", piece, w_out, preferred_element_type=jnp.float32)
    act_grad = part
    grad_w_out = weight_grad
    gelu_back = jax.vjp(gelu_tanh, pre_act)[1]
    pre_low = gelu_back(act_grad.reshape(seq_total * seq_count, hidden))[0].astype(jnp.bfloat16)
    grad_b_in = jnp.sum(pre_low, axis=0, dtype=jnp.float32)
    grad_w_in = jnp.einsum(
        "rd,rf->df",
        second_full.reshape(seq_total * seq_count, model_width),
        pre_low,
        preferred_element_type=jnp.float32,
    )
    pre_rows = pre_low.reshape(seq_total, seq_count, hidden)
    piece = pre_rows
    second_grad = lax.psum_scatter(
        jnp.einsum("rsf,df->rsd", piece, w_in, preferred_element_type=jnp.float32).astype(
            jnp.bfloat16
        ),
        "tensor",
        scatter_dimension=0,
        tiled=True,
    ).astype(jnp.float32)
    norm_two_back = jax.vjp(layer_norm, middle, ln2_gain, ln2_bias)[1]
    middle_part, grad_ln2_gain, grad_ln2_bias = norm_two_back(second_grad)
    middle_grad = upstream.astype(jnp.float32) + middle_part
    branch_low = middle_grad.astype(jnp.bfloat16)
    grad_b_o = jnp.sum(branch_low, axis=(0, 1), dtype=jnp.float32)
    grad_b_out = jnp.sum(upstream, axis=(0, 1), dtype=jnp.float32)
    piece = lax.all_gather(branch_low, "tensor", axis=0, tiled=True)
    feed_part, piece = lax.optimization_barrier((feed_part, piece))
    feed = (
        lax.psum_scatter(feed_part, "tensor", scatter_dimension=0, tiled=True).astype(
            jnp.float32
        )
        + b_out
    )
    output = (middle + feed).astype(jnp.bfloat16)
    weight_grad = jnp.einsum("rse,rsd->ed", attended, piece, preferred_element_type=jnp.float32)
    part = jnp.einsum("rsd,ed->rse", piece, out_weight, preferred_element_type=jnp.float32)
    attended_grad = part.astype(jnp.bfloat16)
    backward_items = [
        attention_backward(
            item(query, s, h),
            item(keys, s, h),
            item(values, s, h),
            item(attended_grad, s, h),
            lse,
            seq_lengths[s : s + 1],
        )
        for (s, h), (_, lse) in zip(pairs, forward_items)
    ]
    joint_grad = jnp.stack(
        [per_row([grads[kind] for grads in backward_items]) for kind in range(3)], axis=2
    )
    grad_b_qv = jnp.sum(joint_grad[:, :, 0::2], axis=(0, 1), dtype=jnp.float32)
    joint_rows = joint_grad.reshape(seq_total, seq_count, 3 * local_width)
    grad_w_qkv = jnp.einsum(
        "rd,rc->dc",
        normed_full.reshape(seq_total * seq_count, model_width),
        joint_rows.reshape(seq_total * seq_count, 3 * local_width),
        preferred_element_type=jnp.float32,
    )
    piece = joint_rows
    normed_grad = lax.psum_scatter(
        jnp.einsum("rsc,dc->rsd", piece, joint_weight, preferred_element_type=jnp.float32).astype(
            jnp.bfloat16
        ),
        "tensor",
        scatter_dimension=0,
        tiled=True,
    ).astype(jnp.float32)
    norm_one_back = jax.vjp(layer_norm, inputs, ln1_gain, ln1_bias)[1]
    input_part, grad_ln1_gain, grad_ln1_bias = norm_one_back(normed_grad)
    input_grad = (middle_grad + input_part).astype(jnp.bfloat16)
    summed = (
        halving_sum(grad_w_qkv.reshape(model_width, 3, local_heads, head_size) * factor, 0),
        halving_sum(weight_grad.reshape(local_heads, head_size, model_width) * factor, 2),
        halving_sum(grad_w_in * factor, 0),
        halving_sum(grad_w_out * factor, 1),
    )
    in_full = lax.dynamic_update_slice_in_dim(
        jnp.zeros((hidden * tensor_count,), jnp.float32), grad_b_in, tensor_rank * hidden, 0
    )
    joint_full = lax.dynamic_update_slice_in_dim(
        jnp.zeros((2, local_width * tensor_count), jnp.float32),
        grad_b_qv,
        tensor_rank * local_width,
        1,
    )
    shard_count = group_count * lax.axis_size("dp")
    vectors = (
        grad_ln1_gain,
        grad_ln1_bias,
        grad_b_o,
        grad_ln2_gain,
        grad_ln2_bias,
        grad_b_out,
        joint_full[0],
        joint_full[1],
        in_full,
    )
    pieces = [
        jnp.transpose(
            (item * factor).reshape(shard_count, tensor_count, -1), (1, 0, 2)
        )
        for item in vectors
    ]
    widths = [piece.shape[2] for piece in pieces]
    packed = jnp.concatenate(pieces, 2)
    packed = halving_steps(packed, 0, [("tensor", tensor_count, 8), ("tensor", tensor_count, 4),
                                       ("tensor", tensor_count, 2), ("tensor", tensor_count, 1)])
    packed = halving_steps(packed, 1, [("group", group_count, 2), ("group", group_count, 1),
                                       ("dp", lax.axis_size("dp"), 1)])
    flat = packed.reshape(-1)
    parts = []
    offset = 0
    for width in widths:
        parts.append(flat[offset : offset + width])
        offset += width
    return (
        output,
        input_grad,
        parts[0],
        parts[1],
        summed[0],
        jnp.stack((parts[6], parts[7])),
        summed[1],
        parts[2],
        parts[3],
        parts[4],
        summed[2],
        parts[8],
        summed[3],
        parts[5],
    )


def halving_steps(value, dim, steps, send_type=None):
    for axis, size, bit in steps:
        half = value.shape[dim] // 2
        low_half = lax.slice_in_dim(value, 0, half, axis=dim)
        high_half = lax.slice_in_dim(value, half, 2 * half, axis=dim)
        upper = (lax.axis_index(axis) // bit) % 2 == 1
        keep = jnp.where(upper, high_half, low_half)
        send = jnp.where(upper, low_half, high_half)
        if send_type is not None:
            send = send.astype(send_type)
        got = lax.ppermute(send, axis, [(i, i ^ bit) for i in range(size)])
        value = keep + got.astype(keep.dtype)
    return value


def halving_sum(value, dim):
    shape = value.shape
    groups = lax.axis_size("group")
    dps = lax.axis_size("dp")
    split = shape[:dim] + (groups * dps, shape[dim] // (groups * dps)) + shape[dim + 1 :]
    value = value.reshape(split)
    value = halving_steps(
        value, dim, [("group", groups, 2), ("group", groups, 1), ("dp", dps, 1)], jnp.bfloat16
    )
    return value.reshape(shape[:dim] + (shape[dim] // (groups * dps),) + shape[dim + 1 :])


def solution(mesh):
    in_specs = (
        P("tensor", ("group", "dp"), None),
        P("tensor", ("group", "dp"), None),
        P(),
        P(),
        P(),
        P(None, None, "tensor", None),
        P(None, "tensor"),
        P("tensor", None, None),
        P(),
        P(),
        P(),
        P(None, "tensor"),
        P("tensor"),
        P("tensor", None),
        P(),
    )
    out_specs = (
        P("tensor", ("group", "dp"), None),
        P("tensor", ("group", "dp"), None),
        P(("group", "dp", "tensor")),
        P(("group", "dp", "tensor")),
        P(("group", "dp"), None, "tensor", None),
        P(None, ("group", "dp", "tensor")),
        P("tensor", None, ("group", "dp")),
        P(("group", "dp", "tensor")),
        P(("group", "dp", "tensor")),
        P(("group", "dp", "tensor")),
        P(("group", "dp"), "tensor"),
        P(("group", "dp", "tensor")),
        P("tensor", ("group", "dp")),
        P(("group", "dp", "tensor")),
    )
    return jax.shard_map(shards, mesh=mesh, in_specs=in_specs, out_specs=out_specs, check_vma=False)
```

```python
from functools import partial
import math

import jax
import jax.numpy as jnp
from jax import lax
from jax.experimental import pallas as pl
from jax.experimental.pallas import tpu as pltpu
from jax.sharding import PartitionSpec as P

EPS = 1e-05
NEGATIVE = -1e30


def layer_norm(value, gain, shift):
    mean = jnp.mean(value, axis=-1, keepdims=True)
    centred = value - mean
    spread = jnp.mean(centred * centred, axis=-1, keepdims=True)
    return centred * lax.rsqrt(spread + EPS) * gain + shift


def gelu_tanh(value):
    return jax.nn.gelu(value, approximate=True)


def _valid(first_q, first_k, rows, cols, length):
    q_pos = first_q + lax.broadcasted_iota(jnp.int32, (rows, cols), 0)
    k_pos = first_k + lax.broadcasted_iota(jnp.int32, (rows, cols), 1)
    return (k_pos <= q_pos) & (k_pos < length)


def _key_blocks(i, block_q, block_k, length):
    causal = (i * block_q + block_q + block_k - 1) // block_k
    live = (length + block_k - 1) // block_k
    return jnp.minimum(causal, live)


def _attn_fwd_kernel(len_ref, q_ref, k_ref, v_ref, o_ref, lse_ref, s_buf, *, block_q, block_k, scale):
    i = pl.program_id(0)
    length = len_ref[0]
    count = _key_blocks(i, block_q, block_k, length)
    q = q_ref[...]

    def scores(j, m):
        first = pl.multiple_of(j * block_k, block_k)
        k = k_ref[pl.ds(first, block_k), :]
        s = lax.dot_general(q, k, (((1,), (1,)), ((), ())), preferred_element_type=jnp.float32)
        s = jnp.where(_valid(i * block_q, first, block_q, block_k, length), s * scale, NEGATIVE)
        s_buf[:, pl.ds(first, block_k)] = s
        return jnp.maximum(m, jnp.max(s, axis=1, keepdims=True))

    peak = lax.fori_loop(0, count, scores, jnp.full((block_q, 1), NEGATIVE, jnp.float32))

    def exps(j, total):
        first = pl.multiple_of(j * block_k, block_k)
        e = jnp.exp(s_buf[:, pl.ds(first, block_k)] - peak)
        s_buf[:, pl.ds(first, block_k)] = e
        return total + jnp.sum(e, axis=1, keepdims=True)

    total = lax.fori_loop(0, count, exps, jnp.zeros((block_q, 1), jnp.float32))

    def mix(j, acc):
        first = pl.multiple_of(j * block_k, block_k)
        probs = (s_buf[:, pl.ds(first, block_k)] / total).astype(jnp.bfloat16)
        return acc + jnp.dot(probs, v_ref[pl.ds(first, block_k), :], preferred_element_type=jnp.float32)

    acc = lax.fori_loop(0, count, mix, jnp.zeros(o_ref.shape, jnp.float32))
    o_ref[...] = acc.astype(o_ref.dtype)
    lse_ref[...] = peak + jnp.log(total)


def attention_forward(q, k, v, length, *, block_q=256, block_k=256):
    n, d = q.shape
    scale = 1.0 / math.sqrt(d)
    kernel = partial(_attn_fwd_kernel, block_q=block_q, block_k=block_k, scale=scale)
    pairs = (n // block_q) * (n // block_k + 1) // 2
    return pl.pallas_call(
        kernel,
        out_shape=(jax.ShapeDtypeStruct((n, d), jnp.bfloat16), jax.ShapeDtypeStruct((n, 1), jnp.float32)),
        grid_spec=pltpu.PrefetchScalarGridSpec(
            num_scalar_prefetch=1,
            grid=(n // block_q,),
            in_specs=[
                pl.BlockSpec((block_q, d), lambda i, lens: (i, 0)),
                pl.BlockSpec((n, d), lambda i, lens: (0, 0)),
                pl.BlockSpec((n, d), lambda i, lens: (0, 0)),
            ],
            out_specs=[
                pl.BlockSpec((block_q, d), lambda i, lens: (i, 0)),
                pl.BlockSpec((block_q, 1), lambda i, lens: (i, 0)),
            ],
            scratch_shapes=[pltpu.VMEM((block_q, n), jnp.float32)],
        ),
        compiler_params=pltpu.CompilerParams(dimension_semantics=("arbitrary",)),
        cost_estimate=pl.CostEstimate(
            flops=4 * pairs * block_q * block_k * d,
            transcendentals=pairs * block_q * block_k,
            bytes_accessed=4 * n * d * 2,
        ),
    )(length, q, k, v)


def _attn_bwd_kernel(len_ref, q_ref, k_ref, v_ref, do_ref, lse_ref, dq_ref, dk_ref, dv_ref,
                     p_buf, dp_buf, dk_acc, dv_acc, *, block_q, block_k, scale):
    i = pl.program_id(0)
    length = len_ref[0]

    @pl.when(i == 0)
    def _():
        dk_acc[...] = jnp.zeros_like(dk_acc)
        dv_acc[...] = jnp.zeros_like(dv_acc)

    live = i * block_q < length

    @pl.when(live)
    def _():
        count = _key_blocks(i, block_q, block_k, length)
        q = q_ref[...]
        do = do_ref[...]
        lse = lse_ref[...]

        def first_pass(j, inner):
            first = pl.multiple_of(j * block_k, block_k)
            k = k_ref[pl.ds(first, block_k), :]
            v = v_ref[pl.ds(first, block_k), :]
            s = lax.dot_general(q, k, (((1,), (1,)), ((), ())), preferred_element_type=jnp.float32)
            valid = _valid(i * block_q, first, block_q, block_k, length)
            s = jnp.where(valid, s * scale, NEGATIVE)
            p = jnp.where(valid, jnp.exp(s - lse), 0.0)
            dp = lax.dot_general(do, v, (((1,), (1,)), ((), ())), preferred_element_type=jnp.float32)
            p_buf[:, pl.ds(first, block_k)] = p
            dp_buf[:, pl.ds(first, block_k)] = dp
            return inner + jnp.sum(p * dp, axis=1, keepdims=True)

        inner = lax.fori_loop(0, count, first_pass, jnp.zeros((block_q, 1), jnp.float32))

        def second_pass(j, dq):
            first = pl.multiple_of(j * block_k, block_k)
            p = p_buf[:, pl.ds(first, block_k)]
            dp = dp_buf[:, pl.ds(first, block_k)]
            ds = (p * (dp - inner)).astype(jnp.bfloat16)
            k = k_ref[pl.ds(first, block_k), :]
            dk_acc[pl.ds(first, block_k), :] += lax.dot_general(
                ds, q, (((0,), (0,)), ((), ())), preferred_element_type=jnp.float32)
            dv_acc[pl.ds(first, block_k), :] += lax.dot_general(
                p.astype(jnp.bfloat16), do, (((0,), (0,)), ((), ())), preferred_element_type=jnp.float32)
            return dq + jnp.dot(ds, k, preferred_element_type=jnp.float32)

        dq = lax.fori_loop(0, count, second_pass, jnp.zeros(dq_ref.shape, jnp.float32))
        dq_ref[...] = (dq * scale).astype(dq_ref.dtype)

    @pl.when(jnp.logical_not(live))
    def _():
        dq_ref[...] = jnp.zeros_like(dq_ref)

    @pl.when(i == pl.num_programs(0) - 1)
    def _():
        dk_ref[...] = (dk_acc[...] * scale).astype(dk_ref.dtype)
        dv_ref[...] = dv_acc[...].astype(dv_ref.dtype)


def attention_backward(q, k, v, do, lse, length, *, block_q=256, block_k=256):
    n, d = q.shape
    scale = 1.0 / math.sqrt(d)
    kernel = partial(_attn_bwd_kernel, block_q=block_q, block_k=block_k, scale=scale)
    pairs = (n // block_q) * (n // block_k + 1) // 2
    full = pl.BlockSpec((n, d), lambda i, lens: (0, 0))
    rows = pl.BlockSpec((block_q, d), lambda i, lens: (i, 0))
    return pl.pallas_call(
        kernel,
        out_shape=tuple(jax.ShapeDtypeStruct((n, d), jnp.bfloat16) for _ in range(3)),
        grid_spec=pltpu.PrefetchScalarGridSpec(
            num_scalar_prefetch=1,
            grid=(n // block_q,),
            in_specs=[rows, full, full, rows, pl.BlockSpec((block_q, 1), lambda i, lens: (i, 0))],
            out_specs=[rows, full, full],
            scratch_shapes=[
                pltpu.VMEM((block_q, n), jnp.float32),
                pltpu.VMEM((block_q, n), jnp.float32),
                pltpu.VMEM((n, d), jnp.float32),
                pltpu.VMEM((n, d), jnp.float32),
            ],
        ),
        compiler_params=pltpu.CompilerParams(dimension_semantics=("arbitrary",)),
        cost_estimate=pl.CostEstimate(
            flops=8 * pairs * block_q * block_k * d,
            transcendentals=pairs * block_q * block_k,
            bytes_accessed=8 * n * d * 2,
        ),
    )(length, q, k, v, do, lse)


GRID = 4


def grid_pairs(axis_of, delta):
    out = []
    for s in range(GRID * GRID):
        x, y = divmod(s, GRID)
        if axis_of == "x":
            out.append((s, ((x + delta) % GRID) * GRID + y))
        else:
            out.append((s, x * GRID + (y + delta) % GRID))
    return out


def grid_position(axis_of):
    t = lax.axis_index("tensor")
    return t // GRID if axis_of == "x" else t % GRID


def gather_line(block, axis_of):
    pos = grid_position(axis_of)
    from_left = lax.ppermute(block, "tensor", grid_pairs(axis_of, 1))
    from_right = lax.ppermute(block, "tensor", grid_pairs(axis_of, -1))
    half = block.shape[0] // 2
    far_low = lax.ppermute(from_left[:half], "tensor", grid_pairs(axis_of, 1))
    far_high = lax.ppermute(from_right[half:], "tensor", grid_pairs(axis_of, -1))
    far = jnp.concatenate([far_low, far_high], 0)
    ring = jnp.stack([block, from_right, far, from_left, block, from_right, far, from_left])
    return lax.dynamic_slice_in_dim(ring, (GRID - pos) % GRID, GRID, 0)


def gather_tensor(block):
    rows, cols = block.shape
    mid = cols // 2
    first = gather_line(block[:, :mid], "y").reshape(GRID * rows, mid)
    first = gather_line(first, "x").reshape(GRID * GRID * rows, mid)
    second = gather_line(block[:, mid:], "x").reshape(GRID * rows, cols - mid)
    second = gather_line(second, "y").reshape(GRID, GRID, rows, cols - mid)
    second = jnp.transpose(second, (1, 0, 2, 3)).reshape(GRID * GRID * rows, cols - mid)
    return jnp.concatenate([first, second], 1)


def scatter_line(blocks, axis_of, wire):
    pos = grid_position(axis_of)
    ring = jnp.concatenate([blocks, blocks], 0)
    rel = lax.dynamic_slice_in_dim(ring, pos, GRID, 0)
    half = blocks.shape[1] // 2
    got_left = lax.ppermute(rel[2, :half].astype(wire), "tensor", grid_pairs(axis_of, 1))
    got_right = lax.ppermute(rel[2, half:].astype(wire), "tensor", grid_pairs(axis_of, -1))
    to_right = rel[1].at[:half].add(got_left.astype(rel.dtype))
    to_left = rel[3].at[half:].add(got_right.astype(rel.dtype))
    got_left = lax.ppermute(to_right.astype(wire), "tensor", grid_pairs(axis_of, 1))
    got_right = lax.ppermute(to_left.astype(wire), "tensor", grid_pairs(axis_of, -1))
    return rel[0] + got_left.astype(rel.dtype) + got_right.astype(rel.dtype)


def scatter_tensor(partial, wire=jnp.bfloat16):
    total, cols = partial.shape
    rows = total // (GRID * GRID)
    mid = cols // 2
    grid = partial.reshape(GRID, GRID, rows, cols)
    first = scatter_line(grid[..., :mid].reshape(GRID, GRID * rows, mid), "x", wire)
    first = scatter_line(first.reshape(GRID, rows, mid), "y", wire)
    second = jnp.transpose(grid[..., mid:], (1, 0, 2, 3)).reshape(GRID, GRID * rows, cols - mid)
    second = scatter_line(second, "y", wire)
    second = scatter_line(second.reshape(GRID, rows, cols - mid), "x", wire)
    return jnp.concatenate([first, second], 1)


def shards(
    tokens,
    cotangent,
    lengths,
    ln1_gain,
    ln1_bias,
    w_qkv,
    b_qv,
    w_o,
    b_o,
    ln2_gain,
    ln2_bias,
    w_in,
    b_in,
    w_out,
    b_out,
):
    row_count, seq_count, model_width = tokens.shape
    tensor_count = lax.axis_size("tensor")
    tensor_rank = lax.axis_index("tensor")
    seq_total = row_count * tensor_count
    local_heads = w_qkv.shape[2]
    head_size = w_qkv.shape[3]
    local_width = local_heads * head_size
    hidden = w_in.shape[1]
    group_count = lax.axis_size("group")
    group_rank = lax.axis_index("group")
    member = group_rank * lax.axis_size("dp") + lax.axis_index("dp")
    seq_lengths = lax.dynamic_slice_in_dim(lengths, member * seq_count, seq_count, 0)
    group_totals = jnp.sum(lengths.reshape(group_count, -1), axis=1).astype(jnp.float32)
    factor = (
        group_count
        * lax.dynamic_index_in_dim(group_totals, group_rank, 0, keepdims=False)
        / jnp.sum(group_totals)
    )
    inputs = tokens.astype(jnp.float32)
    normed_low = layer_norm(inputs, ln1_gain, ln1_bias).astype(jnp.bfloat16)
    normed_full = gather_tensor(normed_low.reshape(row_count, seq_count * model_width)).reshape(
        seq_total, seq_count, model_width
    )
    joint_weight = w_qkv.reshape(model_width, 3 * local_width)
    projected = jnp.dot(
        normed_full.reshape(seq_total * seq_count, model_width),
        joint_weight,
        preferred_element_type=jnp.float32,
    )
    projected = projected.reshape(seq_total, seq_count, 3, local_width)
    query = (projected[:, :, 0] + b_qv[0]).astype(jnp.bfloat16)
    keys = projected[:, :, 1].astype(jnp.bfloat16)
    values = (projected[:, :, 2] + b_qv[1]).astype(jnp.bfloat16)

    def item(array, s, h):
        return array[:, s, h * head_size : (h + 1) * head_size]

    def per_row(items):
        stacked = jnp.stack(items).reshape(seq_count, local_heads, seq_total, head_size)
        return jnp.transpose(stacked, (2, 0, 1, 3)).reshape(seq_total, seq_count, local_width)

    pairs = [(s, h) for s in range(seq_count) for h in range(local_heads)]
    forward_items = [
        attention_forward(
            item(query, s, h), item(keys, s, h), item(values, s, h), seq_lengths[s : s + 1]
        )
        for s, h in pairs
    ]
    attended = per_row([o for o, _ in forward_items])
    out_weight = w_o.reshape(local_width, model_width)
    positions = tensor_rank * row_count + jnp.arange(row_count, dtype=jnp.int32)
    live = positions[:, None] < seq_lengths[None, :]
    upstream = jnp.where(live[:, :, None], cotangent, jnp.zeros_like(cotangent))
    upstream, normed_full = lax.optimization_barrier((upstream, normed_full))
    upstream_full = lax.all_gather(upstream, "tensor", axis=0, tiled=True)
    attention_part = jnp.einsum(
        "rse,ed->rsd", attended, out_weight, preferred_element_type=jnp.float32
    )
    attention = (
        scatter_tensor(attention_part.reshape(seq_total, seq_count * model_width)).reshape(
            row_count, seq_count, model_width
        )
        + b_o
    )
    middle = inputs + attention
    second_low = layer_norm(middle, ln2_gain, ln2_bias).astype(jnp.bfloat16)
    second_full = gather_tensor(second_low.reshape(row_count, seq_count * model_width)).reshape(
        seq_total, seq_count, model_width
    )
    pre_act = (
        jnp.dot(
            second_full.reshape(seq_total * seq_count, model_width),
            w_in,
            preferred_element_type=jnp.float32,
        )
        + b_in
    )
    activated = gelu_tanh(pre_act).astype(jnp.bfloat16).reshape(seq_total, seq_count, hidden)
    feed_part = jnp.einsum(
        "rsf,fd->rsd", activated, w_out, preferred_element_type=jnp.float32
    ).astype(jnp.bfloat16)
    piece = upstream_full
    weight_grad = jnp.einsum("rsf,rsd->fd", activated, piece, preferred_element_type=jnp.float32)
    part = jnp.einsum("rsd,fd->rsf", piece, w_out, preferred_element_type=jnp.float32)
    act_grad = part
    grad_w_out = weight_grad
    gelu_back = jax.vjp(gelu_tanh, pre_act)[1]
    pre_low = gelu_back(act_grad.reshape(seq_total * seq_count, hidden))[0].astype(jnp.bfloat16)
    grad_b_in = jnp.sum(pre_low, axis=0, dtype=jnp.float32)
    grad_w_in = jnp.einsum(
        "rd,rf->df",
        second_full.reshape(seq_total * seq_count, model_width),
        pre_low,
        preferred_element_type=jnp.float32,
    )
    pre_rows = pre_low.reshape(seq_total, seq_count, hidden)
    piece = pre_rows
    second_grad = scatter_tensor(
        jnp.einsum("rsf,df->rsd", piece, w_in, preferred_element_type=jnp.float32).reshape(
            seq_total, seq_count * model_width
        )
    ).reshape(row_count, seq_count, model_width)
    norm_two_back = jax.vjp(layer_norm, middle, ln2_gain, ln2_bias)[1]
    middle_part, grad_ln2_gain, grad_ln2_bias = norm_two_back(second_grad)
    middle_grad = upstream.astype(jnp.float32) + middle_part
    branch_low = middle_grad.astype(jnp.bfloat16)
    grad_b_o = jnp.sum(branch_low, axis=(0, 1), dtype=jnp.float32)
    grad_b_out = jnp.sum(upstream, axis=(0, 1), dtype=jnp.float32)
    piece = gather_tensor(branch_low.reshape(row_count, seq_count * model_width)).reshape(
        seq_total, seq_count, model_width
    )
    feed_part, piece = lax.optimization_barrier((feed_part, piece))
    feed = (
        lax.psum_scatter(feed_part, "tensor", scatter_dimension=0, tiled=True).astype(
            jnp.float32
        )
        + b_out
    )
    output = (middle + feed).astype(jnp.bfloat16)
    weight_grad = jnp.einsum("rse,rsd->ed", attended, piece, preferred_element_type=jnp.float32)
    part = jnp.einsum("rsd,ed->rse", piece, out_weight, preferred_element_type=jnp.float32)
    attended_grad = part.astype(jnp.bfloat16)
    backward_items = [
        attention_backward(
            item(query, s, h),
            item(keys, s, h),
            item(values, s, h),
            item(attended_grad, s, h),
            lse,
            seq_lengths[s : s + 1],
        )
        for (s, h), (_, lse) in zip(pairs, forward_items)
    ]
    joint_grad = jnp.stack(
        [per_row([grads[kind] for grads in backward_items]) for kind in range(3)], axis=2
    )
    grad_b_qv = jnp.sum(joint_grad[:, :, 0::2], axis=(0, 1), dtype=jnp.float32)
    joint_rows = joint_grad.reshape(seq_total, seq_count, 3 * local_width)
    grad_w_qkv = jnp.einsum(
        "rd,rc->dc",
        normed_full.reshape(seq_total * seq_count, model_width),
        joint_rows.reshape(seq_total * seq_count, 3 * local_width),
        preferred_element_type=jnp.float32,
    )
    piece = joint_rows
    normed_grad = scatter_tensor(
        jnp.einsum("rsc,dc->rsd", piece, joint_weight, preferred_element_type=jnp.float32).reshape(
            seq_total, seq_count * model_width
        )
    ).reshape(row_count, seq_count, model_width)
    norm_one_back = jax.vjp(layer_norm, inputs, ln1_gain, ln1_bias)[1]
    input_part, grad_ln1_gain, grad_ln1_bias = norm_one_back(normed_grad)
    input_grad = (middle_grad + input_part).astype(jnp.bfloat16)
    summed = (
        halving_sum(grad_w_qkv.reshape(model_width, 3, local_heads, head_size) * factor, 0),
        halving_sum(weight_grad.reshape(local_heads, head_size, model_width) * factor, 2),
        halving_sum(grad_w_in * factor, 0),
        halving_sum(grad_w_out * factor, 1),
    )
    in_full = lax.dynamic_update_slice_in_dim(
        jnp.zeros((hidden * tensor_count,), jnp.float32), grad_b_in, tensor_rank * hidden, 0
    )
    joint_full = lax.dynamic_update_slice_in_dim(
        jnp.zeros((2, local_width * tensor_count), jnp.float32),
        grad_b_qv,
        tensor_rank * local_width,
        1,
    )
    shard_count = group_count * lax.axis_size("dp")
    vectors = (
        grad_ln1_gain,
        grad_ln1_bias,
        grad_b_o,
        grad_ln2_gain,
        grad_ln2_bias,
        grad_b_out,
        joint_full[0],
        joint_full[1],
        in_full,
    )
    pieces = [
        jnp.transpose(
            (item * factor).reshape(shard_count, tensor_count, -1), (1, 0, 2)
        )
        for item in vectors
    ]
    widths = [piece.shape[2] for piece in pieces]
    packed = jnp.concatenate(pieces, 2)
    packed = halving_steps(packed, 0, [("tensor", tensor_count, 8), ("tensor", tensor_count, 4),
                                       ("tensor", tensor_count, 2), ("tensor", tensor_count, 1)])
    packed = halving_steps(packed, 1, [("group", group_count, 2), ("group", group_count, 1),
                                       ("dp", lax.axis_size("dp"), 1)])
    flat = packed.reshape(-1)
    parts = []
    offset = 0
    for width in widths:
        parts.append(flat[offset : offset + width])
        offset += width
    return (
        output,
        input_grad,
        parts[0],
        parts[1],
        summed[0],
        jnp.stack((parts[6], parts[7])),
        summed[1],
        parts[2],
        parts[3],
        parts[4],
        summed[2],
        parts[8],
        summed[3],
        parts[5],
    )


def halving_steps(value, dim, steps, send_type=None):
    for axis, size, bit in steps:
        half = value.shape[dim] // 2
        low_half = lax.slice_in_dim(value, 0, half, axis=dim)
        high_half = lax.slice_in_dim(value, half, 2 * half, axis=dim)
        upper = (lax.axis_index(axis) // bit) % 2 == 1
        keep = jnp.where(upper, high_half, low_half)
        send = jnp.where(upper, low_half, high_half)
        if send_type is not None:
            send = send.astype(send_type)
        got = lax.ppermute(send, axis, [(i, i ^ bit) for i in range(size)])
        value = keep + got.astype(keep.dtype)
    return value


def halving_sum(value, dim):
    shape = value.shape
    groups = lax.axis_size("group")
    dps = lax.axis_size("dp")
    split = shape[:dim] + (groups * dps, shape[dim] // (groups * dps)) + shape[dim + 1 :]
    value = value.reshape(split)
    value = halving_steps(
        value, dim, [("group", groups, 2), ("group", groups, 1), ("dp", dps, 1)], jnp.bfloat16
    )
    return value.reshape(shape[:dim] + (shape[dim] // (groups * dps),) + shape[dim + 1 :])


def solution(mesh):
    in_specs = (
        P("tensor", ("group", "dp"), None),
        P("tensor", ("group", "dp"), None),
        P(),
        P(),
        P(),
        P(None, None, "tensor", None),
        P(None, "tensor"),
        P("tensor", None, None),
        P(),
        P(),
        P(),
        P(None, "tensor"),
        P("tensor"),
        P("tensor", None),
        P(),
    )
    out_specs = (
        P("tensor", ("group", "dp"), None),
        P("tensor", ("group", "dp"), None),
        P(("group", "dp", "tensor")),
        P(("group", "dp", "tensor")),
        P(("group", "dp"), None, "tensor", None),
        P(None, ("group", "dp", "tensor")),
        P("tensor", None, ("group", "dp")),
        P(("group", "dp", "tensor")),
        P(("group", "dp", "tensor")),
        P(("group", "dp", "tensor")),
        P(("group", "dp"), "tensor"),
        P(("group", "dp", "tensor")),
        P("tensor", ("group", "dp")),
        P(("group", "dp", "tensor")),
    )
    return jax.shard_map(shards, mesh=mesh, in_specs=in_specs, out_specs=out_specs, check_vma=False)
```

```python
from functools import partial
import math

import jax
import jax.numpy as jnp
from jax import lax
from jax.experimental import pallas as pl
from jax.experimental.pallas import tpu as pltpu
from jax.sharding import PartitionSpec as P

EPS = 1e-05
NEGATIVE = -1e30


def layer_norm(value, gain, shift):
    mean = jnp.mean(value, axis=-1, keepdims=True)
    centred = value - mean
    spread = jnp.mean(centred * centred, axis=-1, keepdims=True)
    return centred * lax.rsqrt(spread + EPS) * gain + shift


def gelu_tanh(value):
    return jax.nn.gelu(value, approximate=True)


def _valid(first_q, first_k, rows, cols, length):
    q_pos = first_q + lax.broadcasted_iota(jnp.int32, (rows, cols), 0)
    k_pos = first_k + lax.broadcasted_iota(jnp.int32, (rows, cols), 1)
    return (k_pos <= q_pos) & (k_pos < length)


def _key_blocks(i, block_q, block_k, length):
    causal = (i * block_q + block_q + block_k - 1) // block_k
    live = (length + block_k - 1) // block_k
    return jnp.minimum(causal, live)


def _attn_fwd_kernel(len_ref, q_ref, k_ref, v_ref, o_ref, lse_ref, s_buf, *, block_q, block_k, scale):
    i = pl.program_id(0)
    length = len_ref[0]
    count = _key_blocks(i, block_q, block_k, length)
    q = q_ref[...]

    def scores(j, m):
        first = pl.multiple_of(j * block_k, block_k)
        k = k_ref[pl.ds(first, block_k), :]
        s = lax.dot_general(q, k, (((1,), (1,)), ((), ())), preferred_element_type=jnp.float32)
        s = jnp.where(_valid(i * block_q, first, block_q, block_k, length), s * scale, NEGATIVE)
        s_buf[:, pl.ds(first, block_k)] = s
        return jnp.maximum(m, jnp.max(s, axis=1, keepdims=True))

    peak = lax.fori_loop(0, count, scores, jnp.full((block_q, 1), NEGATIVE, jnp.float32))

    def exps(j, total):
        first = pl.multiple_of(j * block_k, block_k)
        e = jnp.exp(s_buf[:, pl.ds(first, block_k)] - peak)
        s_buf[:, pl.ds(first, block_k)] = e
        return total + jnp.sum(e, axis=1, keepdims=True)

    total = lax.fori_loop(0, count, exps, jnp.zeros((block_q, 1), jnp.float32))

    inverse = 1.0 / total

    def mix(j, acc):
        first = pl.multiple_of(j * block_k, block_k)
        probs = (s_buf[:, pl.ds(first, block_k)] * inverse).astype(jnp.bfloat16)
        return acc + jnp.dot(probs, v_ref[pl.ds(first, block_k), :], preferred_element_type=jnp.float32)

    acc = lax.fori_loop(0, count, mix, jnp.zeros(o_ref.shape, jnp.float32))
    o_ref[...] = acc.astype(o_ref.dtype)
    lse_ref[...] = peak + jnp.log(total)


def attention_forward(q, k, v, length, *, block_q=256, block_k=256):
    n, d = q.shape
    scale = 1.0 / math.sqrt(d)
    kernel = partial(_attn_fwd_kernel, block_q=block_q, block_k=block_k, scale=scale)
    pairs = (n // block_q) * (n // block_k + 1) // 2
    return pl.pallas_call(
        kernel,
        out_shape=(jax.ShapeDtypeStruct((n, d), jnp.bfloat16), jax.ShapeDtypeStruct((n, 1), jnp.float32)),
        grid_spec=pltpu.PrefetchScalarGridSpec(
            num_scalar_prefetch=1,
            grid=(n // block_q,),
            in_specs=[
                pl.BlockSpec((block_q, d), lambda i, lens: (i, 0)),
                pl.BlockSpec((n, d), lambda i, lens: (0, 0)),
                pl.BlockSpec((n, d), lambda i, lens: (0, 0)),
            ],
            out_specs=[
                pl.BlockSpec((block_q, d), lambda i, lens: (i, 0)),
                pl.BlockSpec((block_q, 1), lambda i, lens: (i, 0)),
            ],
            scratch_shapes=[pltpu.VMEM((block_q, n), jnp.float32)],
        ),
        compiler_params=pltpu.CompilerParams(dimension_semantics=("arbitrary",)),
        cost_estimate=pl.CostEstimate(
            flops=4 * pairs * block_q * block_k * d,
            transcendentals=pairs * block_q * block_k,
            bytes_accessed=4 * n * d * 2,
        ),
    )(length, q, k, v)


def _attn_bwd_kernel(len_ref, q_ref, k_ref, v_ref, do_ref, lse_ref, dq_ref, dk_ref, dv_ref,
                     p_buf, dp_buf, dk_acc, dv_acc, *, block_q, block_k, scale):
    i = pl.program_id(0)
    length = len_ref[0]

    @pl.when(i == 0)
    def _():
        dk_acc[...] = jnp.zeros_like(dk_acc)
        dv_acc[...] = jnp.zeros_like(dv_acc)

    live = i * block_q < length

    @pl.when(live)
    def _():
        count = _key_blocks(i, block_q, block_k, length)
        q = q_ref[...]
        do = do_ref[...]
        lse = lse_ref[...]

        def first_pass(j, inner):
            first = pl.multiple_of(j * block_k, block_k)
            k = k_ref[pl.ds(first, block_k), :]
            v = v_ref[pl.ds(first, block_k), :]
            s = lax.dot_general(q, k, (((1,), (1,)), ((), ())), preferred_element_type=jnp.float32)
            valid = _valid(i * block_q, first, block_q, block_k, length)
            s = jnp.where(valid, s * scale, NEGATIVE)
            p = jnp.where(valid, jnp.exp(s - lse), 0.0)
            dp = lax.dot_general(do, v, (((1,), (1,)), ((), ())), preferred_element_type=jnp.float32)
            p_buf[:, pl.ds(first, block_k)] = p
            dp_buf[:, pl.ds(first, block_k)] = dp
            return inner + jnp.sum(p * dp, axis=1, keepdims=True)

        inner = lax.fori_loop(0, count, first_pass, jnp.zeros((block_q, 1), jnp.float32))

        def second_pass(j, dq):
            first = pl.multiple_of(j * block_k, block_k)
            p = p_buf[:, pl.ds(first, block_k)]
            dp = dp_buf[:, pl.ds(first, block_k)]
            ds = (p * (dp - inner)).astype(jnp.bfloat16)
            k = k_ref[pl.ds(first, block_k), :]
            dk_acc[pl.ds(first, block_k), :] += lax.dot_general(
                ds, q, (((0,), (0,)), ((), ())), preferred_element_type=jnp.float32)
            dv_acc[pl.ds(first, block_k), :] += lax.dot_general(
                p.astype(jnp.bfloat16), do, (((0,), (0,)), ((), ())), preferred_element_type=jnp.float32)
            return dq + jnp.dot(ds, k, preferred_element_type=jnp.float32)

        dq = lax.fori_loop(0, count, second_pass, jnp.zeros(dq_ref.shape, jnp.float32))
        dq_ref[...] = (dq * scale).astype(dq_ref.dtype)

    @pl.when(jnp.logical_not(live))
    def _():
        dq_ref[...] = jnp.zeros_like(dq_ref)

    @pl.when(i == pl.num_programs(0) - 1)
    def _():
        dk_ref[...] = (dk_acc[...] * scale).astype(dk_ref.dtype)
        dv_ref[...] = dv_acc[...].astype(dv_ref.dtype)


def attention_backward(q, k, v, do, lse, length, *, block_q=256, block_k=256):
    n, d = q.shape
    scale = 1.0 / math.sqrt(d)
    kernel = partial(_attn_bwd_kernel, block_q=block_q, block_k=block_k, scale=scale)
    pairs = (n // block_q) * (n // block_k + 1) // 2
    full = pl.BlockSpec((n, d), lambda i, lens: (0, 0))
    rows = pl.BlockSpec((block_q, d), lambda i, lens: (i, 0))
    return pl.pallas_call(
        kernel,
        out_shape=tuple(jax.ShapeDtypeStruct((n, d), jnp.bfloat16) for _ in range(3)),
        grid_spec=pltpu.PrefetchScalarGridSpec(
            num_scalar_prefetch=1,
            grid=(n // block_q,),
            in_specs=[rows, full, full, rows, pl.BlockSpec((block_q, 1), lambda i, lens: (i, 0))],
            out_specs=[rows, full, full],
            scratch_shapes=[
                pltpu.VMEM((block_q, n), jnp.float32),
                pltpu.VMEM((block_q, n), jnp.float32),
                pltpu.VMEM((n, d), jnp.float32),
                pltpu.VMEM((n, d), jnp.float32),
            ],
        ),
        compiler_params=pltpu.CompilerParams(dimension_semantics=("arbitrary",)),
        cost_estimate=pl.CostEstimate(
            flops=8 * pairs * block_q * block_k * d,
            transcendentals=pairs * block_q * block_k,
            bytes_accessed=8 * n * d * 2,
        ),
    )(length, q, k, v, do, lse)


def shards(
    tokens,
    cotangent,
    lengths,
    ln1_gain,
    ln1_bias,
    w_qkv,
    b_qv,
    w_o,
    b_o,
    ln2_gain,
    ln2_bias,
    w_in,
    b_in,
    w_out,
    b_out,
):
    row_count, seq_count, model_width = tokens.shape
    tensor_count = lax.axis_size("tensor")
    tensor_rank = lax.axis_index("tensor")
    seq_total = row_count * tensor_count
    local_heads = w_qkv.shape[2]
    head_size = w_qkv.shape[3]
    local_width = local_heads * head_size
    hidden = w_in.shape[1]
    group_count = lax.axis_size("group")
    group_rank = lax.axis_index("group")
    member = group_rank * lax.axis_size("dp") + lax.axis_index("dp")
    seq_lengths = lax.dynamic_slice_in_dim(lengths, member * seq_count, seq_count, 0)
    group_totals = jnp.sum(lengths.reshape(group_count, -1), axis=1).astype(jnp.float32)
    factor = (
        group_count
        * lax.dynamic_index_in_dim(group_totals, group_rank, 0, keepdims=False)
        / jnp.sum(group_totals)
    )
    inputs = tokens.astype(jnp.float32)
    normed_low = layer_norm(inputs, ln1_gain, ln1_bias).astype(jnp.bfloat16)
    normed_full = lax.all_gather(normed_low, "tensor", axis=0, tiled=True)
    joint_weight = w_qkv.reshape(model_width, 3 * local_width)
    projected = jnp.dot(
        normed_full.reshape(seq_total * seq_count, model_width),
        joint_weight,
        preferred_element_type=jnp.float32,
    )
    projected = projected.reshape(seq_total, seq_count, 3, local_width)
    query = (projected[:, :, 0] + b_qv[0]).astype(jnp.bfloat16)
    keys = projected[:, :, 1].astype(jnp.bfloat16)
    values = (projected[:, :, 2] + b_qv[1]).astype(jnp.bfloat16)

    def item(array, s, h):
        return array[:, s, h * head_size : (h + 1) * head_size]

    def per_row(items):
        stacked = jnp.stack(items).reshape(seq_count, local_heads, seq_total, head_size)
        return jnp.transpose(stacked, (2, 0, 1, 3)).reshape(seq_total, seq_count, local_width)

    pairs = [(s, h) for s in range(seq_count) for h in range(local_heads)]
    forward_items = [
        attention_forward(
            item(query, s, h), item(keys, s, h), item(values, s, h), seq_lengths[s : s + 1]
        )
        for s, h in pairs
    ]
    attended = per_row([o for o, _ in forward_items])
    out_weight = w_o.reshape(local_width, model_width)
    positions = tensor_rank * row_count + jnp.arange(row_count, dtype=jnp.int32)
    live = positions[:, None] < seq_lengths[None, :]
    upstream = jnp.where(live[:, :, None], cotangent, jnp.zeros_like(cotangent))
    upstream_full = lax.all_gather(upstream, "tensor", axis=0, tiled=True)
    attention_part = jnp.einsum(
        "rse,ed->rsd", attended, out_weight, preferred_element_type=jnp.float32
    ).astype(jnp.bfloat16)
    attention_part, upstream_full = lax.optimization_barrier((attention_part, upstream_full))
    attention = (
        lax.psum_scatter(attention_part, "tensor", scatter_dimension=0, tiled=True).astype(
            jnp.float32
        )
        + b_o
    )
    middle = inputs + attention
    act_grad = jnp.einsum("rsd,fd->rsf", upstream_full, w_out, preferred_element_type=jnp.float32)
    middle, act_grad = lax.optimization_barrier((middle, act_grad))
    second_low = layer_norm(middle, ln2_gain, ln2_bias).astype(jnp.bfloat16)
    second_full = lax.all_gather(second_low, "tensor", axis=0, tiled=True)
    pre_act = (
        jnp.dot(
            second_full.reshape(seq_total * seq_count, model_width),
            w_in,
            preferred_element_type=jnp.float32,
        )
        + b_in
    )
    activated = gelu_tanh(pre_act).astype(jnp.bfloat16).reshape(seq_total, seq_count, hidden)
    piece = upstream_full
    grad_w_out = jnp.einsum("rsf,rsd->fd", activated, piece, preferred_element_type=jnp.float32)
    gelu_back = jax.vjp(gelu_tanh, pre_act)[1]
    pre_low = gelu_back(act_grad.reshape(seq_total * seq_count, hidden))[0].astype(jnp.bfloat16)
    grad_b_in = jnp.sum(pre_low, axis=0, dtype=jnp.float32)
    grad_w_in = jnp.einsum(
        "rd,rf->df",
        second_full.reshape(seq_total * seq_count, model_width),
        pre_low,
        preferred_element_type=jnp.float32,
    )
    pre_rows = pre_low.reshape(seq_total, seq_count, hidden)
    piece = pre_rows
    second_part = jnp.einsum("rsf,df->rsd", piece, w_in, preferred_element_type=jnp.float32)
    second_part = second_part.astype(jnp.bfloat16)
    feed_input, second_part = lax.optimization_barrier((activated, second_part))
    second_grad = lax.psum_scatter(
        second_part, "tensor", scatter_dimension=0, tiled=True
    ).astype(jnp.float32)
    feed_part = jnp.einsum(
        "rsf,fd->rsd", feed_input, w_out, preferred_element_type=jnp.float32
    ).astype(jnp.bfloat16)
    feed_part, second_grad = lax.optimization_barrier((feed_part, second_grad))
    norm_two_back = jax.vjp(layer_norm, middle, ln2_gain, ln2_bias)[1]
    middle_part, grad_ln2_gain, grad_ln2_bias = norm_two_back(second_grad)
    middle_grad = upstream.astype(jnp.float32) + middle_part
    branch_low = middle_grad.astype(jnp.bfloat16)
    grad_b_o = jnp.sum(branch_low, axis=(0, 1), dtype=jnp.float32)
    grad_b_out = jnp.sum(upstream, axis=(0, 1), dtype=jnp.float32)
    piece = lax.all_gather(branch_low, "tensor", axis=0, tiled=True)
    weight_grad = jnp.einsum("rse,rsd->ed", attended, piece, preferred_element_type=jnp.float32)
    part = jnp.einsum("rsd,ed->rse", piece, out_weight, preferred_element_type=jnp.float32)
    attended_grad = part.astype(jnp.bfloat16)
    backward_items = [
        attention_backward(
            item(query, s, h),
            item(keys, s, h),
            item(values, s, h),
            item(attended_grad, s, h),
            lse,
            seq_lengths[s : s + 1],
        )
        for (s, h), (_, lse) in zip(pairs, forward_items)
    ]
    joint_grad = jnp.stack(
        [per_row([grads[kind] for grads in backward_items]) for kind in range(3)], axis=2
    )
    grad_b_qv = jnp.sum(joint_grad[:, :, 0::2], axis=(0, 1), dtype=jnp.float32)
    joint_rows = joint_grad.reshape(seq_total, seq_count, 3 * local_width)
    grad_w_qkv = jnp.einsum(
        "rd,rc->dc",
        normed_full.reshape(seq_total * seq_count, model_width),
        joint_rows.reshape(seq_total * seq_count, 3 * local_width),
        preferred_element_type=jnp.float32,
    )
    piece = joint_rows
    normed_part = jnp.einsum(
        "rsc,dc->rsd", piece, joint_weight, preferred_element_type=jnp.float32
    ).astype(jnp.bfloat16)
    both = lax.psum_scatter(
        jnp.concatenate([normed_part, feed_part], 2), "tensor", scatter_dimension=0, tiled=True
    ).astype(jnp.float32)
    normed_grad = both[:, :, :model_width]
    feed = both[:, :, model_width:] + b_out
    output = (middle + feed).astype(jnp.bfloat16)
    norm_one_back = jax.vjp(layer_norm, inputs, ln1_gain, ln1_bias)[1]
    input_part, grad_ln1_gain, grad_ln1_bias = norm_one_back(normed_grad)
    input_grad = (middle_grad + input_part).astype(jnp.bfloat16)
    summed = (
        halving_sum(grad_w_qkv.reshape(model_width, 3, local_heads, head_size) * factor, 0),
        halving_sum(weight_grad.reshape(local_heads, head_size, model_width) * factor, 2),
        halving_sum(grad_w_in * factor, 0),
        halving_sum(grad_w_out * factor, 1),
    )
    in_full = lax.dynamic_update_slice_in_dim(
        jnp.zeros((hidden * tensor_count,), jnp.float32), grad_b_in, tensor_rank * hidden, 0
    )
    joint_full = lax.dynamic_update_slice_in_dim(
        jnp.zeros((2, local_width * tensor_count), jnp.float32),
        grad_b_qv,
        tensor_rank * local_width,
        1,
    )
    shard_count = group_count * lax.axis_size("dp")
    vectors = (
        grad_ln1_gain,
        grad_ln1_bias,
        grad_b_o,
        grad_ln2_gain,
        grad_ln2_bias,
        grad_b_out,
        joint_full[0],
        joint_full[1],
        in_full,
    )
    pieces = [
        jnp.transpose(
            (item * factor).reshape(shard_count, tensor_count, -1), (1, 0, 2)
        )
        for item in vectors
    ]
    widths = [piece.shape[2] for piece in pieces]
    packed = jnp.concatenate(pieces, 2)
    packed = halving_steps(packed, 0, [("tensor", tensor_count, 8), ("tensor", tensor_count, 4),
                                       ("tensor", tensor_count, 2), ("tensor", tensor_count, 1)])
    packed = halving_steps(packed, 1, [("group", group_count, 2), ("group", group_count, 1),
                                       ("dp", lax.axis_size("dp"), 1)])
    flat = packed.reshape(-1)
    parts = []
    offset = 0
    for width in widths:
        parts.append(flat[offset : offset + width])
        offset += width
    return (
        output,
        input_grad,
        parts[0],
        parts[1],
        summed[0],
        jnp.stack((parts[6], parts[7])),
        summed[1],
        parts[2],
        parts[3],
        parts[4],
        summed[2],
        parts[8],
        summed[3],
        parts[5],
    )


def halving_steps(value, dim, steps, send_type=None):
    for axis, size, bit in steps:
        half = value.shape[dim] // 2
        low_half = lax.slice_in_dim(value, 0, half, axis=dim)
        high_half = lax.slice_in_dim(value, half, 2 * half, axis=dim)
        upper = (lax.axis_index(axis) // bit) % 2 == 1
        keep = jnp.where(upper, high_half, low_half)
        send = jnp.where(upper, low_half, high_half)
        if send_type is not None:
            send = send.astype(send_type)
        got = lax.ppermute(send, axis, [(i, i ^ bit) for i in range(size)])
        value = keep + got.astype(keep.dtype)
    return value


def halving_sum(value, dim):
    shape = value.shape
    groups = lax.axis_size("group")
    dps = lax.axis_size("dp")
    split = shape[:dim] + (groups * dps, shape[dim] // (groups * dps)) + shape[dim + 1 :]
    value = value.reshape(split)
    value = halving_steps(
        value, dim, [("group", groups, 2), ("group", groups, 1), ("dp", dps, 1)], jnp.bfloat16
    )
    return value.reshape(shape[:dim] + (shape[dim] // (groups * dps),) + shape[dim + 1 :])


def solution(mesh):
    in_specs = (
        P("tensor", ("group", "dp"), None),
        P("tensor", ("group", "dp"), None),
        P(),
        P(),
        P(),
        P(None, None, "tensor", None),
        P(None, "tensor"),
        P("tensor", None, None),
        P(),
        P(),
        P(),
        P(None, "tensor"),
        P("tensor"),
        P("tensor", None),
        P(),
    )
    out_specs = (
        P("tensor", ("group", "dp"), None),
        P("tensor", ("group", "dp"), None),
        P(("group", "dp", "tensor")),
        P(("group", "dp", "tensor")),
        P(("group", "dp"), None, "tensor", None),
        P(None, ("group", "dp", "tensor")),
        P("tensor", None, ("group", "dp")),
        P(("group", "dp", "tensor")),
        P(("group", "dp", "tensor")),
        P(("group", "dp", "tensor")),
        P(("group", "dp"), "tensor"),
        P(("group", "dp", "tensor")),
        P("tensor", ("group", "dp")),
        P(("group", "dp", "tensor")),
    )
    return jax.shard_map(shards, mesh=mesh, in_specs=in_specs, out_specs=out_specs, check_vma=False)
```

```python
from functools import partial
import math

import jax
import jax.numpy as jnp
from jax import lax
from jax.experimental import pallas as pl
from jax.experimental.pallas import tpu as pltpu
from jax.sharding import PartitionSpec as P

EPS = 1e-05
NEGATIVE = -1e30


def layer_norm(value, gain, shift):
    mean = jnp.mean(value, axis=-1, keepdims=True)
    centred = value - mean
    spread = jnp.mean(centred * centred, axis=-1, keepdims=True)
    return centred * lax.rsqrt(spread + EPS) * gain + shift


def gelu_tanh(value):
    return jax.nn.gelu(value, approximate=True)


def _valid(first_q, first_k, rows, cols, length):
    q_pos = first_q + lax.broadcasted_iota(jnp.int32, (rows, cols), 0)
    k_pos = first_k + lax.broadcasted_iota(jnp.int32, (rows, cols), 1)
    return (k_pos <= q_pos) & (k_pos < length)


def _key_blocks(i, block_q, block_k, length):
    causal = (i * block_q + block_q + block_k - 1) // block_k
    live = (length + block_k - 1) // block_k
    return jnp.minimum(causal, live)


def _attn_fwd_kernel(len_ref, q_ref, k_ref, v_ref, o_ref, lse_ref, s_buf, *, block_q, block_k, scale):
    i = pl.program_id(0)
    length = len_ref[0]
    count = _key_blocks(i, block_q, block_k, length)
    q = q_ref[...]

    def scores(j, m):
        first = pl.multiple_of(j * block_k, block_k)
        k = k_ref[pl.ds(first, block_k), :]
        s = lax.dot_general(q, k, (((1,), (1,)), ((), ())), preferred_element_type=jnp.float32)
        s = jnp.where(_valid(i * block_q, first, block_q, block_k, length), s * scale, NEGATIVE)
        s_buf[:, pl.ds(first, block_k)] = s
        return jnp.maximum(m, jnp.max(s, axis=1, keepdims=True))

    peak = lax.fori_loop(0, count, scores, jnp.full((block_q, 1), NEGATIVE, jnp.float32))

    def exps(j, total):
        first = pl.multiple_of(j * block_k, block_k)
        e = jnp.exp(s_buf[:, pl.ds(first, block_k)] - peak)
        s_buf[:, pl.ds(first, block_k)] = e
        return total + jnp.sum(e, axis=1, keepdims=True)

    total = lax.fori_loop(0, count, exps, jnp.zeros((block_q, 1), jnp.float32))

    inverse = 1.0 / total

    def mix(j, acc):
        first = pl.multiple_of(j * block_k, block_k)
        probs = (s_buf[:, pl.ds(first, block_k)] * inverse).astype(jnp.bfloat16)
        return acc + jnp.dot(probs, v_ref[pl.ds(first, block_k), :], preferred_element_type=jnp.float32)

    acc = lax.fori_loop(0, count, mix, jnp.zeros(o_ref.shape, jnp.float32))
    o_ref[...] = acc.astype(o_ref.dtype)
    lse_ref[...] = peak + jnp.log(total)


def attention_forward(q, k, v, length, *, block_q=256, block_k=256):
    n, d = q.shape
    scale = 1.0 / math.sqrt(d)
    kernel = partial(_attn_fwd_kernel, block_q=block_q, block_k=block_k, scale=scale)
    pairs = (n // block_q) * (n // block_k + 1) // 2
    return pl.pallas_call(
        kernel,
        out_shape=(jax.ShapeDtypeStruct((n, d), jnp.bfloat16), jax.ShapeDtypeStruct((n, 1), jnp.float32)),
        grid_spec=pltpu.PrefetchScalarGridSpec(
            num_scalar_prefetch=1,
            grid=(n // block_q,),
            in_specs=[
                pl.BlockSpec((block_q, d), lambda i, lens: (i, 0)),
                pl.BlockSpec((n, d), lambda i, lens: (0, 0)),
                pl.BlockSpec((n, d), lambda i, lens: (0, 0)),
            ],
            out_specs=[
                pl.BlockSpec((block_q, d), lambda i, lens: (i, 0)),
                pl.BlockSpec((block_q, 1), lambda i, lens: (i, 0)),
            ],
            scratch_shapes=[pltpu.VMEM((block_q, n), jnp.float32)],
        ),
        compiler_params=pltpu.CompilerParams(dimension_semantics=("arbitrary",)),
        cost_estimate=pl.CostEstimate(
            flops=4 * pairs * block_q * block_k * d,
            transcendentals=pairs * block_q * block_k,
            bytes_accessed=4 * n * d * 2,
        ),
    )(length, q, k, v)


def _attn_bwd_kernel(len_ref, q_ref, k_ref, v_ref, do_ref, lse_ref, dq_ref, dk_ref, dv_ref,
                     p_buf, dp_buf, dk_acc, dv_acc, *, block_q, block_k, scale):
    i = pl.program_id(0)
    length = len_ref[0]

    @pl.when(i == 0)
    def _():
        dk_acc[...] = jnp.zeros_like(dk_acc)
        dv_acc[...] = jnp.zeros_like(dv_acc)

    live = i * block_q < length

    @pl.when(live)
    def _():
        count = _key_blocks(i, block_q, block_k, length)
        q = q_ref[...]
        do = do_ref[...]
        lse = lse_ref[...]

        def first_pass(j, inner):
            first = pl.multiple_of(j * block_k, block_k)
            k = k_ref[pl.ds(first, block_k), :]
            v = v_ref[pl.ds(first, block_k), :]
            s = lax.dot_general(q, k, (((1,), (1,)), ((), ())), preferred_element_type=jnp.float32)
            valid = _valid(i * block_q, first, block_q, block_k, length)
            s = jnp.where(valid, s * scale, NEGATIVE)
            p = jnp.where(valid, jnp.exp(s - lse), 0.0)
            dp = lax.dot_general(do, v, (((1,), (1,)), ((), ())), preferred_element_type=jnp.float32)
            p_buf[:, pl.ds(first, block_k)] = p
            dp_buf[:, pl.ds(first, block_k)] = dp
            return inner + jnp.sum(p * dp, axis=1, keepdims=True)

        inner = lax.fori_loop(0, count, first_pass, jnp.zeros((block_q, 1), jnp.float32))

        def second_pass(j, dq):
            first = pl.multiple_of(j * block_k, block_k)
            p = p_buf[:, pl.ds(first, block_k)]
            dp = dp_buf[:, pl.ds(first, block_k)]
            ds = (p * (dp - inner)).astype(jnp.bfloat16)
            k = k_ref[pl.ds(first, block_k), :]
            dk_acc[pl.ds(first, block_k), :] += lax.dot_general(
                ds, q, (((0,), (0,)), ((), ())), preferred_element_type=jnp.float32)
            dv_acc[pl.ds(first, block_k), :] += lax.dot_general(
                p.astype(jnp.bfloat16), do, (((0,), (0,)), ((), ())), preferred_element_type=jnp.float32)
            return dq + jnp.dot(ds, k, preferred_element_type=jnp.float32)

        dq = lax.fori_loop(0, count, second_pass, jnp.zeros(dq_ref.shape, jnp.float32))
        dq_ref[...] = (dq * scale).astype(dq_ref.dtype)

    @pl.when(jnp.logical_not(live))
    def _():
        dq_ref[...] = jnp.zeros_like(dq_ref)

    @pl.when(i == pl.num_programs(0) - 1)
    def _():
        dk_ref[...] = (dk_acc[...] * scale).astype(dk_ref.dtype)
        dv_ref[...] = dv_acc[...].astype(dv_ref.dtype)


def attention_backward(q, k, v, do, lse, length, *, block_q=256, block_k=256):
    n, d = q.shape
    scale = 1.0 / math.sqrt(d)
    kernel = partial(_attn_bwd_kernel, block_q=block_q, block_k=block_k, scale=scale)
    pairs = (n // block_q) * (n // block_k + 1) // 2
    full = pl.BlockSpec((n, d), lambda i, lens: (0, 0))
    rows = pl.BlockSpec((block_q, d), lambda i, lens: (i, 0))
    return pl.pallas_call(
        kernel,
        out_shape=tuple(jax.ShapeDtypeStruct((n, d), jnp.bfloat16) for _ in range(3)),
        grid_spec=pltpu.PrefetchScalarGridSpec(
            num_scalar_prefetch=1,
            grid=(n // block_q,),
            in_specs=[rows, full, full, rows, pl.BlockSpec((block_q, 1), lambda i, lens: (i, 0))],
            out_specs=[rows, full, full],
            scratch_shapes=[
                pltpu.VMEM((block_q, n), jnp.float32),
                pltpu.VMEM((block_q, n), jnp.float32),
                pltpu.VMEM((n, d), jnp.float32),
                pltpu.VMEM((n, d), jnp.float32),
            ],
        ),
        compiler_params=pltpu.CompilerParams(dimension_semantics=("arbitrary",)),
        cost_estimate=pl.CostEstimate(
            flops=8 * pairs * block_q * block_k * d,
            transcendentals=pairs * block_q * block_k,
            bytes_accessed=8 * n * d * 2,
        ),
    )(length, q, k, v, do, lse)


def shards(
    tokens,
    cotangent,
    lengths,
    ln1_gain,
    ln1_bias,
    w_qkv,
    b_qv,
    w_o,
    b_o,
    ln2_gain,
    ln2_bias,
    w_in,
    b_in,
    w_out,
    b_out,
):
    row_count, seq_count, model_width = tokens.shape
    tensor_count = lax.axis_size("tensor")
    tensor_rank = lax.axis_index("tensor")
    seq_total = row_count * tensor_count
    local_heads = w_qkv.shape[2]
    head_size = w_qkv.shape[3]
    local_width = local_heads * head_size
    hidden = w_in.shape[1]
    group_count = lax.axis_size("group")
    group_rank = lax.axis_index("group")
    member = group_rank * lax.axis_size("dp") + lax.axis_index("dp")
    seq_lengths = lax.dynamic_slice_in_dim(lengths, member * seq_count, seq_count, 0)
    group_totals = jnp.sum(lengths.reshape(group_count, -1), axis=1).astype(jnp.float32)
    factor = (
        group_count
        * lax.dynamic_index_in_dim(group_totals, group_rank, 0, keepdims=False)
        / jnp.sum(group_totals)
    )
    inputs = tokens.astype(jnp.float32)
    normed_low = layer_norm(inputs, ln1_gain, ln1_bias).astype(jnp.bfloat16)
    normed_full = lax.all_gather(normed_low, "tensor", axis=0, tiled=True)
    joint_weight = w_qkv.reshape(model_width, 3 * local_width)
    projected = jnp.dot(
        normed_full.reshape(seq_total * seq_count, model_width),
        joint_weight,
        preferred_element_type=jnp.float32,
    )
    projected = projected.reshape(seq_total, seq_count, 3, local_width)
    query = (projected[:, :, 0] + b_qv[0]).astype(jnp.bfloat16)
    keys = projected[:, :, 1].astype(jnp.bfloat16)
    values = (projected[:, :, 2] + b_qv[1]).astype(jnp.bfloat16)

    def item(array, s, h):
        return array[:, s, h * head_size : (h + 1) * head_size]

    def per_row(items):
        stacked = jnp.stack(items).reshape(seq_count, local_heads, seq_total, head_size)
        return jnp.transpose(stacked, (2, 0, 1, 3)).reshape(seq_total, seq_count, local_width)

    pairs = [(s, h) for s in range(seq_count) for h in range(local_heads)]
    forward_items = [
        attention_forward(
            item(query, s, h), item(keys, s, h), item(values, s, h), seq_lengths[s : s + 1]
        )
        for s, h in pairs
    ]
    attended = per_row([o for o, _ in forward_items])
    out_weight = w_o.reshape(local_width, model_width)
    positions = tensor_rank * row_count + jnp.arange(row_count, dtype=jnp.int32)
    live = positions[:, None] < seq_lengths[None, :]
    upstream = jnp.where(live[:, :, None], cotangent, jnp.zeros_like(cotangent))
    upstream_full = lax.all_gather(upstream, "tensor", axis=0, tiled=True)
    attention_part = jnp.einsum(
        "rse,ed->rsd", attended, out_weight, preferred_element_type=jnp.float32
    ).astype(jnp.bfloat16)
    attention_part, upstream_full = lax.optimization_barrier((attention_part, upstream_full))
    attention = (
        lax.psum_scatter(attention_part, "tensor", scatter_dimension=0, tiled=True).astype(
            jnp.float32
        )
        + b_o
    )
    middle = inputs + attention
    act_grad = jnp.einsum("rsd,fd->rsf", upstream_full, w_out, preferred_element_type=jnp.float32)
    middle, act_grad = lax.optimization_barrier((middle, act_grad))
    second_low = layer_norm(middle, ln2_gain, ln2_bias).astype(jnp.bfloat16)
    second_full = lax.all_gather(second_low, "tensor", axis=0, tiled=True)
    pre_act = (
        jnp.dot(
            second_full.reshape(seq_total * seq_count, model_width),
            w_in,
            preferred_element_type=jnp.float32,
        )
        + b_in
    )
    activated = gelu_tanh(pre_act).astype(jnp.bfloat16).reshape(seq_total, seq_count, hidden)
    piece = upstream_full
    grad_w_out = jnp.einsum("rsf,rsd->fd", activated, piece, preferred_element_type=jnp.float32)
    gelu_back = jax.vjp(gelu_tanh, pre_act)[1]
    pre_low = gelu_back(act_grad.reshape(seq_total * seq_count, hidden))[0].astype(jnp.bfloat16)
    grad_b_in = jnp.sum(pre_low, axis=0, dtype=jnp.float32)
    grad_w_in = jnp.einsum(
        "rd,rf->df",
        second_full.reshape(seq_total * seq_count, model_width),
        pre_low,
        preferred_element_type=jnp.float32,
    )
    pre_rows = pre_low.reshape(seq_total, seq_count, hidden)
    piece = pre_rows
    second_part = jnp.einsum("rsf,df->rsd", piece, w_in, preferred_element_type=jnp.float32)
    second_part = second_part.astype(jnp.bfloat16)
    feed_input, second_part = lax.optimization_barrier((activated, second_part))
    second_grad = lax.psum_scatter(
        second_part, "tensor", scatter_dimension=0, tiled=True
    ).astype(jnp.float32)
    feed_part = jnp.einsum(
        "rsf,fd->rsd", feed_input, w_out, preferred_element_type=jnp.float32
    ).astype(jnp.bfloat16)
    feed_buffer = jnp.concatenate([jnp.zeros_like(feed_part), feed_part], 2)
    feed_buffer, second_grad = lax.optimization_barrier((feed_buffer, second_grad))
    norm_two_back = jax.vjp(layer_norm, middle, ln2_gain, ln2_bias)[1]
    middle_part, grad_ln2_gain, grad_ln2_bias = norm_two_back(second_grad)
    middle_grad = upstream.astype(jnp.float32) + middle_part
    branch_low = middle_grad.astype(jnp.bfloat16)
    grad_b_o = jnp.sum(branch_low, axis=(0, 1), dtype=jnp.float32)
    grad_b_out = jnp.sum(upstream, axis=(0, 1), dtype=jnp.float32)
    piece = lax.all_gather(branch_low, "tensor", axis=0, tiled=True)
    weight_grad = jnp.einsum("rse,rsd->ed", attended, piece, preferred_element_type=jnp.float32)
    part = jnp.einsum("rsd,ed->rse", piece, out_weight, preferred_element_type=jnp.float32)
    attended_grad = part.astype(jnp.bfloat16)
    backward_items = [
        attention_backward(
            item(query, s, h),
            item(keys, s, h),
            item(values, s, h),
            item(attended_grad, s, h),
            lse,
            seq_lengths[s : s + 1],
        )
        for (s, h), (_, lse) in zip(pairs, forward_items)
    ]
    joint_grad = jnp.stack(
        [per_row([grads[kind] for grads in backward_items]) for kind in range(3)], axis=2
    )
    grad_b_qv = jnp.sum(joint_grad[:, :, 0::2], axis=(0, 1), dtype=jnp.float32)
    joint_rows = joint_grad.reshape(seq_total, seq_count, 3 * local_width)
    grad_w_qkv = jnp.einsum(
        "rd,rc->dc",
        normed_full.reshape(seq_total * seq_count, model_width),
        joint_rows.reshape(seq_total * seq_count, 3 * local_width),
        preferred_element_type=jnp.float32,
    )
    normed_part = jnp.einsum(
        "rsc,dc->rsd", joint_rows, joint_weight, preferred_element_type=jnp.float32
    ).astype(jnp.bfloat16)
    joint_sums = jnp.sum(joint_rows, axis=(0, 1), dtype=jnp.float32)
    grad_ln1_bias = jnp.dot(
        joint_weight.astype(jnp.float32), joint_sums, precision=lax.Precision.HIGHEST
    )
    merged = lax.dynamic_update_slice(feed_buffer, normed_part, (0, 0, 0))
    both = lax.psum_scatter(merged, "tensor", scatter_dimension=0, tiled=True)
    summed = (
        halving_sum(grad_w_qkv.reshape(model_width, 3, local_heads, head_size) * factor, 0),
        halving_sum(weight_grad.reshape(local_heads, head_size, model_width) * factor, 2),
        halving_sum(grad_w_in * factor, 0),
        halving_sum(grad_w_out * factor, 1),
    )
    in_full = lax.dynamic_update_slice_in_dim(
        jnp.zeros((hidden * tensor_count,), jnp.float32), grad_b_in, tensor_rank * hidden, 0
    )
    joint_full = lax.dynamic_update_slice_in_dim(
        jnp.zeros((2, local_width * tensor_count), jnp.float32),
        grad_b_qv,
        tensor_rank * local_width,
        1,
    )
    early = reduce_vectors(
        (
            grad_ln1_bias,
            grad_b_o,
            grad_ln2_gain,
            grad_ln2_bias,
            grad_b_out,
            joint_full[0],
            joint_full[1],
            in_full,
        ),
        factor,
    )
    both, summed, early = lax.optimization_barrier((both, summed, early))
    both = both.astype(jnp.float32)
    normed_grad = both[:, :, :model_width]
    feed = both[:, :, model_width:] + b_out
    output = (middle + feed).astype(jnp.bfloat16)
    norm_one_back = jax.vjp(layer_norm, inputs, ln1_gain, ln1_bias)[1]
    input_part, grad_ln1_gain, _ = norm_one_back(normed_grad)
    input_grad = (middle_grad + input_part).astype(jnp.bfloat16)
    (late,) = reduce_vectors((grad_ln1_gain,), factor)
    return (
        output,
        input_grad,
        late,
        early[0],
        summed[0],
        jnp.stack((early[5], early[6])),
        summed[1],
        early[1],
        early[2],
        early[3],
        summed[2],
        early[7],
        summed[3],
        early[4],
    )


def reduce_vectors(vectors, factor):
    tensor_count = lax.axis_size("tensor")
    group_count = lax.axis_size("group")
    dp_count = lax.axis_size("dp")
    pieces = [
        jnp.transpose((item * factor).reshape(group_count * dp_count, tensor_count, -1), (1, 0, 2))
        for item in vectors
    ]
    widths = [piece.shape[2] for piece in pieces]
    packed = jnp.concatenate(pieces, 2)
    packed = halving_steps(
        packed, 0, [("tensor", tensor_count, bit) for bit in (8, 4, 2, 1)]
    )
    packed = halving_steps(
        packed, 1, [("group", group_count, 2), ("group", group_count, 1), ("dp", dp_count, 1)]
    )
    flat = packed.reshape(-1)
    parts = []
    offset = 0
    for width in widths:
        parts.append(flat[offset : offset + width])
        offset += width
    return tuple(parts)


def halving_steps(value, dim, steps, send_type=None):
    for axis, size, bit in steps:
        half = value.shape[dim] // 2
        low_half = lax.slice_in_dim(value, 0, half, axis=dim)
        high_half = lax.slice_in_dim(value, half, 2 * half, axis=dim)
        upper = (lax.axis_index(axis) // bit) % 2 == 1
        keep = jnp.where(upper, high_half, low_half)
        send = jnp.where(upper, low_half, high_half)
        if send_type is not None:
            send = send.astype(send_type)
        got = lax.ppermute(send, axis, [(i, i ^ bit) for i in range(size)])
        value = keep + got.astype(keep.dtype)
    return value


def halving_sum(value, dim):
    shape = value.shape
    groups = lax.axis_size("group")
    dps = lax.axis_size("dp")
    split = shape[:dim] + (groups * dps, shape[dim] // (groups * dps)) + shape[dim + 1 :]
    value = value.reshape(split)
    value = halving_steps(
        value, dim, [("group", groups, 2), ("group", groups, 1), ("dp", dps, 1)], jnp.bfloat16
    )
    return value.reshape(shape[:dim] + (shape[dim] // (groups * dps),) + shape[dim + 1 :])


def solution(mesh):
    in_specs = (
        P("tensor", ("group", "dp"), None),
        P("tensor", ("group", "dp"), None),
        P(),
        P(),
        P(),
        P(None, None, "tensor", None),
        P(None, "tensor"),
        P("tensor", None, None),
        P(),
        P(),
        P(),
        P(None, "tensor"),
        P("tensor"),
        P("tensor", None),
        P(),
    )
    out_specs = (
        P("tensor", ("group", "dp"), None),
        P("tensor", ("group", "dp"), None),
        P(("group", "dp", "tensor")),
        P(("group", "dp", "tensor")),
        P(("group", "dp"), None, "tensor", None),
        P(None, ("group", "dp", "tensor")),
        P("tensor", None, ("group", "dp")),
        P(("group", "dp", "tensor")),
        P(("group", "dp", "tensor")),
        P(("group", "dp", "tensor")),
        P(("group", "dp"), "tensor"),
        P(("group", "dp", "tensor")),
        P("tensor", ("group", "dp")),
        P(("group", "dp", "tensor")),
    )
    return jax.shard_map(shards, mesh=mesh, in_specs=in_specs, out_specs=out_specs, check_vma=False)
```

```python
from functools import partial
import math

import jax
import jax.numpy as jnp
from jax import lax
from jax.experimental import pallas as pl
from jax.experimental.pallas import tpu as pltpu
from jax.sharding import PartitionSpec as P

EPS = 1e-05
NEGATIVE = -1e30


def layer_norm(value, gain, shift):
    mean = jnp.mean(value, axis=-1, keepdims=True)
    centred = value - mean
    spread = jnp.mean(centred * centred, axis=-1, keepdims=True)
    return centred * lax.rsqrt(spread + EPS) * gain + shift


def gelu_tanh(value):
    return jax.nn.gelu(value, approximate=True)


def _valid(first_q, first_k, rows, cols, length):
    q_pos = first_q + lax.broadcasted_iota(jnp.int32, (rows, cols), 0)
    k_pos = first_k + lax.broadcasted_iota(jnp.int32, (rows, cols), 1)
    return (k_pos <= q_pos) & (k_pos < length)


def _key_blocks(i, block_q, block_k, length):
    causal = (i * block_q + block_q + block_k - 1) // block_k
    live = (length + block_k - 1) // block_k
    return jnp.minimum(causal, live)


def _attn_fwd_kernel(len_ref, q_ref, k_ref, v_ref, o_ref, lse_ref, s_buf, *, block_q, block_k, scale):
    i = pl.program_id(0)
    length = len_ref[0]
    count = _key_blocks(i, block_q, block_k, length)
    q = q_ref[...]

    def scores(j, m):
        first = pl.multiple_of(j * block_k, block_k)
        k = k_ref[pl.ds(first, block_k), :]
        s = lax.dot_general(q, k, (((1,), (1,)), ((), ())), preferred_element_type=jnp.float32)
        s = jnp.where(_valid(i * block_q, first, block_q, block_k, length), s * scale, NEGATIVE)
        s_buf[:, pl.ds(first, block_k)] = s
        return jnp.maximum(m, jnp.max(s, axis=1, keepdims=True))

    peak = lax.fori_loop(0, count, scores, jnp.full((block_q, 1), NEGATIVE, jnp.float32))

    def exps(j, total):
        first = pl.multiple_of(j * block_k, block_k)
        e = jnp.exp(s_buf[:, pl.ds(first, block_k)] - peak)
        s_buf[:, pl.ds(first, block_k)] = e
        return total + jnp.sum(e, axis=1, keepdims=True)

    total = lax.fori_loop(0, count, exps, jnp.zeros((block_q, 1), jnp.float32))

    inverse = 1.0 / total

    def mix(j, acc):
        first = pl.multiple_of(j * block_k, block_k)
        probs = (s_buf[:, pl.ds(first, block_k)] * inverse).astype(jnp.bfloat16)
        return acc + jnp.dot(probs, v_ref[pl.ds(first, block_k), :], preferred_element_type=jnp.float32)

    acc = lax.fori_loop(0, count, mix, jnp.zeros(o_ref.shape, jnp.float32))
    o_ref[...] = acc.astype(o_ref.dtype)
    lse_ref[...] = peak + jnp.log(total)


def attention_forward(q, k, v, length, *, block_q=256, block_k=256):
    n, d = q.shape
    scale = 1.0 / math.sqrt(d)
    kernel = partial(_attn_fwd_kernel, block_q=block_q, block_k=block_k, scale=scale)
    pairs = (n // block_q) * (n // block_k + 1) // 2
    return pl.pallas_call(
        kernel,
        out_shape=(jax.ShapeDtypeStruct((n, d), jnp.bfloat16), jax.ShapeDtypeStruct((n, 1), jnp.float32)),
        grid_spec=pltpu.PrefetchScalarGridSpec(
            num_scalar_prefetch=1,
            grid=(n // block_q,),
            in_specs=[
                pl.BlockSpec((block_q, d), lambda i, lens: (i, 0)),
                pl.BlockSpec((n, d), lambda i, lens: (0, 0)),
                pl.BlockSpec((n, d), lambda i, lens: (0, 0)),
            ],
            out_specs=[
                pl.BlockSpec((block_q, d), lambda i, lens: (i, 0)),
                pl.BlockSpec((block_q, 1), lambda i, lens: (i, 0)),
            ],
            scratch_shapes=[pltpu.VMEM((block_q, n), jnp.float32)],
        ),
        compiler_params=pltpu.CompilerParams(dimension_semantics=("arbitrary",)),
        cost_estimate=pl.CostEstimate(
            flops=4 * pairs * block_q * block_k * d,
            transcendentals=pairs * block_q * block_k,
            bytes_accessed=4 * n * d * 2,
        ),
    )(length, q, k, v)


def _attn_bwd_kernel(len_ref, q_ref, k_ref, v_ref, do_ref, lse_ref, dq_ref, dk_ref, dv_ref,
                     p_buf, dp_buf, dk_acc, dv_acc, *, block_q, block_k, scale):
    i = pl.program_id(0)
    length = len_ref[0]

    @pl.when(i == 0)
    def _():
        dk_acc[...] = jnp.zeros_like(dk_acc)
        dv_acc[...] = jnp.zeros_like(dv_acc)

    live = i * block_q < length

    @pl.when(live)
    def _():
        count = _key_blocks(i, block_q, block_k, length)
        q = q_ref[...]
        do = do_ref[...]
        lse = lse_ref[...]

        def first_pass(j, inner):
            first = pl.multiple_of(j * block_k, block_k)
            k = k_ref[pl.ds(first, block_k), :]
            v = v_ref[pl.ds(first, block_k), :]
            s = lax.dot_general(q, k, (((1,), (1,)), ((), ())), preferred_element_type=jnp.float32)
            valid = _valid(i * block_q, first, block_q, block_k, length)
            s = jnp.where(valid, s * scale, NEGATIVE)
            p = jnp.where(valid, jnp.exp(s - lse), 0.0)
            dp = lax.dot_general(do, v, (((1,), (1,)), ((), ())), preferred_element_type=jnp.float32)
            p_buf[:, pl.ds(first, block_k)] = p
            dp_buf[:, pl.ds(first, block_k)] = dp
            return inner + jnp.sum(p * dp, axis=1, keepdims=True)

        inner = lax.fori_loop(0, count, first_pass, jnp.zeros((block_q, 1), jnp.float32))

        def second_pass(j, dq):
            first = pl.multiple_of(j * block_k, block_k)
            p = p_buf[:, pl.ds(first, block_k)]
            dp = dp_buf[:, pl.ds(first, block_k)]
            ds = (p * (dp - inner)).astype(jnp.bfloat16)
            k = k_ref[pl.ds(first, block_k), :]
            dk_acc[pl.ds(first, block_k), :] += lax.dot_general(
                ds, q, (((0,), (0,)), ((), ())), preferred_element_type=jnp.float32)
            dv_acc[pl.ds(first, block_k), :] += lax.dot_general(
                p.astype(jnp.bfloat16), do, (((0,), (0,)), ((), ())), preferred_element_type=jnp.float32)
            return dq + jnp.dot(ds, k, preferred_element_type=jnp.float32)

        dq = lax.fori_loop(0, count, second_pass, jnp.zeros(dq_ref.shape, jnp.float32))
        dq_ref[...] = (dq * scale).astype(dq_ref.dtype)

    @pl.when(jnp.logical_not(live))
    def _():
        dq_ref[...] = jnp.zeros_like(dq_ref)

    @pl.when(i == pl.num_programs(0) - 1)
    def _():
        dk_ref[...] = (dk_acc[...] * scale).astype(dk_ref.dtype)
        dv_ref[...] = dv_acc[...].astype(dv_ref.dtype)


def attention_backward(q, k, v, do, lse, length, *, block_q=256, block_k=256):
    n, d = q.shape
    scale = 1.0 / math.sqrt(d)
    kernel = partial(_attn_bwd_kernel, block_q=block_q, block_k=block_k, scale=scale)
    pairs = (n // block_q) * (n // block_k + 1) // 2
    full = pl.BlockSpec((n, d), lambda i, lens: (0, 0))
    rows = pl.BlockSpec((block_q, d), lambda i, lens: (i, 0))
    return pl.pallas_call(
        kernel,
        out_shape=tuple(jax.ShapeDtypeStruct((n, d), jnp.bfloat16) for _ in range(3)),
        grid_spec=pltpu.PrefetchScalarGridSpec(
            num_scalar_prefetch=1,
            grid=(n // block_q,),
            in_specs=[rows, full, full, rows, pl.BlockSpec((block_q, 1), lambda i, lens: (i, 0))],
            out_specs=[rows, full, full],
            scratch_shapes=[
                pltpu.VMEM((block_q, n), jnp.float32),
                pltpu.VMEM((block_q, n), jnp.float32),
                pltpu.VMEM((n, d), jnp.float32),
                pltpu.VMEM((n, d), jnp.float32),
            ],
        ),
        compiler_params=pltpu.CompilerParams(dimension_semantics=("arbitrary",)),
        cost_estimate=pl.CostEstimate(
            flops=8 * pairs * block_q * block_k * d,
            transcendentals=pairs * block_q * block_k,
            bytes_accessed=8 * n * d * 2,
        ),
    )(length, q, k, v, do, lse)


def shards(
    tokens,
    cotangent,
    lengths,
    ln1_gain,
    ln1_bias,
    w_qkv,
    b_qv,
    w_o,
    b_o,
    ln2_gain,
    ln2_bias,
    w_in,
    b_in,
    w_out,
    b_out,
):
    row_count, seq_count, model_width = tokens.shape
    tensor_count = lax.axis_size("tensor")
    tensor_rank = lax.axis_index("tensor")
    seq_total = row_count * tensor_count
    local_heads = w_qkv.shape[2]
    head_size = w_qkv.shape[3]
    local_width = local_heads * head_size
    hidden = w_in.shape[1]
    group_count = lax.axis_size("group")
    group_rank = lax.axis_index("group")
    member = group_rank * lax.axis_size("dp") + lax.axis_index("dp")
    seq_lengths = lax.dynamic_slice_in_dim(lengths, member * seq_count, seq_count, 0)
    group_totals = jnp.sum(lengths.reshape(group_count, -1), axis=1).astype(jnp.float32)
    factor = (
        group_count
        * lax.dynamic_index_in_dim(group_totals, group_rank, 0, keepdims=False)
        / jnp.sum(group_totals)
    )
    inputs = tokens.astype(jnp.float32)
    normed_low = layer_norm(inputs, ln1_gain, ln1_bias).astype(jnp.bfloat16)
    normed_full = lax.all_gather(normed_low, "tensor", axis=0, tiled=True)
    joint_weight = w_qkv.reshape(model_width, 3 * local_width)
    projected = jnp.dot(
        normed_full.reshape(seq_total * seq_count, model_width),
        joint_weight,
        preferred_element_type=jnp.float32,
    )
    projected = projected.reshape(seq_total, seq_count, 3, local_width)
    query = (projected[:, :, 0] + b_qv[0]).astype(jnp.bfloat16)
    keys = projected[:, :, 1].astype(jnp.bfloat16)
    values = (projected[:, :, 2] + b_qv[1]).astype(jnp.bfloat16)

    def item(array, s, h):
        return array[:, s, h * head_size : (h + 1) * head_size]

    def per_row(items):
        stacked = jnp.stack(items).reshape(seq_count, local_heads, seq_total, head_size)
        return jnp.transpose(stacked, (2, 0, 1, 3)).reshape(seq_total, seq_count, local_width)

    pairs = [(s, h) for s in range(seq_count) for h in range(local_heads)]
    forward_items = [
        attention_forward(
            item(query, s, h), item(keys, s, h), item(values, s, h), seq_lengths[s : s + 1]
        )
        for s, h in pairs
    ]
    attended = per_row([o for o, _ in forward_items])
    out_weight = w_o.reshape(local_width, model_width)
    positions = tensor_rank * row_count + jnp.arange(row_count, dtype=jnp.int32)
    live = positions[:, None] < seq_lengths[None, :]
    upstream = jnp.where(live[:, :, None], cotangent, jnp.zeros_like(cotangent))
    upstream_full = lax.all_gather(upstream, "tensor", axis=0, tiled=True)
    attention_part = jnp.einsum(
        "rse,ed->rsd", attended, out_weight, preferred_element_type=jnp.float32
    ).astype(jnp.bfloat16)
    attention_part, upstream_full = lax.optimization_barrier((attention_part, upstream_full))
    attention = (
        lax.psum_scatter(attention_part, "tensor", scatter_dimension=0, tiled=True).astype(
            jnp.float32
        )
        + b_o
    )
    middle = inputs + attention
    act_grad = jnp.einsum("rsd,fd->rsf", upstream_full, w_out, preferred_element_type=jnp.float32)
    middle, act_grad = lax.optimization_barrier((middle, act_grad))
    second_low = layer_norm(middle, ln2_gain, ln2_bias).astype(jnp.bfloat16)
    second_full = lax.all_gather(second_low, "tensor", axis=0, tiled=True)
    pre_act = (
        jnp.dot(
            second_full.reshape(seq_total * seq_count, model_width),
            w_in,
            preferred_element_type=jnp.float32,
        )
        + b_in
    )
    activated = gelu_tanh(pre_act).astype(jnp.bfloat16).reshape(seq_total, seq_count, hidden)
    piece = upstream_full
    grad_w_out = jnp.einsum("rsf,rsd->fd", activated, piece, preferred_element_type=jnp.float32)
    gelu_back = jax.vjp(gelu_tanh, pre_act)[1]
    pre_low = gelu_back(act_grad.reshape(seq_total * seq_count, hidden))[0].astype(jnp.bfloat16)
    grad_b_in = jnp.sum(pre_low, axis=0, dtype=jnp.float32)
    grad_w_in = jnp.einsum(
        "rd,rf->df",
        second_full.reshape(seq_total * seq_count, model_width),
        pre_low,
        preferred_element_type=jnp.float32,
    )
    pre_rows = pre_low.reshape(seq_total, seq_count, hidden)
    piece = pre_rows
    second_part = jnp.einsum("rsf,df->rsd", piece, w_in, preferred_element_type=jnp.float32)
    second_part = second_part.astype(jnp.bfloat16)
    feed_input, second_part = lax.optimization_barrier((activated, second_part))
    second_grad = lax.psum_scatter(
        second_part, "tensor", scatter_dimension=0, tiled=True
    ).astype(jnp.float32)
    feed_part = jnp.einsum(
        "rsf,fd->rsd", feed_input, w_out, preferred_element_type=jnp.float32
    ).astype(jnp.bfloat16)
    feed_buffer = jnp.concatenate([jnp.zeros_like(feed_part), feed_part], 2)
    feed_buffer, second_grad = lax.optimization_barrier((feed_buffer, second_grad))
    norm_two_back = jax.vjp(layer_norm, middle, ln2_gain, ln2_bias)[1]
    middle_part, grad_ln2_gain, grad_ln2_bias = norm_two_back(second_grad)
    middle_grad = upstream.astype(jnp.float32) + middle_part
    branch_low = middle_grad.astype(jnp.bfloat16)
    grad_b_o = jnp.sum(branch_low, axis=(0, 1), dtype=jnp.float32)
    grad_b_out = jnp.sum(upstream, axis=(0, 1), dtype=jnp.float32)
    summed_in = halving_sum(grad_w_in * factor, 0)
    summed_out = halving_sum(grad_w_out * factor, 1)
    summed_in, summed_out, branch_low = lax.optimization_barrier(
        (summed_in, summed_out, branch_low)
    )
    piece = lax.all_gather(branch_low, "tensor", axis=0, tiled=True)
    weight_grad = jnp.einsum("rse,rsd->ed", attended, piece, preferred_element_type=jnp.float32)
    part = jnp.einsum("rsd,ed->rse", piece, out_weight, preferred_element_type=jnp.float32)
    attended_grad = part.astype(jnp.bfloat16)
    backward_items = [
        attention_backward(
            item(query, s, h),
            item(keys, s, h),
            item(values, s, h),
            item(attended_grad, s, h),
            lse,
            seq_lengths[s : s + 1],
        )
        for (s, h), (_, lse) in zip(pairs, forward_items)
    ]
    joint_grad = jnp.stack(
        [per_row([grads[kind] for grads in backward_items]) for kind in range(3)], axis=2
    )
    grad_b_qv = jnp.sum(joint_grad[:, :, 0::2], axis=(0, 1), dtype=jnp.float32)
    joint_rows = joint_grad.reshape(seq_total, seq_count, 3 * local_width)
    grad_w_qkv = jnp.einsum(
        "rd,rc->dc",
        normed_full.reshape(seq_total * seq_count, model_width),
        joint_rows.reshape(seq_total * seq_count, 3 * local_width),
        preferred_element_type=jnp.float32,
    )
    normed_part = jnp.einsum(
        "rsc,dc->rsd", joint_rows, joint_weight, preferred_element_type=jnp.float32
    ).astype(jnp.bfloat16)
    joint_sums = jnp.sum(joint_rows, axis=(0, 1), dtype=jnp.float32)
    grad_ln1_bias = jnp.dot(
        joint_weight.astype(jnp.float32), joint_sums, precision=lax.Precision.HIGHEST
    )
    merged = lax.dynamic_update_slice(feed_buffer, normed_part, (0, 0, 0))
    both = lax.psum_scatter(merged, "tensor", scatter_dimension=0, tiled=True)
    summed = (
        halving_sum(grad_w_qkv * factor, 0).reshape(-1, 3, local_heads, head_size),
        halving_sum(weight_grad.reshape(local_heads, head_size, model_width) * factor, 2),
        summed_in,
        summed_out,
    )
    in_full = lax.dynamic_update_slice_in_dim(
        jnp.zeros((hidden * tensor_count,), jnp.float32), grad_b_in, tensor_rank * hidden, 0
    )
    joint_full = lax.dynamic_update_slice_in_dim(
        jnp.zeros((2, local_width * tensor_count), jnp.float32),
        grad_b_qv,
        tensor_rank * local_width,
        1,
    )
    early = reduce_vectors(
        (
            grad_ln1_bias,
            grad_b_o,
            grad_ln2_gain,
            grad_ln2_bias,
            grad_b_out,
            joint_full[0],
            joint_full[1],
            in_full,
        ),
        factor,
    )
    both, summed, early = lax.optimization_barrier((both, summed, early))
    both = both.astype(jnp.float32)
    normed_grad = both[:, :, :model_width]
    feed = both[:, :, model_width:] + b_out
    output = (middle + feed).astype(jnp.bfloat16)
    norm_one_back = jax.vjp(layer_norm, inputs, ln1_gain, ln1_bias)[1]
    input_part, grad_ln1_gain, _ = norm_one_back(normed_grad)
    input_grad = (middle_grad + input_part).astype(jnp.bfloat16)
    (late,) = reduce_vectors((grad_ln1_gain,), factor)
    return (
        output,
        input_grad,
        late,
        early[0],
        summed[0],
        jnp.stack((early[5], early[6])),
        summed[1],
        early[1],
        early[2],
        early[3],
        summed[2],
        early[7],
        summed[3],
        early[4],
    )


def reduce_vectors(vectors, factor):
    tensor_count = lax.axis_size("tensor")
    group_count = lax.axis_size("group")
    dp_count = lax.axis_size("dp")
    pieces = [
        jnp.transpose((item * factor).reshape(group_count * dp_count, tensor_count, -1), (1, 0, 2))
        for item in vectors
    ]
    widths = [piece.shape[2] for piece in pieces]
    packed = jnp.concatenate(pieces, 2)
    packed = halving_steps(
        packed, 0, [("tensor", tensor_count, bit) for bit in (8, 4, 2, 1)]
    )
    packed = halving_steps(
        packed, 1, [("group", group_count, 2), ("group", group_count, 1), ("dp", dp_count, 1)]
    )
    flat = packed.reshape(-1)
    parts = []
    offset = 0
    for width in widths:
        parts.append(flat[offset : offset + width])
        offset += width
    return tuple(parts)


def halving_steps(value, dim, steps, send_type=None):
    for axis, size, bit in steps:
        half = value.shape[dim] // 2
        low_half = lax.slice_in_dim(value, 0, half, axis=dim)
        high_half = lax.slice_in_dim(value, half, 2 * half, axis=dim)
        upper = (lax.axis_index(axis) // bit) % 2 == 1
        keep = jnp.where(upper, high_half, low_half)
        send = jnp.where(upper, low_half, high_half)
        if send_type is not None:
            send = send.astype(send_type)
        got = lax.ppermute(send, axis, [(i, i ^ bit) for i in range(size)])
        value = keep + got.astype(keep.dtype)
    return value


def halving_sum(value, dim):
    shape = value.shape
    groups = lax.axis_size("group")
    dps = lax.axis_size("dp")
    split = shape[:dim] + (groups * dps, shape[dim] // (groups * dps)) + shape[dim + 1 :]
    value = value.reshape(split)
    value = halving_steps(
        value, dim, [("group", groups, 2), ("group", groups, 1), ("dp", dps, 1)], jnp.bfloat16
    )
    return value.reshape(shape[:dim] + (shape[dim] // (groups * dps),) + shape[dim + 1 :])


def solution(mesh):
    in_specs = (
        P("tensor", ("group", "dp"), None),
        P("tensor", ("group", "dp"), None),
        P(),
        P(),
        P(),
        P(None, None, "tensor", None),
        P(None, "tensor"),
        P("tensor", None, None),
        P(),
        P(),
        P(),
        P(None, "tensor"),
        P("tensor"),
        P("tensor", None),
        P(),
    )
    out_specs = (
        P("tensor", ("group", "dp"), None),
        P("tensor", ("group", "dp"), None),
        P(("group", "dp", "tensor")),
        P(("group", "dp", "tensor")),
        P(("group", "dp"), None, "tensor", None),
        P(None, ("group", "dp", "tensor")),
        P("tensor", None, ("group", "dp")),
        P(("group", "dp", "tensor")),
        P(("group", "dp", "tensor")),
        P(("group", "dp", "tensor")),
        P(("group", "dp"), "tensor"),
        P(("group", "dp", "tensor")),
        P("tensor", ("group", "dp")),
        P(("group", "dp", "tensor")),
    )
    return jax.shard_map(shards, mesh=mesh, in_specs=in_specs, out_specs=out_specs, check_vma=False)
```

```python
from functools import partial
import math

import jax
import jax.numpy as jnp
from jax import lax
from jax.experimental import pallas as pl
from jax.experimental.pallas import tpu as pltpu
from jax.sharding import PartitionSpec as P

EPS = 1e-05
NEGATIVE = -1e30


def layer_norm(value, gain, shift):
    mean = jnp.mean(value, axis=-1, keepdims=True)
    centred = value - mean
    spread = jnp.mean(centred * centred, axis=-1, keepdims=True)
    return centred * lax.rsqrt(spread + EPS) * gain + shift


def gelu_tanh(value):
    return jax.nn.gelu(value, approximate=True)


def _valid(first_q, first_k, rows, cols, length):
    q_pos = first_q + lax.broadcasted_iota(jnp.int32, (rows, cols), 0)
    k_pos = first_k + lax.broadcasted_iota(jnp.int32, (rows, cols), 1)
    return (k_pos <= q_pos) & (k_pos < length)


def _key_blocks(i, block_q, block_k, length):
    causal = (i * block_q + block_q + block_k - 1) // block_k
    live = (length + block_k - 1) // block_k
    return jnp.minimum(causal, live)


def _attn_fwd_kernel(len_ref, q_ref, k_ref, v_ref, o_ref, lse_ref, s_buf, *, block_q, block_k, scale):
    i = pl.program_id(0)
    length = len_ref[0]
    count = _key_blocks(i, block_q, block_k, length)
    q = q_ref[...]

    def scores(j, m):
        first = pl.multiple_of(j * block_k, block_k)
        k = k_ref[pl.ds(first, block_k), :]
        s = lax.dot_general(q, k, (((1,), (1,)), ((), ())), preferred_element_type=jnp.float32)
        s = jnp.where(_valid(i * block_q, first, block_q, block_k, length), s * scale, NEGATIVE)
        s_buf[:, pl.ds(first, block_k)] = s
        return jnp.maximum(m, jnp.max(s, axis=1, keepdims=True))

    peak = lax.fori_loop(0, count, scores, jnp.full((block_q, 1), NEGATIVE, jnp.float32))

    def exps(j, total):
        first = pl.multiple_of(j * block_k, block_k)
        e = jnp.exp(s_buf[:, pl.ds(first, block_k)] - peak)
        s_buf[:, pl.ds(first, block_k)] = e
        return total + jnp.sum(e, axis=1, keepdims=True)

    total = lax.fori_loop(0, count, exps, jnp.zeros((block_q, 1), jnp.float32))

    inverse = 1.0 / total

    def mix(j, acc):
        first = pl.multiple_of(j * block_k, block_k)
        probs = (s_buf[:, pl.ds(first, block_k)] * inverse).astype(jnp.bfloat16)
        return acc + jnp.dot(probs, v_ref[pl.ds(first, block_k), :], preferred_element_type=jnp.float32)

    acc = lax.fori_loop(0, count, mix, jnp.zeros(o_ref.shape, jnp.float32))
    o_ref[...] = acc.astype(o_ref.dtype)
    lse_ref[...] = peak + jnp.log(total)


def attention_forward(q, k, v, length, *, block_q=256, block_k=256):
    n, d = q.shape
    scale = 1.0 / math.sqrt(d)
    kernel = partial(_attn_fwd_kernel, block_q=block_q, block_k=block_k, scale=scale)
    pairs = (n // block_q) * (n // block_k + 1) // 2
    return pl.pallas_call(
        kernel,
        out_shape=(jax.ShapeDtypeStruct((n, d), jnp.bfloat16), jax.ShapeDtypeStruct((n, 1), jnp.float32)),
        grid_spec=pltpu.PrefetchScalarGridSpec(
            num_scalar_prefetch=1,
            grid=(n // block_q,),
            in_specs=[
                pl.BlockSpec((block_q, d), lambda i, lens: (i, 0)),
                pl.BlockSpec((n, d), lambda i, lens: (0, 0)),
                pl.BlockSpec((n, d), lambda i, lens: (0, 0)),
            ],
            out_specs=[
                pl.BlockSpec((block_q, d), lambda i, lens: (i, 0)),
                pl.BlockSpec((block_q, 1), lambda i, lens: (i, 0)),
            ],
            scratch_shapes=[pltpu.VMEM((block_q, n), jnp.float32)],
        ),
        compiler_params=pltpu.CompilerParams(dimension_semantics=("arbitrary",)),
        cost_estimate=pl.CostEstimate(
            flops=4 * pairs * block_q * block_k * d,
            transcendentals=pairs * block_q * block_k,
            bytes_accessed=4 * n * d * 2,
        ),
    )(length, q, k, v)


def _attn_bwd_kernel(len_ref, q_ref, k_ref, v_ref, do_ref, lse_ref, dq_ref, dk_ref, dv_ref,
                     p_buf, dp_buf, dk_acc, dv_acc, *, block_q, block_k, scale):
    i = pl.program_id(0)
    length = len_ref[0]

    @pl.when(i == 0)
    def _():
        dk_acc[...] = jnp.zeros_like(dk_acc)
        dv_acc[...] = jnp.zeros_like(dv_acc)

    live = i * block_q < length

    @pl.when(live)
    def _():
        count = _key_blocks(i, block_q, block_k, length)
        q = q_ref[...]
        do = do_ref[...]
        lse = lse_ref[...]

        def first_pass(j, inner):
            first = pl.multiple_of(j * block_k, block_k)
            k = k_ref[pl.ds(first, block_k), :]
            v = v_ref[pl.ds(first, block_k), :]
            s = lax.dot_general(q, k, (((1,), (1,)), ((), ())), preferred_element_type=jnp.float32)
            valid = _valid(i * block_q, first, block_q, block_k, length)
            s = jnp.where(valid, s * scale, NEGATIVE)
            p = jnp.where(valid, jnp.exp(s - lse), 0.0)
            dp = lax.dot_general(do, v, (((1,), (1,)), ((), ())), preferred_element_type=jnp.float32)
            p_buf[:, pl.ds(first, block_k)] = p
            dp_buf[:, pl.ds(first, block_k)] = dp
            return inner + jnp.sum(p * dp, axis=1, keepdims=True)

        inner = lax.fori_loop(0, count, first_pass, jnp.zeros((block_q, 1), jnp.float32))

        def second_pass(j, dq):
            first = pl.multiple_of(j * block_k, block_k)
            p = p_buf[:, pl.ds(first, block_k)]
            dp = dp_buf[:, pl.ds(first, block_k)]
            ds = (p * (dp - inner)).astype(jnp.bfloat16)
            k = k_ref[pl.ds(first, block_k), :]
            dk_acc[pl.ds(first, block_k), :] += lax.dot_general(
                ds, q, (((0,), (0,)), ((), ())), preferred_element_type=jnp.float32)
            dv_acc[pl.ds(first, block_k), :] += lax.dot_general(
                p.astype(jnp.bfloat16), do, (((0,), (0,)), ((), ())), preferred_element_type=jnp.float32)
            return dq + jnp.dot(ds, k, preferred_element_type=jnp.float32)

        dq = lax.fori_loop(0, count, second_pass, jnp.zeros(dq_ref.shape, jnp.float32))
        dq_ref[...] = (dq * scale).astype(dq_ref.dtype)

    @pl.when(jnp.logical_not(live))
    def _():
        dq_ref[...] = jnp.zeros_like(dq_ref)

    @pl.when(i == pl.num_programs(0) - 1)
    def _():
        dk_ref[...] = (dk_acc[...] * scale).astype(dk_ref.dtype)
        dv_ref[...] = dv_acc[...].astype(dv_ref.dtype)


def attention_backward(q, k, v, do, lse, length, *, block_q=256, block_k=256):
    n, d = q.shape
    scale = 1.0 / math.sqrt(d)
    kernel = partial(_attn_bwd_kernel, block_q=block_q, block_k=block_k, scale=scale)
    pairs = (n // block_q) * (n // block_k + 1) // 2
    full = pl.BlockSpec((n, d), lambda i, lens: (0, 0))
    rows = pl.BlockSpec((block_q, d), lambda i, lens: (i, 0))
    return pl.pallas_call(
        kernel,
        out_shape=tuple(jax.ShapeDtypeStruct((n, d), jnp.bfloat16) for _ in range(3)),
        grid_spec=pltpu.PrefetchScalarGridSpec(
            num_scalar_prefetch=1,
            grid=(n // block_q,),
            in_specs=[rows, full, full, rows, pl.BlockSpec((block_q, 1), lambda i, lens: (i, 0))],
            out_specs=[rows, full, full],
            scratch_shapes=[
                pltpu.VMEM((block_q, n), jnp.float32),
                pltpu.VMEM((block_q, n), jnp.float32),
                pltpu.VMEM((n, d), jnp.float32),
                pltpu.VMEM((n, d), jnp.float32),
            ],
        ),
        compiler_params=pltpu.CompilerParams(dimension_semantics=("arbitrary",)),
        cost_estimate=pl.CostEstimate(
            flops=8 * pairs * block_q * block_k * d,
            transcendentals=pairs * block_q * block_k,
            bytes_accessed=8 * n * d * 2,
        ),
    )(length, q, k, v, do, lse)


def shards(
    tokens,
    cotangent,
    lengths,
    ln1_gain,
    ln1_bias,
    w_qkv,
    b_qv,
    w_o,
    b_o,
    ln2_gain,
    ln2_bias,
    w_in,
    b_in,
    w_out,
    b_out,
):
    row_count, seq_count, model_width = tokens.shape
    tensor_count = lax.axis_size("tensor")
    tensor_rank = lax.axis_index("tensor")
    seq_total = row_count * tensor_count
    local_heads = w_qkv.shape[2]
    head_size = w_qkv.shape[3]
    local_width = local_heads * head_size
    hidden = w_in.shape[1]
    group_count = lax.axis_size("group")
    group_rank = lax.axis_index("group")
    member = group_rank * lax.axis_size("dp") + lax.axis_index("dp")
    seq_lengths = lax.dynamic_slice_in_dim(lengths, member * seq_count, seq_count, 0)
    group_totals = jnp.sum(lengths.reshape(group_count, -1), axis=1).astype(jnp.float32)
    factor = (
        group_count
        * lax.dynamic_index_in_dim(group_totals, group_rank, 0, keepdims=False)
        / jnp.sum(group_totals)
    )
    inputs = tokens.astype(jnp.float32)
    normed_low = layer_norm(inputs, ln1_gain, ln1_bias).astype(jnp.bfloat16)
    normed_full = lax.all_gather(normed_low, "tensor", axis=0, tiled=True)
    joint_weight = w_qkv.reshape(model_width, 3 * local_width)
    projected = jnp.dot(
        normed_full.reshape(seq_total * seq_count, model_width),
        joint_weight,
        preferred_element_type=jnp.float32,
    )
    projected = projected.reshape(seq_total, seq_count, 3, local_width)
    query = (projected[:, :, 0] + b_qv[0]).astype(jnp.bfloat16)
    keys = projected[:, :, 1].astype(jnp.bfloat16)
    values = (projected[:, :, 2] + b_qv[1]).astype(jnp.bfloat16)

    def item(array, s, h):
        return array[:, s, h * head_size : (h + 1) * head_size]

    def per_row(items):
        stacked = jnp.stack(items).reshape(seq_count, local_heads, seq_total, head_size)
        return jnp.transpose(stacked, (2, 0, 1, 3)).reshape(seq_total, seq_count, local_width)

    pairs = [(s, h) for s in range(seq_count) for h in range(local_heads)]
    forward_items = [
        attention_forward(
            item(query, s, h), item(keys, s, h), item(values, s, h), seq_lengths[s : s + 1]
        )
        for s, h in pairs
    ]
    attended = per_row([o for o, _ in forward_items])
    out_weight = w_o.reshape(local_width, model_width)
    positions = tensor_rank * row_count + jnp.arange(row_count, dtype=jnp.int32)
    live = positions[:, None] < seq_lengths[None, :]
    upstream = jnp.where(live[:, :, None], cotangent, jnp.zeros_like(cotangent))
    upstream_full = lax.all_gather(upstream, "tensor", axis=0, tiled=True)
    attention_part = jnp.einsum(
        "rse,ed->rsd", attended, out_weight, preferred_element_type=jnp.float32
    ).astype(jnp.bfloat16)
    attention_part, upstream_full = lax.optimization_barrier((attention_part, upstream_full))
    attention = (
        lax.psum_scatter(attention_part, "tensor", scatter_dimension=0, tiled=True).astype(
            jnp.float32
        )
        + b_o
    )
    middle = inputs + attention
    act_grad = jnp.einsum("rsd,fd->rsf", upstream_full, w_out, preferred_element_type=jnp.float32)
    middle, act_grad = lax.optimization_barrier((middle, act_grad))
    second_low = layer_norm(middle, ln2_gain, ln2_bias).astype(jnp.bfloat16)
    second_full = lax.all_gather(second_low, "tensor", axis=0, tiled=True)
    pre_act = (
        jnp.dot(
            second_full.reshape(seq_total * seq_count, model_width),
            w_in,
            preferred_element_type=jnp.float32,
        )
        + b_in
    )
    activated = gelu_tanh(pre_act).astype(jnp.bfloat16).reshape(seq_total, seq_count, hidden)
    piece = upstream_full
    grad_w_out = jnp.einsum("rsf,rsd->fd", activated, piece, preferred_element_type=jnp.float32)
    gelu_back = jax.vjp(gelu_tanh, pre_act)[1]
    pre_low = gelu_back(act_grad.reshape(seq_total * seq_count, hidden))[0].astype(jnp.bfloat16)
    grad_b_in = jnp.sum(pre_low, axis=0, dtype=jnp.float32)
    grad_w_in = jnp.einsum(
        "rd,rf->df",
        second_full.reshape(seq_total * seq_count, model_width),
        pre_low,
        preferred_element_type=jnp.float32,
    )
    pre_rows = pre_low.reshape(seq_total, seq_count, hidden)
    piece = pre_rows
    second_part = jnp.einsum("rsf,df->rsd", piece, w_in, preferred_element_type=jnp.float32)
    second_part = second_part.astype(jnp.bfloat16)
    feed_input, second_part = lax.optimization_barrier((activated, second_part))
    second_grad = lax.psum_scatter(
        second_part, "tensor", scatter_dimension=0, tiled=True
    ).astype(jnp.float32)
    feed_part = jnp.einsum(
        "rsf,fd->rsd", feed_input, w_out, preferred_element_type=jnp.float32
    ).astype(jnp.bfloat16)
    feed_buffer = lax.dynamic_update_slice(
        jnp.zeros(feed_part.shape[:2] + (2 * model_width,), feed_part.dtype),
        feed_part,
        (0, 0, model_width),
    )
    feed_buffer, second_grad = lax.optimization_barrier((feed_buffer, second_grad))
    norm_two_back = jax.vjp(layer_norm, middle, ln2_gain, ln2_bias)[1]
    middle_part, grad_ln2_gain, grad_ln2_bias = norm_two_back(second_grad)
    middle_grad = upstream.astype(jnp.float32) + middle_part
    branch_low = middle_grad.astype(jnp.bfloat16)
    grad_b_o = jnp.sum(branch_low, axis=(0, 1), dtype=jnp.float32)
    grad_b_out = jnp.sum(upstream, axis=(0, 1), dtype=jnp.float32)
    summed_in = halving_sum(grad_w_in * factor, 0)
    summed_out = halving_sum(grad_w_out * factor, 1)
    summed_in, summed_out, branch_low = lax.optimization_barrier(
        (summed_in, summed_out, branch_low)
    )
    piece = lax.all_gather(branch_low, "tensor", axis=0, tiled=True)
    weight_grad = jnp.einsum("rse,rsd->ed", attended, piece, preferred_element_type=jnp.float32)
    part = jnp.einsum("rsd,ed->rse", piece, out_weight, preferred_element_type=jnp.float32)
    attended_grad = part.astype(jnp.bfloat16)
    backward_items = [
        attention_backward(
            item(query, s, h),
            item(keys, s, h),
            item(values, s, h),
            item(attended_grad, s, h),
            lse,
            seq_lengths[s : s + 1],
        )
        for (s, h), (_, lse) in zip(pairs, forward_items)
    ]
    joint_grad = jnp.stack(
        [per_row([grads[kind] for grads in backward_items]) for kind in range(3)], axis=2
    )
    grad_b_qv = jnp.sum(joint_grad[:, :, 0::2], axis=(0, 1), dtype=jnp.float32)
    joint_rows = joint_grad.reshape(seq_total, seq_count, 3 * local_width)
    grad_w_qkv = jnp.einsum(
        "rd,rc->dc",
        normed_full.reshape(seq_total * seq_count, model_width),
        joint_rows.reshape(seq_total * seq_count, 3 * local_width),
        preferred_element_type=jnp.float32,
    )
    normed_part = jnp.einsum(
        "rsc,dc->rsd", joint_rows, joint_weight, preferred_element_type=jnp.float32
    ).astype(jnp.bfloat16)
    joint_sums = jnp.sum(joint_rows, axis=(0, 1), dtype=jnp.float32)
    grad_ln1_bias = jnp.dot(
        joint_weight.astype(jnp.float32), joint_sums, precision=lax.Precision.HIGHEST
    )
    merged = lax.dynamic_update_slice(feed_buffer, normed_part, (0, 0, 0))
    both = lax.psum_scatter(merged, "tensor", scatter_dimension=0, tiled=True)
    summed = (
        halving_sum(grad_w_qkv * factor, 0).reshape(-1, 3, local_heads, head_size),
        halving_sum(weight_grad.reshape(local_heads, head_size, model_width) * factor, 2),
        summed_in,
        summed_out,
    )
    in_full = lax.dynamic_update_slice_in_dim(
        jnp.zeros((hidden * tensor_count,), jnp.float32), grad_b_in, tensor_rank * hidden, 0
    )
    joint_full = lax.dynamic_update_slice_in_dim(
        jnp.zeros((2, local_width * tensor_count), jnp.float32),
        grad_b_qv,
        tensor_rank * local_width,
        1,
    )
    early = reduce_vectors(
        (
            grad_ln1_bias,
            grad_b_o,
            grad_ln2_gain,
            grad_ln2_bias,
            grad_b_out,
            joint_full[0],
            joint_full[1],
            in_full,
        ),
        factor,
    )
    both, summed, early = lax.optimization_barrier((both, summed, early))
    both = both.astype(jnp.float32)
    normed_grad = both[:, :, :model_width]
    feed = both[:, :, model_width:] + b_out
    output = (middle + feed).astype(jnp.bfloat16)
    norm_one_back = jax.vjp(layer_norm, inputs, ln1_gain, ln1_bias)[1]
    input_part, grad_ln1_gain, _ = norm_one_back(normed_grad)
    input_grad = (middle_grad + input_part).astype(jnp.bfloat16)
    (late,) = reduce_vectors((grad_ln1_gain,), factor)
    return (
        output,
        input_grad,
        late,
        early[0],
        summed[0],
        jnp.stack((early[5], early[6])),
        summed[1],
        early[1],
        early[2],
        early[3],
        summed[2],
        early[7],
        summed[3],
        early[4],
    )


def reduce_vectors(vectors, factor):
    tensor_count = lax.axis_size("tensor")
    group_count = lax.axis_size("group")
    dp_count = lax.axis_size("dp")
    pieces = [
        jnp.transpose((item * factor).reshape(group_count * dp_count, tensor_count, -1), (1, 0, 2))
        for item in vectors
    ]
    widths = [piece.shape[2] for piece in pieces]
    packed = jnp.concatenate(pieces, 2)
    packed = halving_steps(
        packed, 0, [("tensor", tensor_count, bit) for bit in (8, 4, 2, 1)]
    )
    packed = halving_steps(
        packed, 1, [("group", group_count, 2), ("group", group_count, 1), ("dp", dp_count, 1)]
    )
    flat = packed.reshape(-1)
    parts = []
    offset = 0
    for width in widths:
        parts.append(flat[offset : offset + width])
        offset += width
    return tuple(parts)


def halving_steps(value, dim, steps, send_type=None):
    for axis, size, bit in steps:
        half = value.shape[dim] // 2
        low_half = lax.slice_in_dim(value, 0, half, axis=dim)
        high_half = lax.slice_in_dim(value, half, 2 * half, axis=dim)
        upper = (lax.axis_index(axis) // bit) % 2 == 1
        keep = jnp.where(upper, high_half, low_half)
        send = jnp.where(upper, low_half, high_half)
        if send_type is not None:
            send = send.astype(send_type)
        got = lax.ppermute(send, axis, [(i, i ^ bit) for i in range(size)])
        value = keep + got.astype(keep.dtype)
    return value


def halving_sum(value, dim):
    shape = value.shape
    groups = lax.axis_size("group")
    dps = lax.axis_size("dp")
    rest = shape[dim] // (groups * dps)
    value = value.reshape(shape[:dim] + (groups // 2, 2, dps * rest) + shape[dim + 1 :])
    value = jnp.swapaxes(value, dim, dim + 1)
    value = value.reshape(shape[:dim] + (groups * dps, rest) + shape[dim + 1 :])
    value = halving_steps(
        value, dim, [("group", groups, 1), ("group", groups, 2), ("dp", dps, 1)], jnp.bfloat16
    )
    return value.reshape(shape[:dim] + (shape[dim] // (groups * dps),) + shape[dim + 1 :])


def solution(mesh):
    in_specs = (
        P("tensor", ("group", "dp"), None),
        P("tensor", ("group", "dp"), None),
        P(),
        P(),
        P(),
        P(None, None, "tensor", None),
        P(None, "tensor"),
        P("tensor", None, None),
        P(),
        P(),
        P(),
        P(None, "tensor"),
        P("tensor"),
        P("tensor", None),
        P(),
    )
    out_specs = (
        P("tensor", ("group", "dp"), None),
        P("tensor", ("group", "dp"), None),
        P(("group", "dp", "tensor")),
        P(("group", "dp", "tensor")),
        P(("group", "dp"), None, "tensor", None),
        P(None, ("group", "dp", "tensor")),
        P("tensor", None, ("group", "dp")),
        P(("group", "dp", "tensor")),
        P(("group", "dp", "tensor")),
        P(("group", "dp", "tensor")),
        P(("group", "dp"), "tensor"),
        P(("group", "dp", "tensor")),
        P("tensor", ("group", "dp")),
        P(("group", "dp", "tensor")),
    )
    return jax.shard_map(shards, mesh=mesh, in_specs=in_specs, out_specs=out_specs, check_vma=False)
```

```python
from functools import partial
import math

import jax
import jax.numpy as jnp
from jax import lax
from jax.experimental import pallas as pl
from jax.experimental.pallas import tpu as pltpu
from jax.sharding import PartitionSpec as P

EPS = 1e-05
NEGATIVE = -1e30


def layer_norm(value, gain, shift):
    mean = jnp.mean(value, axis=-1, keepdims=True)
    centred = value - mean
    spread = jnp.mean(centred * centred, axis=-1, keepdims=True)
    return centred * lax.rsqrt(spread + EPS) * gain + shift


def gelu_tanh(value):
    return jax.nn.gelu(value, approximate=True)


def _valid(first_q, first_k, rows, cols, length):
    q_pos = first_q + lax.broadcasted_iota(jnp.int32, (rows, cols), 0)
    k_pos = first_k + lax.broadcasted_iota(jnp.int32, (rows, cols), 1)
    return (k_pos <= q_pos) & (k_pos < length)


def _key_blocks(i, block_q, block_k, length):
    causal = (i * block_q + block_q + block_k - 1) // block_k
    live = (length + block_k - 1) // block_k
    return jnp.minimum(causal, live)


def _attn_fwd_kernel(len_ref, q_ref, k_ref, v_ref, o_ref, lse_ref, s_buf, *, block_q, block_k, scale):
    i = pl.program_id(0)
    length = len_ref[0]
    count = _key_blocks(i, block_q, block_k, length)
    q = q_ref[...]

    def scores(j, m):
        first = pl.multiple_of(j * block_k, block_k)
        k = k_ref[pl.ds(first, block_k), :]
        s = lax.dot_general(q, k, (((1,), (1,)), ((), ())), preferred_element_type=jnp.float32)
        s = jnp.where(_valid(i * block_q, first, block_q, block_k, length), s * scale, NEGATIVE)
        s_buf[:, pl.ds(first, block_k)] = s
        return jnp.maximum(m, jnp.max(s, axis=1, keepdims=True))

    peak = lax.fori_loop(0, count, scores, jnp.full((block_q, 1), NEGATIVE, jnp.float32))

    def exps(j, total):
        first = pl.multiple_of(j * block_k, block_k)
        e = jnp.exp(s_buf[:, pl.ds(first, block_k)] - peak)
        s_buf[:, pl.ds(first, block_k)] = e
        return total + jnp.sum(e, axis=1, keepdims=True)

    total = lax.fori_loop(0, count, exps, jnp.zeros((block_q, 1), jnp.float32))

    inverse = 1.0 / total

    def mix(j, acc):
        first = pl.multiple_of(j * block_k, block_k)
        probs = (s_buf[:, pl.ds(first, block_k)] * inverse).astype(jnp.bfloat16)
        return acc + jnp.dot(probs, v_ref[pl.ds(first, block_k), :], preferred_element_type=jnp.float32)

    acc = lax.fori_loop(0, count, mix, jnp.zeros(o_ref.shape, jnp.float32))
    o_ref[...] = acc.astype(o_ref.dtype)
    lse_ref[...] = peak + jnp.log(total)


def attention_forward(q, k, v, length, *, block_q=256, block_k=256):
    n, d = q.shape
    scale = 1.0 / math.sqrt(d)
    kernel = partial(_attn_fwd_kernel, block_q=block_q, block_k=block_k, scale=scale)
    pairs = (n // block_q) * (n // block_k + 1) // 2
    return pl.pallas_call(
        kernel,
        out_shape=(jax.ShapeDtypeStruct((n, d), jnp.bfloat16), jax.ShapeDtypeStruct((n, 1), jnp.float32)),
        grid_spec=pltpu.PrefetchScalarGridSpec(
            num_scalar_prefetch=1,
            grid=(n // block_q,),
            in_specs=[
                pl.BlockSpec((block_q, d), lambda i, lens: (i, 0)),
                pl.BlockSpec((n, d), lambda i, lens: (0, 0)),
                pl.BlockSpec((n, d), lambda i, lens: (0, 0)),
            ],
            out_specs=[
                pl.BlockSpec((block_q, d), lambda i, lens: (i, 0)),
                pl.BlockSpec((block_q, 1), lambda i, lens: (i, 0)),
            ],
            scratch_shapes=[pltpu.VMEM((block_q, n), jnp.float32)],
        ),
        compiler_params=pltpu.CompilerParams(dimension_semantics=("arbitrary",)),
        cost_estimate=pl.CostEstimate(
            flops=4 * pairs * block_q * block_k * d,
            transcendentals=pairs * block_q * block_k,
            bytes_accessed=4 * n * d * 2,
        ),
    )(length, q, k, v)


def _attn_bwd_kernel(len_ref, q_ref, k_ref, v_ref, do_ref, lse_ref, dq_ref, dk_ref, dv_ref,
                     p_buf, dp_buf, dk_acc, dv_acc, *, block_q, block_k, scale):
    i = pl.program_id(0)
    length = len_ref[0]

    @pl.when(i == 0)
    def _():
        dk_acc[...] = jnp.zeros_like(dk_acc)
        dv_acc[...] = jnp.zeros_like(dv_acc)

    live = i * block_q < length

    @pl.when(live)
    def _():
        count = _key_blocks(i, block_q, block_k, length)
        q = q_ref[...]
        do = do_ref[...]
        lse = lse_ref[...]

        def first_pass(j, inner):
            first = pl.multiple_of(j * block_k, block_k)
            k = k_ref[pl.ds(first, block_k), :]
            v = v_ref[pl.ds(first, block_k), :]
            s = lax.dot_general(q, k, (((1,), (1,)), ((), ())), preferred_element_type=jnp.float32)
            valid = _valid(i * block_q, first, block_q, block_k, length)
            s = jnp.where(valid, s * scale, NEGATIVE)
            p = jnp.where(valid, jnp.exp(s - lse), 0.0)
            dp = lax.dot_general(do, v, (((1,), (1,)), ((), ())), preferred_element_type=jnp.float32)
            p_buf[:, pl.ds(first, block_k)] = p
            dp_buf[:, pl.ds(first, block_k)] = dp
            return inner + jnp.sum(p * dp, axis=1, keepdims=True)

        inner = lax.fori_loop(0, count, first_pass, jnp.zeros((block_q, 1), jnp.float32))

        def second_pass(j, dq):
            first = pl.multiple_of(j * block_k, block_k)
            p = p_buf[:, pl.ds(first, block_k)]
            dp = dp_buf[:, pl.ds(first, block_k)]
            ds = (p * (dp - inner)).astype(jnp.bfloat16)
            k = k_ref[pl.ds(first, block_k), :]
            dk_acc[pl.ds(first, block_k), :] += lax.dot_general(
                ds, q, (((0,), (0,)), ((), ())), preferred_element_type=jnp.float32)
            dv_acc[pl.ds(first, block_k), :] += lax.dot_general(
                p.astype(jnp.bfloat16), do, (((0,), (0,)), ((), ())), preferred_element_type=jnp.float32)
            return dq + jnp.dot(ds, k, preferred_element_type=jnp.float32)

        dq = lax.fori_loop(0, count, second_pass, jnp.zeros(dq_ref.shape, jnp.float32))
        dq_ref[...] = (dq * scale).astype(dq_ref.dtype)

    @pl.when(jnp.logical_not(live))
    def _():
        dq_ref[...] = jnp.zeros_like(dq_ref)

    @pl.when(i == pl.num_programs(0) - 1)
    def _():
        dk_ref[...] = (dk_acc[...] * scale).astype(dk_ref.dtype)
        dv_ref[...] = dv_acc[...].astype(dv_ref.dtype)


def attention_backward(q, k, v, do, lse, length, *, block_q=256, block_k=256):
    n, d = q.shape
    scale = 1.0 / math.sqrt(d)
    kernel = partial(_attn_bwd_kernel, block_q=block_q, block_k=block_k, scale=scale)
    pairs = (n // block_q) * (n // block_k + 1) // 2
    full = pl.BlockSpec((n, d), lambda i, lens: (0, 0))
    rows = pl.BlockSpec((block_q, d), lambda i, lens: (i, 0))
    return pl.pallas_call(
        kernel,
        out_shape=tuple(jax.ShapeDtypeStruct((n, d), jnp.bfloat16) for _ in range(3)),
        grid_spec=pltpu.PrefetchScalarGridSpec(
            num_scalar_prefetch=1,
            grid=(n // block_q,),
            in_specs=[rows, full, full, rows, pl.BlockSpec((block_q, 1), lambda i, lens: (i, 0))],
            out_specs=[rows, full, full],
            scratch_shapes=[
                pltpu.VMEM((block_q, n), jnp.float32),
                pltpu.VMEM((block_q, n), jnp.float32),
                pltpu.VMEM((n, d), jnp.float32),
                pltpu.VMEM((n, d), jnp.float32),
            ],
        ),
        compiler_params=pltpu.CompilerParams(dimension_semantics=("arbitrary",)),
        cost_estimate=pl.CostEstimate(
            flops=8 * pairs * block_q * block_k * d,
            transcendentals=pairs * block_q * block_k,
            bytes_accessed=8 * n * d * 2,
        ),
    )(length, q, k, v, do, lse)


GRID = 4


def grid_pairs(axis_of, delta):
    out = []
    for s in range(GRID * GRID):
        x, y = divmod(s, GRID)
        if axis_of == "x":
            out.append((s, ((x + delta) % GRID) * GRID + y))
        else:
            out.append((s, x * GRID + (y + delta) % GRID))
    return out


def grid_position(axis_of):
    t = lax.axis_index("tensor")
    return t // GRID if axis_of == "x" else t % GRID


def gather_line(block, axis_of):
    pos = grid_position(axis_of)
    from_left = lax.ppermute(block, "tensor", grid_pairs(axis_of, 1))
    from_right = lax.ppermute(block, "tensor", grid_pairs(axis_of, -1))
    half = block.shape[0] // 2
    far_low = lax.ppermute(from_left[:half], "tensor", grid_pairs(axis_of, 1))
    far_high = lax.ppermute(from_right[half:], "tensor", grid_pairs(axis_of, -1))
    far = jnp.concatenate([far_low, far_high], 0)
    ring = jnp.stack([block, from_right, far, from_left, block, from_right, far, from_left])
    return lax.dynamic_slice_in_dim(ring, (GRID - pos) % GRID, GRID, 0)


def gather_tensor(block):
    rows, cols = block.shape
    mid = cols // 2
    first = gather_line(block[:, :mid], "y").reshape(GRID * rows, mid)
    first = gather_line(first, "x").reshape(GRID * GRID * rows, mid)
    second = gather_line(block[:, mid:], "x").reshape(GRID * rows, cols - mid)
    second = gather_line(second, "y").reshape(GRID, GRID, rows, cols - mid)
    second = jnp.transpose(second, (1, 0, 2, 3)).reshape(GRID * GRID * rows, cols - mid)
    return jnp.concatenate([first, second], 1)


def shards(
    tokens,
    cotangent,
    lengths,
    ln1_gain,
    ln1_bias,
    w_qkv,
    b_qv,
    w_o,
    b_o,
    ln2_gain,
    ln2_bias,
    w_in,
    b_in,
    w_out,
    b_out,
):
    row_count, seq_count, model_width = tokens.shape
    tensor_count = lax.axis_size("tensor")
    tensor_rank = lax.axis_index("tensor")
    seq_total = row_count * tensor_count
    local_heads = w_qkv.shape[2]
    head_size = w_qkv.shape[3]
    local_width = local_heads * head_size
    hidden = w_in.shape[1]
    group_count = lax.axis_size("group")
    group_rank = lax.axis_index("group")
    member = group_rank * lax.axis_size("dp") + lax.axis_index("dp")
    seq_lengths = lax.dynamic_slice_in_dim(lengths, member * seq_count, seq_count, 0)
    group_totals = jnp.sum(lengths.reshape(group_count, -1), axis=1).astype(jnp.float32)
    factor = (
        group_count
        * lax.dynamic_index_in_dim(group_totals, group_rank, 0, keepdims=False)
        / jnp.sum(group_totals)
    )
    inputs = tokens.astype(jnp.float32)
    normed_low = layer_norm(inputs, ln1_gain, ln1_bias).astype(jnp.bfloat16)
    normed_full = lax.all_gather(normed_low, "tensor", axis=0, tiled=True)
    joint_weight = w_qkv.reshape(model_width, 3 * local_width)
    projected = jnp.dot(
        normed_full.reshape(seq_total * seq_count, model_width),
        joint_weight,
        preferred_element_type=jnp.float32,
    )
    projected = projected.reshape(seq_total, seq_count, 3, local_width)
    query = (projected[:, :, 0] + b_qv[0]).astype(jnp.bfloat16)
    keys = projected[:, :, 1].astype(jnp.bfloat16)
    values = (projected[:, :, 2] + b_qv[1]).astype(jnp.bfloat16)

    def item(array, s, h):
        return array[:, s, h * head_size : (h + 1) * head_size]

    def per_row(items):
        stacked = jnp.stack(items).reshape(seq_count, local_heads, seq_total, head_size)
        return jnp.transpose(stacked, (2, 0, 1, 3)).reshape(seq_total, seq_count, local_width)

    pairs = [(s, h) for s in range(seq_count) for h in range(local_heads)]
    forward_items = [
        attention_forward(
            item(query, s, h), item(keys, s, h), item(values, s, h), seq_lengths[s : s + 1]
        )
        for s, h in pairs
    ]
    attended = per_row([o for o, _ in forward_items])
    out_weight = w_o.reshape(local_width, model_width)
    positions = tensor_rank * row_count + jnp.arange(row_count, dtype=jnp.int32)
    live = positions[:, None] < seq_lengths[None, :]
    upstream = jnp.where(live[:, :, None], cotangent, jnp.zeros_like(cotangent))
    upstream_full = gather_tensor(upstream.reshape(row_count, seq_count * model_width)).reshape(
        seq_total, seq_count, model_width
    )
    attention_part = jnp.einsum(
        "rse,ed->rsd", attended, out_weight, preferred_element_type=jnp.float32
    ).astype(jnp.bfloat16)
    attention_part, upstream_full = lax.optimization_barrier((attention_part, upstream_full))
    attention = (
        lax.psum_scatter(attention_part, "tensor", scatter_dimension=0, tiled=True).astype(
            jnp.float32
        )
        + b_o
    )
    middle = inputs + attention
    act_grad = jnp.einsum("rsd,fd->rsf", upstream_full, w_out, preferred_element_type=jnp.float32)
    middle, act_grad = lax.optimization_barrier((middle, act_grad))
    second_low = layer_norm(middle, ln2_gain, ln2_bias).astype(jnp.bfloat16)
    second_full = lax.all_gather(second_low, "tensor", axis=0, tiled=True)
    pre_act = (
        jnp.dot(
            second_full.reshape(seq_total * seq_count, model_width),
            w_in,
            preferred_element_type=jnp.float32,
        )
        + b_in
    )
    activated = gelu_tanh(pre_act).astype(jnp.bfloat16).reshape(seq_total, seq_count, hidden)
    piece = upstream_full
    grad_w_out = jnp.einsum("rsf,rsd->fd", activated, piece, preferred_element_type=jnp.float32)
    gelu_back = jax.vjp(gelu_tanh, pre_act)[1]
    pre_low = gelu_back(act_grad.reshape(seq_total * seq_count, hidden))[0].astype(jnp.bfloat16)
    grad_b_in = jnp.sum(pre_low, axis=0, dtype=jnp.float32)
    grad_w_in = jnp.einsum(
        "rd,rf->df",
        second_full.reshape(seq_total * seq_count, model_width),
        pre_low,
        preferred_element_type=jnp.float32,
    )
    pre_rows = pre_low.reshape(seq_total, seq_count, hidden)
    piece = pre_rows
    second_part = jnp.einsum("rsf,df->rsd", piece, w_in, preferred_element_type=jnp.float32)
    second_part = second_part.astype(jnp.bfloat16)
    feed_input, second_part = lax.optimization_barrier((activated, second_part))
    second_grad = lax.psum_scatter(
        second_part, "tensor", scatter_dimension=0, tiled=True
    ).astype(jnp.float32)
    feed_part = jnp.einsum(
        "rsf,fd->rsd", feed_input, w_out, preferred_element_type=jnp.float32
    ).astype(jnp.bfloat16)
    feed_buffer = lax.dynamic_update_slice(
        jnp.zeros(feed_part.shape[:2] + (2 * model_width,), feed_part.dtype),
        feed_part,
        (0, 0, model_width),
    )
    feed_buffer, second_grad = lax.optimization_barrier((feed_buffer, second_grad))
    norm_two_back = jax.vjp(layer_norm, middle, ln2_gain, ln2_bias)[1]
    middle_part, grad_ln2_gain, grad_ln2_bias = norm_two_back(second_grad)
    middle_grad = upstream.astype(jnp.float32) + middle_part
    branch_low = middle_grad.astype(jnp.bfloat16)
    grad_b_o = jnp.sum(branch_low, axis=(0, 1), dtype=jnp.float32)
    grad_b_out = jnp.sum(upstream, axis=(0, 1), dtype=jnp.float32)
    feed_buffer, scaled_in = lax.optimization_barrier((feed_buffer, grad_w_in * factor))
    summed_in = halving_sum(scaled_in, 0)
    summed_out = halving_sum(grad_w_out * factor, 1)
    summed_in, summed_out, branch_low = lax.optimization_barrier(
        (summed_in, summed_out, branch_low)
    )
    piece = lax.all_gather(branch_low, "tensor", axis=0, tiled=True)
    weight_grad = jnp.einsum("rse,rsd->ed", attended, piece, preferred_element_type=jnp.float32)
    part = jnp.einsum("rsd,ed->rse", piece, out_weight, preferred_element_type=jnp.float32)
    attended_grad = part.astype(jnp.bfloat16)
    backward_items = [
        attention_backward(
            item(query, s, h),
            item(keys, s, h),
            item(values, s, h),
            item(attended_grad, s, h),
            lse,
            seq_lengths[s : s + 1],
        )
        for (s, h), (_, lse) in zip(pairs, forward_items)
    ]
    joint_grad = jnp.stack(
        [per_row([grads[kind] for grads in backward_items]) for kind in range(3)], axis=2
    )
    grad_b_qv = jnp.sum(joint_grad[:, :, 0::2], axis=(0, 1), dtype=jnp.float32)
    joint_rows = joint_grad.reshape(seq_total, seq_count, 3 * local_width)
    grad_w_qkv = jnp.einsum(
        "rd,rc->dc",
        normed_full.reshape(seq_total * seq_count, model_width),
        joint_rows.reshape(seq_total * seq_count, 3 * local_width),
        preferred_element_type=jnp.float32,
    )
    normed_part = jnp.einsum(
        "rsc,dc->rsd", joint_rows, joint_weight, preferred_element_type=jnp.float32
    ).astype(jnp.bfloat16)
    joint_sums = jnp.sum(joint_rows, axis=(0, 1), dtype=jnp.float32)
    grad_ln1_bias = jnp.dot(
        joint_weight.astype(jnp.float32), joint_sums, precision=lax.Precision.HIGHEST
    )
    merged = lax.dynamic_update_slice(feed_buffer, normed_part, (0, 0, 0))
    both = lax.psum_scatter(merged, "tensor", scatter_dimension=0, tiled=True)
    summed = (
        halving_sum(grad_w_qkv * factor, 0).reshape(-1, 3, local_heads, head_size),
        halving_sum(weight_grad.reshape(local_heads, head_size, model_width) * factor, 2),
        summed_in,
        summed_out,
    )
    in_full = lax.dynamic_update_slice_in_dim(
        jnp.zeros((hidden * tensor_count,), jnp.float32), grad_b_in, tensor_rank * hidden, 0
    )
    joint_full = lax.dynamic_update_slice_in_dim(
        jnp.zeros((2, local_width * tensor_count), jnp.float32),
        grad_b_qv,
        tensor_rank * local_width,
        1,
    )
    early = reduce_vectors(
        (
            grad_ln1_bias,
            grad_b_o,
            grad_ln2_gain,
            grad_ln2_bias,
            grad_b_out,
            joint_full[0],
            joint_full[1],
            in_full,
        ),
        factor,
    )
    both, summed, early = lax.optimization_barrier((both, summed, early))
    both = both.astype(jnp.float32)
    normed_grad = both[:, :, :model_width]
    feed = both[:, :, model_width:] + b_out
    output = (middle + feed).astype(jnp.bfloat16)
    norm_one_back = jax.vjp(layer_norm, inputs, ln1_gain, ln1_bias)[1]
    input_part, grad_ln1_gain, _ = norm_one_back(normed_grad)
    input_grad = (middle_grad + input_part).astype(jnp.bfloat16)
    (late,) = reduce_vectors((grad_ln1_gain,), factor)
    return (
        output,
        input_grad,
        late,
        early[0],
        summed[0],
        jnp.stack((early[5], early[6])),
        summed[1],
        early[1],
        early[2],
        early[3],
        summed[2],
        early[7],
        summed[3],
        early[4],
    )


def reduce_vectors(vectors, factor):
    tensor_count = lax.axis_size("tensor")
    group_count = lax.axis_size("group")
    dp_count = lax.axis_size("dp")
    pieces = [
        jnp.transpose((item * factor).reshape(group_count * dp_count, tensor_count, -1), (1, 0, 2))
        for item in vectors
    ]
    widths = [piece.shape[2] for piece in pieces]
    packed = jnp.concatenate(pieces, 2)
    packed = halving_steps(
        packed, 0, [("tensor", tensor_count, bit) for bit in (8, 4, 2, 1)]
    )
    packed = halving_steps(
        packed, 1, [("group", group_count, 2), ("group", group_count, 1), ("dp", dp_count, 1)]
    )
    flat = packed.reshape(-1)
    parts = []
    offset = 0
    for width in widths:
        parts.append(flat[offset : offset + width])
        offset += width
    return tuple(parts)


def halving_steps(value, dim, steps, send_type=None):
    for axis, size, bit in steps:
        half = value.shape[dim] // 2
        low_half = lax.slice_in_dim(value, 0, half, axis=dim)
        high_half = lax.slice_in_dim(value, half, 2 * half, axis=dim)
        upper = (lax.axis_index(axis) // bit) % 2 == 1
        keep = jnp.where(upper, high_half, low_half)
        send = jnp.where(upper, low_half, high_half)
        if send_type is not None:
            send = send.astype(send_type)
        got = lax.ppermute(send, axis, [(i, i ^ bit) for i in range(size)])
        value = keep + got.astype(keep.dtype)
    return value


def halving_sum(value, dim):
    shape = value.shape
    groups = lax.axis_size("group")
    dps = lax.axis_size("dp")
    rest = shape[dim] // (groups * dps)
    value = value.reshape(shape[:dim] + (groups // 2, 2, dps * rest) + shape[dim + 1 :])
    value = jnp.swapaxes(value, dim, dim + 1)
    value = value.reshape(shape[:dim] + (groups * dps, rest) + shape[dim + 1 :])
    value = halving_steps(
        value, dim, [("group", groups, 1), ("group", groups, 2), ("dp", dps, 1)], jnp.bfloat16
    )
    return value.reshape(shape[:dim] + (shape[dim] // (groups * dps),) + shape[dim + 1 :])


def solution(mesh):
    in_specs = (
        P("tensor", ("group", "dp"), None),
        P("tensor", ("group", "dp"), None),
        P(),
        P(),
        P(),
        P(None, None, "tensor", None),
        P(None, "tensor"),
        P("tensor", None, None),
        P(),
        P(),
        P(),
        P(None, "tensor"),
        P("tensor"),
        P("tensor", None),
        P(),
    )
    out_specs = (
        P("tensor", ("group", "dp"), None),
        P("tensor", ("group", "dp"), None),
        P(("group", "dp", "tensor")),
        P(("group", "dp", "tensor")),
        P(("group", "dp"), None, "tensor", None),
        P(None, ("group", "dp", "tensor")),
        P("tensor", None, ("group", "dp")),
        P(("group", "dp", "tensor")),
        P(("group", "dp", "tensor")),
        P(("group", "dp", "tensor")),
        P(("group", "dp"), "tensor"),
        P(("group", "dp", "tensor")),
        P("tensor", ("group", "dp")),
        P(("group", "dp", "tensor")),
    )
    return jax.shard_map(shards, mesh=mesh, in_specs=in_specs, out_specs=out_specs, check_vma=False)
```

```python
from functools import partial
import math

import jax
import jax.numpy as jnp
from jax import lax
from jax.experimental import pallas as pl
from jax.experimental.pallas import tpu as pltpu
from jax.sharding import PartitionSpec as P

EPS = 1e-05
NEGATIVE = -1e30


def layer_norm(value, gain, shift):
    mean = jnp.mean(value, axis=-1, keepdims=True)
    centred = value - mean
    spread = jnp.mean(centred * centred, axis=-1, keepdims=True)
    return centred * lax.rsqrt(spread + EPS) * gain + shift


def gelu_tanh(value):
    return jax.nn.gelu(value, approximate=True)


def _valid(first_q, first_k, rows, cols, length):
    q_pos = first_q + lax.broadcasted_iota(jnp.int32, (rows, cols), 0)
    k_pos = first_k + lax.broadcasted_iota(jnp.int32, (rows, cols), 1)
    return (k_pos <= q_pos) & (k_pos < length)


def _key_blocks(i, block_q, block_k, length):
    causal = (i * block_q + block_q + block_k - 1) // block_k
    live = (length + block_k - 1) // block_k
    return jnp.minimum(causal, live)


def _attn_fwd_kernel(len_ref, q_ref, k_ref, v_ref, o_ref, lse_ref, s_buf, *, block_q, block_k, scale):
    i = pl.program_id(0)
    length = len_ref[0]
    count = _key_blocks(i, block_q, block_k, length)
    q = q_ref[...]

    def scores(j, m):
        first = pl.multiple_of(j * block_k, block_k)
        k = k_ref[pl.ds(first, block_k), :]
        s = lax.dot_general(q, k, (((1,), (1,)), ((), ())), preferred_element_type=jnp.float32) * scale
        edge = (first + block_k > i * block_q) | (first + block_k > length)
        s = lax.cond(
            edge,
            lambda v: jnp.where(_valid(i * block_q, first, block_q, block_k, length), v, NEGATIVE),
            lambda v: v,
            s,
        )
        s_buf[:, pl.ds(first, block_k)] = s
        return jnp.maximum(m, jnp.max(s, axis=1, keepdims=True))

    peak = lax.fori_loop(0, count, scores, jnp.full((block_q, 1), NEGATIVE, jnp.float32))

    def exps(j, total):
        first = pl.multiple_of(j * block_k, block_k)
        e = jnp.exp(s_buf[:, pl.ds(first, block_k)] - peak)
        s_buf[:, pl.ds(first, block_k)] = e
        return total + jnp.sum(e, axis=1, keepdims=True)

    total = lax.fori_loop(0, count, exps, jnp.zeros((block_q, 1), jnp.float32))

    inverse = 1.0 / total

    def mix(j, acc):
        first = pl.multiple_of(j * block_k, block_k)
        probs = (s_buf[:, pl.ds(first, block_k)] * inverse).astype(jnp.bfloat16)
        return acc + jnp.dot(probs, v_ref[pl.ds(first, block_k), :], preferred_element_type=jnp.float32)

    acc = lax.fori_loop(0, count, mix, jnp.zeros(o_ref.shape, jnp.float32))
    o_ref[...] = acc.astype(o_ref.dtype)
    lse_ref[...] = peak + jnp.log(total)


def attention_forward(q, k, v, length, *, block_q=256, block_k=256):
    n, d = q.shape
    scale = 1.0 / math.sqrt(d)
    kernel = partial(_attn_fwd_kernel, block_q=block_q, block_k=block_k, scale=scale)
    pairs = (n // block_q) * (n // block_k + 1) // 2
    return pl.pallas_call(
        kernel,
        out_shape=(jax.ShapeDtypeStruct((n, d), jnp.bfloat16), jax.ShapeDtypeStruct((n, 1), jnp.float32)),
        grid_spec=pltpu.PrefetchScalarGridSpec(
            num_scalar_prefetch=1,
            grid=(n // block_q,),
            in_specs=[
                pl.BlockSpec((block_q, d), lambda i, lens: (i, 0)),
                pl.BlockSpec((n, d), lambda i, lens: (0, 0)),
                pl.BlockSpec((n, d), lambda i, lens: (0, 0)),
            ],
            out_specs=[
                pl.BlockSpec((block_q, d), lambda i, lens: (i, 0)),
                pl.BlockSpec((block_q, 1), lambda i, lens: (i, 0)),
            ],
            scratch_shapes=[pltpu.VMEM((block_q, n), jnp.float32)],
        ),
        compiler_params=pltpu.CompilerParams(dimension_semantics=("arbitrary",)),
        cost_estimate=pl.CostEstimate(
            flops=4 * pairs * block_q * block_k * d,
            transcendentals=pairs * block_q * block_k,
            bytes_accessed=4 * n * d * 2,
        ),
    )(length, q, k, v)


def _attn_bwd_kernel(len_ref, q_ref, k_ref, v_ref, do_ref, lse_ref, dq_ref, dk_ref, dv_ref,
                     p_buf, dp_buf, dk_acc, dv_acc, *, block_q, block_k, scale):
    i = pl.program_id(0)
    length = len_ref[0]

    @pl.when(i == 0)
    def _():
        dk_acc[...] = jnp.zeros_like(dk_acc)
        dv_acc[...] = jnp.zeros_like(dv_acc)

    live = i * block_q < length

    @pl.when(live)
    def _():
        count = _key_blocks(i, block_q, block_k, length)
        q = q_ref[...]
        do = do_ref[...]
        lse = lse_ref[...]

        def first_pass(j, inner):
            first = pl.multiple_of(j * block_k, block_k)
            k = k_ref[pl.ds(first, block_k), :]
            v = v_ref[pl.ds(first, block_k), :]
            s = lax.dot_general(q, k, (((1,), (1,)), ((), ())), preferred_element_type=jnp.float32)
            edge = (first + block_k > i * block_q) | (first + block_k > length)
            p = lax.cond(
                edge,
                lambda v: jnp.where(
                    _valid(i * block_q, first, block_q, block_k, length),
                    jnp.exp(jnp.where(_valid(i * block_q, first, block_q, block_k, length), v, NEGATIVE) - lse),
                    0.0,
                ),
                lambda v: jnp.exp(v - lse),
                s * scale,
            )
            dp = lax.dot_general(do, v, (((1,), (1,)), ((), ())), preferred_element_type=jnp.float32)
            p_buf[:, pl.ds(first, block_k)] = p
            dp_buf[:, pl.ds(first, block_k)] = dp
            return inner + jnp.sum(p * dp, axis=1, keepdims=True)

        inner = lax.fori_loop(0, count, first_pass, jnp.zeros((block_q, 1), jnp.float32))

        def second_pass(j, dq):
            first = pl.multiple_of(j * block_k, block_k)
            p = p_buf[:, pl.ds(first, block_k)]
            dp = dp_buf[:, pl.ds(first, block_k)]
            ds = (p * (dp - inner)).astype(jnp.bfloat16)
            k = k_ref[pl.ds(first, block_k), :]
            dk_acc[pl.ds(first, block_k), :] += lax.dot_general(
                ds, q, (((0,), (0,)), ((), ())), preferred_element_type=jnp.float32)
            dv_acc[pl.ds(first, block_k), :] += lax.dot_general(
                p.astype(jnp.bfloat16), do, (((0,), (0,)), ((), ())), preferred_element_type=jnp.float32)
            return dq + jnp.dot(ds, k, preferred_element_type=jnp.float32)

        dq = lax.fori_loop(0, count, second_pass, jnp.zeros(dq_ref.shape, jnp.float32))
        dq_ref[...] = (dq * scale).astype(dq_ref.dtype)

    @pl.when(jnp.logical_not(live))
    def _():
        dq_ref[...] = jnp.zeros_like(dq_ref)

    @pl.when(i == pl.num_programs(0) - 1)
    def _():
        dk_ref[...] = (dk_acc[...] * scale).astype(dk_ref.dtype)
        dv_ref[...] = dv_acc[...].astype(dv_ref.dtype)


def attention_backward(q, k, v, do, lse, length, *, block_q=256, block_k=256):
    n, d = q.shape
    scale = 1.0 / math.sqrt(d)
    kernel = partial(_attn_bwd_kernel, block_q=block_q, block_k=block_k, scale=scale)
    pairs = (n // block_q) * (n // block_k + 1) // 2
    full = pl.BlockSpec((n, d), lambda i, lens: (0, 0))
    rows = pl.BlockSpec((block_q, d), lambda i, lens: (i, 0))
    return pl.pallas_call(
        kernel,
        out_shape=tuple(jax.ShapeDtypeStruct((n, d), jnp.bfloat16) for _ in range(3)),
        grid_spec=pltpu.PrefetchScalarGridSpec(
            num_scalar_prefetch=1,
            grid=(n // block_q,),
            in_specs=[rows, full, full, rows, pl.BlockSpec((block_q, 1), lambda i, lens: (i, 0))],
            out_specs=[rows, full, full],
            scratch_shapes=[
                pltpu.VMEM((block_q, n), jnp.float32),
                pltpu.VMEM((block_q, n), jnp.float32),
                pltpu.VMEM((n, d), jnp.float32),
                pltpu.VMEM((n, d), jnp.float32),
            ],
        ),
        compiler_params=pltpu.CompilerParams(dimension_semantics=("arbitrary",)),
        cost_estimate=pl.CostEstimate(
            flops=8 * pairs * block_q * block_k * d,
            transcendentals=pairs * block_q * block_k,
            bytes_accessed=8 * n * d * 2,
        ),
    )(length, q, k, v, do, lse)


def shards(
    tokens,
    cotangent,
    lengths,
    ln1_gain,
    ln1_bias,
    w_qkv,
    b_qv,
    w_o,
    b_o,
    ln2_gain,
    ln2_bias,
    w_in,
    b_in,
    w_out,
    b_out,
):
    row_count, seq_count, model_width = tokens.shape
    tensor_count = lax.axis_size("tensor")
    tensor_rank = lax.axis_index("tensor")
    seq_total = row_count * tensor_count
    local_heads = w_qkv.shape[2]
    head_size = w_qkv.shape[3]
    local_width = local_heads * head_size
    hidden = w_in.shape[1]
    group_count = lax.axis_size("group")
    group_rank = lax.axis_index("group")
    member = group_rank * lax.axis_size("dp") + lax.axis_index("dp")
    seq_lengths = lax.dynamic_slice_in_dim(lengths, member * seq_count, seq_count, 0)
    group_totals = jnp.sum(lengths.reshape(group_count, -1), axis=1).astype(jnp.float32)
    factor = (
        group_count
        * lax.dynamic_index_in_dim(group_totals, group_rank, 0, keepdims=False)
        / jnp.sum(group_totals)
    )
    inputs = tokens.astype(jnp.float32)
    normed_low = layer_norm(inputs, ln1_gain, ln1_bias).astype(jnp.bfloat16)
    normed_full = lax.all_gather(normed_low, "tensor", axis=0, tiled=True)
    joint_weight = w_qkv.reshape(model_width, 3 * local_width)
    projected = jnp.dot(
        normed_full.reshape(seq_total * seq_count, model_width),
        joint_weight,
        preferred_element_type=jnp.float32,
    )
    projected = projected.reshape(seq_total, seq_count, 3, local_width)
    query = (projected[:, :, 0] + b_qv[0]).astype(jnp.bfloat16)
    keys = projected[:, :, 1].astype(jnp.bfloat16)
    values = (projected[:, :, 2] + b_qv[1]).astype(jnp.bfloat16)

    def item(array, s, h):
        return array[:, s, h * head_size : (h + 1) * head_size]

    def per_row(items):
        stacked = jnp.stack(items).reshape(seq_count, local_heads, seq_total, head_size)
        return jnp.transpose(stacked, (2, 0, 1, 3)).reshape(seq_total, seq_count, local_width)

    pairs = [(s, h) for s in range(seq_count) for h in range(local_heads)]
    forward_items = [
        attention_forward(
            item(query, s, h), item(keys, s, h), item(values, s, h), seq_lengths[s : s + 1]
        )
        for s, h in pairs
    ]
    attended = per_row([o for o, _ in forward_items])
    out_weight = w_o.reshape(local_width, model_width)
    positions = tensor_rank * row_count + jnp.arange(row_count, dtype=jnp.int32)
    live = positions[:, None] < seq_lengths[None, :]
    upstream = jnp.where(live[:, :, None], cotangent, jnp.zeros_like(cotangent))
    upstream_full = lax.all_gather(upstream, "tensor", axis=0, tiled=True)
    attention_part = jnp.einsum(
        "rse,ed->rsd", attended, out_weight, preferred_element_type=jnp.float32
    ).astype(jnp.bfloat16)
    attention_part, upstream_full = lax.optimization_barrier((attention_part, upstream_full))
    attention = (
        lax.psum_scatter(attention_part, "tensor", scatter_dimension=0, tiled=True).astype(
            jnp.float32
        )
        + b_o
    )
    middle = inputs + attention
    act_grad = jnp.einsum("rsd,fd->rsf", upstream_full, w_out, preferred_element_type=jnp.float32)
    middle, act_grad = lax.optimization_barrier((middle, act_grad))
    second_low = layer_norm(middle, ln2_gain, ln2_bias).astype(jnp.bfloat16)
    second_full = lax.all_gather(second_low, "tensor", axis=0, tiled=True)
    pre_act = (
        jnp.dot(
            second_full.reshape(seq_total * seq_count, model_width),
            w_in,
            preferred_element_type=jnp.float32,
        )
        + b_in
    )
    activated = gelu_tanh(pre_act).astype(jnp.bfloat16).reshape(seq_total, seq_count, hidden)
    piece = upstream_full
    grad_w_out = jnp.einsum("rsf,rsd->fd", activated, piece, preferred_element_type=jnp.float32)
    gelu_back = jax.vjp(gelu_tanh, pre_act)[1]
    pre_low = gelu_back(act_grad.reshape(seq_total * seq_count, hidden))[0].astype(jnp.bfloat16)
    grad_b_in = jnp.sum(pre_low, axis=0, dtype=jnp.float32)
    grad_w_in = jnp.einsum(
        "rd,rf->df",
        second_full.reshape(seq_total * seq_count, model_width),
        pre_low,
        preferred_element_type=jnp.float32,
    )
    pre_rows = pre_low.reshape(seq_total, seq_count, hidden)
    piece = pre_rows
    second_part = jnp.einsum("rsf,df->rsd", piece, w_in, preferred_element_type=jnp.float32)
    second_part = second_part.astype(jnp.bfloat16)
    feed_input, second_part = lax.optimization_barrier((activated, second_part))
    second_grad = lax.psum_scatter(
        second_part, "tensor", scatter_dimension=0, tiled=True
    ).astype(jnp.float32)
    feed_part = jnp.einsum(
        "rsf,fd->rsd", feed_input, w_out, preferred_element_type=jnp.float32
    ).astype(jnp.bfloat16)
    feed_buffer = lax.dynamic_update_slice(
        jnp.zeros(feed_part.shape[:2] + (2 * model_width,), feed_part.dtype),
        feed_part,
        (0, 0, model_width),
    )
    feed_buffer, second_grad = lax.optimization_barrier((feed_buffer, second_grad))
    norm_two_back = jax.vjp(layer_norm, middle, ln2_gain, ln2_bias)[1]
    middle_part, grad_ln2_gain, grad_ln2_bias = norm_two_back(second_grad)
    middle_grad = upstream.astype(jnp.float32) + middle_part
    branch_low = middle_grad.astype(jnp.bfloat16)
    grad_b_o = jnp.sum(branch_low, axis=(0, 1), dtype=jnp.float32)
    grad_b_out = jnp.sum(upstream, axis=(0, 1), dtype=jnp.float32)
    feed_buffer, scaled_in = lax.optimization_barrier((feed_buffer, grad_w_in * factor))
    summed_in = halving_sum(scaled_in, 0)
    summed_out = halving_sum(grad_w_out * factor, 1)
    summed_in, summed_out, branch_low = lax.optimization_barrier(
        (summed_in, summed_out, branch_low)
    )
    piece = lax.all_gather(branch_low, "tensor", axis=0, tiled=True)
    weight_grad = jnp.einsum("rse,rsd->ed", attended, piece, preferred_element_type=jnp.float32)
    part = jnp.einsum("rsd,ed->rse", piece, out_weight, preferred_element_type=jnp.float32)
    attended_grad = part.astype(jnp.bfloat16)
    backward_items = [
        attention_backward(
            item(query, s, h),
            item(keys, s, h),
            item(values, s, h),
            item(attended_grad, s, h),
            lse,
            seq_lengths[s : s + 1],
        )
        for (s, h), (_, lse) in zip(pairs, forward_items)
    ]
    joint_grad = jnp.stack(
        [per_row([grads[kind] for grads in backward_items]) for kind in range(3)], axis=2
    )
    grad_b_qv = jnp.sum(joint_grad[:, :, 0::2], axis=(0, 1), dtype=jnp.float32)
    joint_rows = joint_grad.reshape(seq_total, seq_count, 3 * local_width)
    grad_w_qkv = jnp.einsum(
        "rd,rc->dc",
        normed_full.reshape(seq_total * seq_count, model_width),
        joint_rows.reshape(seq_total * seq_count, 3 * local_width),
        preferred_element_type=jnp.float32,
    )
    normed_part = jnp.einsum(
        "rsc,dc->rsd", joint_rows, joint_weight, preferred_element_type=jnp.float32
    ).astype(jnp.bfloat16)
    joint_sums = jnp.sum(joint_rows, axis=(0, 1), dtype=jnp.float32)
    grad_ln1_bias = jnp.dot(
        joint_weight.astype(jnp.float32), joint_sums, precision=lax.Precision.HIGHEST
    )
    merged = lax.dynamic_update_slice(feed_buffer, normed_part, (0, 0, 0))
    both = lax.psum_scatter(merged, "tensor", scatter_dimension=0, tiled=True)
    summed = (
        halving_sum(grad_w_qkv * factor, 0).reshape(-1, 3, local_heads, head_size),
        halving_sum(weight_grad.reshape(local_heads, head_size, model_width) * factor, 2),
        summed_in,
        summed_out,
    )
    in_full = lax.dynamic_update_slice_in_dim(
        jnp.zeros((hidden * tensor_count,), jnp.float32), grad_b_in, tensor_rank * hidden, 0
    )
    joint_full = lax.dynamic_update_slice_in_dim(
        jnp.zeros((2, local_width * tensor_count), jnp.float32),
        grad_b_qv,
        tensor_rank * local_width,
        1,
    )
    early = reduce_vectors(
        (
            grad_ln1_bias,
            grad_b_o,
            grad_ln2_gain,
            grad_ln2_bias,
            grad_b_out,
            joint_full[0],
            joint_full[1],
            in_full,
        ),
        factor,
    )
    both, summed, early = lax.optimization_barrier((both, summed, early))
    both = both.astype(jnp.float32)
    normed_grad = both[:, :, :model_width]
    feed = both[:, :, model_width:] + b_out
    output = (middle + feed).astype(jnp.bfloat16)
    norm_one_back = jax.vjp(layer_norm, inputs, ln1_gain, ln1_bias)[1]
    input_part, grad_ln1_gain, _ = norm_one_back(normed_grad)
    input_grad = (middle_grad + input_part).astype(jnp.bfloat16)
    (late,) = reduce_vectors((grad_ln1_gain,), factor)
    return (
        output,
        input_grad,
        late,
        early[0],
        summed[0],
        jnp.stack((early[5], early[6])),
        summed[1],
        early[1],
        early[2],
        early[3],
        summed[2],
        early[7],
        summed[3],
        early[4],
    )


def reduce_vectors(vectors, factor):
    devices = lax.axis_size("group") * lax.axis_size("dp") * lax.axis_size("tensor")
    pieces = [(item * factor).reshape(devices, -1) for item in vectors]
    widths = [piece.shape[1] for piece in pieces]
    packed = jnp.concatenate(pieces, 1)
    packed = lax.all_to_all(packed, ("group", "dp", "tensor"), 0, 0, tiled=True)
    flat = jnp.sum(packed, axis=0)
    parts = []
    offset = 0
    for width in widths:
        parts.append(flat[offset : offset + width])
        offset += width
    return tuple(parts)


def halving_steps(value, dim, steps, send_type=None):
    for axis, size, bit in steps:
        half = value.shape[dim] // 2
        low_half = lax.slice_in_dim(value, 0, half, axis=dim)
        high_half = lax.slice_in_dim(value, half, 2 * half, axis=dim)
        upper = (lax.axis_index(axis) // bit) % 2 == 1
        keep = jnp.where(upper, high_half, low_half)
        send = jnp.where(upper, low_half, high_half)
        if send_type is not None:
            send = send.astype(send_type)
        got = lax.ppermute(send, axis, [(i, i ^ bit) for i in range(size)])
        value = keep + got.astype(keep.dtype)
    return value


def halving_sum(value, dim):
    shape = value.shape
    groups = lax.axis_size("group")
    dps = lax.axis_size("dp")
    rest = shape[dim] // (groups * dps)
    value = value.reshape(shape[:dim] + (groups // 2, 2, dps * rest) + shape[dim + 1 :])
    value = jnp.swapaxes(value, dim, dim + 1)
    value = value.reshape(shape[:dim] + (groups * dps, rest) + shape[dim + 1 :])
    value = halving_steps(
        value, dim, [("group", groups, 1), ("group", groups, 2), ("dp", dps, 1)], jnp.bfloat16
    )
    return value.reshape(shape[:dim] + (shape[dim] // (groups * dps),) + shape[dim + 1 :])


def solution(mesh):
    in_specs = (
        P("tensor", ("group", "dp"), None),
        P("tensor", ("group", "dp"), None),
        P(),
        P(),
        P(),
        P(None, None, "tensor", None),
        P(None, "tensor"),
        P("tensor", None, None),
        P(),
        P(),
        P(),
        P(None, "tensor"),
        P("tensor"),
        P("tensor", None),
        P(),
    )
    out_specs = (
        P("tensor", ("group", "dp"), None),
        P("tensor", ("group", "dp"), None),
        P(("group", "dp", "tensor")),
        P(("group", "dp", "tensor")),
        P(("group", "dp"), None, "tensor", None),
        P(None, ("group", "dp", "tensor")),
        P("tensor", None, ("group", "dp")),
        P(("group", "dp", "tensor")),
        P(("group", "dp", "tensor")),
        P(("group", "dp", "tensor")),
        P(("group", "dp"), "tensor"),
        P(("group", "dp", "tensor")),
        P("tensor", ("group", "dp")),
        P(("group", "dp", "tensor")),
    )
    return jax.shard_map(shards, mesh=mesh, in_specs=in_specs, out_specs=out_specs, check_vma=False)
```

```python
from functools import partial
import math

import jax
import jax.numpy as jnp
from jax import lax
from jax.experimental import pallas as pl
from jax.experimental.pallas import tpu as pltpu
from jax.sharding import PartitionSpec as P

EPS = 1e-05
NEGATIVE = -1e30


def layer_norm(value, gain, shift):
    mean = jnp.mean(value, axis=-1, keepdims=True)
    centred = value - mean
    spread = jnp.mean(centred * centred, axis=-1, keepdims=True)
    return centred * lax.rsqrt(spread + EPS) * gain + shift


def gelu_tanh(value):
    return jax.nn.gelu(value, approximate=True)


def _valid(first_q, first_k, rows, cols, length):
    q_pos = first_q + lax.broadcasted_iota(jnp.int32, (rows, cols), 0)
    k_pos = first_k + lax.broadcasted_iota(jnp.int32, (rows, cols), 1)
    return (k_pos <= q_pos) & (k_pos < length)


def _key_blocks(i, block_q, block_k, length):
    causal = (i * block_q + block_q + block_k - 1) // block_k
    live = (length + block_k - 1) // block_k
    return jnp.minimum(causal, live)


def _attn_fwd_kernel(len_ref, q_ref, k_ref, v_ref, o_ref, lse_ref, s_buf, *, block_q, block_k, scale):
    i = pl.program_id(0)
    length = len_ref[0]
    count = _key_blocks(i, block_q, block_k, length)
    q = q_ref[...]

    def scores(j, m):
        first = pl.multiple_of(j * block_k, block_k)
        k = k_ref[pl.ds(first, block_k), :]
        s = lax.dot_general(q, k, (((1,), (1,)), ((), ())), preferred_element_type=jnp.float32) * scale
        edge = (first + block_k > i * block_q) | (first + block_k > length)
        s = lax.cond(
            edge,
            lambda v: jnp.where(_valid(i * block_q, first, block_q, block_k, length), v, NEGATIVE),
            lambda v: v,
            s,
        )
        s_buf[:, pl.ds(first, block_k)] = s
        return jnp.maximum(m, jnp.max(s, axis=1, keepdims=True))

    peak = lax.fori_loop(0, count, scores, jnp.full((block_q, 1), NEGATIVE, jnp.float32))

    def exps(j, total):
        first = pl.multiple_of(j * block_k, block_k)
        e = jnp.exp(s_buf[:, pl.ds(first, block_k)] - peak)
        s_buf[:, pl.ds(first, block_k)] = e
        return total + jnp.sum(e, axis=1, keepdims=True)

    total = lax.fori_loop(0, count, exps, jnp.zeros((block_q, 1), jnp.float32))

    inverse = 1.0 / total

    def mix(j, acc):
        first = pl.multiple_of(j * block_k, block_k)
        probs = (s_buf[:, pl.ds(first, block_k)] * inverse).astype(jnp.bfloat16)
        return acc + jnp.dot(probs, v_ref[pl.ds(first, block_k), :], preferred_element_type=jnp.float32)

    acc = lax.fori_loop(0, count, mix, jnp.zeros(o_ref.shape, jnp.float32))
    o_ref[...] = acc.astype(o_ref.dtype)
    lse_ref[...] = peak + jnp.log(total)


def attention_forward(q, k, v, length, *, block_q=256, block_k=256):
    n, d = q.shape
    scale = 1.0 / math.sqrt(d)
    kernel = partial(_attn_fwd_kernel, block_q=block_q, block_k=block_k, scale=scale)
    pairs = (n // block_q) * (n // block_k + 1) // 2
    return pl.pallas_call(
        kernel,
        out_shape=(jax.ShapeDtypeStruct((n, d), jnp.bfloat16), jax.ShapeDtypeStruct((n, 1), jnp.float32)),
        grid_spec=pltpu.PrefetchScalarGridSpec(
            num_scalar_prefetch=1,
            grid=(n // block_q,),
            in_specs=[
                pl.BlockSpec((block_q, d), lambda i, lens: (i, 0)),
                pl.BlockSpec((n, d), lambda i, lens: (0, 0)),
                pl.BlockSpec((n, d), lambda i, lens: (0, 0)),
            ],
            out_specs=[
                pl.BlockSpec((block_q, d), lambda i, lens: (i, 0)),
                pl.BlockSpec((block_q, 1), lambda i, lens: (i, 0)),
            ],
            scratch_shapes=[pltpu.VMEM((block_q, n), jnp.float32)],
        ),
        compiler_params=pltpu.CompilerParams(dimension_semantics=("arbitrary",)),
        cost_estimate=pl.CostEstimate(
            flops=4 * pairs * block_q * block_k * d,
            transcendentals=pairs * block_q * block_k,
            bytes_accessed=4 * n * d * 2,
        ),
    )(length, q, k, v)


def _attn_bwd_kernel(len_ref, q_ref, k_ref, v_ref, do_ref, lse_ref, dq_ref, dk_ref, dv_ref,
                     p_buf, dp_buf, dk_acc, dv_acc, *, block_q, block_k, scale):
    i = pl.program_id(0)
    length = len_ref[0]

    @pl.when(i == 0)
    def _():
        dk_acc[...] = jnp.zeros_like(dk_acc)
        dv_acc[...] = jnp.zeros_like(dv_acc)

    live = i * block_q < length

    @pl.when(live)
    def _():
        count = _key_blocks(i, block_q, block_k, length)
        q = q_ref[...]
        do = do_ref[...]
        lse = lse_ref[...]

        def first_pass(j, inner):
            first = pl.multiple_of(j * block_k, block_k)
            k = k_ref[pl.ds(first, block_k), :]
            v = v_ref[pl.ds(first, block_k), :]
            s = lax.dot_general(q, k, (((1,), (1,)), ((), ())), preferred_element_type=jnp.float32)
            edge = (first + block_k > i * block_q) | (first + block_k > length)
            p = lax.cond(
                edge,
                lambda v: jnp.where(
                    _valid(i * block_q, first, block_q, block_k, length),
                    jnp.exp(jnp.where(_valid(i * block_q, first, block_q, block_k, length), v, NEGATIVE) - lse),
                    0.0,
                ),
                lambda v: jnp.exp(v - lse),
                s * scale,
            )
            dp = lax.dot_general(do, v, (((1,), (1,)), ((), ())), preferred_element_type=jnp.float32)
            p_buf[:, pl.ds(first, block_k)] = p
            dp_buf[:, pl.ds(first, block_k)] = dp
            return inner + jnp.sum(p * dp, axis=1, keepdims=True)

        inner = lax.fori_loop(0, count, first_pass, jnp.zeros((block_q, 1), jnp.float32))

        def second_pass(j, dq):
            first = pl.multiple_of(j * block_k, block_k)
            p = p_buf[:, pl.ds(first, block_k)]
            dp = dp_buf[:, pl.ds(first, block_k)]
            ds = (p * (dp - inner)).astype(jnp.bfloat16)
            k = k_ref[pl.ds(first, block_k), :]
            dk_acc[pl.ds(first, block_k), :] += lax.dot_general(
                ds, q, (((0,), (0,)), ((), ())), preferred_element_type=jnp.float32)
            dv_acc[pl.ds(first, block_k), :] += lax.dot_general(
                p.astype(jnp.bfloat16), do, (((0,), (0,)), ((), ())), preferred_element_type=jnp.float32)
            return dq + jnp.dot(ds, k, preferred_element_type=jnp.float32)

        dq = lax.fori_loop(0, count, second_pass, jnp.zeros(dq_ref.shape, jnp.float32))
        dq_ref[...] = (dq * scale).astype(dq_ref.dtype)

    @pl.when(jnp.logical_not(live))
    def _():
        dq_ref[...] = jnp.zeros_like(dq_ref)

    @pl.when(i == pl.num_programs(0) - 1)
    def _():
        dk_ref[...] = (dk_acc[...] * scale).astype(dk_ref.dtype)
        dv_ref[...] = dv_acc[...].astype(dv_ref.dtype)


def attention_backward(q, k, v, do, lse, length, *, block_q=256, block_k=256):
    n, d = q.shape
    scale = 1.0 / math.sqrt(d)
    kernel = partial(_attn_bwd_kernel, block_q=block_q, block_k=block_k, scale=scale)
    pairs = (n // block_q) * (n // block_k + 1) // 2
    full = pl.BlockSpec((n, d), lambda i, lens: (0, 0))
    rows = pl.BlockSpec((block_q, d), lambda i, lens: (i, 0))
    return pl.pallas_call(
        kernel,
        out_shape=tuple(jax.ShapeDtypeStruct((n, d), jnp.bfloat16) for _ in range(3)),
        grid_spec=pltpu.PrefetchScalarGridSpec(
            num_scalar_prefetch=1,
            grid=(n // block_q,),
            in_specs=[rows, full, full, rows, pl.BlockSpec((block_q, 1), lambda i, lens: (i, 0))],
            out_specs=[rows, full, full],
            scratch_shapes=[
                pltpu.VMEM((block_q, n), jnp.float32),
                pltpu.VMEM((block_q, n), jnp.float32),
                pltpu.VMEM((n, d), jnp.float32),
                pltpu.VMEM((n, d), jnp.float32),
            ],
        ),
        compiler_params=pltpu.CompilerParams(dimension_semantics=("arbitrary",)),
        cost_estimate=pl.CostEstimate(
            flops=8 * pairs * block_q * block_k * d,
            transcendentals=pairs * block_q * block_k,
            bytes_accessed=8 * n * d * 2,
        ),
    )(length, q, k, v, do, lse)


def shards(
    tokens,
    cotangent,
    lengths,
    ln1_gain,
    ln1_bias,
    w_qkv,
    b_qv,
    w_o,
    b_o,
    ln2_gain,
    ln2_bias,
    w_in,
    b_in,
    w_out,
    b_out,
):
    row_count, seq_count, model_width = tokens.shape
    tensor_count = lax.axis_size("tensor")
    tensor_rank = lax.axis_index("tensor")
    seq_total = row_count * tensor_count
    local_heads = w_qkv.shape[2]
    head_size = w_qkv.shape[3]
    local_width = local_heads * head_size
    hidden = w_in.shape[1]
    group_count = lax.axis_size("group")
    group_rank = lax.axis_index("group")
    member = group_rank * lax.axis_size("dp") + lax.axis_index("dp")
    seq_lengths = lax.dynamic_slice_in_dim(lengths, member * seq_count, seq_count, 0)
    group_totals = jnp.sum(lengths.reshape(group_count, -1), axis=1).astype(jnp.float32)
    factor = (
        group_count
        * lax.dynamic_index_in_dim(group_totals, group_rank, 0, keepdims=False)
        / jnp.sum(group_totals)
    )
    inputs = tokens.astype(jnp.float32)
    normed_low = layer_norm(inputs, ln1_gain, ln1_bias).astype(jnp.bfloat16)
    normed_full = lax.all_gather(normed_low, "tensor", axis=0, tiled=True)
    joint_weight = w_qkv.reshape(model_width, 3 * local_width)
    projected = jnp.dot(
        normed_full.reshape(seq_total * seq_count, model_width),
        joint_weight,
        preferred_element_type=jnp.float32,
    )
    projected = projected.reshape(seq_total, seq_count, 3, local_width)
    query = (projected[:, :, 0] + b_qv[0]).astype(jnp.bfloat16)
    keys = projected[:, :, 1].astype(jnp.bfloat16)
    values = (projected[:, :, 2] + b_qv[1]).astype(jnp.bfloat16)

    def item(array, s, h):
        return array[:, s, h * head_size : (h + 1) * head_size]

    def per_row(items):
        stacked = jnp.stack(items).reshape(seq_count, local_heads, seq_total, head_size)
        return jnp.transpose(stacked, (2, 0, 1, 3)).reshape(seq_total, seq_count, local_width)

    pairs = [(s, h) for s in range(seq_count) for h in range(local_heads)]
    forward_items = [
        attention_forward(
            item(query, s, h), item(keys, s, h), item(values, s, h), seq_lengths[s : s + 1]
        )
        for s, h in pairs
    ]
    attended = per_row([o for o, _ in forward_items])
    out_weight = w_o.reshape(local_width, model_width)
    positions = tensor_rank * row_count + jnp.arange(row_count, dtype=jnp.int32)
    live = positions[:, None] < seq_lengths[None, :]
    upstream = jnp.where(live[:, :, None], cotangent, jnp.zeros_like(cotangent))
    upstream_full = lax.all_gather(upstream, "tensor", axis=0, tiled=True)
    attention_part = jnp.einsum(
        "rse,ed->rsd", attended, out_weight, preferred_element_type=jnp.float32
    ).astype(jnp.bfloat16)
    attention_part, upstream_full = lax.optimization_barrier((attention_part, upstream_full))
    attention = (
        lax.psum_scatter(attention_part, "tensor", scatter_dimension=0, tiled=True).astype(
            jnp.float32
        )
        + b_o
    )
    middle = inputs + attention
    act_grad = jnp.einsum("rsd,fd->rsf", upstream_full, w_out, preferred_element_type=jnp.float32)
    middle, act_grad = lax.optimization_barrier((middle, act_grad))
    second_low = layer_norm(middle, ln2_gain, ln2_bias).astype(jnp.bfloat16)
    second_full = lax.all_gather(second_low, "tensor", axis=0, tiled=True)
    pre_act = (
        jnp.dot(
            second_full.reshape(seq_total * seq_count, model_width),
            w_in,
            preferred_element_type=jnp.float32,
        )
        + b_in
    )
    activated = gelu_tanh(pre_act).astype(jnp.bfloat16).reshape(seq_total, seq_count, hidden)
    piece = upstream_full
    grad_w_out = jnp.einsum("rsf,rsd->fd", activated, piece, preferred_element_type=jnp.float32)
    gelu_back = jax.vjp(gelu_tanh, pre_act)[1]
    pre_low = gelu_back(act_grad.reshape(seq_total * seq_count, hidden))[0].astype(jnp.bfloat16)
    grad_b_in = jnp.sum(pre_low, axis=0, dtype=jnp.float32)
    grad_w_in = jnp.einsum(
        "rd,rf->df",
        second_full.reshape(seq_total * seq_count, model_width),
        pre_low,
        preferred_element_type=jnp.float32,
    )
    pre_rows = pre_low.reshape(seq_total, seq_count, hidden)
    piece = pre_rows
    second_part = jnp.einsum("rsf,df->rsd", piece, w_in, preferred_element_type=jnp.float32)
    second_part = second_part.astype(jnp.bfloat16)
    feed_input, second_part = lax.optimization_barrier((activated, second_part))
    second_grad = lax.psum_scatter(
        second_part, "tensor", scatter_dimension=0, tiled=True
    ).astype(jnp.float32)
    feed_part = jnp.einsum(
        "rsf,fd->rsd", feed_input, w_out, preferred_element_type=jnp.float32
    ).astype(jnp.bfloat16)
    feed_buffer = lax.dynamic_update_slice(
        jnp.zeros(feed_part.shape[:2] + (2 * model_width,), feed_part.dtype),
        feed_part,
        (0, 0, model_width),
    )
    feed_buffer, second_grad = lax.optimization_barrier((feed_buffer, second_grad))
    norm_two_back = jax.vjp(layer_norm, middle, ln2_gain, ln2_bias)[1]
    middle_part, grad_ln2_gain, grad_ln2_bias = norm_two_back(second_grad)
    middle_grad = upstream.astype(jnp.float32) + middle_part
    branch_low = middle_grad.astype(jnp.bfloat16)
    grad_b_o = jnp.sum(branch_low, axis=(0, 1), dtype=jnp.float32)
    grad_b_out = jnp.sum(upstream, axis=(0, 1), dtype=jnp.float32)
    summed_in = halving_sum(grad_w_in * factor, 0)
    summed_out = halving_sum(grad_w_out * factor, 1)
    summed_in, summed_out, branch_low = lax.optimization_barrier(
        (summed_in, summed_out, branch_low)
    )
    piece = lax.all_gather(branch_low, "tensor", axis=0, tiled=True)
    weight_grad = jnp.einsum("rse,rsd->ed", attended, piece, preferred_element_type=jnp.float32)
    part = jnp.einsum("rsd,ed->rse", piece, out_weight, preferred_element_type=jnp.float32)
    attended_grad = part.astype(jnp.bfloat16)
    backward_items = [
        attention_backward(
            item(query, s, h),
            item(keys, s, h),
            item(values, s, h),
            item(attended_grad, s, h),
            lse,
            seq_lengths[s : s + 1],
        )
        for (s, h), (_, lse) in zip(pairs, forward_items)
    ]
    joint_grad = jnp.stack(
        [per_row([grads[kind] for grads in backward_items]) for kind in range(3)], axis=2
    )
    grad_b_qv = jnp.sum(joint_grad[:, :, 0::2], axis=(0, 1), dtype=jnp.float32)
    joint_rows = joint_grad.reshape(seq_total, seq_count, 3 * local_width)
    grad_w_qkv = jnp.einsum(
        "rd,rc->dc",
        normed_full.reshape(seq_total * seq_count, model_width),
        joint_rows.reshape(seq_total * seq_count, 3 * local_width),
        preferred_element_type=jnp.float32,
    )
    normed_part = jnp.einsum(
        "rsc,dc->rsd", joint_rows, joint_weight, preferred_element_type=jnp.float32
    ).astype(jnp.bfloat16)
    joint_sums = jnp.sum(joint_rows, axis=(0, 1), dtype=jnp.float32)
    grad_ln1_bias = jnp.dot(
        joint_weight.astype(jnp.float32), joint_sums, precision=lax.Precision.HIGHEST
    )
    merged = lax.dynamic_update_slice(feed_buffer, normed_part, (0, 0, 0))
    both = lax.psum_scatter(merged, "tensor", scatter_dimension=0, tiled=True)
    summed = (
        halving_sum(grad_w_qkv * factor, 0).reshape(-1, 3, local_heads, head_size),
        halving_sum(weight_grad.reshape(local_heads, head_size, model_width) * factor, 2),
        summed_in,
        summed_out,
    )
    in_full = lax.dynamic_update_slice_in_dim(
        jnp.zeros((hidden * tensor_count,), jnp.float32), grad_b_in, tensor_rank * hidden, 0
    )
    joint_full = lax.dynamic_update_slice_in_dim(
        jnp.zeros((2, local_width * tensor_count), jnp.float32),
        grad_b_qv,
        tensor_rank * local_width,
        1,
    )
    early = reduce_vectors(
        (
            grad_ln1_bias,
            grad_b_o,
            grad_ln2_gain,
            grad_ln2_bias,
            grad_b_out,
            joint_full[0],
            joint_full[1],
            in_full,
        ),
        factor,
    )
    both, summed, early = lax.optimization_barrier((both, summed, early))
    both = both.astype(jnp.float32)
    normed_grad = both[:, :, :model_width]
    feed = both[:, :, model_width:] + b_out
    output = (middle + feed).astype(jnp.bfloat16)
    norm_one_back = jax.vjp(layer_norm, inputs, ln1_gain, ln1_bias)[1]
    input_part, grad_ln1_gain, _ = norm_one_back(normed_grad)
    input_grad = (middle_grad + input_part).astype(jnp.bfloat16)
    (late,) = reduce_vectors((grad_ln1_gain,), factor)
    return (
        output,
        input_grad,
        late,
        early[0],
        summed[0],
        jnp.stack((early[5], early[6])),
        summed[1],
        early[1],
        early[2],
        early[3],
        summed[2],
        early[7],
        summed[3],
        early[4],
    )


def reduce_vectors(vectors, factor):
    devices = lax.axis_size("group") * lax.axis_size("dp") * lax.axis_size("tensor")
    pieces = [(item * factor).reshape(devices, -1) for item in vectors]
    widths = [piece.shape[1] for piece in pieces]
    packed = jnp.concatenate(pieces, 1)
    packed = lax.all_to_all(packed, ("group", "dp", "tensor"), 0, 0, tiled=True)
    flat = jnp.sum(packed, axis=0)
    parts = []
    offset = 0
    for width in widths:
        parts.append(flat[offset : offset + width])
        offset += width
    return tuple(parts)


def halving_steps(value, dim, steps, send_type=None):
    for axis, size, bit in steps:
        half = value.shape[dim] // 2
        low_half = lax.slice_in_dim(value, 0, half, axis=dim)
        high_half = lax.slice_in_dim(value, half, 2 * half, axis=dim)
        upper = (lax.axis_index(axis) // bit) % 2 == 1
        keep = jnp.where(upper, high_half, low_half)
        send = jnp.where(upper, low_half, high_half)
        if send_type is not None:
            send = send.astype(send_type)
        got = lax.ppermute(send, axis, [(i, i ^ bit) for i in range(size)])
        value = keep + got.astype(keep.dtype)
    return value


def halving_sum(value, dim):
    shape = value.shape
    groups = lax.axis_size("group")
    dps = lax.axis_size("dp")
    rest = shape[dim] // (groups * dps)
    value = value.reshape(shape[:dim] + (groups // 2, 2, dps * rest) + shape[dim + 1 :])
    value = jnp.swapaxes(value, dim, dim + 1)
    value = value.reshape(shape[:dim] + (groups * dps, rest) + shape[dim + 1 :])
    value = halving_steps(
        value, dim, [("group", groups, 1), ("group", groups, 2), ("dp", dps, 1)], jnp.bfloat16
    )
    return value.reshape(shape[:dim] + (shape[dim] // (groups * dps),) + shape[dim + 1 :])


def solution(mesh):
    in_specs = (
        P("tensor", ("group", "dp"), None),
        P("tensor", ("group", "dp"), None),
        P(),
        P(),
        P(),
        P(None, None, "tensor", None),
        P(None, "tensor"),
        P("tensor", None, None),
        P(),
        P(),
        P(),
        P(None, "tensor"),
        P("tensor"),
        P("tensor", None),
        P(),
    )
    out_specs = (
        P("tensor", ("group", "dp"), None),
        P("tensor", ("group", "dp"), None),
        P(("group", "dp", "tensor")),
        P(("group", "dp", "tensor")),
        P(("group", "dp"), None, "tensor", None),
        P(None, ("group", "dp", "tensor")),
        P("tensor", None, ("group", "dp")),
        P(("group", "dp", "tensor")),
        P(("group", "dp", "tensor")),
        P(("group", "dp", "tensor")),
        P(("group", "dp"), "tensor"),
        P(("group", "dp", "tensor")),
        P("tensor", ("group", "dp")),
        P(("group", "dp", "tensor")),
    )
    return jax.shard_map(shards, mesh=mesh, in_specs=in_specs, out_specs=out_specs, check_vma=False)
```

```python
from functools import partial
import math

import jax
import jax.numpy as jnp
from jax import lax
from jax.experimental import pallas as pl
from jax.experimental.pallas import tpu as pltpu
from jax.sharding import PartitionSpec as P

EPS = 1e-05
NEGATIVE = -1e30


def layer_norm(value, gain, shift):
    mean = jnp.mean(value, axis=-1, keepdims=True)
    centred = value - mean
    spread = jnp.mean(centred * centred, axis=-1, keepdims=True)
    return centred * lax.rsqrt(spread + EPS) * gain + shift


def gelu_tanh(value):
    return jax.nn.gelu(value, approximate=True)


def _valid(first_q, first_k, rows, cols, length):
    q_pos = first_q + lax.broadcasted_iota(jnp.int32, (rows, cols), 0)
    k_pos = first_k + lax.broadcasted_iota(jnp.int32, (rows, cols), 1)
    return (k_pos <= q_pos) & (k_pos < length)


def _key_blocks(i, block_q, block_k, length):
    causal = (i * block_q + block_q + block_k - 1) // block_k
    live = (length + block_k - 1) // block_k
    return jnp.minimum(causal, live)


def _attn_fwd_kernel(len_ref, q_ref, k_ref, v_ref, o_ref, lse_ref, s_buf, *, block_q, block_k, scale):
    i = pl.program_id(0)
    length = len_ref[0]
    count = _key_blocks(i, block_q, block_k, length)
    q = q_ref[...]

    def scores(j, m):
        first = pl.multiple_of(j * block_k, block_k)
        k = k_ref[pl.ds(first, block_k), :]
        s = lax.dot_general(q, k, (((1,), (1,)), ((), ())), preferred_element_type=jnp.float32) * scale
        edge = (first + block_k > i * block_q) | (first + block_k > length)
        s = lax.cond(
            edge,
            lambda v: jnp.where(_valid(i * block_q, first, block_q, block_k, length), v, NEGATIVE),
            lambda v: v,
            s,
        )
        s_buf[:, pl.ds(first, block_k)] = s
        return jnp.maximum(m, jnp.max(s, axis=1, keepdims=True))

    peak = lax.fori_loop(0, count, scores, jnp.full((block_q, 1), NEGATIVE, jnp.float32))

    def exps(j, total):
        first = pl.multiple_of(j * block_k, block_k)
        e = jnp.exp(s_buf[:, pl.ds(first, block_k)] - peak)
        s_buf[:, pl.ds(first, block_k)] = e
        return total + jnp.sum(e, axis=1, keepdims=True)

    total = lax.fori_loop(0, count, exps, jnp.zeros((block_q, 1), jnp.float32))

    inverse = 1.0 / total

    def mix(j, acc):
        first = pl.multiple_of(j * block_k, block_k)
        probs = (s_buf[:, pl.ds(first, block_k)] * inverse).astype(jnp.bfloat16)
        return acc + jnp.dot(probs, v_ref[pl.ds(first, block_k), :], preferred_element_type=jnp.float32)

    acc = lax.fori_loop(0, count, mix, jnp.zeros(o_ref.shape, jnp.float32))
    o_ref[...] = acc.astype(o_ref.dtype)
    lse_ref[...] = peak + jnp.log(total)


def attention_forward(q, k, v, length, *, block_q=512, block_k=512):
    n, d = q.shape
    scale = 1.0 / math.sqrt(d)
    kernel = partial(_attn_fwd_kernel, block_q=block_q, block_k=block_k, scale=scale)
    pairs = (n // block_q) * (n // block_k + 1) // 2
    return pl.pallas_call(
        kernel,
        out_shape=(jax.ShapeDtypeStruct((n, d), jnp.bfloat16), jax.ShapeDtypeStruct((n, 1), jnp.float32)),
        grid_spec=pltpu.PrefetchScalarGridSpec(
            num_scalar_prefetch=1,
            grid=(n // block_q,),
            in_specs=[
                pl.BlockSpec((block_q, d), lambda i, lens: (i, 0)),
                pl.BlockSpec((n, d), lambda i, lens: (0, 0)),
                pl.BlockSpec((n, d), lambda i, lens: (0, 0)),
            ],
            out_specs=[
                pl.BlockSpec((block_q, d), lambda i, lens: (i, 0)),
                pl.BlockSpec((block_q, 1), lambda i, lens: (i, 0)),
            ],
            scratch_shapes=[pltpu.VMEM((block_q, n), jnp.float32)],
        ),
        compiler_params=pltpu.CompilerParams(dimension_semantics=("arbitrary",)),
        cost_estimate=pl.CostEstimate(
            flops=4 * pairs * block_q * block_k * d,
            transcendentals=pairs * block_q * block_k,
            bytes_accessed=4 * n * d * 2,
        ),
    )(length, q, k, v)


def _attn_bwd_kernel(len_ref, q_ref, k_ref, v_ref, do_ref, lse_ref, dq_ref, dk_ref, dv_ref,
                     p_buf, dp_buf, dk_acc, dv_acc, *, block_q, block_k, scale):
    i = pl.program_id(0)
    length = len_ref[0]

    @pl.when(i == 0)
    def _():
        dk_acc[...] = jnp.zeros_like(dk_acc)
        dv_acc[...] = jnp.zeros_like(dv_acc)

    live = i * block_q < length

    @pl.when(live)
    def _():
        count = _key_blocks(i, block_q, block_k, length)
        q = q_ref[...]
        do = do_ref[...]
        lse = lse_ref[...]

        def first_pass(j, inner):
            first = pl.multiple_of(j * block_k, block_k)
            k = k_ref[pl.ds(first, block_k), :]
            v = v_ref[pl.ds(first, block_k), :]
            s = lax.dot_general(q, k, (((1,), (1,)), ((), ())), preferred_element_type=jnp.float32)
            edge = (first + block_k > i * block_q) | (first + block_k > length)
            p = lax.cond(
                edge,
                lambda v: jnp.where(
                    _valid(i * block_q, first, block_q, block_k, length),
                    jnp.exp(jnp.where(_valid(i * block_q, first, block_q, block_k, length), v, NEGATIVE) - lse),
                    0.0,
                ),
                lambda v: jnp.exp(v - lse),
                s * scale,
            )
            dp = lax.dot_general(do, v, (((1,), (1,)), ((), ())), preferred_element_type=jnp.float32)
            p_buf[:, pl.ds(first, block_k)] = p
            dp_buf[:, pl.ds(first, block_k)] = dp
            return inner + jnp.sum(p * dp, axis=1, keepdims=True)

        inner = lax.fori_loop(0, count, first_pass, jnp.zeros((block_q, 1), jnp.float32))

        def second_pass(j, dq):
            first = pl.multiple_of(j * block_k, block_k)
            p = p_buf[:, pl.ds(first, block_k)]
            dp = dp_buf[:, pl.ds(first, block_k)]
            ds = (p * (dp - inner)).astype(jnp.bfloat16)
            k = k_ref[pl.ds(first, block_k), :]
            dk_acc[pl.ds(first, block_k), :] += lax.dot_general(
                ds, q, (((0,), (0,)), ((), ())), preferred_element_type=jnp.float32)
            dv_acc[pl.ds(first, block_k), :] += lax.dot_general(
                p.astype(jnp.bfloat16), do, (((0,), (0,)), ((), ())), preferred_element_type=jnp.float32)
            return dq + jnp.dot(ds, k, preferred_element_type=jnp.float32)

        dq = lax.fori_loop(0, count, second_pass, jnp.zeros(dq_ref.shape, jnp.float32))
        dq_ref[...] = (dq * scale).astype(dq_ref.dtype)

    @pl.when(jnp.logical_not(live))
    def _():
        dq_ref[...] = jnp.zeros_like(dq_ref)

    @pl.when(i == pl.num_programs(0) - 1)
    def _():
        dk_ref[...] = (dk_acc[...] * scale).astype(dk_ref.dtype)
        dv_ref[...] = dv_acc[...].astype(dv_ref.dtype)


def attention_backward(q, k, v, do, lse, length, *, block_q=512, block_k=512):
    n, d = q.shape
    scale = 1.0 / math.sqrt(d)
    kernel = partial(_attn_bwd_kernel, block_q=block_q, block_k=block_k, scale=scale)
    pairs = (n // block_q) * (n // block_k + 1) // 2
    full = pl.BlockSpec((n, d), lambda i, lens: (0, 0))
    rows = pl.BlockSpec((block_q, d), lambda i, lens: (i, 0))
    return pl.pallas_call(
        kernel,
        out_shape=tuple(jax.ShapeDtypeStruct((n, d), jnp.bfloat16) for _ in range(3)),
        grid_spec=pltpu.PrefetchScalarGridSpec(
            num_scalar_prefetch=1,
            grid=(n // block_q,),
            in_specs=[rows, full, full, rows, pl.BlockSpec((block_q, 1), lambda i, lens: (i, 0))],
            out_specs=[rows, full, full],
            scratch_shapes=[
                pltpu.VMEM((block_q, n), jnp.float32),
                pltpu.VMEM((block_q, n), jnp.float32),
                pltpu.VMEM((n, d), jnp.float32),
                pltpu.VMEM((n, d), jnp.float32),
            ],
        ),
        compiler_params=pltpu.CompilerParams(dimension_semantics=("arbitrary",)),
        cost_estimate=pl.CostEstimate(
            flops=8 * pairs * block_q * block_k * d,
            transcendentals=pairs * block_q * block_k,
            bytes_accessed=8 * n * d * 2,
        ),
    )(length, q, k, v, do, lse)


def shards(
    tokens,
    cotangent,
    lengths,
    ln1_gain,
    ln1_bias,
    w_qkv,
    b_qv,
    w_o,
    b_o,
    ln2_gain,
    ln2_bias,
    w_in,
    b_in,
    w_out,
    b_out,
):
    row_count, seq_count, model_width = tokens.shape
    tensor_count = lax.axis_size("tensor")
    tensor_rank = lax.axis_index("tensor")
    seq_total = row_count * tensor_count
    local_heads = w_qkv.shape[2]
    head_size = w_qkv.shape[3]
    local_width = local_heads * head_size
    hidden = w_in.shape[1]
    group_count = lax.axis_size("group")
    group_rank = lax.axis_index("group")
    member = group_rank * lax.axis_size("dp") + lax.axis_index("dp")
    seq_lengths = lax.dynamic_slice_in_dim(lengths, member * seq_count, seq_count, 0)
    group_totals = jnp.sum(lengths.reshape(group_count, -1), axis=1).astype(jnp.float32)
    factor = (
        group_count
        * lax.dynamic_index_in_dim(group_totals, group_rank, 0, keepdims=False)
        / jnp.sum(group_totals)
    )
    inputs = tokens.astype(jnp.float32)
    normed_low = layer_norm(inputs, ln1_gain, ln1_bias).astype(jnp.bfloat16)
    normed_full = lax.all_gather(normed_low, "tensor", axis=0, tiled=True)
    joint_weight = w_qkv.reshape(model_width, 3 * local_width)
    projected = jnp.dot(
        normed_full.reshape(seq_total * seq_count, model_width),
        joint_weight,
        preferred_element_type=jnp.float32,
    )
    projected = projected.reshape(seq_total, seq_count, 3, local_width)
    query = (projected[:, :, 0] + b_qv[0]).astype(jnp.bfloat16)
    keys = projected[:, :, 1].astype(jnp.bfloat16)
    values = (projected[:, :, 2] + b_qv[1]).astype(jnp.bfloat16)

    def item(array, s, h):
        return array[:, s, h * head_size : (h + 1) * head_size]

    def per_row(items):
        stacked = jnp.stack(items).reshape(seq_count, local_heads, seq_total, head_size)
        return jnp.transpose(stacked, (2, 0, 1, 3)).reshape(seq_total, seq_count, local_width)

    pairs = [(s, h) for s in range(seq_count) for h in range(local_heads)]
    forward_items = [
        attention_forward(
            item(query, s, h), item(keys, s, h), item(values, s, h), seq_lengths[s : s + 1]
        )
        for s, h in pairs
    ]
    attended = per_row([o for o, _ in forward_items])
    out_weight = w_o.reshape(local_width, model_width)
    positions = tensor_rank * row_count + jnp.arange(row_count, dtype=jnp.int32)
    live = positions[:, None] < seq_lengths[None, :]
    upstream = jnp.where(live[:, :, None], cotangent, jnp.zeros_like(cotangent))
    upstream_full = lax.all_gather(upstream, "tensor", axis=0, tiled=True)
    attention_part = jnp.einsum(
        "rse,ed->rsd", attended, out_weight, preferred_element_type=jnp.float32
    ).astype(jnp.bfloat16)
    attention_part, upstream_full = lax.optimization_barrier((attention_part, upstream_full))
    attention = (
        lax.psum_scatter(attention_part, "tensor", scatter_dimension=0, tiled=True).astype(
            jnp.float32
        )
        + b_o
    )
    middle = inputs + attention
    act_grad = jnp.einsum("rsd,fd->rsf", upstream_full, w_out, preferred_element_type=jnp.float32)
    middle, act_grad = lax.optimization_barrier((middle, act_grad))
    second_low = layer_norm(middle, ln2_gain, ln2_bias).astype(jnp.bfloat16)
    second_full = lax.all_gather(second_low, "tensor", axis=0, tiled=True)
    pre_act = (
        jnp.dot(
            second_full.reshape(seq_total * seq_count, model_width),
            w_in,
            preferred_element_type=jnp.float32,
        )
        + b_in
    )
    activated = gelu_tanh(pre_act).astype(jnp.bfloat16).reshape(seq_total, seq_count, hidden)
    piece = upstream_full
    grad_w_out = jnp.einsum("rsf,rsd->fd", activated, piece, preferred_element_type=jnp.float32)
    gelu_back = jax.vjp(gelu_tanh, pre_act)[1]
    pre_low = gelu_back(act_grad.reshape(seq_total * seq_count, hidden))[0].astype(jnp.bfloat16)
    grad_b_in = jnp.sum(pre_low, axis=0, dtype=jnp.float32)
    grad_w_in = jnp.einsum(
        "rd,rf->df",
        second_full.reshape(seq_total * seq_count, model_width),
        pre_low,
        preferred_element_type=jnp.float32,
    )
    pre_rows = pre_low.reshape(seq_total, seq_count, hidden)
    piece = pre_rows
    second_part = jnp.einsum("rsf,df->rsd", piece, w_in, preferred_element_type=jnp.float32)
    second_part = second_part.astype(jnp.bfloat16)
    feed_input, second_part = lax.optimization_barrier((activated, second_part))
    second_grad = lax.psum_scatter(
        second_part, "tensor", scatter_dimension=0, tiled=True
    ).astype(jnp.float32)
    feed_part = jnp.einsum(
        "rsf,fd->rsd", feed_input, w_out, preferred_element_type=jnp.float32
    ).astype(jnp.bfloat16)
    feed_buffer = lax.dynamic_update_slice(
        jnp.zeros(feed_part.shape[:2] + (2 * model_width,), feed_part.dtype),
        feed_part,
        (0, 0, model_width),
    )
    feed_buffer, second_grad = lax.optimization_barrier((feed_buffer, second_grad))
    norm_two_back = jax.vjp(layer_norm, middle, ln2_gain, ln2_bias)[1]
    middle_part, grad_ln2_gain, grad_ln2_bias = norm_two_back(second_grad)
    middle_grad = upstream.astype(jnp.float32) + middle_part
    branch_low = middle_grad.astype(jnp.bfloat16)
    grad_b_o = jnp.sum(branch_low, axis=(0, 1), dtype=jnp.float32)
    grad_b_out = jnp.sum(upstream, axis=(0, 1), dtype=jnp.float32)
    summed_in = halving_sum(grad_w_in * factor, 0)
    summed_out = halving_sum(grad_w_out * factor, 1)
    summed_in, summed_out, branch_low = lax.optimization_barrier(
        (summed_in, summed_out, branch_low)
    )
    piece = lax.all_gather(branch_low, "tensor", axis=0, tiled=True)
    weight_grad = jnp.einsum("rse,rsd->ed", attended, piece, preferred_element_type=jnp.float32)
    part = jnp.einsum("rsd,ed->rse", piece, out_weight, preferred_element_type=jnp.float32)
    attended_grad = part.astype(jnp.bfloat16)
    backward_items = [
        attention_backward(
            item(query, s, h),
            item(keys, s, h),
            item(values, s, h),
            item(attended_grad, s, h),
            lse,
            seq_lengths[s : s + 1],
        )
        for (s, h), (_, lse) in zip(pairs, forward_items)
    ]
    joint_grad = jnp.stack(
        [per_row([grads[kind] for grads in backward_items]) for kind in range(3)], axis=2
    )
    grad_b_qv = jnp.sum(joint_grad[:, :, 0::2], axis=(0, 1), dtype=jnp.float32)
    joint_rows = joint_grad.reshape(seq_total, seq_count, 3 * local_width)
    grad_w_qkv = jnp.einsum(
        "rd,rc->dc",
        normed_full.reshape(seq_total * seq_count, model_width),
        joint_rows.reshape(seq_total * seq_count, 3 * local_width),
        preferred_element_type=jnp.float32,
    )
    normed_part = jnp.einsum(
        "rsc,dc->rsd", joint_rows, joint_weight, preferred_element_type=jnp.float32
    ).astype(jnp.bfloat16)
    joint_sums = jnp.sum(joint_rows, axis=(0, 1), dtype=jnp.float32)
    grad_ln1_bias = jnp.dot(
        joint_weight.astype(jnp.float32), joint_sums, precision=lax.Precision.HIGHEST
    )
    merged = lax.dynamic_update_slice(feed_buffer, normed_part, (0, 0, 0))
    both = lax.psum_scatter(merged, "tensor", scatter_dimension=0, tiled=True)
    summed = (
        halving_sum(grad_w_qkv * factor, 0).reshape(-1, 3, local_heads, head_size),
        halving_sum(weight_grad.reshape(local_heads, head_size, model_width) * factor, 2),
        summed_in,
        summed_out,
    )
    in_full = lax.dynamic_update_slice_in_dim(
        jnp.zeros((hidden * tensor_count,), jnp.float32), grad_b_in, tensor_rank * hidden, 0
    )
    joint_full = lax.dynamic_update_slice_in_dim(
        jnp.zeros((2, local_width * tensor_count), jnp.float32),
        grad_b_qv,
        tensor_rank * local_width,
        1,
    )
    early = reduce_vectors(
        (
            grad_ln1_bias,
            grad_b_o,
            grad_ln2_gain,
            grad_ln2_bias,
            grad_b_out,
            joint_full[0],
            joint_full[1],
            in_full,
        ),
        factor,
    )
    both, summed, early = lax.optimization_barrier((both, summed, early))
    both = both.astype(jnp.float32)
    normed_grad = both[:, :, :model_width]
    feed = both[:, :, model_width:] + b_out
    output = (middle + feed).astype(jnp.bfloat16)
    norm_one_back = jax.vjp(layer_norm, inputs, ln1_gain, ln1_bias)[1]
    input_part, grad_ln1_gain, _ = norm_one_back(normed_grad)
    input_grad = (middle_grad + input_part).astype(jnp.bfloat16)
    (late,) = reduce_vectors((grad_ln1_gain,), factor)
    return (
        output,
        input_grad,
        late,
        early[0],
        summed[0],
        jnp.stack((early[5], early[6])),
        summed[1],
        early[1],
        early[2],
        early[3],
        summed[2],
        early[7],
        summed[3],
        early[4],
    )


def reduce_vectors(vectors, factor):
    devices = lax.axis_size("group") * lax.axis_size("dp") * lax.axis_size("tensor")
    pieces = [(item * factor).reshape(devices, -1) for item in vectors]
    widths = [piece.shape[1] for piece in pieces]
    packed = jnp.concatenate(pieces, 1)
    packed = lax.all_to_all(packed, ("group", "dp", "tensor"), 0, 0, tiled=True)
    flat = jnp.sum(packed, axis=0)
    parts = []
    offset = 0
    for width in widths:
        parts.append(flat[offset : offset + width])
        offset += width
    return tuple(parts)


def halving_steps(value, dim, steps, send_type=None):
    for axis, size, bit in steps:
        half = value.shape[dim] // 2
        low_half = lax.slice_in_dim(value, 0, half, axis=dim)
        high_half = lax.slice_in_dim(value, half, 2 * half, axis=dim)
        upper = (lax.axis_index(axis) // bit) % 2 == 1
        keep = jnp.where(upper, high_half, low_half)
        send = jnp.where(upper, low_half, high_half)
        if send_type is not None:
            send = send.astype(send_type)
        got = lax.ppermute(send, axis, [(i, i ^ bit) for i in range(size)])
        value = keep + got.astype(keep.dtype)
    return value


def halving_sum(value, dim):
    shape = value.shape
    groups = lax.axis_size("group")
    dps = lax.axis_size("dp")
    rest = shape[dim] // (groups * dps)
    value = value.reshape(shape[:dim] + (groups // 2, 2, dps * rest) + shape[dim + 1 :])
    value = jnp.swapaxes(value, dim, dim + 1)
    value = value.reshape(shape[:dim] + (groups * dps, rest) + shape[dim + 1 :])
    value = halving_steps(
        value, dim, [("group", groups, 1), ("group", groups, 2), ("dp", dps, 1)], jnp.bfloat16
    )
    return value.reshape(shape[:dim] + (shape[dim] // (groups * dps),) + shape[dim + 1 :])


def solution(mesh):
    in_specs = (
        P("tensor", ("group", "dp"), None),
        P("tensor", ("group", "dp"), None),
        P(),
        P(),
        P(),
        P(None, None, "tensor", None),
        P(None, "tensor"),
        P("tensor", None, None),
        P(),
        P(),
        P(),
        P(None, "tensor"),
        P("tensor"),
        P("tensor", None),
        P(),
    )
    out_specs = (
        P("tensor", ("group", "dp"), None),
        P("tensor", ("group", "dp"), None),
        P(("group", "dp", "tensor")),
        P(("group", "dp", "tensor")),
        P(("group", "dp"), None, "tensor", None),
        P(None, ("group", "dp", "tensor")),
        P("tensor", None, ("group", "dp")),
        P(("group", "dp", "tensor")),
        P(("group", "dp", "tensor")),
        P(("group", "dp", "tensor")),
        P(("group", "dp"), "tensor"),
        P(("group", "dp", "tensor")),
        P("tensor", ("group", "dp")),
        P(("group", "dp", "tensor")),
    )
    return jax.shard_map(shards, mesh=mesh, in_specs=in_specs, out_specs=out_specs, check_vma=False)
```

```python
from functools import partial
import math

import jax
import jax.numpy as jnp
from jax import lax
from jax.experimental import pallas as pl
from jax.experimental.pallas import tpu as pltpu
from jax.sharding import PartitionSpec as P

EPS = 1e-05
NEGATIVE = -1e30


def layer_norm(value, gain, shift):
    mean = jnp.mean(value, axis=-1, keepdims=True)
    centred = value - mean
    spread = jnp.mean(centred * centred, axis=-1, keepdims=True)
    return centred * lax.rsqrt(spread + EPS) * gain + shift


def gelu_tanh(value):
    return jax.nn.gelu(value, approximate=True)


def _valid(first_q, first_k, rows, cols, length):
    q_pos = first_q + lax.broadcasted_iota(jnp.int32, (rows, cols), 0)
    k_pos = first_k + lax.broadcasted_iota(jnp.int32, (rows, cols), 1)
    return (k_pos <= q_pos) & (k_pos < length)


def _key_blocks(i, block_q, block_k, length):
    causal = (i * block_q + block_q + block_k - 1) // block_k
    live = (length + block_k - 1) // block_k
    return jnp.minimum(causal, live)


def _attn_fwd_kernel(len_ref, q_ref, k_ref, v_ref, o_ref, lse_ref, s_buf, *, block_q, block_k, scale):
    i = pl.program_id(0)
    length = len_ref[0]
    count = _key_blocks(i, block_q, block_k, length)
    q = q_ref[...]

    def scores(j, m):
        first = pl.multiple_of(j * block_k, block_k)
        k = k_ref[pl.ds(first, block_k), :]
        s = lax.dot_general(q, k, (((1,), (1,)), ((), ())), preferred_element_type=jnp.float32) * scale
        edge = (first + block_k > i * block_q) | (first + block_k > length)
        s = lax.cond(
            edge,
            lambda v: jnp.where(_valid(i * block_q, first, block_q, block_k, length), v, NEGATIVE),
            lambda v: v,
            s,
        )
        s_buf[:, pl.ds(first, block_k)] = s
        return jnp.maximum(m, jnp.max(s, axis=1, keepdims=True))

    peak = lax.fori_loop(0, count, scores, jnp.full((block_q, 1), NEGATIVE, jnp.float32))

    def exps(j, total):
        first = pl.multiple_of(j * block_k, block_k)
        e = jnp.exp(s_buf[:, pl.ds(first, block_k)] - peak)
        s_buf[:, pl.ds(first, block_k)] = e
        return total + jnp.sum(e, axis=1, keepdims=True)

    total = lax.fori_loop(0, count, exps, jnp.zeros((block_q, 1), jnp.float32))

    inverse = 1.0 / total

    def mix(j, acc):
        first = pl.multiple_of(j * block_k, block_k)
        probs = (s_buf[:, pl.ds(first, block_k)] * inverse).astype(jnp.bfloat16)
        return acc + jnp.dot(probs, v_ref[pl.ds(first, block_k), :], preferred_element_type=jnp.float32)

    acc = lax.fori_loop(0, count, mix, jnp.zeros(o_ref.shape, jnp.float32))
    o_ref[...] = acc.astype(o_ref.dtype)
    lse_ref[...] = peak + jnp.log(total)


def attention_forward(q, k, v, length, *, block_q=512, block_k=512):
    n, d = q.shape
    scale = 1.0 / math.sqrt(d)
    kernel = partial(_attn_fwd_kernel, block_q=block_q, block_k=block_k, scale=scale)
    pairs = (n // block_q) * (n // block_k + 1) // 2
    return pl.pallas_call(
        kernel,
        out_shape=(jax.ShapeDtypeStruct((n, d), jnp.bfloat16), jax.ShapeDtypeStruct((n, 1), jnp.float32)),
        grid_spec=pltpu.PrefetchScalarGridSpec(
            num_scalar_prefetch=1,
            grid=(n // block_q,),
            in_specs=[
                pl.BlockSpec((block_q, d), lambda i, lens: (i, 0)),
                pl.BlockSpec((n, d), lambda i, lens: (0, 0)),
                pl.BlockSpec((n, d), lambda i, lens: (0, 0)),
            ],
            out_specs=[
                pl.BlockSpec((block_q, d), lambda i, lens: (i, 0)),
                pl.BlockSpec((block_q, 1), lambda i, lens: (i, 0)),
            ],
            scratch_shapes=[pltpu.VMEM((block_q, n), jnp.float32)],
        ),
        compiler_params=pltpu.CompilerParams(dimension_semantics=("arbitrary",)),
        cost_estimate=pl.CostEstimate(
            flops=4 * pairs * block_q * block_k * d,
            transcendentals=pairs * block_q * block_k,
            bytes_accessed=4 * n * d * 2,
        ),
    )(length, q, k, v)


def _attn_bwd_kernel(len_ref, q_ref, k_ref, v_ref, do_ref, lse_ref, dq_ref, dk_ref, dv_ref,
                     p_buf, dp_buf, dk_acc, dv_acc, *, block_q, block_k, scale):
    i = pl.program_id(0)
    length = len_ref[0]

    @pl.when(i == 0)
    def _():
        dk_acc[...] = jnp.zeros_like(dk_acc)
        dv_acc[...] = jnp.zeros_like(dv_acc)

    live = i * block_q < length

    @pl.when(live)
    def _():
        count = _key_blocks(i, block_q, block_k, length)
        q = q_ref[...]
        do = do_ref[...]
        lse = lse_ref[...]

        def first_pass(j, inner):
            first = pl.multiple_of(j * block_k, block_k)
            k = k_ref[pl.ds(first, block_k), :]
            v = v_ref[pl.ds(first, block_k), :]
            s = lax.dot_general(q, k, (((1,), (1,)), ((), ())), preferred_element_type=jnp.float32)
            edge = (first + block_k > i * block_q) | (first + block_k > length)
            p = lax.cond(
                edge,
                lambda v: jnp.where(
                    _valid(i * block_q, first, block_q, block_k, length),
                    jnp.exp(jnp.where(_valid(i * block_q, first, block_q, block_k, length), v, NEGATIVE) - lse),
                    0.0,
                ),
                lambda v: jnp.exp(v - lse),
                s * scale,
            )
            dp = lax.dot_general(do, v, (((1,), (1,)), ((), ())), preferred_element_type=jnp.float32)
            p_buf[:, pl.ds(first, block_k)] = p
            dp_buf[:, pl.ds(first, block_k)] = dp
            return inner + jnp.sum(p * dp, axis=1, keepdims=True)

        inner = lax.fori_loop(0, count, first_pass, jnp.zeros((block_q, 1), jnp.float32))

        def second_pass(j, dq):
            first = pl.multiple_of(j * block_k, block_k)
            p = p_buf[:, pl.ds(first, block_k)]
            dp = dp_buf[:, pl.ds(first, block_k)]
            ds = (p * (dp - inner)).astype(jnp.bfloat16)
            k = k_ref[pl.ds(first, block_k), :]
            dk_acc[pl.ds(first, block_k), :] += lax.dot_general(
                ds, q, (((0,), (0,)), ((), ())), preferred_element_type=jnp.float32)
            dv_acc[pl.ds(first, block_k), :] += lax.dot_general(
                p.astype(jnp.bfloat16), do, (((0,), (0,)), ((), ())), preferred_element_type=jnp.float32)
            return dq + jnp.dot(ds, k, preferred_element_type=jnp.float32)

        dq = lax.fori_loop(0, count, second_pass, jnp.zeros(dq_ref.shape, jnp.float32))
        dq_ref[...] = (dq * scale).astype(dq_ref.dtype)

    @pl.when(jnp.logical_not(live))
    def _():
        dq_ref[...] = jnp.zeros_like(dq_ref)

    @pl.when(i == pl.num_programs(0) - 1)
    def _():
        dk_ref[...] = (dk_acc[...] * scale).astype(dk_ref.dtype)
        dv_ref[...] = dv_acc[...].astype(dv_ref.dtype)


def attention_backward(q, k, v, do, lse, length, *, block_q=512, block_k=512):
    n, d = q.shape
    scale = 1.0 / math.sqrt(d)
    kernel = partial(_attn_bwd_kernel, block_q=block_q, block_k=block_k, scale=scale)
    pairs = (n // block_q) * (n // block_k + 1) // 2
    full = pl.BlockSpec((n, d), lambda i, lens: (0, 0))
    rows = pl.BlockSpec((block_q, d), lambda i, lens: (i, 0))
    return pl.pallas_call(
        kernel,
        out_shape=tuple(jax.ShapeDtypeStruct((n, d), jnp.bfloat16) for _ in range(3)),
        grid_spec=pltpu.PrefetchScalarGridSpec(
            num_scalar_prefetch=1,
            grid=(n // block_q,),
            in_specs=[rows, full, full, rows, pl.BlockSpec((block_q, 1), lambda i, lens: (i, 0))],
            out_specs=[rows, full, full],
            scratch_shapes=[
                pltpu.VMEM((block_q, n), jnp.float32),
                pltpu.VMEM((block_q, n), jnp.float32),
                pltpu.VMEM((n, d), jnp.float32),
                pltpu.VMEM((n, d), jnp.float32),
            ],
        ),
        compiler_params=pltpu.CompilerParams(dimension_semantics=("arbitrary",)),
        cost_estimate=pl.CostEstimate(
            flops=8 * pairs * block_q * block_k * d,
            transcendentals=pairs * block_q * block_k,
            bytes_accessed=8 * n * d * 2,
        ),
    )(length, q, k, v, do, lse)


def shards(
    tokens,
    cotangent,
    lengths,
    ln1_gain,
    ln1_bias,
    w_qkv,
    b_qv,
    w_o,
    b_o,
    ln2_gain,
    ln2_bias,
    w_in,
    b_in,
    w_out,
    b_out,
):
    row_count, seq_count, model_width = tokens.shape
    tensor_count = lax.axis_size("tensor")
    tensor_rank = lax.axis_index("tensor")
    seq_total = row_count * tensor_count
    local_heads = w_qkv.shape[2]
    head_size = w_qkv.shape[3]
    local_width = local_heads * head_size
    hidden = w_in.shape[1]
    group_count = lax.axis_size("group")
    group_rank = lax.axis_index("group")
    member = group_rank * lax.axis_size("dp") + lax.axis_index("dp")
    seq_lengths = lax.dynamic_slice_in_dim(lengths, member * seq_count, seq_count, 0)
    group_totals = jnp.sum(lengths.reshape(group_count, -1), axis=1).astype(jnp.float32)
    factor = (
        group_count
        * lax.dynamic_index_in_dim(group_totals, group_rank, 0, keepdims=False)
        / jnp.sum(group_totals)
    )
    inputs = tokens.astype(jnp.float32)
    normed_low = layer_norm(inputs, ln1_gain, ln1_bias).astype(jnp.bfloat16)
    positions = tensor_rank * row_count + jnp.arange(row_count, dtype=jnp.int32)
    live = positions[:, None] < seq_lengths[None, :]
    upstream = jnp.where(live[:, :, None], cotangent, jnp.zeros_like(cotangent))
    front = jnp.concatenate(
        [
            normed_low.reshape(row_count, seq_count * model_width),
            upstream.reshape(row_count, seq_count * model_width),
            w_o.reshape(row_count, -1),
        ],
        1,
    )
    front = lax.all_gather(front, "tensor", axis=0, tiled=True)
    wide = seq_count * model_width
    normed_full = front[:, :wide].reshape(seq_total, seq_count, model_width)
    upstream_full = front[:, wide : 2 * wide].reshape(seq_total, seq_count, model_width)
    out_full = front[:, 2 * wide :].reshape(-1, model_width)
    joint_weight = w_qkv.reshape(model_width, 3 * local_width)
    projected = jnp.dot(
        normed_full.reshape(seq_total * seq_count, model_width),
        joint_weight,
        preferred_element_type=jnp.float32,
    )
    projected = projected.reshape(seq_total, seq_count, 3, local_width)
    query = (projected[:, :, 0] + b_qv[0]).astype(jnp.bfloat16)
    keys = projected[:, :, 1].astype(jnp.bfloat16)
    values = (projected[:, :, 2] + b_qv[1]).astype(jnp.bfloat16)

    def item(array, s, h):
        return array[:, s, h * head_size : (h + 1) * head_size]

    def per_row(items):
        stacked = jnp.stack(items).reshape(seq_count, local_heads, seq_total, head_size)
        return jnp.transpose(stacked, (2, 0, 1, 3)).reshape(seq_total, seq_count, local_width)

    pairs = [(s, h) for s in range(seq_count) for h in range(local_heads)]
    forward_items = [
        attention_forward(
            item(query, s, h), item(keys, s, h), item(values, s, h), seq_lengths[s : s + 1]
        )
        for s, h in pairs
    ]
    attended = per_row([o for o, _ in forward_items])
    out_weight = w_o.reshape(local_width, model_width)
    own_rows = lax.all_to_all(
        jnp.transpose(attended, (1, 0, 2)).reshape(seq_count * seq_total, local_width),
        "tensor",
        0,
        1,
        tiled=True,
    )
    attention = (
        jnp.dot(own_rows, out_full, preferred_element_type=jnp.float32).reshape(
            seq_count, row_count, model_width
        )
    )
    attention = jnp.transpose(attention, (1, 0, 2)) + b_o
    middle = inputs + attention
    act_grad = jnp.einsum("rsd,fd->rsf", upstream_full, w_out, preferred_element_type=jnp.float32)
    second_low = layer_norm(middle, ln2_gain, ln2_bias).astype(jnp.bfloat16)
    second_full = lax.all_gather(second_low, "tensor", axis=0, tiled=True)
    second_full, act_grad = lax.optimization_barrier((second_full, act_grad))
    pre_act = (
        jnp.dot(
            second_full.reshape(seq_total * seq_count, model_width),
            w_in,
            preferred_element_type=jnp.float32,
        )
        + b_in
    )
    activated = gelu_tanh(pre_act).astype(jnp.bfloat16).reshape(seq_total, seq_count, hidden)
    piece = upstream_full
    grad_w_out = jnp.einsum("rsf,rsd->fd", activated, piece, preferred_element_type=jnp.float32)
    gelu_back = jax.vjp(gelu_tanh, pre_act)[1]
    pre_low = gelu_back(act_grad.reshape(seq_total * seq_count, hidden))[0].astype(jnp.bfloat16)
    grad_b_in = jnp.sum(pre_low, axis=0, dtype=jnp.float32)
    grad_w_in = jnp.einsum(
        "rd,rf->df",
        second_full.reshape(seq_total * seq_count, model_width),
        pre_low,
        preferred_element_type=jnp.float32,
    )
    pre_rows = pre_low.reshape(seq_total, seq_count, hidden)
    piece = pre_rows
    second_part = jnp.einsum("rsf,df->rsd", piece, w_in, preferred_element_type=jnp.float32)
    second_part = second_part.astype(jnp.bfloat16)
    feed_input, second_part = lax.optimization_barrier((activated, second_part))
    second_grad = lax.psum_scatter(
        second_part, "tensor", scatter_dimension=0, tiled=True
    ).astype(jnp.float32)
    feed_part = jnp.einsum(
        "rsf,fd->rsd", feed_input, w_out, preferred_element_type=jnp.float32
    ).astype(jnp.bfloat16)
    feed_buffer = lax.dynamic_update_slice(
        jnp.zeros(feed_part.shape[:2] + (2 * model_width,), feed_part.dtype),
        feed_part,
        (0, 0, model_width),
    )
    feed_buffer, second_grad = lax.optimization_barrier((feed_buffer, second_grad))
    norm_two_back = jax.vjp(layer_norm, middle, ln2_gain, ln2_bias)[1]
    middle_part, grad_ln2_gain, grad_ln2_bias = norm_two_back(second_grad)
    middle_grad = upstream.astype(jnp.float32) + middle_part
    branch_low = middle_grad.astype(jnp.bfloat16)
    grad_b_o = jnp.sum(branch_low, axis=(0, 1), dtype=jnp.float32)
    grad_b_out = jnp.sum(upstream, axis=(0, 1), dtype=jnp.float32)
    summed_in = halving_sum(grad_w_in * factor, 0)
    summed_out = halving_sum(grad_w_out * factor, 1)
    summed_in, summed_out, branch_low = lax.optimization_barrier(
        (summed_in, summed_out, branch_low)
    )
    piece = lax.all_gather(branch_low, "tensor", axis=0, tiled=True)
    weight_grad = jnp.einsum("rse,rsd->ed", attended, piece, preferred_element_type=jnp.float32)
    part = jnp.einsum("rsd,ed->rse", piece, out_weight, preferred_element_type=jnp.float32)
    attended_grad = part.astype(jnp.bfloat16)
    backward_items = [
        attention_backward(
            item(query, s, h),
            item(keys, s, h),
            item(values, s, h),
            item(attended_grad, s, h),
            lse,
            seq_lengths[s : s + 1],
        )
        for (s, h), (_, lse) in zip(pairs, forward_items)
    ]
    joint_grad = jnp.stack(
        [per_row([grads[kind] for grads in backward_items]) for kind in range(3)], axis=2
    )
    grad_b_qv = jnp.sum(joint_grad[:, :, 0::2], axis=(0, 1), dtype=jnp.float32)
    joint_rows = joint_grad.reshape(seq_total, seq_count, 3 * local_width)
    grad_w_qkv = jnp.einsum(
        "rd,rc->dc",
        normed_full.reshape(seq_total * seq_count, model_width),
        joint_rows.reshape(seq_total * seq_count, 3 * local_width),
        preferred_element_type=jnp.float32,
    )
    normed_part = jnp.einsum(
        "rsc,dc->rsd", joint_rows, joint_weight, preferred_element_type=jnp.float32
    ).astype(jnp.bfloat16)
    joint_sums = jnp.sum(joint_rows, axis=(0, 1), dtype=jnp.float32)
    grad_ln1_bias = jnp.dot(
        joint_weight.astype(jnp.float32), joint_sums, precision=lax.Precision.HIGHEST
    )
    merged = lax.dynamic_update_slice(feed_buffer, normed_part, (0, 0, 0))
    both = lax.psum_scatter(merged, "tensor", scatter_dimension=0, tiled=True)
    summed = (
        halving_sum(grad_w_qkv * factor, 0).reshape(-1, 3, local_heads, head_size),
        halving_sum(weight_grad.reshape(local_heads, head_size, model_width) * factor, 2),
        summed_in,
        summed_out,
    )
    in_full = lax.dynamic_update_slice_in_dim(
        jnp.zeros((hidden * tensor_count,), jnp.float32), grad_b_in, tensor_rank * hidden, 0
    )
    joint_full = lax.dynamic_update_slice_in_dim(
        jnp.zeros((2, local_width * tensor_count), jnp.float32),
        grad_b_qv,
        tensor_rank * local_width,
        1,
    )
    early = reduce_vectors(
        (
            grad_ln1_bias,
            grad_b_o,
            grad_ln2_gain,
            grad_ln2_bias,
            grad_b_out,
            joint_full[0],
            joint_full[1],
            in_full,
        ),
        factor,
    )
    both, summed, early = lax.optimization_barrier((both, summed, early))
    both = both.astype(jnp.float32)
    normed_grad = both[:, :, :model_width]
    feed = both[:, :, model_width:] + b_out
    output = (middle + feed).astype(jnp.bfloat16)
    norm_one_back = jax.vjp(layer_norm, inputs, ln1_gain, ln1_bias)[1]
    input_part, grad_ln1_gain, _ = norm_one_back(normed_grad)
    input_grad = (middle_grad + input_part).astype(jnp.bfloat16)
    (late,) = reduce_vectors((grad_ln1_gain,), factor)
    return (
        output,
        input_grad,
        late,
        early[0],
        summed[0],
        jnp.stack((early[5], early[6])),
        summed[1],
        early[1],
        early[2],
        early[3],
        summed[2],
        early[7],
        summed[3],
        early[4],
    )


def reduce_vectors(vectors, factor):
    devices = lax.axis_size("group") * lax.axis_size("dp") * lax.axis_size("tensor")
    pieces = [(item * factor).reshape(devices, -1) for item in vectors]
    widths = [piece.shape[1] for piece in pieces]
    packed = jnp.concatenate(pieces, 1)
    packed = lax.all_to_all(packed, ("group", "dp", "tensor"), 0, 0, tiled=True)
    flat = jnp.sum(packed, axis=0)
    parts = []
    offset = 0
    for width in widths:
        parts.append(flat[offset : offset + width])
        offset += width
    return tuple(parts)


def halving_steps(value, dim, steps, send_type=None):
    for axis, size, bit in steps:
        half = value.shape[dim] // 2
        low_half = lax.slice_in_dim(value, 0, half, axis=dim)
        high_half = lax.slice_in_dim(value, half, 2 * half, axis=dim)
        upper = (lax.axis_index(axis) // bit) % 2 == 1
        keep = jnp.where(upper, high_half, low_half)
        send = jnp.where(upper, low_half, high_half)
        if send_type is not None:
            send = send.astype(send_type)
        got = lax.ppermute(send, axis, [(i, i ^ bit) for i in range(size)])
        value = keep + got.astype(keep.dtype)
    return value


def halving_sum(value, dim):
    shape = value.shape
    groups = lax.axis_size("group")
    dps = lax.axis_size("dp")
    rest = shape[dim] // (groups * dps)
    value = value.reshape(shape[:dim] + (groups // 2, 2, dps * rest) + shape[dim + 1 :])
    value = jnp.swapaxes(value, dim, dim + 1)
    value = value.reshape(shape[:dim] + (groups * dps, rest) + shape[dim + 1 :])
    value = halving_steps(
        value, dim, [("group", groups, 1), ("group", groups, 2), ("dp", dps, 1)], jnp.bfloat16
    )
    return value.reshape(shape[:dim] + (shape[dim] // (groups * dps),) + shape[dim + 1 :])


def solution(mesh):
    in_specs = (
        P("tensor", ("group", "dp"), None),
        P("tensor", ("group", "dp"), None),
        P(),
        P(),
        P(),
        P(None, None, "tensor", None),
        P(None, "tensor"),
        P("tensor", None, None),
        P(),
        P(),
        P(),
        P(None, "tensor"),
        P("tensor"),
        P("tensor", None),
        P(),
    )
    out_specs = (
        P("tensor", ("group", "dp"), None),
        P("tensor", ("group", "dp"), None),
        P(("group", "dp", "tensor")),
        P(("group", "dp", "tensor")),
        P(("group", "dp"), None, "tensor", None),
        P(None, ("group", "dp", "tensor")),
        P("tensor", None, ("group", "dp")),
        P(("group", "dp", "tensor")),
        P(("group", "dp", "tensor")),
        P(("group", "dp", "tensor")),
        P(("group", "dp"), "tensor"),
        P(("group", "dp", "tensor")),
        P("tensor", ("group", "dp")),
        P(("group", "dp", "tensor")),
    )
    return jax.shard_map(shards, mesh=mesh, in_specs=in_specs, out_specs=out_specs, check_vma=False)
```

```python
from functools import partial
import math

import jax
import jax.numpy as jnp
from jax import lax
from jax.experimental import pallas as pl
from jax.experimental.pallas import tpu as pltpu
from jax.sharding import PartitionSpec as P

EPS = 1e-05
NEGATIVE = -1e30


def layer_norm(value, gain, shift):
    mean = jnp.mean(value, axis=-1, keepdims=True)
    centred = value - mean
    spread = jnp.mean(centred * centred, axis=-1, keepdims=True)
    return centred * lax.rsqrt(spread + EPS) * gain + shift


def gelu_tanh(value):
    return jax.nn.gelu(value, approximate=True)


def _valid(first_q, first_k, rows, cols, length):
    q_pos = first_q + lax.broadcasted_iota(jnp.int32, (rows, cols), 0)
    k_pos = first_k + lax.broadcasted_iota(jnp.int32, (rows, cols), 1)
    return (k_pos <= q_pos) & (k_pos < length)


def _key_blocks(i, block_q, block_k, length):
    causal = (i * block_q + block_q + block_k - 1) // block_k
    live = (length + block_k - 1) // block_k
    return jnp.minimum(causal, live)


def _attn_fwd_kernel(len_ref, q_ref, k_ref, v_ref, o_ref, lse_ref, s_buf, *, block_q, block_k, scale):
    i = pl.program_id(0)
    length = len_ref[0]
    count = _key_blocks(i, block_q, block_k, length)
    q = q_ref[...]

    def scores(j, m):
        first = pl.multiple_of(j * block_k, block_k)
        k = k_ref[pl.ds(first, block_k), :]
        s = lax.dot_general(q, k, (((1,), (1,)), ((), ())), preferred_element_type=jnp.float32) * scale
        edge = (first + block_k > i * block_q) | (first + block_k > length)
        s = lax.cond(
            edge,
            lambda v: jnp.where(_valid(i * block_q, first, block_q, block_k, length), v, NEGATIVE),
            lambda v: v,
            s,
        )
        s_buf[:, pl.ds(first, block_k)] = s
        return jnp.maximum(m, jnp.max(s, axis=1, keepdims=True))

    peak = lax.fori_loop(0, count, scores, jnp.full((block_q, 1), NEGATIVE, jnp.float32))

    def exps(j, total):
        first = pl.multiple_of(j * block_k, block_k)
        e = jnp.exp(s_buf[:, pl.ds(first, block_k)] - peak)
        s_buf[:, pl.ds(first, block_k)] = e
        return total + jnp.sum(e, axis=1, keepdims=True)

    total = lax.fori_loop(0, count, exps, jnp.zeros((block_q, 1), jnp.float32))

    inverse = 1.0 / total

    def mix(j, acc):
        first = pl.multiple_of(j * block_k, block_k)
        probs = (s_buf[:, pl.ds(first, block_k)] * inverse).astype(jnp.bfloat16)
        return acc + jnp.dot(probs, v_ref[pl.ds(first, block_k), :], preferred_element_type=jnp.float32)

    acc = lax.fori_loop(0, count, mix, jnp.zeros(o_ref.shape, jnp.float32))
    o_ref[...] = acc.astype(o_ref.dtype)
    lse_ref[...] = peak + jnp.log(total)


def attention_forward(q, k, v, length, *, block_q=512, block_k=512):
    n, d = q.shape
    scale = 1.0 / math.sqrt(d)
    kernel = partial(_attn_fwd_kernel, block_q=block_q, block_k=block_k, scale=scale)
    pairs = (n // block_q) * (n // block_k + 1) // 2
    return pl.pallas_call(
        kernel,
        out_shape=(jax.ShapeDtypeStruct((n, d), jnp.bfloat16), jax.ShapeDtypeStruct((n, 1), jnp.float32)),
        grid_spec=pltpu.PrefetchScalarGridSpec(
            num_scalar_prefetch=1,
            grid=(n // block_q,),
            in_specs=[
                pl.BlockSpec((block_q, d), lambda i, lens: (i, 0)),
                pl.BlockSpec((n, d), lambda i, lens: (0, 0)),
                pl.BlockSpec((n, d), lambda i, lens: (0, 0)),
            ],
            out_specs=[
                pl.BlockSpec((block_q, d), lambda i, lens: (i, 0)),
                pl.BlockSpec((block_q, 1), lambda i, lens: (i, 0)),
            ],
            scratch_shapes=[pltpu.VMEM((block_q, n), jnp.float32)],
        ),
        compiler_params=pltpu.CompilerParams(dimension_semantics=("arbitrary",)),
        cost_estimate=pl.CostEstimate(
            flops=4 * pairs * block_q * block_k * d,
            transcendentals=pairs * block_q * block_k,
            bytes_accessed=4 * n * d * 2,
        ),
    )(length, q, k, v)


def _attn_bwd_kernel(len_ref, q_ref, k_ref, v_ref, do_ref, lse_ref, dq_ref, dk_ref, dv_ref,
                     p_buf, dp_buf, dk_acc, dv_acc, *, block_q, block_k, scale):
    i = pl.program_id(0)
    length = len_ref[0]

    @pl.when(i == 0)
    def _():
        dk_acc[...] = jnp.zeros_like(dk_acc)
        dv_acc[...] = jnp.zeros_like(dv_acc)

    live = i * block_q < length

    @pl.when(live)
    def _():
        count = _key_blocks(i, block_q, block_k, length)
        q = q_ref[...]
        do = do_ref[...]
        lse = lse_ref[...]

        def first_pass(j, inner):
            first = pl.multiple_of(j * block_k, block_k)
            k = k_ref[pl.ds(first, block_k), :]
            v = v_ref[pl.ds(first, block_k), :]
            s = lax.dot_general(q, k, (((1,), (1,)), ((), ())), preferred_element_type=jnp.float32)
            edge = (first + block_k > i * block_q) | (first + block_k > length)
            p = lax.cond(
                edge,
                lambda v: jnp.where(
                    _valid(i * block_q, first, block_q, block_k, length),
                    jnp.exp(jnp.where(_valid(i * block_q, first, block_q, block_k, length), v, NEGATIVE) - lse),
                    0.0,
                ),
                lambda v: jnp.exp(v - lse),
                s * scale,
            )
            dp = lax.dot_general(do, v, (((1,), (1,)), ((), ())), preferred_element_type=jnp.float32)
            p_buf[:, pl.ds(first, block_k)] = p
            dp_buf[:, pl.ds(first, block_k)] = dp
            return inner + jnp.sum(p * dp, axis=1, keepdims=True)

        inner = lax.fori_loop(0, count, first_pass, jnp.zeros((block_q, 1), jnp.float32))

        def second_pass(j, dq):
            first = pl.multiple_of(j * block_k, block_k)
            p = p_buf[:, pl.ds(first, block_k)]
            dp = dp_buf[:, pl.ds(first, block_k)]
            ds = (p * (dp - inner)).astype(jnp.bfloat16)
            k = k_ref[pl.ds(first, block_k), :]
            dk_acc[pl.ds(first, block_k), :] += lax.dot_general(
                ds, q, (((0,), (0,)), ((), ())), preferred_element_type=jnp.float32)
            dv_acc[pl.ds(first, block_k), :] += lax.dot_general(
                p.astype(jnp.bfloat16), do, (((0,), (0,)), ((), ())), preferred_element_type=jnp.float32)
            return dq + jnp.dot(ds, k, preferred_element_type=jnp.float32)

        dq = lax.fori_loop(0, count, second_pass, jnp.zeros(dq_ref.shape, jnp.float32))
        dq_ref[...] = (dq * scale).astype(dq_ref.dtype)

    @pl.when(jnp.logical_not(live))
    def _():
        dq_ref[...] = jnp.zeros_like(dq_ref)

    @pl.when(i == pl.num_programs(0) - 1)
    def _():
        dk_ref[...] = (dk_acc[...] * scale).astype(dk_ref.dtype)
        dv_ref[...] = dv_acc[...].astype(dv_ref.dtype)


def attention_backward(q, k, v, do, lse, length, *, block_q=512, block_k=512):
    n, d = q.shape
    scale = 1.0 / math.sqrt(d)
    kernel = partial(_attn_bwd_kernel, block_q=block_q, block_k=block_k, scale=scale)
    pairs = (n // block_q) * (n // block_k + 1) // 2
    full = pl.BlockSpec((n, d), lambda i, lens: (0, 0))
    rows = pl.BlockSpec((block_q, d), lambda i, lens: (i, 0))
    return pl.pallas_call(
        kernel,
        out_shape=tuple(jax.ShapeDtypeStruct((n, d), jnp.bfloat16) for _ in range(3)),
        grid_spec=pltpu.PrefetchScalarGridSpec(
            num_scalar_prefetch=1,
            grid=(n // block_q,),
            in_specs=[rows, full, full, rows, pl.BlockSpec((block_q, 1), lambda i, lens: (i, 0))],
            out_specs=[rows, full, full],
            scratch_shapes=[
                pltpu.VMEM((block_q, n), jnp.float32),
                pltpu.VMEM((block_q, n), jnp.float32),
                pltpu.VMEM((n, d), jnp.float32),
                pltpu.VMEM((n, d), jnp.float32),
            ],
        ),
        compiler_params=pltpu.CompilerParams(dimension_semantics=("arbitrary",)),
        cost_estimate=pl.CostEstimate(
            flops=8 * pairs * block_q * block_k * d,
            transcendentals=pairs * block_q * block_k,
            bytes_accessed=8 * n * d * 2,
        ),
    )(length, q, k, v, do, lse)


def shards(
    tokens,
    cotangent,
    lengths,
    ln1_gain,
    ln1_bias,
    w_qkv,
    b_qv,
    w_o,
    b_o,
    ln2_gain,
    ln2_bias,
    w_in,
    b_in,
    w_out,
    b_out,
):
    row_count, seq_count, model_width = tokens.shape
    tensor_count = lax.axis_size("tensor")
    tensor_rank = lax.axis_index("tensor")
    seq_total = row_count * tensor_count
    local_heads = w_qkv.shape[2]
    head_size = w_qkv.shape[3]
    local_width = local_heads * head_size
    hidden = w_in.shape[1]
    group_count = lax.axis_size("group")
    group_rank = lax.axis_index("group")
    member = group_rank * lax.axis_size("dp") + lax.axis_index("dp")
    seq_lengths = lax.dynamic_slice_in_dim(lengths, member * seq_count, seq_count, 0)
    group_totals = jnp.sum(lengths.reshape(group_count, -1), axis=1).astype(jnp.float32)
    factor = (
        group_count
        * lax.dynamic_index_in_dim(group_totals, group_rank, 0, keepdims=False)
        / jnp.sum(group_totals)
    )
    inputs = tokens.astype(jnp.float32)
    normed_low = layer_norm(inputs, ln1_gain, ln1_bias).astype(jnp.bfloat16)
    positions = tensor_rank * row_count + jnp.arange(row_count, dtype=jnp.int32)
    live = positions[:, None] < seq_lengths[None, :]
    upstream = jnp.where(live[:, :, None], cotangent, jnp.zeros_like(cotangent))
    front = jnp.concatenate(
        [normed_low.reshape(row_count, seq_count * model_width), w_o.reshape(row_count, -1)], 1
    )
    front = lax.all_gather(front, "tensor", axis=0, tiled=True)
    wide = seq_count * model_width
    normed_full = front[:, :wide].reshape(seq_total, seq_count, model_width)
    out_full = front[:, wide:].reshape(-1, model_width)
    upstream, front = lax.optimization_barrier((upstream, front))
    upstream_full = lax.all_gather(upstream, "tensor", axis=0, tiled=True)
    joint_weight = w_qkv.reshape(model_width, 3 * local_width)
    projected = jnp.dot(
        normed_full.reshape(seq_total * seq_count, model_width),
        joint_weight,
        preferred_element_type=jnp.float32,
    )
    projected = projected.reshape(seq_total, seq_count, 3, local_width)
    query = (projected[:, :, 0] + b_qv[0]).astype(jnp.bfloat16)
    keys = projected[:, :, 1].astype(jnp.bfloat16)
    values = (projected[:, :, 2] + b_qv[1]).astype(jnp.bfloat16)

    def item(array, s, h):
        return array[:, s, h * head_size : (h + 1) * head_size]

    def per_row(items):
        stacked = jnp.stack(items).reshape(seq_count, local_heads, seq_total, head_size)
        return jnp.transpose(stacked, (2, 0, 1, 3)).reshape(seq_total, seq_count, local_width)

    pairs = [(s, h) for s in range(seq_count) for h in range(local_heads)]
    forward_items = [
        attention_forward(
            item(query, s, h), item(keys, s, h), item(values, s, h), seq_lengths[s : s + 1]
        )
        for s, h in pairs
    ]
    attended = per_row([o for o, _ in forward_items])
    out_weight = w_o.reshape(local_width, model_width)
    own_rows = lax.all_to_all(
        jnp.transpose(attended, (1, 0, 2)).reshape(seq_count * seq_total, local_width),
        "tensor",
        0,
        1,
        tiled=True,
    )
    attention = (
        jnp.dot(own_rows, out_full, preferred_element_type=jnp.float32).reshape(
            seq_count, row_count, model_width
        )
    )
    attention = jnp.transpose(attention, (1, 0, 2)) + b_o
    middle = inputs + attention
    act_grad = jnp.einsum("rsd,fd->rsf", upstream_full, w_out, preferred_element_type=jnp.float32)
    second_low = layer_norm(middle, ln2_gain, ln2_bias).astype(jnp.bfloat16)
    second_low, upstream_full = lax.optimization_barrier((second_low, upstream_full))
    second_full = lax.all_gather(second_low, "tensor", axis=0, tiled=True)
    second_full, act_grad = lax.optimization_barrier((second_full, act_grad))
    pre_act = (
        jnp.dot(
            second_full.reshape(seq_total * seq_count, model_width),
            w_in,
            preferred_element_type=jnp.float32,
        )
        + b_in
    )
    activated = gelu_tanh(pre_act).astype(jnp.bfloat16).reshape(seq_total, seq_count, hidden)
    piece = upstream_full
    grad_w_out = jnp.einsum("rsf,rsd->fd", activated, piece, preferred_element_type=jnp.float32)
    gelu_back = jax.vjp(gelu_tanh, pre_act)[1]
    pre_low = gelu_back(act_grad.reshape(seq_total * seq_count, hidden))[0].astype(jnp.bfloat16)
    grad_b_in = jnp.sum(pre_low, axis=0, dtype=jnp.float32)
    grad_w_in = jnp.einsum(
        "rd,rf->df",
        second_full.reshape(seq_total * seq_count, model_width),
        pre_low,
        preferred_element_type=jnp.float32,
    )
    pre_rows = pre_low.reshape(seq_total, seq_count, hidden)
    piece = pre_rows
    second_part = jnp.einsum("rsf,df->rsd", piece, w_in, preferred_element_type=jnp.float32)
    second_part = second_part.astype(jnp.bfloat16)
    feed_input, second_part = lax.optimization_barrier((activated, second_part))
    second_grad = lax.psum_scatter(
        second_part, "tensor", scatter_dimension=0, tiled=True
    ).astype(jnp.float32)
    feed_part = jnp.einsum(
        "rsf,fd->rsd", feed_input, w_out, preferred_element_type=jnp.float32
    ).astype(jnp.bfloat16)
    feed_buffer = lax.dynamic_update_slice(
        jnp.zeros(feed_part.shape[:2] + (2 * model_width,), feed_part.dtype),
        feed_part,
        (0, 0, model_width),
    )
    feed_buffer, second_grad = lax.optimization_barrier((feed_buffer, second_grad))
    norm_two_back = jax.vjp(layer_norm, middle, ln2_gain, ln2_bias)[1]
    middle_part, grad_ln2_gain, grad_ln2_bias = norm_two_back(second_grad)
    middle_grad = upstream.astype(jnp.float32) + middle_part
    branch_low = middle_grad.astype(jnp.bfloat16)
    grad_b_o = jnp.sum(branch_low, axis=(0, 1), dtype=jnp.float32)
    grad_b_out = jnp.sum(upstream, axis=(0, 1), dtype=jnp.float32)
    summed_in = halving_sum(grad_w_in * factor, 0)
    summed_out = halving_sum(grad_w_out * factor, 1)
    summed_in, summed_out, branch_low = lax.optimization_barrier(
        (summed_in, summed_out, branch_low)
    )
    piece = lax.all_gather(branch_low, "tensor", axis=0, tiled=True)
    weight_grad = jnp.einsum("rse,rsd->ed", attended, piece, preferred_element_type=jnp.float32)
    part = jnp.einsum("rsd,ed->rse", piece, out_weight, preferred_element_type=jnp.float32)
    attended_grad = part.astype(jnp.bfloat16)
    backward_items = [
        attention_backward(
            item(query, s, h),
            item(keys, s, h),
            item(values, s, h),
            item(attended_grad, s, h),
            lse,
            seq_lengths[s : s + 1],
        )
        for (s, h), (_, lse) in zip(pairs, forward_items)
    ]
    joint_grad = jnp.stack(
        [per_row([grads[kind] for grads in backward_items]) for kind in range(3)], axis=2
    )
    grad_b_qv = jnp.sum(joint_grad[:, :, 0::2], axis=(0, 1), dtype=jnp.float32)
    joint_rows = joint_grad.reshape(seq_total, seq_count, 3 * local_width)
    grad_w_qkv = jnp.einsum(
        "rd,rc->dc",
        normed_full.reshape(seq_total * seq_count, model_width),
        joint_rows.reshape(seq_total * seq_count, 3 * local_width),
        preferred_element_type=jnp.float32,
    )
    normed_part = jnp.einsum(
        "rsc,dc->rsd", joint_rows, joint_weight, preferred_element_type=jnp.float32
    ).astype(jnp.bfloat16)
    joint_sums = jnp.sum(joint_rows, axis=(0, 1), dtype=jnp.float32)
    grad_ln1_bias = jnp.dot(
        joint_weight.astype(jnp.float32), joint_sums, precision=lax.Precision.HIGHEST
    )
    merged = lax.dynamic_update_slice(feed_buffer, normed_part, (0, 0, 0))
    both = lax.psum_scatter(merged, "tensor", scatter_dimension=0, tiled=True)
    summed = (
        halving_sum(grad_w_qkv * factor, 0).reshape(-1, 3, local_heads, head_size),
        halving_sum(weight_grad.reshape(local_heads, head_size, model_width) * factor, 2),
        summed_in,
        summed_out,
    )
    in_full = lax.dynamic_update_slice_in_dim(
        jnp.zeros((hidden * tensor_count,), jnp.float32), grad_b_in, tensor_rank * hidden, 0
    )
    joint_full = lax.dynamic_update_slice_in_dim(
        jnp.zeros((2, local_width * tensor_count), jnp.float32),
        grad_b_qv,
        tensor_rank * local_width,
        1,
    )
    early = reduce_vectors(
        (
            grad_ln1_bias,
            grad_b_o,
            grad_ln2_gain,
            grad_ln2_bias,
            grad_b_out,
            joint_full[0],
            joint_full[1],
            in_full,
        ),
        factor,
    )
    both, summed, early = lax.optimization_barrier((both, summed, early))
    both = both.astype(jnp.float32)
    normed_grad = both[:, :, :model_width]
    feed = both[:, :, model_width:] + b_out
    output = (middle + feed).astype(jnp.bfloat16)
    norm_one_back = jax.vjp(layer_norm, inputs, ln1_gain, ln1_bias)[1]
    input_part, grad_ln1_gain, _ = norm_one_back(normed_grad)
    input_grad = (middle_grad + input_part).astype(jnp.bfloat16)
    (late,) = reduce_vectors((grad_ln1_gain,), factor)
    return (
        output,
        input_grad,
        late,
        early[0],
        summed[0],
        jnp.stack((early[5], early[6])),
        summed[1],
        early[1],
        early[2],
        early[3],
        summed[2],
        early[7],
        summed[3],
        early[4],
    )


def reduce_vectors(vectors, factor):
    devices = lax.axis_size("group") * lax.axis_size("dp") * lax.axis_size("tensor")
    pieces = [(item * factor).reshape(devices, -1) for item in vectors]
    widths = [piece.shape[1] for piece in pieces]
    packed = jnp.concatenate(pieces, 1)
    packed = lax.all_to_all(packed, ("group", "dp", "tensor"), 0, 0, tiled=True)
    flat = jnp.sum(packed, axis=0)
    parts = []
    offset = 0
    for width in widths:
        parts.append(flat[offset : offset + width])
        offset += width
    return tuple(parts)


def halving_steps(value, dim, steps, send_type=None):
    for axis, size, bit in steps:
        half = value.shape[dim] // 2
        low_half = lax.slice_in_dim(value, 0, half, axis=dim)
        high_half = lax.slice_in_dim(value, half, 2 * half, axis=dim)
        upper = (lax.axis_index(axis) // bit) % 2 == 1
        keep = jnp.where(upper, high_half, low_half)
        send = jnp.where(upper, low_half, high_half)
        if send_type is not None:
            send = send.astype(send_type)
        got = lax.ppermute(send, axis, [(i, i ^ bit) for i in range(size)])
        value = keep + got.astype(keep.dtype)
    return value


def halving_sum(value, dim):
    shape = value.shape
    groups = lax.axis_size("group")
    dps = lax.axis_size("dp")
    rest = shape[dim] // (groups * dps)
    value = value.reshape(shape[:dim] + (groups // 2, 2, dps * rest) + shape[dim + 1 :])
    value = jnp.swapaxes(value, dim, dim + 1)
    value = value.reshape(shape[:dim] + (groups * dps, rest) + shape[dim + 1 :])
    value = halving_steps(
        value, dim, [("group", groups, 1), ("group", groups, 2), ("dp", dps, 1)], jnp.bfloat16
    )
    return value.reshape(shape[:dim] + (shape[dim] // (groups * dps),) + shape[dim + 1 :])


def solution(mesh):
    in_specs = (
        P("tensor", ("group", "dp"), None),
        P("tensor", ("group", "dp"), None),
        P(),
        P(),
        P(),
        P(None, None, "tensor", None),
        P(None, "tensor"),
        P("tensor", None, None),
        P(),
        P(),
        P(),
        P(None, "tensor"),
        P("tensor"),
        P("tensor", None),
        P(),
    )
    out_specs = (
        P("tensor", ("group", "dp"), None),
        P("tensor", ("group", "dp"), None),
        P(("group", "dp", "tensor")),
        P(("group", "dp", "tensor")),
        P(("group", "dp"), None, "tensor", None),
        P(None, ("group", "dp", "tensor")),
        P("tensor", None, ("group", "dp")),
        P(("group", "dp", "tensor")),
        P(("group", "dp", "tensor")),
        P(("group", "dp", "tensor")),
        P(("group", "dp"), "tensor"),
        P(("group", "dp", "tensor")),
        P("tensor", ("group", "dp")),
        P(("group", "dp", "tensor")),
    )
    return jax.shard_map(shards, mesh=mesh, in_specs=in_specs, out_specs=out_specs, check_vma=False)
```

```python
from functools import partial
import math

import jax
import jax.numpy as jnp
from jax import lax
from jax.experimental import pallas as pl
from jax.experimental.pallas import tpu as pltpu
from jax.sharding import PartitionSpec as P

EPS = 1e-05
NEGATIVE = -1e30


def layer_norm(value, gain, shift):
    mean = jnp.mean(value, axis=-1, keepdims=True)
    centred = value - mean
    spread = jnp.mean(centred * centred, axis=-1, keepdims=True)
    return centred * lax.rsqrt(spread + EPS) * gain + shift


def gelu_tanh(value):
    return jax.nn.gelu(value, approximate=True)


def _valid(first_q, first_k, rows, cols, length):
    q_pos = first_q + lax.broadcasted_iota(jnp.int32, (rows, cols), 0)
    k_pos = first_k + lax.broadcasted_iota(jnp.int32, (rows, cols), 1)
    return (k_pos <= q_pos) & (k_pos < length)


def _key_blocks(i, block_q, block_k, length):
    causal = (i * block_q + block_q + block_k - 1) // block_k
    live = (length + block_k - 1) // block_k
    return jnp.minimum(causal, live)


def _attn_fwd_kernel(len_ref, q_ref, k_ref, v_ref, o_ref, lse_ref, s_buf, *, block_q, block_k, scale):
    i = pl.program_id(0)
    length = len_ref[0]
    count = _key_blocks(i, block_q, block_k, length)
    q = q_ref[...]

    def scores(j, m):
        first = pl.multiple_of(j * block_k, block_k)
        k = k_ref[pl.ds(first, block_k), :]
        s = lax.dot_general(q, k, (((1,), (1,)), ((), ())), preferred_element_type=jnp.float32) * scale
        edge = (first + block_k > i * block_q) | (first + block_k > length)
        s = lax.cond(
            edge,
            lambda v: jnp.where(_valid(i * block_q, first, block_q, block_k, length), v, NEGATIVE),
            lambda v: v,
            s,
        )
        s_buf[:, pl.ds(first, block_k)] = s
        return jnp.maximum(m, jnp.max(s, axis=1, keepdims=True))

    peak = lax.fori_loop(0, count, scores, jnp.full((block_q, 1), NEGATIVE, jnp.float32))

    def exps(j, total):
        first = pl.multiple_of(j * block_k, block_k)
        e = jnp.exp(s_buf[:, pl.ds(first, block_k)] - peak)
        s_buf[:, pl.ds(first, block_k)] = e
        return total + jnp.sum(e, axis=1, keepdims=True)

    total = lax.fori_loop(0, count, exps, jnp.zeros((block_q, 1), jnp.float32))

    inverse = 1.0 / total

    def mix(j, acc):
        first = pl.multiple_of(j * block_k, block_k)
        probs = (s_buf[:, pl.ds(first, block_k)] * inverse).astype(jnp.bfloat16)
        return acc + jnp.dot(probs, v_ref[pl.ds(first, block_k), :], preferred_element_type=jnp.float32)

    acc = lax.fori_loop(0, count, mix, jnp.zeros(o_ref.shape, jnp.float32))
    o_ref[...] = acc.astype(o_ref.dtype)
    lse_ref[...] = peak + jnp.log(total)


def attention_forward(q, k, v, length, *, block_q=512, block_k=512):
    n, d = q.shape
    scale = 1.0 / math.sqrt(d)
    kernel = partial(_attn_fwd_kernel, block_q=block_q, block_k=block_k, scale=scale)
    pairs = (n // block_q) * (n // block_k + 1) // 2
    return pl.pallas_call(
        kernel,
        out_shape=(jax.ShapeDtypeStruct((n, d), jnp.bfloat16), jax.ShapeDtypeStruct((n, 1), jnp.float32)),
        grid_spec=pltpu.PrefetchScalarGridSpec(
            num_scalar_prefetch=1,
            grid=(n // block_q,),
            in_specs=[
                pl.BlockSpec((block_q, d), lambda i, lens: (i, 0)),
                pl.BlockSpec((n, d), lambda i, lens: (0, 0)),
                pl.BlockSpec((n, d), lambda i, lens: (0, 0)),
            ],
            out_specs=[
                pl.BlockSpec((block_q, d), lambda i, lens: (i, 0)),
                pl.BlockSpec((block_q, 1), lambda i, lens: (i, 0)),
            ],
            scratch_shapes=[pltpu.VMEM((block_q, n), jnp.float32)],
        ),
        compiler_params=pltpu.CompilerParams(dimension_semantics=("arbitrary",)),
        cost_estimate=pl.CostEstimate(
            flops=4 * pairs * block_q * block_k * d,
            transcendentals=pairs * block_q * block_k,
            bytes_accessed=4 * n * d * 2,
        ),
    )(length, q, k, v)


def _attn_bwd_kernel(len_ref, q_ref, k_ref, v_ref, do_ref, lse_ref, dq_ref, dk_ref, dv_ref,
                     p_buf, dp_buf, dk_acc, dv_acc, *, block_q, block_k, scale):
    i = pl.program_id(0)
    length = len_ref[0]

    @pl.when(i == 0)
    def _():
        dk_acc[...] = jnp.zeros_like(dk_acc)
        dv_acc[...] = jnp.zeros_like(dv_acc)

    live = i * block_q < length

    @pl.when(live)
    def _():
        count = _key_blocks(i, block_q, block_k, length)
        q = q_ref[...]
        do = do_ref[...]
        lse = lse_ref[...]

        def first_pass(j, inner):
            first = pl.multiple_of(j * block_k, block_k)
            k = k_ref[pl.ds(first, block_k), :]
            v = v_ref[pl.ds(first, block_k), :]
            s = lax.dot_general(q, k, (((1,), (1,)), ((), ())), preferred_element_type=jnp.float32)
            edge = (first + block_k > i * block_q) | (first + block_k > length)
            p = lax.cond(
                edge,
                lambda v: jnp.where(
                    _valid(i * block_q, first, block_q, block_k, length),
                    jnp.exp(jnp.where(_valid(i * block_q, first, block_q, block_k, length), v, NEGATIVE) - lse),
                    0.0,
                ),
                lambda v: jnp.exp(v - lse),
                s * scale,
            )
            dp = lax.dot_general(do, v, (((1,), (1,)), ((), ())), preferred_element_type=jnp.float32)
            p_buf[:, pl.ds(first, block_k)] = p
            dp_buf[:, pl.ds(first, block_k)] = dp
            return inner + jnp.sum(p * dp, axis=1, keepdims=True)

        inner = lax.fori_loop(0, count, first_pass, jnp.zeros((block_q, 1), jnp.float32))

        def second_pass(j, dq):
            first = pl.multiple_of(j * block_k, block_k)
            p = p_buf[:, pl.ds(first, block_k)]
            dp = dp_buf[:, pl.ds(first, block_k)]
            ds = (p * (dp - inner)).astype(jnp.bfloat16)
            k = k_ref[pl.ds(first, block_k), :]
            dk_acc[pl.ds(first, block_k), :] += lax.dot_general(
                ds, q, (((0,), (0,)), ((), ())), preferred_element_type=jnp.float32)
            dv_acc[pl.ds(first, block_k), :] += lax.dot_general(
                p.astype(jnp.bfloat16), do, (((0,), (0,)), ((), ())), preferred_element_type=jnp.float32)
            return dq + jnp.dot(ds, k, preferred_element_type=jnp.float32)

        dq = lax.fori_loop(0, count, second_pass, jnp.zeros(dq_ref.shape, jnp.float32))
        dq_ref[...] = (dq * scale).astype(dq_ref.dtype)

    @pl.when(jnp.logical_not(live))
    def _():
        dq_ref[...] = jnp.zeros_like(dq_ref)

    @pl.when(i == pl.num_programs(0) - 1)
    def _():
        dk_ref[...] = (dk_acc[...] * scale).astype(dk_ref.dtype)
        dv_ref[...] = dv_acc[...].astype(dv_ref.dtype)


def attention_backward(q, k, v, do, lse, length, *, block_q=512, block_k=512):
    n, d = q.shape
    scale = 1.0 / math.sqrt(d)
    kernel = partial(_attn_bwd_kernel, block_q=block_q, block_k=block_k, scale=scale)
    pairs = (n // block_q) * (n // block_k + 1) // 2
    full = pl.BlockSpec((n, d), lambda i, lens: (0, 0))
    rows = pl.BlockSpec((block_q, d), lambda i, lens: (i, 0))
    return pl.pallas_call(
        kernel,
        out_shape=tuple(jax.ShapeDtypeStruct((n, d), jnp.bfloat16) for _ in range(3)),
        grid_spec=pltpu.PrefetchScalarGridSpec(
            num_scalar_prefetch=1,
            grid=(n // block_q,),
            in_specs=[rows, full, full, rows, pl.BlockSpec((block_q, 1), lambda i, lens: (i, 0))],
            out_specs=[rows, full, full],
            scratch_shapes=[
                pltpu.VMEM((block_q, n), jnp.float32),
                pltpu.VMEM((block_q, n), jnp.float32),
                pltpu.VMEM((n, d), jnp.float32),
                pltpu.VMEM((n, d), jnp.float32),
            ],
        ),
        compiler_params=pltpu.CompilerParams(dimension_semantics=("arbitrary",)),
        cost_estimate=pl.CostEstimate(
            flops=8 * pairs * block_q * block_k * d,
            transcendentals=pairs * block_q * block_k,
            bytes_accessed=8 * n * d * 2,
        ),
    )(length, q, k, v, do, lse)


def shards(
    tokens,
    cotangent,
    lengths,
    ln1_gain,
    ln1_bias,
    w_qkv,
    b_qv,
    w_o,
    b_o,
    ln2_gain,
    ln2_bias,
    w_in,
    b_in,
    w_out,
    b_out,
):
    row_count, seq_count, model_width = tokens.shape
    tensor_count = lax.axis_size("tensor")
    tensor_rank = lax.axis_index("tensor")
    seq_total = row_count * tensor_count
    local_heads = w_qkv.shape[2]
    head_size = w_qkv.shape[3]
    local_width = local_heads * head_size
    hidden = w_in.shape[1]
    group_count = lax.axis_size("group")
    group_rank = lax.axis_index("group")
    member = group_rank * lax.axis_size("dp") + lax.axis_index("dp")
    seq_lengths = lax.dynamic_slice_in_dim(lengths, member * seq_count, seq_count, 0)
    group_totals = jnp.sum(lengths.reshape(group_count, -1), axis=1).astype(jnp.float32)
    factor = (
        group_count
        * lax.dynamic_index_in_dim(group_totals, group_rank, 0, keepdims=False)
        / jnp.sum(group_totals)
    )
    inputs = tokens.astype(jnp.float32)
    normed_low = layer_norm(inputs, ln1_gain, ln1_bias).astype(jnp.bfloat16)
    positions = tensor_rank * row_count + jnp.arange(row_count, dtype=jnp.int32)
    live = positions[:, None] < seq_lengths[None, :]
    upstream = jnp.where(live[:, :, None], cotangent, jnp.zeros_like(cotangent))
    front = jnp.concatenate(
        [normed_low.reshape(row_count, seq_count * model_width), w_o.reshape(row_count, -1)], 1
    )
    front = lax.all_gather(front, "tensor", axis=0, tiled=True)
    wide = seq_count * model_width
    normed_full = front[:, :wide].reshape(seq_total, seq_count, model_width)
    out_full = front[:, wide:].reshape(-1, model_width)
    upstream, front = lax.optimization_barrier((upstream, front))
    upstream_full = lax.all_gather(upstream, "tensor", axis=0, tiled=True)
    joint_weight = w_qkv.reshape(model_width, 3 * local_width)
    projected = jnp.dot(
        normed_full.reshape(seq_total * seq_count, model_width),
        joint_weight,
        preferred_element_type=jnp.float32,
    )
    projected = projected.reshape(seq_total, seq_count, 3, local_width)
    query = (projected[:, :, 0] + b_qv[0]).astype(jnp.bfloat16)
    keys = projected[:, :, 1].astype(jnp.bfloat16)
    values = (projected[:, :, 2] + b_qv[1]).astype(jnp.bfloat16)

    def item(array, s, h):
        return array[:, s, h * head_size : (h + 1) * head_size]

    def per_row(items):
        stacked = jnp.stack(items).reshape(seq_count, local_heads, seq_total, head_size)
        return jnp.transpose(stacked, (2, 0, 1, 3)).reshape(seq_total, seq_count, local_width)

    pairs = [(s, h) for s in range(seq_count) for h in range(local_heads)]
    forward_items = [
        attention_forward(
            item(query, s, h), item(keys, s, h), item(values, s, h), seq_lengths[s : s + 1]
        )
        for s, h in pairs
    ]
    attended = per_row([o for o, _ in forward_items])
    out_weight = w_o.reshape(local_width, model_width)
    own_rows = lax.all_to_all(
        jnp.transpose(attended, (1, 0, 2)).reshape(seq_count * seq_total, local_width),
        "tensor",
        0,
        1,
        tiled=True,
    )
    attention = (
        jnp.dot(own_rows, out_full, preferred_element_type=jnp.float32).reshape(
            seq_count, row_count, model_width
        )
    )
    attention = jnp.transpose(attention, (1, 0, 2)) + b_o
    middle = inputs + attention
    act_grad = jnp.einsum("rsd,fd->rsf", upstream_full, w_out, preferred_element_type=jnp.float32)
    second_low = layer_norm(middle, ln2_gain, ln2_bias).astype(jnp.bfloat16)
    second_low, upstream_full = lax.optimization_barrier((second_low, upstream_full))
    second_full = lax.all_gather(second_low, "tensor", axis=0, tiled=True)
    second_full, act_grad = lax.optimization_barrier((second_full, act_grad))
    pre_act = (
        jnp.dot(
            second_full.reshape(seq_total * seq_count, model_width),
            w_in,
            preferred_element_type=jnp.float32,
        )
        + b_in
    )
    activated = gelu_tanh(pre_act).astype(jnp.bfloat16).reshape(seq_total, seq_count, hidden)
    piece = upstream_full
    grad_w_out = jnp.einsum("rsf,rsd->fd", activated, piece, preferred_element_type=jnp.float32)
    gelu_back = jax.vjp(gelu_tanh, pre_act)[1]
    pre_low = gelu_back(act_grad.reshape(seq_total * seq_count, hidden))[0].astype(jnp.bfloat16)
    grad_b_in = jnp.sum(pre_low, axis=0, dtype=jnp.float32)
    grad_w_in = jnp.einsum(
        "rd,rf->df",
        second_full.reshape(seq_total * seq_count, model_width),
        pre_low,
        preferred_element_type=jnp.float32,
    )
    pre_rows = pre_low.reshape(seq_total, seq_count, hidden)
    piece = pre_rows
    second_part = jnp.einsum("rsf,df->rsd", piece, w_in, preferred_element_type=jnp.float32)
    second_part = second_part.astype(jnp.bfloat16)
    feed_input, second_part = lax.optimization_barrier((activated, second_part))
    second_grad = lax.psum_scatter(
        second_part, "tensor", scatter_dimension=0, tiled=True
    ).astype(jnp.float32)
    feed_part = jnp.einsum(
        "rsf,fd->rsd", feed_input, w_out, preferred_element_type=jnp.float32
    ).astype(jnp.bfloat16)
    feed_buffer = lax.dynamic_update_slice(
        jnp.zeros(feed_part.shape[:2] + (2 * model_width,), feed_part.dtype),
        feed_part,
        (0, 0, model_width),
    )
    feed_buffer, second_grad = lax.optimization_barrier((feed_buffer, second_grad))
    norm_two_back = jax.vjp(layer_norm, middle, ln2_gain, ln2_bias)[1]
    middle_part, grad_ln2_gain, grad_ln2_bias = norm_two_back(second_grad)
    middle_grad = upstream.astype(jnp.float32) + middle_part
    branch_low = middle_grad.astype(jnp.bfloat16)
    grad_b_o = jnp.sum(branch_low, axis=(0, 1), dtype=jnp.float32)
    grad_b_out = jnp.sum(upstream, axis=(0, 1), dtype=jnp.float32)
    summed_in = halving_sum(grad_w_in * factor, 0)
    summed_out = halving_sum(grad_w_out * factor, 1)
    summed_in, summed_out, branch_low = lax.optimization_barrier(
        (summed_in, summed_out, branch_low)
    )
    piece = lax.all_gather(branch_low, "tensor", axis=0, tiled=True)
    weight_grad = jnp.einsum("rse,rsd->ed", attended, piece, preferred_element_type=jnp.float32)
    heads_grad = jnp.dot(
        branch_low.reshape(row_count * seq_count, model_width),
        out_full.T,
        preferred_element_type=jnp.float32,
    ).astype(jnp.bfloat16)
    attended_grad = lax.all_to_all(heads_grad, "tensor", 1, 0, tiled=True).reshape(
        seq_total, seq_count, local_width
    )
    backward_items = [
        attention_backward(
            item(query, s, h),
            item(keys, s, h),
            item(values, s, h),
            item(attended_grad, s, h),
            lse,
            seq_lengths[s : s + 1],
        )
        for (s, h), (_, lse) in zip(pairs, forward_items)
    ]
    joint_grad = jnp.stack(
        [per_row([grads[kind] for grads in backward_items]) for kind in range(3)], axis=2
    )
    grad_b_qv = jnp.sum(joint_grad[:, :, 0::2], axis=(0, 1), dtype=jnp.float32)
    joint_rows = joint_grad.reshape(seq_total, seq_count, 3 * local_width)
    grad_w_qkv = jnp.einsum(
        "rd,rc->dc",
        normed_full.reshape(seq_total * seq_count, model_width),
        joint_rows.reshape(seq_total * seq_count, 3 * local_width),
        preferred_element_type=jnp.float32,
    )
    normed_part = jnp.einsum(
        "rsc,dc->rsd", joint_rows, joint_weight, preferred_element_type=jnp.float32
    ).astype(jnp.bfloat16)
    joint_sums = jnp.sum(joint_rows, axis=(0, 1), dtype=jnp.float32)
    grad_ln1_bias = jnp.dot(
        joint_weight.astype(jnp.float32), joint_sums, precision=lax.Precision.HIGHEST
    )
    merged = lax.dynamic_update_slice(feed_buffer, normed_part, (0, 0, 0))
    both = lax.psum_scatter(merged, "tensor", scatter_dimension=0, tiled=True)
    summed = (
        halving_sum(grad_w_qkv * factor, 0).reshape(-1, 3, local_heads, head_size),
        halving_sum(weight_grad.reshape(local_heads, head_size, model_width) * factor, 2),
        summed_in,
        summed_out,
    )
    in_full = lax.dynamic_update_slice_in_dim(
        jnp.zeros((hidden * tensor_count,), jnp.float32), grad_b_in, tensor_rank * hidden, 0
    )
    joint_full = lax.dynamic_update_slice_in_dim(
        jnp.zeros((2, local_width * tensor_count), jnp.float32),
        grad_b_qv,
        tensor_rank * local_width,
        1,
    )
    early = reduce_vectors(
        (
            grad_ln1_bias,
            grad_b_o,
            grad_ln2_gain,
            grad_ln2_bias,
            grad_b_out,
            joint_full[0],
            joint_full[1],
            in_full,
        ),
        factor,
    )
    both, summed, early = lax.optimization_barrier((both, summed, early))
    both = both.astype(jnp.float32)
    normed_grad = both[:, :, :model_width]
    feed = both[:, :, model_width:] + b_out
    output = (middle + feed).astype(jnp.bfloat16)
    norm_one_back = jax.vjp(layer_norm, inputs, ln1_gain, ln1_bias)[1]
    input_part, grad_ln1_gain, _ = norm_one_back(normed_grad)
    input_grad = (middle_grad + input_part).astype(jnp.bfloat16)
    (late,) = reduce_vectors((grad_ln1_gain,), factor)
    return (
        output,
        input_grad,
        late,
        early[0],
        summed[0],
        jnp.stack((early[5], early[6])),
        summed[1],
        early[1],
        early[2],
        early[3],
        summed[2],
        early[7],
        summed[3],
        early[4],
    )


def reduce_vectors(vectors, factor):
    devices = lax.axis_size("group") * lax.axis_size("dp") * lax.axis_size("tensor")
    pieces = [(item * factor).reshape(devices, -1) for item in vectors]
    widths = [piece.shape[1] for piece in pieces]
    packed = jnp.concatenate(pieces, 1)
    packed = lax.all_to_all(packed, ("group", "dp", "tensor"), 0, 0, tiled=True)
    flat = jnp.sum(packed, axis=0)
    parts = []
    offset = 0
    for width in widths:
        parts.append(flat[offset : offset + width])
        offset += width
    return tuple(parts)


def halving_steps(value, dim, steps, send_type=None):
    for axis, size, bit in steps:
        half = value.shape[dim] // 2
        low_half = lax.slice_in_dim(value, 0, half, axis=dim)
        high_half = lax.slice_in_dim(value, half, 2 * half, axis=dim)
        upper = (lax.axis_index(axis) // bit) % 2 == 1
        keep = jnp.where(upper, high_half, low_half)
        send = jnp.where(upper, low_half, high_half)
        if send_type is not None:
            send = send.astype(send_type)
        got = lax.ppermute(send, axis, [(i, i ^ bit) for i in range(size)])
        value = keep + got.astype(keep.dtype)
    return value


def halving_sum(value, dim):
    shape = value.shape
    groups = lax.axis_size("group")
    dps = lax.axis_size("dp")
    rest = shape[dim] // (groups * dps)
    value = value.reshape(shape[:dim] + (groups // 2, 2, dps * rest) + shape[dim + 1 :])
    value = jnp.swapaxes(value, dim, dim + 1)
    value = value.reshape(shape[:dim] + (groups * dps, rest) + shape[dim + 1 :])
    value = halving_steps(
        value, dim, [("group", groups, 1), ("group", groups, 2), ("dp", dps, 1)], jnp.bfloat16
    )
    return value.reshape(shape[:dim] + (shape[dim] // (groups * dps),) + shape[dim + 1 :])


def solution(mesh):
    in_specs = (
        P("tensor", ("group", "dp"), None),
        P("tensor", ("group", "dp"), None),
        P(),
        P(),
        P(),
        P(None, None, "tensor", None),
        P(None, "tensor"),
        P("tensor", None, None),
        P(),
        P(),
        P(),
        P(None, "tensor"),
        P("tensor"),
        P("tensor", None),
        P(),
    )
    out_specs = (
        P("tensor", ("group", "dp"), None),
        P("tensor", ("group", "dp"), None),
        P(("group", "dp", "tensor")),
        P(("group", "dp", "tensor")),
        P(("group", "dp"), None, "tensor", None),
        P(None, ("group", "dp", "tensor")),
        P("tensor", None, ("group", "dp")),
        P(("group", "dp", "tensor")),
        P(("group", "dp", "tensor")),
        P(("group", "dp", "tensor")),
        P(("group", "dp"), "tensor"),
        P(("group", "dp", "tensor")),
        P("tensor", ("group", "dp")),
        P(("group", "dp", "tensor")),
    )
    return jax.shard_map(shards, mesh=mesh, in_specs=in_specs, out_specs=out_specs, check_vma=False)
```

```python
from functools import partial
import math

import jax
import jax.numpy as jnp
from jax import lax
from jax.experimental import pallas as pl
from jax.experimental.pallas import tpu as pltpu
from jax.sharding import PartitionSpec as P

EPS = 1e-05
NEGATIVE = -1e30


def layer_norm(value, gain, shift):
    mean = jnp.mean(value, axis=-1, keepdims=True)
    centred = value - mean
    spread = jnp.mean(centred * centred, axis=-1, keepdims=True)
    return centred * lax.rsqrt(spread + EPS) * gain + shift


def gelu_tanh(value):
    return jax.nn.gelu(value, approximate=True)


def _valid(first_q, first_k, rows, cols, length):
    q_pos = first_q + lax.broadcasted_iota(jnp.int32, (rows, cols), 0)
    k_pos = first_k + lax.broadcasted_iota(jnp.int32, (rows, cols), 1)
    return (k_pos <= q_pos) & (k_pos < length)


def _key_blocks(i, block_q, block_k, length):
    causal = (i * block_q + block_q + block_k - 1) // block_k
    live = (length + block_k - 1) // block_k
    return jnp.minimum(causal, live)


def _attn_fwd_kernel(len_ref, q_ref, k_ref, v_ref, o_ref, lse_ref, s_buf, *, block_q, block_k, scale):
    i = pl.program_id(0)
    length = len_ref[0]
    count = _key_blocks(i, block_q, block_k, length)
    q = q_ref[...]

    def scores(j, m):
        first = pl.multiple_of(j * block_k, block_k)
        k = k_ref[pl.ds(first, block_k), :]
        s = lax.dot_general(q, k, (((1,), (1,)), ((), ())), preferred_element_type=jnp.float32) * scale
        edge = (first + block_k > i * block_q) | (first + block_k > length)
        s = lax.cond(
            edge,
            lambda v: jnp.where(_valid(i * block_q, first, block_q, block_k, length), v, NEGATIVE),
            lambda v: v,
            s,
        )
        s_buf[:, pl.ds(first, block_k)] = s
        return jnp.maximum(m, jnp.max(s, axis=1, keepdims=True))

    peak = lax.fori_loop(0, count, scores, jnp.full((block_q, 1), NEGATIVE, jnp.float32))

    def exps(j, total):
        first = pl.multiple_of(j * block_k, block_k)
        e = jnp.exp(s_buf[:, pl.ds(first, block_k)] - peak)
        s_buf[:, pl.ds(first, block_k)] = e
        return total + jnp.sum(e, axis=1, keepdims=True)

    total = lax.fori_loop(0, count, exps, jnp.zeros((block_q, 1), jnp.float32))

    inverse = 1.0 / total

    def mix(j, acc):
        first = pl.multiple_of(j * block_k, block_k)
        probs = (s_buf[:, pl.ds(first, block_k)] * inverse).astype(jnp.bfloat16)
        return acc + jnp.dot(probs, v_ref[pl.ds(first, block_k), :], preferred_element_type=jnp.float32)

    acc = lax.fori_loop(0, count, mix, jnp.zeros(o_ref.shape, jnp.float32))
    o_ref[...] = acc.astype(o_ref.dtype)
    lse_ref[...] = peak + jnp.log(total)


def attention_forward(q, k, v, length, *, block_q=512, block_k=512):
    n, d = q.shape
    scale = 1.0 / math.sqrt(d)
    kernel = partial(_attn_fwd_kernel, block_q=block_q, block_k=block_k, scale=scale)
    pairs = (n // block_q) * (n // block_k + 1) // 2
    return pl.pallas_call(
        kernel,
        out_shape=(jax.ShapeDtypeStruct((n, d), jnp.bfloat16), jax.ShapeDtypeStruct((n, 1), jnp.float32)),
        grid_spec=pltpu.PrefetchScalarGridSpec(
            num_scalar_prefetch=1,
            grid=(n // block_q,),
            in_specs=[
                pl.BlockSpec((block_q, d), lambda i, lens: (i, 0)),
                pl.BlockSpec((n, d), lambda i, lens: (0, 0)),
                pl.BlockSpec((n, d), lambda i, lens: (0, 0)),
            ],
            out_specs=[
                pl.BlockSpec((block_q, d), lambda i, lens: (i, 0)),
                pl.BlockSpec((block_q, 1), lambda i, lens: (i, 0)),
            ],
            scratch_shapes=[pltpu.VMEM((block_q, n), jnp.float32)],
        ),
        compiler_params=pltpu.CompilerParams(dimension_semantics=("arbitrary",)),
        cost_estimate=pl.CostEstimate(
            flops=4 * pairs * block_q * block_k * d,
            transcendentals=pairs * block_q * block_k,
            bytes_accessed=4 * n * d * 2,
        ),
    )(length, q, k, v)


def _attn_bwd_kernel(len_ref, q_ref, k_ref, v_ref, do_ref, lse_ref, dq_ref, dk_ref, dv_ref,
                     p_buf, dp_buf, dk_acc, dv_acc, *, block_q, block_k, scale):
    i = pl.program_id(0)
    length = len_ref[0]

    @pl.when(i == 0)
    def _():
        dk_acc[...] = jnp.zeros_like(dk_acc)
        dv_acc[...] = jnp.zeros_like(dv_acc)

    live = i * block_q < length

    @pl.when(live)
    def _():
        count = _key_blocks(i, block_q, block_k, length)
        q = q_ref[...]
        do = do_ref[...]
        lse = lse_ref[...]

        def first_pass(j, inner):
            first = pl.multiple_of(j * block_k, block_k)
            k = k_ref[pl.ds(first, block_k), :]
            v = v_ref[pl.ds(first, block_k), :]
            s = lax.dot_general(q, k, (((1,), (1,)), ((), ())), preferred_element_type=jnp.float32)
            edge = (first + block_k > i * block_q) | (first + block_k > length)
            p = lax.cond(
                edge,
                lambda v: jnp.where(
                    _valid(i * block_q, first, block_q, block_k, length),
                    jnp.exp(jnp.where(_valid(i * block_q, first, block_q, block_k, length), v, NEGATIVE) - lse),
                    0.0,
                ),
                lambda v: jnp.exp(v - lse),
                s * scale,
            )
            dp = lax.dot_general(do, v, (((1,), (1,)), ((), ())), preferred_element_type=jnp.float32)
            p_buf[:, pl.ds(first, block_k)] = p
            dp_buf[:, pl.ds(first, block_k)] = dp
            return inner + jnp.sum(p * dp, axis=1, keepdims=True)

        inner = lax.fori_loop(0, count, first_pass, jnp.zeros((block_q, 1), jnp.float32))

        def second_pass(j, dq):
            first = pl.multiple_of(j * block_k, block_k)
            p = p_buf[:, pl.ds(first, block_k)]
            dp = dp_buf[:, pl.ds(first, block_k)]
            ds = (p * (dp - inner)).astype(jnp.bfloat16)
            k = k_ref[pl.ds(first, block_k), :]
            dk_acc[pl.ds(first, block_k), :] += lax.dot_general(
                ds, q, (((0,), (0,)), ((), ())), preferred_element_type=jnp.float32)
            dv_acc[pl.ds(first, block_k), :] += lax.dot_general(
                p.astype(jnp.bfloat16), do, (((0,), (0,)), ((), ())), preferred_element_type=jnp.float32)
            return dq + jnp.dot(ds, k, preferred_element_type=jnp.float32)

        dq = lax.fori_loop(0, count, second_pass, jnp.zeros(dq_ref.shape, jnp.float32))
        dq_ref[...] = (dq * scale).astype(dq_ref.dtype)

    @pl.when(jnp.logical_not(live))
    def _():
        dq_ref[...] = jnp.zeros_like(dq_ref)

    @pl.when(i == pl.num_programs(0) - 1)
    def _():
        dk_ref[...] = (dk_acc[...] * scale).astype(dk_ref.dtype)
        dv_ref[...] = dv_acc[...].astype(dv_ref.dtype)


def attention_backward(q, k, v, do, lse, length, *, block_q=512, block_k=512):
    n, d = q.shape
    scale = 1.0 / math.sqrt(d)
    kernel = partial(_attn_bwd_kernel, block_q=block_q, block_k=block_k, scale=scale)
    pairs = (n // block_q) * (n // block_k + 1) // 2
    full = pl.BlockSpec((n, d), lambda i, lens: (0, 0))
    rows = pl.BlockSpec((block_q, d), lambda i, lens: (i, 0))
    return pl.pallas_call(
        kernel,
        out_shape=tuple(jax.ShapeDtypeStruct((n, d), jnp.bfloat16) for _ in range(3)),
        grid_spec=pltpu.PrefetchScalarGridSpec(
            num_scalar_prefetch=1,
            grid=(n // block_q,),
            in_specs=[rows, full, full, rows, pl.BlockSpec((block_q, 1), lambda i, lens: (i, 0))],
            out_specs=[rows, full, full],
            scratch_shapes=[
                pltpu.VMEM((block_q, n), jnp.float32),
                pltpu.VMEM((block_q, n), jnp.float32),
                pltpu.VMEM((n, d), jnp.float32),
                pltpu.VMEM((n, d), jnp.float32),
            ],
        ),
        compiler_params=pltpu.CompilerParams(dimension_semantics=("arbitrary",)),
        cost_estimate=pl.CostEstimate(
            flops=8 * pairs * block_q * block_k * d,
            transcendentals=pairs * block_q * block_k,
            bytes_accessed=8 * n * d * 2,
        ),
    )(length, q, k, v, do, lse)


def shards(
    tokens,
    cotangent,
    lengths,
    ln1_gain,
    ln1_bias,
    w_qkv,
    b_qv,
    w_o,
    b_o,
    ln2_gain,
    ln2_bias,
    w_in,
    b_in,
    w_out,
    b_out,
):
    row_count, seq_count, model_width = tokens.shape
    tensor_count = lax.axis_size("tensor")
    tensor_rank = lax.axis_index("tensor")
    seq_total = row_count * tensor_count
    local_heads = w_qkv.shape[2]
    head_size = w_qkv.shape[3]
    local_width = local_heads * head_size
    hidden = w_in.shape[1]
    group_count = lax.axis_size("group")
    group_rank = lax.axis_index("group")
    member = group_rank * lax.axis_size("dp") + lax.axis_index("dp")
    seq_lengths = lax.dynamic_slice_in_dim(lengths, member * seq_count, seq_count, 0)
    group_totals = jnp.sum(lengths.reshape(group_count, -1), axis=1).astype(jnp.float32)
    factor = (
        group_count
        * lax.dynamic_index_in_dim(group_totals, group_rank, 0, keepdims=False)
        / jnp.sum(group_totals)
    )
    inputs = tokens.astype(jnp.float32)
    normed_low = layer_norm(inputs, ln1_gain, ln1_bias).astype(jnp.bfloat16)
    positions = tensor_rank * row_count + jnp.arange(row_count, dtype=jnp.int32)
    live = positions[:, None] < seq_lengths[None, :]
    upstream = jnp.where(live[:, :, None], cotangent, jnp.zeros_like(cotangent))
    core = group_rank % 2
    half_width = model_width // 2
    front = jnp.concatenate(
        [
            normed_low.reshape(row_count, seq_count * model_width),
            lax.dynamic_slice_in_dim(w_o.reshape(row_count, -1), core * half_width, half_width, 1),
        ],
        1,
    )
    front = lax.all_gather(front, "tensor", axis=0, tiled=True)
    wide = seq_count * model_width
    normed_full = front[:, :wide].reshape(seq_total, seq_count, model_width)
    out_mine = front[:, wide:]
    out_other = lax.ppermute(out_mine, "group", [(g, g ^ 1) for g in range(group_count)])
    upstream, front = lax.optimization_barrier((upstream, front))
    upstream_full = lax.all_gather(upstream, "tensor", axis=0, tiled=True)
    joint_weight = w_qkv.reshape(model_width, 3 * local_width)
    projected = jnp.dot(
        normed_full.reshape(seq_total * seq_count, model_width),
        joint_weight,
        preferred_element_type=jnp.float32,
    )
    projected = projected.reshape(seq_total, seq_count, 3, local_width)
    query = (projected[:, :, 0] + b_qv[0]).astype(jnp.bfloat16)
    keys = projected[:, :, 1].astype(jnp.bfloat16)
    values = (projected[:, :, 2] + b_qv[1]).astype(jnp.bfloat16)

    def item(array, s, h):
        return array[:, s, h * head_size : (h + 1) * head_size]

    def per_row(items):
        stacked = jnp.stack(items).reshape(seq_count, local_heads, seq_total, head_size)
        return jnp.transpose(stacked, (2, 0, 1, 3)).reshape(seq_total, seq_count, local_width)

    pairs = [(s, h) for s in range(seq_count) for h in range(local_heads)]
    forward_items = [
        attention_forward(
            item(query, s, h), item(keys, s, h), item(values, s, h), seq_lengths[s : s + 1]
        )
        for s, h in pairs
    ]
    attended = per_row([o for o, _ in forward_items])
    out_weight = w_o.reshape(local_width, model_width)
    own_rows = lax.all_to_all(
        jnp.transpose(attended, (1, 0, 2)).reshape(seq_count * seq_total, local_width),
        "tensor",
        0,
        1,
        tiled=True,
    )
    attention = (
        half_columns(
            jnp.dot(own_rows, out_mine, preferred_element_type=jnp.float32),
            jnp.dot(own_rows, out_other, preferred_element_type=jnp.float32),
            core,
        ).reshape(
            seq_count, row_count, model_width
        )
    )
    attention = jnp.transpose(attention, (1, 0, 2)) + b_o
    middle = inputs + attention
    act_grad = jnp.einsum("rsd,fd->rsf", upstream_full, w_out, preferred_element_type=jnp.float32)
    second_low = layer_norm(middle, ln2_gain, ln2_bias).astype(jnp.bfloat16)
    second_low, upstream_full = lax.optimization_barrier((second_low, upstream_full))
    second_full = lax.all_gather(second_low, "tensor", axis=0, tiled=True)
    second_full, act_grad = lax.optimization_barrier((second_full, act_grad))
    pre_act = (
        jnp.dot(
            second_full.reshape(seq_total * seq_count, model_width),
            w_in,
            preferred_element_type=jnp.float32,
        )
        + b_in
    )
    activated = gelu_tanh(pre_act).astype(jnp.bfloat16).reshape(seq_total, seq_count, hidden)
    piece = upstream_full
    grad_w_out = jnp.einsum("rsf,rsd->fd", activated, piece, preferred_element_type=jnp.float32)
    gelu_back = jax.vjp(gelu_tanh, pre_act)[1]
    pre_low = gelu_back(act_grad.reshape(seq_total * seq_count, hidden))[0].astype(jnp.bfloat16)
    grad_b_in = jnp.sum(pre_low, axis=0, dtype=jnp.float32)
    grad_w_in = jnp.einsum(
        "rd,rf->df",
        second_full.reshape(seq_total * seq_count, model_width),
        pre_low,
        preferred_element_type=jnp.float32,
    )
    pre_rows = pre_low.reshape(seq_total, seq_count, hidden)
    piece = pre_rows
    second_part = jnp.einsum("rsf,df->rsd", piece, w_in, preferred_element_type=jnp.float32)
    second_part = second_part.astype(jnp.bfloat16)
    feed_input, second_part = lax.optimization_barrier((activated, second_part))
    second_grad = lax.psum_scatter(
        second_part, "tensor", scatter_dimension=0, tiled=True
    ).astype(jnp.float32)
    feed_part = jnp.einsum(
        "rsf,fd->rsd", feed_input, w_out, preferred_element_type=jnp.float32
    ).astype(jnp.bfloat16)
    feed_buffer = lax.dynamic_update_slice(
        jnp.zeros(feed_part.shape[:2] + (2 * model_width,), feed_part.dtype),
        feed_part,
        (0, 0, model_width),
    )
    feed_buffer, second_grad = lax.optimization_barrier((feed_buffer, second_grad))
    norm_two_back = jax.vjp(layer_norm, middle, ln2_gain, ln2_bias)[1]
    middle_part, grad_ln2_gain, grad_ln2_bias = norm_two_back(second_grad)
    middle_grad = upstream.astype(jnp.float32) + middle_part
    branch_low = middle_grad.astype(jnp.bfloat16)
    grad_b_o = jnp.sum(branch_low, axis=(0, 1), dtype=jnp.float32)
    grad_b_out = jnp.sum(upstream, axis=(0, 1), dtype=jnp.float32)
    summed_in = halving_sum(grad_w_in * factor, 0)
    summed_out = halving_sum(grad_w_out * factor, 1)
    summed_in, summed_out, branch_low = lax.optimization_barrier(
        (summed_in, summed_out, branch_low)
    )
    piece = lax.all_gather(branch_low, "tensor", axis=0, tiled=True)
    weight_grad = jnp.einsum("rse,rsd->ed", attended, piece, preferred_element_type=jnp.float32)
    branch_rows = branch_low.reshape(row_count * seq_count, model_width)
    heads_grad = (
        jnp.dot(
            lax.dynamic_slice_in_dim(branch_rows, core * half_width, half_width, 1),
            out_mine.T,
            preferred_element_type=jnp.float32,
        )
        + jnp.dot(
            lax.dynamic_slice_in_dim(branch_rows, (1 - core) * half_width, half_width, 1),
            out_other.T,
            preferred_element_type=jnp.float32,
        )
    ).astype(jnp.bfloat16)
    attended_grad = lax.all_to_all(heads_grad, "tensor", 1, 0, tiled=True).reshape(
        seq_total, seq_count, local_width
    )
    backward_items = [
        attention_backward(
            item(query, s, h),
            item(keys, s, h),
            item(values, s, h),
            item(attended_grad, s, h),
            lse,
            seq_lengths[s : s + 1],
        )
        for (s, h), (_, lse) in zip(pairs, forward_items)
    ]
    joint_grad = jnp.stack(
        [per_row([grads[kind] for grads in backward_items]) for kind in range(3)], axis=2
    )
    grad_b_qv = jnp.sum(joint_grad[:, :, 0::2], axis=(0, 1), dtype=jnp.float32)
    joint_rows = joint_grad.reshape(seq_total, seq_count, 3 * local_width)
    grad_w_qkv = jnp.einsum(
        "rd,rc->dc",
        normed_full.reshape(seq_total * seq_count, model_width),
        joint_rows.reshape(seq_total * seq_count, 3 * local_width),
        preferred_element_type=jnp.float32,
    )
    normed_part = jnp.einsum(
        "rsc,dc->rsd", joint_rows, joint_weight, preferred_element_type=jnp.float32
    ).astype(jnp.bfloat16)
    joint_sums = jnp.sum(joint_rows, axis=(0, 1), dtype=jnp.float32)
    grad_ln1_bias = jnp.dot(
        joint_weight.astype(jnp.float32), joint_sums, precision=lax.Precision.HIGHEST
    )
    merged = lax.dynamic_update_slice(feed_buffer, normed_part, (0, 0, 0))
    both = lax.psum_scatter(merged, "tensor", scatter_dimension=0, tiled=True)
    summed = (
        halving_sum(grad_w_qkv * factor, 0).reshape(-1, 3, local_heads, head_size),
        halving_sum(weight_grad.reshape(local_heads, head_size, model_width) * factor, 2),
        summed_in,
        summed_out,
    )
    in_full = lax.dynamic_update_slice_in_dim(
        jnp.zeros((hidden * tensor_count,), jnp.float32), grad_b_in, tensor_rank * hidden, 0
    )
    joint_full = lax.dynamic_update_slice_in_dim(
        jnp.zeros((2, local_width * tensor_count), jnp.float32),
        grad_b_qv,
        tensor_rank * local_width,
        1,
    )
    early = reduce_vectors(
        (
            grad_ln1_bias,
            grad_b_o,
            grad_ln2_gain,
            grad_ln2_bias,
            grad_b_out,
            joint_full[0],
            joint_full[1],
            in_full,
        ),
        factor,
    )
    both, summed, early = lax.optimization_barrier((both, summed, early))
    both = both.astype(jnp.float32)
    normed_grad = both[:, :, :model_width]
    feed = both[:, :, model_width:] + b_out
    output = (middle + feed).astype(jnp.bfloat16)
    norm_one_back = jax.vjp(layer_norm, inputs, ln1_gain, ln1_bias)[1]
    input_part, grad_ln1_gain, _ = norm_one_back(normed_grad)
    input_grad = (middle_grad + input_part).astype(jnp.bfloat16)
    (late,) = reduce_vectors((grad_ln1_gain,), factor)
    return (
        output,
        input_grad,
        late,
        early[0],
        summed[0],
        jnp.stack((early[5], early[6])),
        summed[1],
        early[1],
        early[2],
        early[3],
        summed[2],
        early[7],
        summed[3],
        early[4],
    )


def reduce_vectors(vectors, factor):
    devices = lax.axis_size("group") * lax.axis_size("dp") * lax.axis_size("tensor")
    pieces = [(item * factor).reshape(devices, -1) for item in vectors]
    widths = [piece.shape[1] for piece in pieces]
    packed = jnp.concatenate(pieces, 1)
    packed = lax.all_to_all(packed, ("group", "dp", "tensor"), 0, 0, tiled=True)
    flat = jnp.sum(packed, axis=0)
    parts = []
    offset = 0
    for width in widths:
        parts.append(flat[offset : offset + width])
        offset += width
    return tuple(parts)


def half_columns(mine, other, core):
    return jnp.where(
        core == 0, jnp.concatenate([mine, other], 1), jnp.concatenate([other, mine], 1)
    )


def halving_steps(value, dim, steps, send_type=None):
    for axis, size, bit in steps:
        half = value.shape[dim] // 2
        low_half = lax.slice_in_dim(value, 0, half, axis=dim)
        high_half = lax.slice_in_dim(value, half, 2 * half, axis=dim)
        upper = (lax.axis_index(axis) // bit) % 2 == 1
        keep = jnp.where(upper, high_half, low_half)
        send = jnp.where(upper, low_half, high_half)
        if send_type is not None:
            send = send.astype(send_type)
        got = lax.ppermute(send, axis, [(i, i ^ bit) for i in range(size)])
        value = keep + got.astype(keep.dtype)
    return value


def halving_sum(value, dim):
    shape = value.shape
    groups = lax.axis_size("group")
    dps = lax.axis_size("dp")
    rest = shape[dim] // (groups * dps)
    value = value.reshape(shape[:dim] + (groups // 2, 2, dps * rest) + shape[dim + 1 :])
    value = jnp.swapaxes(value, dim, dim + 1)
    value = value.reshape(shape[:dim] + (groups * dps, rest) + shape[dim + 1 :])
    value = halving_steps(
        value, dim, [("group", groups, 1), ("group", groups, 2), ("dp", dps, 1)], jnp.bfloat16
    )
    return value.reshape(shape[:dim] + (shape[dim] // (groups * dps),) + shape[dim + 1 :])


def solution(mesh):
    in_specs = (
        P("tensor", ("group", "dp"), None),
        P("tensor", ("group", "dp"), None),
        P(),
        P(),
        P(),
        P(None, None, "tensor", None),
        P(None, "tensor"),
        P("tensor", None, None),
        P(),
        P(),
        P(),
        P(None, "tensor"),
        P("tensor"),
        P("tensor", None),
        P(),
    )
    out_specs = (
        P("tensor", ("group", "dp"), None),
        P("tensor", ("group", "dp"), None),
        P(("group", "dp", "tensor")),
        P(("group", "dp", "tensor")),
        P(("group", "dp"), None, "tensor", None),
        P(None, ("group", "dp", "tensor")),
        P("tensor", None, ("group", "dp")),
        P(("group", "dp", "tensor")),
        P(("group", "dp", "tensor")),
        P(("group", "dp", "tensor")),
        P(("group", "dp"), "tensor"),
        P(("group", "dp", "tensor")),
        P("tensor", ("group", "dp")),
        P(("group", "dp", "tensor")),
    )
    return jax.shard_map(shards, mesh=mesh, in_specs=in_specs, out_specs=out_specs, check_vma=False)
```

```python
from functools import partial
import math

import jax
import jax.numpy as jnp
from jax import lax
from jax.experimental import pallas as pl
from jax.experimental.pallas import tpu as pltpu
from jax.sharding import PartitionSpec as P

EPS = 1e-05
NEGATIVE = -1e30


def layer_norm(value, gain, shift):
    mean = jnp.mean(value, axis=-1, keepdims=True)
    centred = value - mean
    spread = jnp.mean(centred * centred, axis=-1, keepdims=True)
    return centred * lax.rsqrt(spread + EPS) * gain + shift


def gelu_tanh(value):
    return jax.nn.gelu(value, approximate=True)


def _valid(first_q, first_k, rows, cols, length):
    q_pos = first_q + lax.broadcasted_iota(jnp.int32, (rows, cols), 0)
    k_pos = first_k + lax.broadcasted_iota(jnp.int32, (rows, cols), 1)
    return (k_pos <= q_pos) & (k_pos < length)


def _key_blocks(i, block_q, block_k, length):
    causal = (i * block_q + block_q + block_k - 1) // block_k
    live = (length + block_k - 1) // block_k
    return jnp.minimum(causal, live)


def _attn_fwd_kernel(len_ref, q_ref, k_ref, v_ref, o_ref, lse_ref, s_buf, *, block_q, block_k, scale):
    i = pl.program_id(0)
    length = len_ref[0]
    count = _key_blocks(i, block_q, block_k, length)
    q = q_ref[...]

    def scores(j, m):
        first = pl.multiple_of(j * block_k, block_k)
        k = k_ref[pl.ds(first, block_k), :]
        s = lax.dot_general(q, k, (((1,), (1,)), ((), ())), preferred_element_type=jnp.float32) * scale
        edge = (first + block_k > i * block_q) | (first + block_k > length)
        s = lax.cond(
            edge,
            lambda v: jnp.where(_valid(i * block_q, first, block_q, block_k, length), v, NEGATIVE),
            lambda v: v,
            s,
        )
        s_buf[:, pl.ds(first, block_k)] = s
        return jnp.maximum(m, jnp.max(s, axis=1, keepdims=True))

    peak = lax.fori_loop(0, count, scores, jnp.full((block_q, 1), NEGATIVE, jnp.float32))

    def exps(j, total):
        first = pl.multiple_of(j * block_k, block_k)
        e = jnp.exp(s_buf[:, pl.ds(first, block_k)] - peak)
        s_buf[:, pl.ds(first, block_k)] = e
        return total + jnp.sum(e, axis=1, keepdims=True)

    total = lax.fori_loop(0, count, exps, jnp.zeros((block_q, 1), jnp.float32))

    inverse = 1.0 / total

    def mix(j, acc):
        first = pl.multiple_of(j * block_k, block_k)
        probs = (s_buf[:, pl.ds(first, block_k)] * inverse).astype(jnp.bfloat16)
        return acc + jnp.dot(probs, v_ref[pl.ds(first, block_k), :], preferred_element_type=jnp.float32)

    acc = lax.fori_loop(0, count, mix, jnp.zeros(o_ref.shape, jnp.float32))
    o_ref[...] = acc.astype(o_ref.dtype)
    lse_ref[...] = peak + jnp.log(total)


def attention_forward(q, k, v, length, *, block_q=512, block_k=512):
    n, d = q.shape
    scale = 1.0 / math.sqrt(d)
    kernel = partial(_attn_fwd_kernel, block_q=block_q, block_k=block_k, scale=scale)
    pairs = (n // block_q) * (n // block_k + 1) // 2
    return pl.pallas_call(
        kernel,
        out_shape=(jax.ShapeDtypeStruct((n, d), jnp.bfloat16), jax.ShapeDtypeStruct((n, 1), jnp.float32)),
        grid_spec=pltpu.PrefetchScalarGridSpec(
            num_scalar_prefetch=1,
            grid=(n // block_q,),
            in_specs=[
                pl.BlockSpec((block_q, d), lambda i, lens: (i, 0)),
                pl.BlockSpec((n, d), lambda i, lens: (0, 0)),
                pl.BlockSpec((n, d), lambda i, lens: (0, 0)),
            ],
            out_specs=[
                pl.BlockSpec((block_q, d), lambda i, lens: (i, 0)),
                pl.BlockSpec((block_q, 1), lambda i, lens: (i, 0)),
            ],
            scratch_shapes=[pltpu.VMEM((block_q, n), jnp.float32)],
        ),
        compiler_params=pltpu.CompilerParams(dimension_semantics=("arbitrary",)),
        cost_estimate=pl.CostEstimate(
            flops=4 * pairs * block_q * block_k * d,
            transcendentals=pairs * block_q * block_k,
            bytes_accessed=4 * n * d * 2,
        ),
    )(length, q, k, v)


def _attn_bwd_kernel(len_ref, q_ref, k_ref, v_ref, do_ref, lse_ref, dq_ref, dk_ref, dv_ref,
                     p_buf, dp_buf, dk_acc, dv_acc, *, block_q, block_k, scale):
    i = pl.program_id(0)
    length = len_ref[0]

    @pl.when(i == 0)
    def _():
        dk_acc[...] = jnp.zeros_like(dk_acc)
        dv_acc[...] = jnp.zeros_like(dv_acc)

    live = i * block_q < length

    @pl.when(live)
    def _():
        count = _key_blocks(i, block_q, block_k, length)
        q = q_ref[...]
        do = do_ref[...]
        lse = lse_ref[...]

        def first_pass(j, inner):
            first = pl.multiple_of(j * block_k, block_k)
            k = k_ref[pl.ds(first, block_k), :]
            v = v_ref[pl.ds(first, block_k), :]
            s = lax.dot_general(q, k, (((1,), (1,)), ((), ())), preferred_element_type=jnp.float32)
            edge = (first + block_k > i * block_q) | (first + block_k > length)
            p = lax.cond(
                edge,
                lambda v: jnp.where(
                    _valid(i * block_q, first, block_q, block_k, length),
                    jnp.exp(jnp.where(_valid(i * block_q, first, block_q, block_k, length), v, NEGATIVE) - lse),
                    0.0,
                ),
                lambda v: jnp.exp(v - lse),
                s * scale,
            )
            dp = lax.dot_general(do, v, (((1,), (1,)), ((), ())), preferred_element_type=jnp.float32)
            p_buf[:, pl.ds(first, block_k)] = p
            dp_buf[:, pl.ds(first, block_k)] = dp
            return inner + jnp.sum(p * dp, axis=1, keepdims=True)

        inner = lax.fori_loop(0, count, first_pass, jnp.zeros((block_q, 1), jnp.float32))

        def second_pass(j, dq):
            first = pl.multiple_of(j * block_k, block_k)
            p = p_buf[:, pl.ds(first, block_k)]
            dp = dp_buf[:, pl.ds(first, block_k)]
            ds = (p * (dp - inner)).astype(jnp.bfloat16)
            k = k_ref[pl.ds(first, block_k), :]
            dk_acc[pl.ds(first, block_k), :] += lax.dot_general(
                ds, q, (((0,), (0,)), ((), ())), preferred_element_type=jnp.float32)
            dv_acc[pl.ds(first, block_k), :] += lax.dot_general(
                p.astype(jnp.bfloat16), do, (((0,), (0,)), ((), ())), preferred_element_type=jnp.float32)
            return dq + jnp.dot(ds, k, preferred_element_type=jnp.float32)

        dq = lax.fori_loop(0, count, second_pass, jnp.zeros(dq_ref.shape, jnp.float32))
        dq_ref[...] = (dq * scale).astype(dq_ref.dtype)

    @pl.when(jnp.logical_not(live))
    def _():
        dq_ref[...] = jnp.zeros_like(dq_ref)

    @pl.when(i == pl.num_programs(0) - 1)
    def _():
        dk_ref[...] = (dk_acc[...] * scale).astype(dk_ref.dtype)
        dv_ref[...] = dv_acc[...].astype(dv_ref.dtype)


def attention_backward(q, k, v, do, lse, length, *, block_q=512, block_k=512):
    n, d = q.shape
    scale = 1.0 / math.sqrt(d)
    kernel = partial(_attn_bwd_kernel, block_q=block_q, block_k=block_k, scale=scale)
    pairs = (n // block_q) * (n // block_k + 1) // 2
    full = pl.BlockSpec((n, d), lambda i, lens: (0, 0))
    rows = pl.BlockSpec((block_q, d), lambda i, lens: (i, 0))
    return pl.pallas_call(
        kernel,
        out_shape=tuple(jax.ShapeDtypeStruct((n, d), jnp.bfloat16) for _ in range(3)),
        grid_spec=pltpu.PrefetchScalarGridSpec(
            num_scalar_prefetch=1,
            grid=(n // block_q,),
            in_specs=[rows, full, full, rows, pl.BlockSpec((block_q, 1), lambda i, lens: (i, 0))],
            out_specs=[rows, full, full],
            scratch_shapes=[
                pltpu.VMEM((block_q, n), jnp.float32),
                pltpu.VMEM((block_q, n), jnp.float32),
                pltpu.VMEM((n, d), jnp.float32),
                pltpu.VMEM((n, d), jnp.float32),
            ],
        ),
        compiler_params=pltpu.CompilerParams(dimension_semantics=("arbitrary",)),
        cost_estimate=pl.CostEstimate(
            flops=8 * pairs * block_q * block_k * d,
            transcendentals=pairs * block_q * block_k,
            bytes_accessed=8 * n * d * 2,
        ),
    )(length, q, k, v, do, lse)


def shards(
    tokens,
    cotangent,
    lengths,
    ln1_gain,
    ln1_bias,
    w_qkv,
    b_qv,
    w_o,
    b_o,
    ln2_gain,
    ln2_bias,
    w_in,
    b_in,
    w_out,
    b_out,
):
    row_count, seq_count, model_width = tokens.shape
    tensor_count = lax.axis_size("tensor")
    tensor_rank = lax.axis_index("tensor")
    seq_total = row_count * tensor_count
    local_heads = w_qkv.shape[2]
    head_size = w_qkv.shape[3]
    local_width = local_heads * head_size
    hidden = w_in.shape[1]
    group_count = lax.axis_size("group")
    group_rank = lax.axis_index("group")
    member = group_rank * lax.axis_size("dp") + lax.axis_index("dp")
    seq_lengths = lax.dynamic_slice_in_dim(lengths, member * seq_count, seq_count, 0)
    group_totals = jnp.sum(lengths.reshape(group_count, -1), axis=1).astype(jnp.float32)
    factor = (
        group_count
        * lax.dynamic_index_in_dim(group_totals, group_rank, 0, keepdims=False)
        / jnp.sum(group_totals)
    )
    inputs = tokens.astype(jnp.float32)
    normed_low = layer_norm(inputs, ln1_gain, ln1_bias).astype(jnp.bfloat16)
    positions = tensor_rank * row_count + jnp.arange(row_count, dtype=jnp.int32)
    live = positions[:, None] < seq_lengths[None, :]
    upstream = jnp.where(live[:, :, None], cotangent, jnp.zeros_like(cotangent))
    core = group_rank % 2
    half_width = model_width // 2
    front = jnp.concatenate(
        [
            normed_low.reshape(row_count, seq_count * model_width),
            lax.dynamic_slice_in_dim(w_o.reshape(row_count, -1), core * half_width, half_width, 1),
        ],
        1,
    )
    front = lax.all_gather(front, "tensor", axis=0, tiled=True)
    wide = seq_count * model_width
    normed_full = front[:, :wide].reshape(seq_total, seq_count, model_width)
    out_mine = front[:, wide:]
    out_other = lax.ppermute(out_mine, "group", [(g, g ^ 1) for g in range(group_count)])
    upstream, front = lax.optimization_barrier((upstream, front))
    upstream_full = lax.all_gather(upstream, "tensor", axis=0, tiled=True)
    joint_weight = w_qkv.reshape(model_width, 3 * local_width)
    projected = jnp.dot(
        normed_full.reshape(seq_total * seq_count, model_width),
        joint_weight,
        preferred_element_type=jnp.float32,
    )
    projected = projected.reshape(seq_total, seq_count, 3, local_width)
    query = (projected[:, :, 0] + b_qv[0]).astype(jnp.bfloat16)
    keys = projected[:, :, 1].astype(jnp.bfloat16)
    values = (projected[:, :, 2] + b_qv[1]).astype(jnp.bfloat16)

    def item(array, s, h):
        return array[:, s, h * head_size : (h + 1) * head_size]

    def per_row(items):
        stacked = jnp.stack(items).reshape(seq_count, local_heads, seq_total, head_size)
        return jnp.transpose(stacked, (2, 0, 1, 3)).reshape(seq_total, seq_count, local_width)

    pairs = [(s, h) for s in range(seq_count) for h in range(local_heads)]
    forward_items = [
        attention_forward(
            item(query, s, h), item(keys, s, h), item(values, s, h), seq_lengths[s : s + 1]
        )
        for s, h in pairs
    ]
    attended = per_row([o for o, _ in forward_items])
    out_weight = w_o.reshape(local_width, model_width)
    own_rows = lax.all_to_all(
        jnp.transpose(attended, (1, 0, 2)).reshape(seq_count * seq_total, local_width),
        "tensor",
        0,
        1,
        tiled=True,
    )
    attention = (
        half_columns(
            jnp.dot(own_rows, out_mine, preferred_element_type=jnp.float32),
            jnp.dot(own_rows, out_other, preferred_element_type=jnp.float32),
            core,
        ).reshape(
            seq_count, row_count, model_width
        )
    )
    attention = jnp.transpose(attention, (1, 0, 2)) + b_o
    middle = inputs + attention
    act_grad = jnp.einsum("rsd,fd->rsf", upstream_full, w_out, preferred_element_type=jnp.float32)
    second_low = layer_norm(middle, ln2_gain, ln2_bias).astype(jnp.bfloat16)
    second_low, upstream_full = lax.optimization_barrier((second_low, upstream_full))
    second_full = lax.all_gather(second_low, "tensor", axis=0, tiled=True)
    second_full, act_grad = lax.optimization_barrier((second_full, act_grad))
    pre_act = (
        jnp.dot(
            second_full.reshape(seq_total * seq_count, model_width),
            w_in,
            preferred_element_type=jnp.float32,
        )
        + b_in
    )
    activated = gelu_tanh(pre_act).astype(jnp.bfloat16).reshape(seq_total, seq_count, hidden)
    piece = upstream_full
    grad_w_out = jnp.einsum("rsf,rsd->fd", activated, piece, preferred_element_type=jnp.float32)
    gelu_back = jax.vjp(gelu_tanh, pre_act)[1]
    pre_low = gelu_back(act_grad.reshape(seq_total * seq_count, hidden))[0].astype(jnp.bfloat16)
    grad_b_in = jnp.sum(pre_low, axis=0, dtype=jnp.float32)
    grad_w_in = jnp.einsum(
        "rd,rf->df",
        second_full.reshape(seq_total * seq_count, model_width),
        pre_low,
        preferred_element_type=jnp.float32,
    )
    pre_rows = pre_low.reshape(seq_total, seq_count, hidden)
    piece = pre_rows
    second_part = jnp.einsum("rsf,df->rsd", piece, w_in, preferred_element_type=jnp.float32)
    second_part = second_part.astype(jnp.bfloat16)
    feed_input, second_part = lax.optimization_barrier((activated, second_part))
    second_grad = lax.psum_scatter(
        second_part, "tensor", scatter_dimension=0, tiled=True
    ).astype(jnp.float32)
    feed_part = jnp.einsum(
        "rsf,fd->rsd", feed_input, w_out, preferred_element_type=jnp.float32
    ).astype(jnp.bfloat16)
    feed_buffer = lax.dynamic_update_slice(
        jnp.zeros(feed_part.shape[:2] + (2 * model_width,), feed_part.dtype),
        feed_part,
        (0, 0, model_width),
    )
    feed_buffer, second_grad = lax.optimization_barrier((feed_buffer, second_grad))
    norm_two_back = jax.vjp(layer_norm, middle, ln2_gain, ln2_bias)[1]
    middle_part, grad_ln2_gain, grad_ln2_bias = norm_two_back(second_grad)
    middle_grad = upstream.astype(jnp.float32) + middle_part
    branch_low = middle_grad.astype(jnp.bfloat16)
    grad_b_o = jnp.sum(branch_low, axis=(0, 1), dtype=jnp.float32)
    grad_b_out = jnp.sum(upstream, axis=(0, 1), dtype=jnp.float32)
    summed_in = halving_sum(grad_w_in * factor, 0)
    summed_out = halving_sum(grad_w_out * factor, 1)
    summed_in, summed_out, branch_low = lax.optimization_barrier(
        (summed_in, summed_out, branch_low)
    )
    piece = lax.all_gather(branch_low, "tensor", axis=0, tiled=True)
    weight_grad = jnp.einsum("rse,rsd->ed", attended, piece, preferred_element_type=jnp.float32)
    branch_rows = branch_low.reshape(row_count * seq_count, model_width)
    heads_grad = (
        jnp.dot(
            lax.dynamic_slice_in_dim(branch_rows, core * half_width, half_width, 1),
            out_mine.T,
            preferred_element_type=jnp.float32,
        )
        + jnp.dot(
            lax.dynamic_slice_in_dim(branch_rows, (1 - core) * half_width, half_width, 1),
            out_other.T,
            preferred_element_type=jnp.float32,
        )
    ).astype(jnp.bfloat16)
    attended_grad = lax.all_to_all(heads_grad, "tensor", 1, 0, tiled=True).reshape(
        seq_total, seq_count, local_width
    )
    backward_items = [
        attention_backward(
            item(query, s, h),
            item(keys, s, h),
            item(values, s, h),
            item(attended_grad, s, h),
            lse,
            seq_lengths[s : s + 1],
        )
        for (s, h), (_, lse) in zip(pairs, forward_items)
    ]
    joint_grad = jnp.stack(
        [per_row([grads[kind] for grads in backward_items]) for kind in range(3)], axis=2
    )
    grad_b_qv = jnp.sum(joint_grad[:, :, 0::2], axis=(0, 1), dtype=jnp.float32)
    joint_rows = joint_grad.reshape(seq_total, seq_count, 3 * local_width)
    grad_w_qkv = jnp.einsum(
        "rd,rc->dc",
        normed_full.reshape(seq_total * seq_count, model_width),
        joint_rows.reshape(seq_total * seq_count, 3 * local_width),
        preferred_element_type=jnp.float32,
    )
    normed_part = jnp.einsum(
        "rsc,dc->rsd", joint_rows, joint_weight, preferred_element_type=jnp.float32
    ).astype(jnp.bfloat16)
    joint_sums = jnp.sum(joint_rows, axis=(0, 1), dtype=jnp.float32)
    grad_ln1_bias = jnp.dot(
        joint_weight.astype(jnp.float32), joint_sums, precision=lax.Precision.HIGHEST
    )
    merged = lax.dynamic_update_slice(feed_buffer, normed_part, (0, 0, 0))
    both = lax.psum_scatter(merged, "tensor", scatter_dimension=0, tiled=True)
    summed = (
        halving_sum(grad_w_qkv * factor, 0).reshape(-1, 3, local_heads, head_size),
        halving_sum(weight_grad.reshape(local_heads, head_size, model_width) * factor, 2),
        summed_in,
        summed_out,
    )
    in_full = lax.dynamic_update_slice_in_dim(
        jnp.zeros((hidden * tensor_count,), jnp.float32), grad_b_in, tensor_rank * hidden, 0
    )
    joint_full = lax.dynamic_update_slice_in_dim(
        jnp.zeros((2, local_width * tensor_count), jnp.float32),
        grad_b_qv,
        tensor_rank * local_width,
        1,
    )
    early = reduce_vectors(
        (
            grad_ln1_bias,
            grad_b_o,
            grad_ln2_gain,
            grad_ln2_bias,
            grad_b_out,
            joint_full[0],
            joint_full[1],
            in_full,
        ),
        factor,
    )
    both, summed, early = lax.optimization_barrier((both, summed, early))
    both = both.astype(jnp.float32)
    normed_grad = both[:, :, :model_width]
    feed = both[:, :, model_width:] + b_out
    output = (middle + feed).astype(jnp.bfloat16)
    norm_one_back = jax.vjp(layer_norm, inputs, ln1_gain, ln1_bias)[1]
    input_part, grad_ln1_gain, _ = norm_one_back(normed_grad)
    input_grad = (middle_grad + input_part).astype(jnp.bfloat16)
    (late,) = reduce_vectors((grad_ln1_gain,), factor)
    return (
        output,
        input_grad,
        late,
        early[0],
        summed[0],
        jnp.stack((early[5], early[6])),
        summed[1],
        early[1],
        early[2],
        early[3],
        summed[2],
        early[7],
        summed[3],
        early[4],
    )


def reduce_vectors(vectors, factor):
    devices = lax.axis_size("group") * lax.axis_size("dp") * lax.axis_size("tensor")
    pieces = [(item * factor).reshape(devices, -1) for item in vectors]
    widths = [piece.shape[1] for piece in pieces]
    packed = jnp.concatenate(pieces, 1)
    packed = lax.all_to_all(packed, ("group", "dp", "tensor"), 0, 0, tiled=True)
    flat = jnp.sum(packed, axis=0)
    parts = []
    offset = 0
    for width in widths:
        parts.append(flat[offset : offset + width])
        offset += width
    return tuple(parts)


def half_columns(mine, other, core):
    return jnp.where(
        core == 0, jnp.concatenate([mine, other], 1), jnp.concatenate([other, mine], 1)
    )


def halving_steps(value, dim, steps, send_type=None):
    for axis, size, bit in steps:
        half = value.shape[dim] // 2
        low_half = lax.slice_in_dim(value, 0, half, axis=dim)
        high_half = lax.slice_in_dim(value, half, 2 * half, axis=dim)
        upper = (lax.axis_index(axis) // bit) % 2 == 1
        keep = jnp.where(upper, high_half, low_half)
        send = jnp.where(upper, low_half, high_half)
        if send_type is not None:
            send = send.astype(send_type)
        got = lax.ppermute(send, axis, [(i, i ^ bit) for i in range(size)])
        value = keep + got.astype(keep.dtype)
    return value


def halving_sum(value, dim):
    shape = value.shape
    groups = lax.axis_size("group")
    dps = lax.axis_size("dp")
    rest = shape[dim] // (groups * dps)
    value = value.reshape(shape[:dim] + (groups * dps, rest) + shape[dim + 1 :])
    value = halving_steps(
        value, dim, [("group", groups, 2), ("group", groups, 1), ("dp", dps, 1)], jnp.bfloat16
    )
    return value.reshape(shape[:dim] + (shape[dim] // (groups * dps),) + shape[dim + 1 :])


def solution(mesh):
    in_specs = (
        P("tensor", ("group", "dp"), None),
        P("tensor", ("group", "dp"), None),
        P(),
        P(),
        P(),
        P(None, None, "tensor", None),
        P(None, "tensor"),
        P("tensor", None, None),
        P(),
        P(),
        P(),
        P(None, "tensor"),
        P("tensor"),
        P("tensor", None),
        P(),
    )
    out_specs = (
        P("tensor", ("group", "dp"), None),
        P("tensor", ("group", "dp"), None),
        P(("group", "dp", "tensor")),
        P(("group", "dp", "tensor")),
        P(("group", "dp"), None, "tensor", None),
        P(None, ("group", "dp", "tensor")),
        P("tensor", None, ("group", "dp")),
        P(("group", "dp", "tensor")),
        P(("group", "dp", "tensor")),
        P(("group", "dp", "tensor")),
        P(("group", "dp"), "tensor"),
        P(("group", "dp", "tensor")),
        P("tensor", ("group", "dp")),
        P(("group", "dp", "tensor")),
    )
    return jax.shard_map(shards, mesh=mesh, in_specs=in_specs, out_specs=out_specs, check_vma=False)
```

```python
from functools import partial
import math

import jax
import jax.numpy as jnp
from jax import lax
from jax.experimental import pallas as pl
from jax.experimental.pallas import tpu as pltpu
from jax.sharding import PartitionSpec as P

EPS = 1e-05
NEGATIVE = -1e30


def layer_norm(value, gain, shift):
    mean = jnp.mean(value, axis=-1, keepdims=True)
    centred = value - mean
    spread = jnp.mean(centred * centred, axis=-1, keepdims=True)
    return centred * lax.rsqrt(spread + EPS) * gain + shift


def gelu_tanh(value):
    return jax.nn.gelu(value, approximate=True)


def _valid(first_q, first_k, rows, cols, length):
    q_pos = first_q + lax.broadcasted_iota(jnp.int32, (rows, cols), 0)
    k_pos = first_k + lax.broadcasted_iota(jnp.int32, (rows, cols), 1)
    return (k_pos <= q_pos) & (k_pos < length)


def _key_blocks(i, block_q, block_k, length):
    causal = (i * block_q + block_q + block_k - 1) // block_k
    live = (length + block_k - 1) // block_k
    return jnp.minimum(causal, live)


def _attn_fwd_kernel(len_ref, q_ref, k_ref, v_ref, o_ref, lse_ref, s_buf, *, block_q, block_k, scale):
    i = pl.program_id(0)
    length = len_ref[0]
    count = _key_blocks(i, block_q, block_k, length)
    q = q_ref[...]

    def scores(j, m):
        first = pl.multiple_of(j * block_k, block_k)
        k = k_ref[pl.ds(first, block_k), :]
        s = lax.dot_general(q, k, (((1,), (1,)), ((), ())), preferred_element_type=jnp.float32) * scale
        edge = (first + block_k > i * block_q) | (first + block_k > length)
        s = lax.cond(
            edge,
            lambda v: jnp.where(_valid(i * block_q, first, block_q, block_k, length), v, NEGATIVE),
            lambda v: v,
            s,
        )
        s_buf[:, pl.ds(first, block_k)] = s
        return jnp.maximum(m, jnp.max(s, axis=1, keepdims=True))

    peak = lax.fori_loop(0, count, scores, jnp.full((block_q, 1), NEGATIVE, jnp.float32))

    def exps(j, total):
        first = pl.multiple_of(j * block_k, block_k)
        e = jnp.exp(s_buf[:, pl.ds(first, block_k)] - peak)
        s_buf[:, pl.ds(first, block_k)] = e
        return total + jnp.sum(e, axis=1, keepdims=True)

    total = lax.fori_loop(0, count, exps, jnp.zeros((block_q, 1), jnp.float32))

    inverse = 1.0 / total

    def mix(j, acc):
        first = pl.multiple_of(j * block_k, block_k)
        probs = (s_buf[:, pl.ds(first, block_k)] * inverse).astype(jnp.bfloat16)
        return acc + jnp.dot(probs, v_ref[pl.ds(first, block_k), :], preferred_element_type=jnp.float32)

    acc = lax.fori_loop(0, count, mix, jnp.zeros(o_ref.shape, jnp.float32))
    o_ref[...] = acc.astype(o_ref.dtype)
    lse_ref[...] = peak + jnp.log(total)


def attention_forward(q, k, v, length, *, block_q=512, block_k=512):
    n, d = q.shape
    scale = 1.0 / math.sqrt(d)
    kernel = partial(_attn_fwd_kernel, block_q=block_q, block_k=block_k, scale=scale)
    pairs = (n // block_q) * (n // block_k + 1) // 2
    return pl.pallas_call(
        kernel,
        out_shape=(jax.ShapeDtypeStruct((n, d), jnp.bfloat16), jax.ShapeDtypeStruct((n, 1), jnp.float32)),
        grid_spec=pltpu.PrefetchScalarGridSpec(
            num_scalar_prefetch=1,
            grid=(n // block_q,),
            in_specs=[
                pl.BlockSpec((block_q, d), lambda i, lens: (i, 0)),
                pl.BlockSpec((n, d), lambda i, lens: (0, 0)),
                pl.BlockSpec((n, d), lambda i, lens: (0, 0)),
            ],
            out_specs=[
                pl.BlockSpec((block_q, d), lambda i, lens: (i, 0)),
                pl.BlockSpec((block_q, 1), lambda i, lens: (i, 0)),
            ],
            scratch_shapes=[pltpu.VMEM((block_q, n), jnp.float32)],
        ),
        compiler_params=pltpu.CompilerParams(dimension_semantics=("arbitrary",)),
        cost_estimate=pl.CostEstimate(
            flops=4 * pairs * block_q * block_k * d,
            transcendentals=pairs * block_q * block_k,
            bytes_accessed=4 * n * d * 2,
        ),
    )(length, q, k, v)


def _attn_bwd_kernel(len_ref, q_ref, k_ref, v_ref, do_ref, lse_ref, dq_ref, dk_ref, dv_ref,
                     p_buf, dp_buf, dk_acc, dv_acc, *, block_q, block_k, scale):
    i = pl.program_id(0)
    length = len_ref[0]

    @pl.when(i == 0)
    def _():
        dk_acc[...] = jnp.zeros_like(dk_acc)
        dv_acc[...] = jnp.zeros_like(dv_acc)

    live = i * block_q < length

    @pl.when(live)
    def _():
        count = _key_blocks(i, block_q, block_k, length)
        q = q_ref[...]
        do = do_ref[...]
        lse = lse_ref[...]

        def first_pass(j, inner):
            first = pl.multiple_of(j * block_k, block_k)
            k = k_ref[pl.ds(first, block_k), :]
            v = v_ref[pl.ds(first, block_k), :]
            s = lax.dot_general(q, k, (((1,), (1,)), ((), ())), preferred_element_type=jnp.float32)
            edge = (first + block_k > i * block_q) | (first + block_k > length)
            p = lax.cond(
                edge,
                lambda v: jnp.where(
                    _valid(i * block_q, first, block_q, block_k, length),
                    jnp.exp(jnp.where(_valid(i * block_q, first, block_q, block_k, length), v, NEGATIVE) - lse),
                    0.0,
                ),
                lambda v: jnp.exp(v - lse),
                s * scale,
            )
            dp = lax.dot_general(do, v, (((1,), (1,)), ((), ())), preferred_element_type=jnp.float32)
            p_buf[:, pl.ds(first, block_k)] = p
            dp_buf[:, pl.ds(first, block_k)] = dp
            return inner + jnp.sum(p * dp, axis=1, keepdims=True)

        inner = lax.fori_loop(0, count, first_pass, jnp.zeros((block_q, 1), jnp.float32))

        def second_pass(j, dq):
            first = pl.multiple_of(j * block_k, block_k)
            p = p_buf[:, pl.ds(first, block_k)]
            dp = dp_buf[:, pl.ds(first, block_k)]
            ds = (p * (dp - inner)).astype(jnp.bfloat16)
            k = k_ref[pl.ds(first, block_k), :]
            dk_acc[pl.ds(first, block_k), :] += lax.dot_general(
                ds, q, (((0,), (0,)), ((), ())), preferred_element_type=jnp.float32)
            dv_acc[pl.ds(first, block_k), :] += lax.dot_general(
                p.astype(jnp.bfloat16), do, (((0,), (0,)), ((), ())), preferred_element_type=jnp.float32)
            return dq + jnp.dot(ds, k, preferred_element_type=jnp.float32)

        dq = lax.fori_loop(0, count, second_pass, jnp.zeros(dq_ref.shape, jnp.float32))
        dq_ref[...] = (dq * scale).astype(dq_ref.dtype)

    @pl.when(jnp.logical_not(live))
    def _():
        dq_ref[...] = jnp.zeros_like(dq_ref)

    @pl.when(i == pl.num_programs(0) - 1)
    def _():
        dk_ref[...] = (dk_acc[...] * scale).astype(dk_ref.dtype)
        dv_ref[...] = dv_acc[...].astype(dv_ref.dtype)


def attention_backward(q, k, v, do, lse, length, *, block_q=512, block_k=512):
    n, d = q.shape
    scale = 1.0 / math.sqrt(d)
    kernel = partial(_attn_bwd_kernel, block_q=block_q, block_k=block_k, scale=scale)
    pairs = (n // block_q) * (n // block_k + 1) // 2
    full = pl.BlockSpec((n, d), lambda i, lens: (0, 0))
    rows = pl.BlockSpec((block_q, d), lambda i, lens: (i, 0))
    return pl.pallas_call(
        kernel,
        out_shape=tuple(jax.ShapeDtypeStruct((n, d), jnp.bfloat16) for _ in range(3)),
        grid_spec=pltpu.PrefetchScalarGridSpec(
            num_scalar_prefetch=1,
            grid=(n // block_q,),
            in_specs=[rows, full, full, rows, pl.BlockSpec((block_q, 1), lambda i, lens: (i, 0))],
            out_specs=[rows, full, full],
            scratch_shapes=[
                pltpu.VMEM((block_q, n), jnp.float32),
                pltpu.VMEM((block_q, n), jnp.float32),
                pltpu.VMEM((n, d), jnp.float32),
                pltpu.VMEM((n, d), jnp.float32),
            ],
        ),
        compiler_params=pltpu.CompilerParams(dimension_semantics=("arbitrary",)),
        cost_estimate=pl.CostEstimate(
            flops=8 * pairs * block_q * block_k * d,
            transcendentals=pairs * block_q * block_k,
            bytes_accessed=8 * n * d * 2,
        ),
    )(length, q, k, v, do, lse)


def shards(
    tokens,
    cotangent,
    lengths,
    ln1_gain,
    ln1_bias,
    w_qkv,
    b_qv,
    w_o,
    b_o,
    ln2_gain,
    ln2_bias,
    w_in,
    b_in,
    w_out,
    b_out,
):
    row_count, seq_count, model_width = tokens.shape
    tensor_count = lax.axis_size("tensor")
    tensor_rank = lax.axis_index("tensor")
    seq_total = row_count * tensor_count
    local_heads = w_qkv.shape[2]
    head_size = w_qkv.shape[3]
    local_width = local_heads * head_size
    hidden = w_in.shape[1]
    group_count = lax.axis_size("group")
    group_rank = lax.axis_index("group")
    member = group_rank * lax.axis_size("dp") + lax.axis_index("dp")
    seq_lengths = lax.dynamic_slice_in_dim(lengths, member * seq_count, seq_count, 0)
    group_totals = jnp.sum(lengths.reshape(group_count, -1), axis=1).astype(jnp.float32)
    factor = (
        group_count
        * lax.dynamic_index_in_dim(group_totals, group_rank, 0, keepdims=False)
        / jnp.sum(group_totals)
    )
    inputs = tokens.astype(jnp.float32)
    normed_low = layer_norm(inputs, ln1_gain, ln1_bias).astype(jnp.bfloat16)
    positions = tensor_rank * row_count + jnp.arange(row_count, dtype=jnp.int32)
    live = positions[:, None] < seq_lengths[None, :]
    upstream = jnp.where(live[:, :, None], cotangent, jnp.zeros_like(cotangent))
    core = group_rank % 2
    half_width = model_width // 2
    front = jnp.concatenate(
        [
            normed_low.reshape(row_count, seq_count * model_width),
            lax.dynamic_slice_in_dim(w_o.reshape(row_count, -1), core * half_width, half_width, 1),
        ],
        1,
    )
    front = lax.all_gather(front, "tensor", axis=0, tiled=True)
    wide = seq_count * model_width
    normed_full = front[:, :wide].reshape(seq_total, seq_count, model_width)
    out_mine = front[:, wide:]
    out_other = lax.ppermute(out_mine, "group", [(g, g ^ 1) for g in range(group_count)])
    upstream, front = lax.optimization_barrier((upstream, front))
    upstream_full = lax.all_gather(upstream, "tensor", axis=0, tiled=True)
    joint_weight = w_qkv.reshape(model_width, 3 * local_width)
    projected = jnp.dot(
        normed_full.reshape(seq_total * seq_count, model_width),
        joint_weight,
        preferred_element_type=jnp.float32,
    )
    projected = projected.reshape(seq_total, seq_count, 3, local_width)
    query = (projected[:, :, 0] + b_qv[0]).astype(jnp.bfloat16)
    keys = projected[:, :, 1].astype(jnp.bfloat16)
    values = (projected[:, :, 2] + b_qv[1]).astype(jnp.bfloat16)

    def item(array, s, h):
        return array[:, s, h * head_size : (h + 1) * head_size]

    def per_row(items):
        stacked = jnp.stack(items).reshape(seq_count, local_heads, seq_total, head_size)
        return jnp.transpose(stacked, (2, 0, 1, 3)).reshape(seq_total, seq_count, local_width)

    pairs = [(s, h) for s in range(seq_count) for h in range(local_heads)]
    forward_items = [
        attention_forward(
            item(query, s, h), item(keys, s, h), item(values, s, h), seq_lengths[s : s + 1]
        )
        for s, h in pairs
    ]
    attended = per_row([o for o, _ in forward_items])
    out_weight = w_o.reshape(local_width, model_width)
    own_rows = lax.all_to_all(
        jnp.transpose(attended, (1, 0, 2)).reshape(seq_count * seq_total, local_width),
        "tensor",
        0,
        1,
        tiled=True,
    )
    attention = (
        half_columns(
            jnp.dot(own_rows, out_mine, preferred_element_type=jnp.float32),
            jnp.dot(own_rows, out_other, preferred_element_type=jnp.float32),
            core,
        ).reshape(
            seq_count, row_count, model_width
        )
    )
    attention = jnp.transpose(attention, (1, 0, 2)) + b_o
    middle = inputs + attention
    act_grad = jnp.einsum("rsd,fd->rsf", upstream_full, w_out, preferred_element_type=jnp.float32)
    second_low = layer_norm(middle, ln2_gain, ln2_bias).astype(jnp.bfloat16)
    second_low, upstream_full = lax.optimization_barrier((second_low, upstream_full))
    second_full = lax.all_gather(second_low, "tensor", axis=0, tiled=True)
    second_full, act_grad = lax.optimization_barrier((second_full, act_grad))
    pre_act = (
        jnp.dot(
            second_full.reshape(seq_total * seq_count, model_width),
            w_in,
            preferred_element_type=jnp.float32,
        )
        + b_in
    )
    activated = gelu_tanh(pre_act).astype(jnp.bfloat16).reshape(seq_total, seq_count, hidden)
    piece = upstream_full
    grad_w_out = jnp.einsum("rsf,rsd->fd", activated, piece, preferred_element_type=jnp.float32)
    gelu_back = jax.vjp(gelu_tanh, pre_act)[1]
    pre_low = gelu_back(act_grad.reshape(seq_total * seq_count, hidden))[0].astype(jnp.bfloat16)
    grad_b_in = jnp.sum(pre_low, axis=0, dtype=jnp.float32)
    grad_w_in = jnp.einsum(
        "rd,rf->df",
        second_full.reshape(seq_total * seq_count, model_width),
        pre_low,
        preferred_element_type=jnp.float32,
    )
    pre_rows = pre_low.reshape(seq_total, seq_count, hidden)
    piece = pre_rows
    second_part = jnp.einsum("rsf,df->rsd", piece, w_in, preferred_element_type=jnp.float32)
    second_part = second_part.astype(jnp.bfloat16)
    feed_input, second_part = lax.optimization_barrier((activated, second_part))
    second_grad = lax.psum_scatter(
        second_part, "tensor", scatter_dimension=0, tiled=True
    ).astype(jnp.float32)
    padded_out = jnp.concatenate([jnp.zeros_like(w_out), w_out], 1)
    feed_buffer = jnp.einsum(
        "rsf,fd->rsd", feed_input, padded_out, preferred_element_type=jnp.float32
    ).astype(jnp.bfloat16)
    feed_buffer, second_grad = lax.optimization_barrier((feed_buffer, second_grad))
    norm_two_back = jax.vjp(layer_norm, middle, ln2_gain, ln2_bias)[1]
    middle_part, grad_ln2_gain, grad_ln2_bias = norm_two_back(second_grad)
    middle_grad = upstream.astype(jnp.float32) + middle_part
    branch_low = middle_grad.astype(jnp.bfloat16)
    grad_b_o = jnp.sum(branch_low, axis=(0, 1), dtype=jnp.float32)
    grad_b_out = jnp.sum(upstream, axis=(0, 1), dtype=jnp.float32)
    summed_in = halving_sum(grad_w_in * factor, 0)
    summed_out = halving_sum(grad_w_out * factor, 1)
    summed_in, summed_out, branch_low = lax.optimization_barrier(
        (summed_in, summed_out, branch_low)
    )
    piece = lax.all_gather(branch_low, "tensor", axis=0, tiled=True)
    weight_grad = jnp.einsum("rse,rsd->ed", attended, piece, preferred_element_type=jnp.float32)
    branch_rows = branch_low.reshape(row_count * seq_count, model_width)
    heads_grad = (
        jnp.dot(
            lax.dynamic_slice_in_dim(branch_rows, core * half_width, half_width, 1),
            out_mine.T,
            preferred_element_type=jnp.float32,
        )
        + jnp.dot(
            lax.dynamic_slice_in_dim(branch_rows, (1 - core) * half_width, half_width, 1),
            out_other.T,
            preferred_element_type=jnp.float32,
        )
    ).astype(jnp.bfloat16)
    attended_grad = lax.all_to_all(heads_grad, "tensor", 1, 0, tiled=True).reshape(
        seq_total, seq_count, local_width
    )
    backward_items = [
        attention_backward(
            item(query, s, h),
            item(keys, s, h),
            item(values, s, h),
            item(attended_grad, s, h),
            lse,
            seq_lengths[s : s + 1],
        )
        for (s, h), (_, lse) in zip(pairs, forward_items)
    ]
    joint_grad = jnp.stack(
        [per_row([grads[kind] for grads in backward_items]) for kind in range(3)], axis=2
    )
    grad_b_qv = jnp.sum(joint_grad[:, :, 0::2], axis=(0, 1), dtype=jnp.float32)
    joint_rows = joint_grad.reshape(seq_total, seq_count, 3 * local_width)
    grad_w_qkv = jnp.einsum(
        "rd,rc->dc",
        normed_full.reshape(seq_total * seq_count, model_width),
        joint_rows.reshape(seq_total * seq_count, 3 * local_width),
        preferred_element_type=jnp.float32,
    )
    normed_part = jnp.einsum(
        "rsc,dc->rsd", joint_rows, joint_weight, preferred_element_type=jnp.float32
    ).astype(jnp.bfloat16)
    joint_sums = jnp.sum(joint_rows, axis=(0, 1), dtype=jnp.float32)
    grad_ln1_bias = jnp.dot(
        joint_weight.astype(jnp.float32), joint_sums, precision=lax.Precision.HIGHEST
    )
    merged = lax.dynamic_update_slice(feed_buffer, normed_part, (0, 0, 0))
    both = lax.psum_scatter(merged, "tensor", scatter_dimension=0, tiled=True)
    summed = (
        halving_sum(grad_w_qkv * factor, 0).reshape(-1, 3, local_heads, head_size),
        halving_sum(weight_grad.reshape(local_heads, head_size, model_width) * factor, 2),
        summed_in,
        summed_out,
    )
    in_full = lax.dynamic_update_slice_in_dim(
        jnp.zeros((hidden * tensor_count,), jnp.float32), grad_b_in, tensor_rank * hidden, 0
    )
    joint_full = lax.dynamic_update_slice_in_dim(
        jnp.zeros((2, local_width * tensor_count), jnp.float32),
        grad_b_qv,
        tensor_rank * local_width,
        1,
    )
    early = reduce_vectors(
        (
            grad_ln1_bias,
            grad_b_o,
            grad_ln2_gain,
            grad_ln2_bias,
            grad_b_out,
            joint_full[0],
            joint_full[1],
            in_full,
        ),
        factor,
    )
    both, summed, early = lax.optimization_barrier((both, summed, early))
    both = both.astype(jnp.float32)
    normed_grad = both[:, :, :model_width]
    feed = both[:, :, model_width:] + b_out
    output = (middle + feed).astype(jnp.bfloat16)
    norm_one_back = jax.vjp(layer_norm, inputs, ln1_gain, ln1_bias)[1]
    input_part, grad_ln1_gain, _ = norm_one_back(normed_grad)
    input_grad = (middle_grad + input_part).astype(jnp.bfloat16)
    (late,) = reduce_vectors((grad_ln1_gain,), factor)
    return (
        output,
        input_grad,
        late,
        early[0],
        summed[0],
        jnp.stack((early[5], early[6])),
        summed[1],
        early[1],
        early[2],
        early[3],
        summed[2],
        early[7],
        summed[3],
        early[4],
    )


def reduce_vectors(vectors, factor):
    devices = lax.axis_size("group") * lax.axis_size("dp") * lax.axis_size("tensor")
    pieces = [(item * factor).reshape(devices, -1) for item in vectors]
    widths = [piece.shape[1] for piece in pieces]
    packed = jnp.concatenate(pieces, 1)
    packed = lax.all_to_all(packed, ("group", "dp", "tensor"), 0, 0, tiled=True)
    flat = jnp.sum(packed, axis=0)
    parts = []
    offset = 0
    for width in widths:
        parts.append(flat[offset : offset + width])
        offset += width
    return tuple(parts)


def half_columns(mine, other, core):
    return jnp.where(
        core == 0, jnp.concatenate([mine, other], 1), jnp.concatenate([other, mine], 1)
    )


def halving_steps(value, dim, steps, send_type=None):
    for axis, size, bit in steps:
        half = value.shape[dim] // 2
        low_half = lax.slice_in_dim(value, 0, half, axis=dim)
        high_half = lax.slice_in_dim(value, half, 2 * half, axis=dim)
        upper = (lax.axis_index(axis) // bit) % 2 == 1
        keep = jnp.where(upper, high_half, low_half)
        send = jnp.where(upper, low_half, high_half)
        if send_type is not None:
            send = send.astype(send_type)
        got = lax.ppermute(send, axis, [(i, i ^ bit) for i in range(size)])
        value = keep + got.astype(keep.dtype)
    return value


def halving_sum(value, dim):
    shape = value.shape
    groups = lax.axis_size("group")
    dps = lax.axis_size("dp")
    rest = shape[dim] // (groups * dps)
    value = value.reshape(shape[:dim] + (groups // 2, 2, dps * rest) + shape[dim + 1 :])
    value = jnp.swapaxes(value, dim, dim + 1)
    value = value.reshape(shape[:dim] + (groups * dps, rest) + shape[dim + 1 :])
    value = halving_steps(
        value, dim, [("group", groups, 1), ("group", groups, 2), ("dp", dps, 1)], jnp.bfloat16
    )
    return value.reshape(shape[:dim] + (shape[dim] // (groups * dps),) + shape[dim + 1 :])


def solution(mesh):
    in_specs = (
        P("tensor", ("group", "dp"), None),
        P("tensor", ("group", "dp"), None),
        P(),
        P(),
        P(),
        P(None, None, "tensor", None),
        P(None, "tensor"),
        P("tensor", None, None),
        P(),
        P(),
        P(),
        P(None, "tensor"),
        P("tensor"),
        P("tensor", None),
        P(),
    )
    out_specs = (
        P("tensor", ("group", "dp"), None),
        P("tensor", ("group", "dp"), None),
        P(("group", "dp", "tensor")),
        P(("group", "dp", "tensor")),
        P(("group", "dp"), None, "tensor", None),
        P(None, ("group", "dp", "tensor")),
        P("tensor", None, ("group", "dp")),
        P(("group", "dp", "tensor")),
        P(("group", "dp", "tensor")),
        P(("group", "dp", "tensor")),
        P(("group", "dp"), "tensor"),
        P(("group", "dp", "tensor")),
        P("tensor", ("group", "dp")),
        P(("group", "dp", "tensor")),
    )
    return jax.shard_map(shards, mesh=mesh, in_specs=in_specs, out_specs=out_specs, check_vma=False)
```

```python
from functools import partial
import math

import jax
import jax.numpy as jnp
from jax import lax
from jax.experimental import pallas as pl
from jax.experimental.pallas import tpu as pltpu
from jax.sharding import PartitionSpec as P

EPS = 1e-05
NEGATIVE = -1e30


def layer_norm(value, gain, shift):
    mean = jnp.mean(value, axis=-1, keepdims=True)
    centred = value - mean
    spread = jnp.mean(centred * centred, axis=-1, keepdims=True)
    return centred * lax.rsqrt(spread + EPS) * gain + shift


def gelu_tanh(value):
    return jax.nn.gelu(value, approximate=True)


def _valid(first_q, first_k, rows, cols, length):
    q_pos = first_q + lax.broadcasted_iota(jnp.int32, (rows, cols), 0)
    k_pos = first_k + lax.broadcasted_iota(jnp.int32, (rows, cols), 1)
    return (k_pos <= q_pos) & (k_pos < length)


def _key_blocks(i, block_q, block_k, length):
    causal = (i * block_q + block_q + block_k - 1) // block_k
    live = (length + block_k - 1) // block_k
    return jnp.minimum(causal, live)


def _attn_fwd_kernel(len_ref, q_ref, k_ref, v_ref, o_ref, lse_ref, s_buf, *, block_q, block_k, scale):
    i = pl.program_id(0)
    length = len_ref[0]
    count = _key_blocks(i, block_q, block_k, length)
    q = q_ref[...]

    def scores(j, m):
        first = pl.multiple_of(j * block_k, block_k)
        k = k_ref[pl.ds(first, block_k), :]
        s = lax.dot_general(q, k, (((1,), (1,)), ((), ())), preferred_element_type=jnp.float32) * scale
        edge = (first + block_k > i * block_q) | (first + block_k > length)
        s = lax.cond(
            edge,
            lambda v: jnp.where(_valid(i * block_q, first, block_q, block_k, length), v, NEGATIVE),
            lambda v: v,
            s,
        )
        s_buf[:, pl.ds(first, block_k)] = s
        return jnp.maximum(m, jnp.max(s, axis=1, keepdims=True))

    peak = lax.fori_loop(0, count, scores, jnp.full((block_q, 1), NEGATIVE, jnp.float32))

    def exps(j, total):
        first = pl.multiple_of(j * block_k, block_k)
        e = jnp.exp(s_buf[:, pl.ds(first, block_k)] - peak)
        s_buf[:, pl.ds(first, block_k)] = e
        return total + jnp.sum(e, axis=1, keepdims=True)

    total = lax.fori_loop(0, count, exps, jnp.zeros((block_q, 1), jnp.float32))

    inverse = 1.0 / total

    def mix(j, acc):
        first = pl.multiple_of(j * block_k, block_k)
        probs = (s_buf[:, pl.ds(first, block_k)] * inverse).astype(jnp.bfloat16)
        return acc + jnp.dot(probs, v_ref[pl.ds(first, block_k), :], preferred_element_type=jnp.float32)

    acc = lax.fori_loop(0, count, mix, jnp.zeros(o_ref.shape, jnp.float32))
    o_ref[...] = acc.astype(o_ref.dtype)
    lse_ref[...] = peak + jnp.log(total)


def attention_forward(q, k, v, length, *, block_q=512, block_k=512):
    n, d = q.shape
    scale = 1.0 / math.sqrt(d)
    kernel = partial(_attn_fwd_kernel, block_q=block_q, block_k=block_k, scale=scale)
    pairs = (n // block_q) * (n // block_k + 1) // 2
    return pl.pallas_call(
        kernel,
        out_shape=(jax.ShapeDtypeStruct((n, d), jnp.bfloat16), jax.ShapeDtypeStruct((n, 1), jnp.float32)),
        grid_spec=pltpu.PrefetchScalarGridSpec(
            num_scalar_prefetch=1,
            grid=(n // block_q,),
            in_specs=[
                pl.BlockSpec((block_q, d), lambda i, lens: (i, 0)),
                pl.BlockSpec((n, d), lambda i, lens: (0, 0)),
                pl.BlockSpec((n, d), lambda i, lens: (0, 0)),
            ],
            out_specs=[
                pl.BlockSpec((block_q, d), lambda i, lens: (i, 0)),
                pl.BlockSpec((block_q, 1), lambda i, lens: (i, 0)),
            ],
            scratch_shapes=[pltpu.VMEM((block_q, n), jnp.float32)],
        ),
        compiler_params=pltpu.CompilerParams(dimension_semantics=("arbitrary",)),
        cost_estimate=pl.CostEstimate(
            flops=4 * pairs * block_q * block_k * d,
            transcendentals=pairs * block_q * block_k,
            bytes_accessed=4 * n * d * 2,
        ),
    )(length, q, k, v)


def _attn_bwd_kernel(len_ref, q_ref, k_ref, v_ref, do_ref, lse_ref, dq_ref, dk_ref, dv_ref,
                     p_buf, dp_buf, dk_acc, dv_acc, *, block_q, block_k, scale):
    i = pl.program_id(0)
    length = len_ref[0]

    @pl.when(i == 0)
    def _():
        dk_acc[...] = jnp.zeros_like(dk_acc)
        dv_acc[...] = jnp.zeros_like(dv_acc)

    live = i * block_q < length

    @pl.when(live)
    def _():
        count = _key_blocks(i, block_q, block_k, length)
        q = q_ref[...]
        do = do_ref[...]
        lse = lse_ref[...]

        def first_pass(j, inner):
            first = pl.multiple_of(j * block_k, block_k)
            k = k_ref[pl.ds(first, block_k), :]
            v = v_ref[pl.ds(first, block_k), :]
            s = lax.dot_general(q, k, (((1,), (1,)), ((), ())), preferred_element_type=jnp.float32)
            edge = (first + block_k > i * block_q) | (first + block_k > length)
            p = lax.cond(
                edge,
                lambda v: jnp.where(
                    _valid(i * block_q, first, block_q, block_k, length),
                    jnp.exp(jnp.where(_valid(i * block_q, first, block_q, block_k, length), v, NEGATIVE) - lse),
                    0.0,
                ),
                lambda v: jnp.exp(v - lse),
                s * scale,
            )
            dp = lax.dot_general(do, v, (((1,), (1,)), ((), ())), preferred_element_type=jnp.float32)
            p_buf[:, pl.ds(first, block_k)] = p
            dp_buf[:, pl.ds(first, block_k)] = dp
            return inner + jnp.sum(p * dp, axis=1, keepdims=True)

        inner = lax.fori_loop(0, count, first_pass, jnp.zeros((block_q, 1), jnp.float32))

        def second_pass(j, dq):
            first = pl.multiple_of(j * block_k, block_k)
            p = p_buf[:, pl.ds(first, block_k)]
            dp = dp_buf[:, pl.ds(first, block_k)]
            ds = (p * (dp - inner)).astype(jnp.bfloat16)
            k = k_ref[pl.ds(first, block_k), :]
            dk_acc[pl.ds(first, block_k), :] += lax.dot_general(
                ds, q, (((0,), (0,)), ((), ())), preferred_element_type=jnp.float32)
            dv_acc[pl.ds(first, block_k), :] += lax.dot_general(
                p.astype(jnp.bfloat16), do, (((0,), (0,)), ((), ())), preferred_element_type=jnp.float32)
            return dq + jnp.dot(ds, k, preferred_element_type=jnp.float32)

        dq = lax.fori_loop(0, count, second_pass, jnp.zeros(dq_ref.shape, jnp.float32))
        dq_ref[...] = (dq * scale).astype(dq_ref.dtype)

    @pl.when(jnp.logical_not(live))
    def _():
        dq_ref[...] = jnp.zeros_like(dq_ref)

    @pl.when(i == pl.num_programs(0) - 1)
    def _():
        dk_ref[...] = (dk_acc[...] * scale).astype(dk_ref.dtype)
        dv_ref[...] = dv_acc[...].astype(dv_ref.dtype)


def attention_backward(q, k, v, do, lse, length, *, block_q=512, block_k=512):
    n, d = q.shape
    scale = 1.0 / math.sqrt(d)
    kernel = partial(_attn_bwd_kernel, block_q=block_q, block_k=block_k, scale=scale)
    pairs = (n // block_q) * (n // block_k + 1) // 2
    full = pl.BlockSpec((n, d), lambda i, lens: (0, 0))
    rows = pl.BlockSpec((block_q, d), lambda i, lens: (i, 0))
    return pl.pallas_call(
        kernel,
        out_shape=tuple(jax.ShapeDtypeStruct((n, d), jnp.bfloat16) for _ in range(3)),
        grid_spec=pltpu.PrefetchScalarGridSpec(
            num_scalar_prefetch=1,
            grid=(n // block_q,),
            in_specs=[rows, full, full, rows, pl.BlockSpec((block_q, 1), lambda i, lens: (i, 0))],
            out_specs=[rows, full, full],
            scratch_shapes=[
                pltpu.VMEM((block_q, n), jnp.float32),
                pltpu.VMEM((block_q, n), jnp.float32),
                pltpu.VMEM((n, d), jnp.float32),
                pltpu.VMEM((n, d), jnp.float32),
            ],
        ),
        compiler_params=pltpu.CompilerParams(dimension_semantics=("arbitrary",)),
        cost_estimate=pl.CostEstimate(
            flops=8 * pairs * block_q * block_k * d,
            transcendentals=pairs * block_q * block_k,
            bytes_accessed=8 * n * d * 2,
        ),
    )(length, q, k, v, do, lse)


def shards(
    tokens,
    cotangent,
    lengths,
    ln1_gain,
    ln1_bias,
    w_qkv,
    b_qv,
    w_o,
    b_o,
    ln2_gain,
    ln2_bias,
    w_in,
    b_in,
    w_out,
    b_out,
):
    row_count, seq_count, model_width = tokens.shape
    tensor_count = lax.axis_size("tensor")
    tensor_rank = lax.axis_index("tensor")
    seq_total = row_count * tensor_count
    local_heads = w_qkv.shape[2]
    head_size = w_qkv.shape[3]
    local_width = local_heads * head_size
    hidden = w_in.shape[1]
    group_count = lax.axis_size("group")
    group_rank = lax.axis_index("group")
    member = group_rank * lax.axis_size("dp") + lax.axis_index("dp")
    seq_lengths = lax.dynamic_slice_in_dim(lengths, member * seq_count, seq_count, 0)
    group_totals = jnp.sum(lengths.reshape(group_count, -1), axis=1).astype(jnp.float32)
    factor = (
        group_count
        * lax.dynamic_index_in_dim(group_totals, group_rank, 0, keepdims=False)
        / jnp.sum(group_totals)
    )
    inputs = tokens.astype(jnp.float32)
    normed_low = layer_norm(inputs, ln1_gain, ln1_bias).astype(jnp.bfloat16)
    positions = tensor_rank * row_count + jnp.arange(row_count, dtype=jnp.int32)
    live = positions[:, None] < seq_lengths[None, :]
    upstream = jnp.where(live[:, :, None], cotangent, jnp.zeros_like(cotangent))
    quarter = model_width // group_count
    front = jnp.concatenate(
        [
            normed_low.reshape(row_count, seq_count * model_width),
            lax.dynamic_slice_in_dim(w_o.reshape(row_count, -1), group_rank * quarter, quarter, 1),
        ],
        1,
    )
    front = lax.all_gather(front, "tensor", axis=0, tiled=True)
    wide = seq_count * model_width
    normed_full = front[:, :wide].reshape(seq_total, seq_count, model_width)
    out_mine = front[:, wide:]
    out_pair = lax.ppermute(out_mine, "group", [(g, g ^ 2) for g in range(group_count)])
    out_both = jnp.concatenate([out_mine, out_pair], 1)
    out_rest = lax.ppermute(out_both, "group", [(g, g ^ 1) for g in range(group_count)])
    quarter_ids = (group_rank, group_rank ^ 2, group_rank ^ 1, group_rank ^ 3)
    quarter_cols = (
        out_mine,
        out_pair,
        out_rest[:, :quarter],
        out_rest[:, quarter:],
    )
    upstream, front = lax.optimization_barrier((upstream, front))
    upstream_full = lax.all_gather(upstream, "tensor", axis=0, tiled=True)
    joint_weight = w_qkv.reshape(model_width, 3 * local_width)
    projected = jnp.dot(
        normed_full.reshape(seq_total * seq_count, model_width),
        joint_weight,
        preferred_element_type=jnp.float32,
    )
    projected = projected.reshape(seq_total, seq_count, 3, local_width)
    query = (projected[:, :, 0] + b_qv[0]).astype(jnp.bfloat16)
    keys = projected[:, :, 1].astype(jnp.bfloat16)
    values = (projected[:, :, 2] + b_qv[1]).astype(jnp.bfloat16)

    def item(array, s, h):
        return array[:, s, h * head_size : (h + 1) * head_size]

    def per_row(items):
        stacked = jnp.stack(items).reshape(seq_count, local_heads, seq_total, head_size)
        return jnp.transpose(stacked, (2, 0, 1, 3)).reshape(seq_total, seq_count, local_width)

    pairs = [(s, h) for s in range(seq_count) for h in range(local_heads)]
    forward_items = [
        attention_forward(
            item(query, s, h), item(keys, s, h), item(values, s, h), seq_lengths[s : s + 1]
        )
        for s, h in pairs
    ]
    attended = per_row([o for o, _ in forward_items])
    out_weight = w_o.reshape(local_width, model_width)
    own_rows = lax.all_to_all(
        jnp.transpose(attended, (1, 0, 2)).reshape(seq_count * seq_total, local_width),
        "tensor",
        0,
        1,
        tiled=True,
    )
    attention = (
        place_columns(
            [jnp.dot(own_rows, cols, preferred_element_type=jnp.float32) for cols in quarter_cols],
            quarter_ids,
            quarter,
        ).reshape(
            seq_count, row_count, model_width
        )
    )
    attention = jnp.transpose(attention, (1, 0, 2)) + b_o
    middle = inputs + attention
    act_grad = jnp.einsum("rsd,fd->rsf", upstream_full, w_out, preferred_element_type=jnp.float32)
    second_low = layer_norm(middle, ln2_gain, ln2_bias).astype(jnp.bfloat16)
    second_low, upstream_full = lax.optimization_barrier((second_low, upstream_full))
    second_full = lax.all_gather(second_low, "tensor", axis=0, tiled=True)
    second_full, act_grad = lax.optimization_barrier((second_full, act_grad))
    pre_act = (
        jnp.dot(
            second_full.reshape(seq_total * seq_count, model_width),
            w_in,
            preferred_element_type=jnp.float32,
        )
        + b_in
    )
    activated = gelu_tanh(pre_act).astype(jnp.bfloat16).reshape(seq_total, seq_count, hidden)
    piece = upstream_full
    grad_w_out = jnp.einsum("rsf,rsd->fd", activated, piece, preferred_element_type=jnp.float32)
    gelu_back = jax.vjp(gelu_tanh, pre_act)[1]
    pre_low = gelu_back(act_grad.reshape(seq_total * seq_count, hidden))[0].astype(jnp.bfloat16)
    grad_b_in = jnp.sum(pre_low, axis=0, dtype=jnp.float32)
    grad_w_in = jnp.einsum(
        "rd,rf->df",
        second_full.reshape(seq_total * seq_count, model_width),
        pre_low,
        preferred_element_type=jnp.float32,
    )
    pre_rows = pre_low.reshape(seq_total, seq_count, hidden)
    piece = pre_rows
    second_part = jnp.einsum("rsf,df->rsd", piece, w_in, preferred_element_type=jnp.float32)
    second_part = second_part.astype(jnp.bfloat16)
    feed_input, second_part = lax.optimization_barrier((activated, second_part))
    second_grad = lax.psum_scatter(
        second_part, "tensor", scatter_dimension=0, tiled=True
    ).astype(jnp.float32)
    feed_part = jnp.einsum(
        "rsf,fd->rsd", feed_input, w_out, preferred_element_type=jnp.float32
    ).astype(jnp.bfloat16)
    feed_buffer = lax.dynamic_update_slice(
        jnp.zeros(feed_part.shape[:2] + (2 * model_width,), feed_part.dtype),
        feed_part,
        (0, 0, model_width),
    )
    feed_buffer, second_grad = lax.optimization_barrier((feed_buffer, second_grad))
    norm_two_back = jax.vjp(layer_norm, middle, ln2_gain, ln2_bias)[1]
    middle_part, grad_ln2_gain, grad_ln2_bias = norm_two_back(second_grad)
    middle_grad = upstream.astype(jnp.float32) + middle_part
    branch_low = middle_grad.astype(jnp.bfloat16)
    grad_b_o = jnp.sum(branch_low, axis=(0, 1), dtype=jnp.float32)
    grad_b_out = jnp.sum(upstream, axis=(0, 1), dtype=jnp.float32)
    summed_in = halving_sum(grad_w_in * factor, 0)
    summed_out = halving_sum(grad_w_out * factor, 1)
    summed_in, summed_out, branch_low = lax.optimization_barrier(
        (summed_in, summed_out, branch_low)
    )
    piece = lax.all_gather(branch_low, "tensor", axis=0, tiled=True)
    weight_grad = jnp.einsum("rse,rsd->ed", attended, piece, preferred_element_type=jnp.float32)
    branch_rows = branch_low.reshape(row_count * seq_count, model_width)
    heads_grad = sum(
        jnp.dot(
            lax.dynamic_slice_in_dim(branch_rows, qid * quarter, quarter, 1),
            cols.T,
            preferred_element_type=jnp.float32,
        )
        for qid, cols in zip(quarter_ids, quarter_cols)
    ).astype(jnp.bfloat16)
    attended_grad = lax.all_to_all(heads_grad, "tensor", 1, 0, tiled=True).reshape(
        seq_total, seq_count, local_width
    )
    backward_items = [
        attention_backward(
            item(query, s, h),
            item(keys, s, h),
            item(values, s, h),
            item(attended_grad, s, h),
            lse,
            seq_lengths[s : s + 1],
        )
        for (s, h), (_, lse) in zip(pairs, forward_items)
    ]
    joint_grad = jnp.stack(
        [per_row([grads[kind] for grads in backward_items]) for kind in range(3)], axis=2
    )
    grad_b_qv = jnp.sum(joint_grad[:, :, 0::2], axis=(0, 1), dtype=jnp.float32)
    joint_rows = joint_grad.reshape(seq_total, seq_count, 3 * local_width)
    grad_w_qkv = jnp.einsum(
        "rd,rc->dc",
        normed_full.reshape(seq_total * seq_count, model_width),
        joint_rows.reshape(seq_total * seq_count, 3 * local_width),
        preferred_element_type=jnp.float32,
    )
    normed_part = jnp.einsum(
        "rsc,dc->rsd", joint_rows, joint_weight, preferred_element_type=jnp.float32
    ).astype(jnp.bfloat16)
    joint_sums = jnp.sum(joint_rows, axis=(0, 1), dtype=jnp.float32)
    grad_ln1_bias = jnp.dot(
        joint_weight.astype(jnp.float32), joint_sums, precision=lax.Precision.HIGHEST
    )
    merged = lax.dynamic_update_slice(feed_buffer, normed_part, (0, 0, 0))
    both = lax.psum_scatter(merged, "tensor", scatter_dimension=0, tiled=True)
    summed = (
        halving_sum(grad_w_qkv * factor, 0).reshape(-1, 3, local_heads, head_size),
        halving_sum(weight_grad.reshape(local_heads, head_size, model_width) * factor, 2),
        summed_in,
        summed_out,
    )
    in_full = lax.dynamic_update_slice_in_dim(
        jnp.zeros((hidden * tensor_count,), jnp.float32), grad_b_in, tensor_rank * hidden, 0
    )
    joint_full = lax.dynamic_update_slice_in_dim(
        jnp.zeros((2, local_width * tensor_count), jnp.float32),
        grad_b_qv,
        tensor_rank * local_width,
        1,
    )
    early = reduce_vectors(
        (
            grad_ln1_bias,
            grad_b_o,
            grad_ln2_gain,
            grad_ln2_bias,
            grad_b_out,
            joint_full[0],
            joint_full[1],
            in_full,
        ),
        factor,
    )
    both, summed, early = lax.optimization_barrier((both, summed, early))
    both = both.astype(jnp.float32)
    normed_grad = both[:, :, :model_width]
    feed = both[:, :, model_width:] + b_out
    output = (middle + feed).astype(jnp.bfloat16)
    norm_one_back = jax.vjp(layer_norm, inputs, ln1_gain, ln1_bias)[1]
    input_part, grad_ln1_gain, _ = norm_one_back(normed_grad)
    input_grad = (middle_grad + input_part).astype(jnp.bfloat16)
    (late,) = reduce_vectors((grad_ln1_gain,), factor)
    return (
        output,
        input_grad,
        late,
        early[0],
        summed[0],
        jnp.stack((early[5], early[6])),
        summed[1],
        early[1],
        early[2],
        early[3],
        summed[2],
        early[7],
        summed[3],
        early[4],
    )


def reduce_vectors(vectors, factor):
    devices = lax.axis_size("group") * lax.axis_size("dp") * lax.axis_size("tensor")
    pieces = [(item * factor).reshape(devices, -1) for item in vectors]
    widths = [piece.shape[1] for piece in pieces]
    packed = jnp.concatenate(pieces, 1)
    packed = lax.all_to_all(packed, ("group", "dp", "tensor"), 0, 0, tiled=True)
    flat = jnp.sum(packed, axis=0)
    parts = []
    offset = 0
    for width in widths:
        parts.append(flat[offset : offset + width])
        offset += width
    return tuple(parts)


def place_columns(blocks, ids, width):
    out = jnp.zeros(blocks[0].shape[:-1] + (width * len(blocks),), blocks[0].dtype)
    for block, index in zip(blocks, ids):
        out = lax.dynamic_update_slice_in_dim(out, block, index * width, out.ndim - 1)
    return out


def half_columns(mine, other, core):
    return jnp.where(
        core == 0, jnp.concatenate([mine, other], 1), jnp.concatenate([other, mine], 1)
    )


def halving_steps(value, dim, steps, send_type=None):
    for axis, size, bit in steps:
        half = value.shape[dim] // 2
        low_half = lax.slice_in_dim(value, 0, half, axis=dim)
        high_half = lax.slice_in_dim(value, half, 2 * half, axis=dim)
        upper = (lax.axis_index(axis) // bit) % 2 == 1
        keep = jnp.where(upper, high_half, low_half)
        send = jnp.where(upper, low_half, high_half)
        if send_type is not None:
            send = send.astype(send_type)
        got = lax.ppermute(send, axis, [(i, i ^ bit) for i in range(size)])
        value = keep + got.astype(keep.dtype)
    return value


def halving_sum(value, dim):
    shape = value.shape
    groups = lax.axis_size("group")
    dps = lax.axis_size("dp")
    rest = shape[dim] // (groups * dps)
    value = value.reshape(shape[:dim] + (groups // 2, 2, dps * rest) + shape[dim + 1 :])
    value = jnp.swapaxes(value, dim, dim + 1)
    value = value.reshape(shape[:dim] + (groups * dps, rest) + shape[dim + 1 :])
    value = halving_steps(
        value, dim, [("group", groups, 1), ("group", groups, 2), ("dp", dps, 1)], jnp.bfloat16
    )
    return value.reshape(shape[:dim] + (shape[dim] // (groups * dps),) + shape[dim + 1 :])


def solution(mesh):
    in_specs = (
        P("tensor", ("group", "dp"), None),
        P("tensor", ("group", "dp"), None),
        P(),
        P(),
        P(),
        P(None, None, "tensor", None),
        P(None, "tensor"),
        P("tensor", None, None),
        P(),
        P(),
        P(),
        P(None, "tensor"),
        P("tensor"),
        P("tensor", None),
        P(),
    )
    out_specs = (
        P("tensor", ("group", "dp"), None),
        P("tensor", ("group", "dp"), None),
        P(("group", "dp", "tensor")),
        P(("group", "dp", "tensor")),
        P(("group", "dp"), None, "tensor", None),
        P(None, ("group", "dp", "tensor")),
        P("tensor", None, ("group", "dp")),
        P(("group", "dp", "tensor")),
        P(("group", "dp", "tensor")),
        P(("group", "dp", "tensor")),
        P(("group", "dp"), "tensor"),
        P(("group", "dp", "tensor")),
        P("tensor", ("group", "dp")),
        P(("group", "dp", "tensor")),
    )
    return jax.shard_map(shards, mesh=mesh, in_specs=in_specs, out_specs=out_specs, check_vma=False)
```

```python
from functools import partial
import math

import jax
import jax.numpy as jnp
from jax import lax
from jax.experimental import pallas as pl
from jax.experimental.pallas import tpu as pltpu
from jax.sharding import PartitionSpec as P

EPS = 1e-05
NEGATIVE = -1e30


def layer_norm(value, gain, shift):
    mean = jnp.mean(value, axis=-1, keepdims=True)
    centred = value - mean
    spread = jnp.mean(centred * centred, axis=-1, keepdims=True)
    return centred * lax.rsqrt(spread + EPS) * gain + shift


def gelu_tanh(value):
    return jax.nn.gelu(value, approximate=True)


def _valid(first_q, first_k, rows, cols, length):
    q_pos = first_q + lax.broadcasted_iota(jnp.int32, (rows, cols), 0)
    k_pos = first_k + lax.broadcasted_iota(jnp.int32, (rows, cols), 1)
    return (k_pos <= q_pos) & (k_pos < length)


def _key_blocks(i, block_q, block_k, length):
    causal = (i * block_q + block_q + block_k - 1) // block_k
    live = (length + block_k - 1) // block_k
    return jnp.minimum(causal, live)


def _attn_fwd_kernel(len_ref, q_ref, k_ref, v_ref, o_ref, lse_ref, s_buf, *, block_q, block_k, scale):
    i = pl.program_id(0)
    length = len_ref[0]
    count = _key_blocks(i, block_q, block_k, length)
    q = q_ref[...]

    def scores(j, m):
        first = pl.multiple_of(j * block_k, block_k)
        k = k_ref[pl.ds(first, block_k), :]
        s = lax.dot_general(q, k, (((1,), (1,)), ((), ())), preferred_element_type=jnp.float32) * scale
        edge = (first + block_k > i * block_q) | (first + block_k > length)
        s = lax.cond(
            edge,
            lambda v: jnp.where(_valid(i * block_q, first, block_q, block_k, length), v, NEGATIVE),
            lambda v: v,
            s,
        )
        s_buf[:, pl.ds(first, block_k)] = s
        return jnp.maximum(m, jnp.max(s, axis=1, keepdims=True))

    peak = lax.fori_loop(0, count, scores, jnp.full((block_q, 1), NEGATIVE, jnp.float32))

    def exps(j, total):
        first = pl.multiple_of(j * block_k, block_k)
        e = jnp.exp(s_buf[:, pl.ds(first, block_k)] - peak)
        s_buf[:, pl.ds(first, block_k)] = e
        return total + jnp.sum(e, axis=1, keepdims=True)

    total = lax.fori_loop(0, count, exps, jnp.zeros((block_q, 1), jnp.float32))

    inverse = 1.0 / total

    def mix(j, acc):
        first = pl.multiple_of(j * block_k, block_k)
        probs = (s_buf[:, pl.ds(first, block_k)] * inverse).astype(jnp.bfloat16)
        return acc + jnp.dot(probs, v_ref[pl.ds(first, block_k), :], preferred_element_type=jnp.float32)

    acc = lax.fori_loop(0, count, mix, jnp.zeros(o_ref.shape, jnp.float32))
    o_ref[...] = acc.astype(o_ref.dtype)
    lse_ref[...] = peak + jnp.log(total)


def attention_forward(q, k, v, length, *, block_q=512, block_k=512):
    n, d = q.shape
    scale = 1.0 / math.sqrt(d)
    kernel = partial(_attn_fwd_kernel, block_q=block_q, block_k=block_k, scale=scale)
    pairs = (n // block_q) * (n // block_k + 1) // 2
    return pl.pallas_call(
        kernel,
        out_shape=(jax.ShapeDtypeStruct((n, d), jnp.bfloat16), jax.ShapeDtypeStruct((n, 1), jnp.float32)),
        grid_spec=pltpu.PrefetchScalarGridSpec(
            num_scalar_prefetch=1,
            grid=(n // block_q,),
            in_specs=[
                pl.BlockSpec((block_q, d), lambda i, lens: (i, 0)),
                pl.BlockSpec((n, d), lambda i, lens: (0, 0)),
                pl.BlockSpec((n, d), lambda i, lens: (0, 0)),
            ],
            out_specs=[
                pl.BlockSpec((block_q, d), lambda i, lens: (i, 0)),
                pl.BlockSpec((block_q, 1), lambda i, lens: (i, 0)),
            ],
            scratch_shapes=[pltpu.VMEM((block_q, n), jnp.float32)],
        ),
        compiler_params=pltpu.CompilerParams(dimension_semantics=("arbitrary",)),
        cost_estimate=pl.CostEstimate(
            flops=4 * pairs * block_q * block_k * d,
            transcendentals=pairs * block_q * block_k,
            bytes_accessed=4 * n * d * 2,
        ),
    )(length, q, k, v)


def _attn_bwd_kernel(len_ref, q_ref, k_ref, v_ref, do_ref, lse_ref, dq_ref, dk_ref, dv_ref,
                     p_buf, dp_buf, dk_acc, dv_acc, *, block_q, block_k, scale):
    i = pl.program_id(0)
    length = len_ref[0]

    @pl.when(i == 0)
    def _():
        dk_acc[...] = jnp.zeros_like(dk_acc)
        dv_acc[...] = jnp.zeros_like(dv_acc)

    live = i * block_q < length

    @pl.when(live)
    def _():
        count = _key_blocks(i, block_q, block_k, length)
        q = q_ref[...]
        do = do_ref[...]
        lse = lse_ref[...]

        def first_pass(j, inner):
            first = pl.multiple_of(j * block_k, block_k)
            k = k_ref[pl.ds(first, block_k), :]
            v = v_ref[pl.ds(first, block_k), :]
            s = lax.dot_general(q, k, (((1,), (1,)), ((), ())), preferred_element_type=jnp.float32)
            edge = (first + block_k > i * block_q) | (first + block_k > length)
            p = lax.cond(
                edge,
                lambda v: jnp.where(
                    _valid(i * block_q, first, block_q, block_k, length),
                    jnp.exp(jnp.where(_valid(i * block_q, first, block_q, block_k, length), v, NEGATIVE) - lse),
                    0.0,
                ),
                lambda v: jnp.exp(v - lse),
                s * scale,
            )
            dp = lax.dot_general(do, v, (((1,), (1,)), ((), ())), preferred_element_type=jnp.float32)
            p_buf[:, pl.ds(first, block_k)] = p
            dp_buf[:, pl.ds(first, block_k)] = dp
            return inner + jnp.sum(p * dp, axis=1, keepdims=True)

        inner = lax.fori_loop(0, count, first_pass, jnp.zeros((block_q, 1), jnp.float32))

        def second_pass(j, dq):
            first = pl.multiple_of(j * block_k, block_k)
            p = p_buf[:, pl.ds(first, block_k)]
            dp = dp_buf[:, pl.ds(first, block_k)]
            ds = (p * (dp - inner)).astype(jnp.bfloat16)
            k = k_ref[pl.ds(first, block_k), :]
            dk_acc[pl.ds(first, block_k), :] += lax.dot_general(
                ds, q, (((0,), (0,)), ((), ())), preferred_element_type=jnp.float32)
            dv_acc[pl.ds(first, block_k), :] += lax.dot_general(
                p.astype(jnp.bfloat16), do, (((0,), (0,)), ((), ())), preferred_element_type=jnp.float32)
            return dq + jnp.dot(ds, k, preferred_element_type=jnp.float32)

        dq = lax.fori_loop(0, count, second_pass, jnp.zeros(dq_ref.shape, jnp.float32))
        dq_ref[...] = (dq * scale).astype(dq_ref.dtype)

    @pl.when(jnp.logical_not(live))
    def _():
        dq_ref[...] = jnp.zeros_like(dq_ref)

    @pl.when(i == pl.num_programs(0) - 1)
    def _():
        dk_ref[...] = (dk_acc[...] * scale).astype(dk_ref.dtype)
        dv_ref[...] = dv_acc[...].astype(dv_ref.dtype)


def attention_backward(q, k, v, do, lse, length, *, block_q=512, block_k=512):
    n, d = q.shape
    scale = 1.0 / math.sqrt(d)
    kernel = partial(_attn_bwd_kernel, block_q=block_q, block_k=block_k, scale=scale)
    pairs = (n // block_q) * (n // block_k + 1) // 2
    full = pl.BlockSpec((n, d), lambda i, lens: (0, 0))
    rows = pl.BlockSpec((block_q, d), lambda i, lens: (i, 0))
    return pl.pallas_call(
        kernel,
        out_shape=tuple(jax.ShapeDtypeStruct((n, d), jnp.bfloat16) for _ in range(3)),
        grid_spec=pltpu.PrefetchScalarGridSpec(
            num_scalar_prefetch=1,
            grid=(n // block_q,),
            in_specs=[rows, full, full, rows, pl.BlockSpec((block_q, 1), lambda i, lens: (i, 0))],
            out_specs=[rows, full, full],
            scratch_shapes=[
                pltpu.VMEM((block_q, n), jnp.float32),
                pltpu.VMEM((block_q, n), jnp.float32),
                pltpu.VMEM((n, d), jnp.float32),
                pltpu.VMEM((n, d), jnp.float32),
            ],
        ),
        compiler_params=pltpu.CompilerParams(dimension_semantics=("arbitrary",)),
        cost_estimate=pl.CostEstimate(
            flops=8 * pairs * block_q * block_k * d,
            transcendentals=pairs * block_q * block_k,
            bytes_accessed=8 * n * d * 2,
        ),
    )(length, q, k, v, do, lse)


def shards(
    tokens,
    cotangent,
    lengths,
    ln1_gain,
    ln1_bias,
    w_qkv,
    b_qv,
    w_o,
    b_o,
    ln2_gain,
    ln2_bias,
    w_in,
    b_in,
    w_out,
    b_out,
):
    row_count, seq_count, model_width = tokens.shape
    tensor_count = lax.axis_size("tensor")
    tensor_rank = lax.axis_index("tensor")
    seq_total = row_count * tensor_count
    local_heads = w_qkv.shape[2]
    head_size = w_qkv.shape[3]
    local_width = local_heads * head_size
    hidden = w_in.shape[1]
    group_count = lax.axis_size("group")
    group_rank = lax.axis_index("group")
    member = group_rank * lax.axis_size("dp") + lax.axis_index("dp")
    seq_lengths = lax.dynamic_slice_in_dim(lengths, member * seq_count, seq_count, 0)
    group_totals = jnp.sum(lengths.reshape(group_count, -1), axis=1).astype(jnp.float32)
    factor = (
        group_count
        * lax.dynamic_index_in_dim(group_totals, group_rank, 0, keepdims=False)
        / jnp.sum(group_totals)
    )
    inputs = tokens.astype(jnp.float32)
    normed_low = layer_norm(inputs, ln1_gain, ln1_bias).astype(jnp.bfloat16)
    positions = tensor_rank * row_count + jnp.arange(row_count, dtype=jnp.int32)
    live = positions[:, None] < seq_lengths[None, :]
    upstream = jnp.where(live[:, :, None], cotangent, jnp.zeros_like(cotangent))
    core = group_rank % 2
    half_width = model_width // 2
    front = jnp.concatenate(
        [
            normed_low.reshape(row_count, seq_count * model_width),
            lax.dynamic_slice_in_dim(w_o.reshape(row_count, -1), core * half_width, half_width, 1),
        ],
        1,
    )
    front = lax.all_gather(front, "tensor", axis=0, tiled=True)
    wide = seq_count * model_width
    normed_full = front[:, :wide].reshape(seq_total, seq_count, model_width)
    out_mine = front[:, wide:]
    out_other = lax.ppermute(out_mine, "group", [(g, g ^ 1) for g in range(group_count)])
    upstream, front = lax.optimization_barrier((upstream, front))
    tensor_count_static = seq_total // row_count
    upstream_full = lax.all_to_all(
        jnp.broadcast_to(upstream[None], (tensor_count_static,) + upstream.shape).reshape(
            (tensor_count_static * row_count,) + upstream.shape[1:]
        ),
        "tensor",
        0,
        0,
        tiled=True,
    )
    joint_weight = w_qkv.reshape(model_width, 3 * local_width)
    projected = jnp.dot(
        normed_full.reshape(seq_total * seq_count, model_width),
        joint_weight,
        preferred_element_type=jnp.float32,
    )
    projected = projected.reshape(seq_total, seq_count, 3, local_width)
    query = (projected[:, :, 0] + b_qv[0]).astype(jnp.bfloat16)
    keys = projected[:, :, 1].astype(jnp.bfloat16)
    values = (projected[:, :, 2] + b_qv[1]).astype(jnp.bfloat16)

    def item(array, s, h):
        return array[:, s, h * head_size : (h + 1) * head_size]

    def per_row(items):
        stacked = jnp.stack(items).reshape(seq_count, local_heads, seq_total, head_size)
        return jnp.transpose(stacked, (2, 0, 1, 3)).reshape(seq_total, seq_count, local_width)

    pairs = [(s, h) for s in range(seq_count) for h in range(local_heads)]
    forward_items = [
        attention_forward(
            item(query, s, h), item(keys, s, h), item(values, s, h), seq_lengths[s : s + 1]
        )
        for s, h in pairs
    ]
    attended = per_row([o for o, _ in forward_items])
    out_weight = w_o.reshape(local_width, model_width)
    own_rows = lax.all_to_all(
        jnp.transpose(attended, (1, 0, 2)).reshape(seq_count * seq_total, local_width),
        "tensor",
        0,
        1,
        tiled=True,
    )
    attention = (
        half_columns(
            jnp.dot(own_rows, out_mine, preferred_element_type=jnp.float32),
            jnp.dot(own_rows, out_other, preferred_element_type=jnp.float32),
            core,
        ).reshape(
            seq_count, row_count, model_width
        )
    )
    attention = jnp.transpose(attention, (1, 0, 2)) + b_o
    middle = inputs + attention
    act_grad = jnp.einsum("rsd,fd->rsf", upstream_full, w_out, preferred_element_type=jnp.float32)
    second_low = layer_norm(middle, ln2_gain, ln2_bias).astype(jnp.bfloat16)
    second_full = lax.all_gather(second_low, "tensor", axis=0, tiled=True)
    second_full, act_grad = lax.optimization_barrier((second_full, act_grad))
    pre_act = (
        jnp.dot(
            second_full.reshape(seq_total * seq_count, model_width),
            w_in,
            preferred_element_type=jnp.float32,
        )
        + b_in
    )
    activated = gelu_tanh(pre_act).astype(jnp.bfloat16).reshape(seq_total, seq_count, hidden)
    piece = upstream_full
    grad_w_out = jnp.einsum("rsf,rsd->fd", activated, piece, preferred_element_type=jnp.float32)
    gelu_back = jax.vjp(gelu_tanh, pre_act)[1]
    pre_low = gelu_back(act_grad.reshape(seq_total * seq_count, hidden))[0].astype(jnp.bfloat16)
    grad_b_in = jnp.sum(pre_low, axis=0, dtype=jnp.float32)
    grad_w_in = jnp.einsum(
        "rd,rf->df",
        second_full.reshape(seq_total * seq_count, model_width),
        pre_low,
        preferred_element_type=jnp.float32,
    )
    pre_rows = pre_low.reshape(seq_total, seq_count, hidden)
    piece = pre_rows
    second_part = jnp.einsum("rsf,df->rsd", piece, w_in, preferred_element_type=jnp.float32)
    second_part = second_part.astype(jnp.bfloat16)
    feed_input, second_part = lax.optimization_barrier((activated, second_part))
    second_grad = lax.psum_scatter(
        second_part, "tensor", scatter_dimension=0, tiled=True
    ).astype(jnp.float32)
    feed_part = jnp.einsum(
        "rsf,fd->rsd", feed_input, w_out, preferred_element_type=jnp.float32
    ).astype(jnp.bfloat16)
    feed_buffer = lax.dynamic_update_slice(
        jnp.zeros(feed_part.shape[:2] + (2 * model_width,), feed_part.dtype),
        feed_part,
        (0, 0, model_width),
    )
    feed_buffer, second_grad = lax.optimization_barrier((feed_buffer, second_grad))
    norm_two_back = jax.vjp(layer_norm, middle, ln2_gain, ln2_bias)[1]
    middle_part, grad_ln2_gain, grad_ln2_bias = norm_two_back(second_grad)
    middle_grad = upstream.astype(jnp.float32) + middle_part
    branch_low = middle_grad.astype(jnp.bfloat16)
    grad_b_o = jnp.sum(branch_low, axis=(0, 1), dtype=jnp.float32)
    grad_b_out = jnp.sum(upstream, axis=(0, 1), dtype=jnp.float32)
    summed_in = halving_sum(grad_w_in * factor, 0)
    summed_out = halving_sum(grad_w_out * factor, 1)
    summed_in, summed_out, branch_low = lax.optimization_barrier(
        (summed_in, summed_out, branch_low)
    )
    piece = lax.all_gather(branch_low, "tensor", axis=0, tiled=True)
    weight_grad = jnp.einsum("rse,rsd->ed", attended, piece, preferred_element_type=jnp.float32)
    branch_rows = branch_low.reshape(row_count * seq_count, model_width)
    heads_grad = (
        jnp.dot(
            lax.dynamic_slice_in_dim(branch_rows, core * half_width, half_width, 1),
            out_mine.T,
            preferred_element_type=jnp.float32,
        )
        + jnp.dot(
            lax.dynamic_slice_in_dim(branch_rows, (1 - core) * half_width, half_width, 1),
            out_other.T,
            preferred_element_type=jnp.float32,
        )
    ).astype(jnp.bfloat16)
    attended_grad = lax.all_to_all(heads_grad, "tensor", 1, 0, tiled=True).reshape(
        seq_total, seq_count, local_width
    )
    backward_items = [
        attention_backward(
            item(query, s, h),
            item(keys, s, h),
            item(values, s, h),
            item(attended_grad, s, h),
            lse,
            seq_lengths[s : s + 1],
        )
        for (s, h), (_, lse) in zip(pairs, forward_items)
    ]
    joint_grad = jnp.stack(
        [per_row([grads[kind] for grads in backward_items]) for kind in range(3)], axis=2
    )
    grad_b_qv = jnp.sum(joint_grad[:, :, 0::2], axis=(0, 1), dtype=jnp.float32)
    joint_rows = joint_grad.reshape(seq_total, seq_count, 3 * local_width)
    grad_w_qkv = jnp.einsum(
        "rd,rc->dc",
        normed_full.reshape(seq_total * seq_count, model_width),
        joint_rows.reshape(seq_total * seq_count, 3 * local_width),
        preferred_element_type=jnp.float32,
    )
    normed_part = jnp.einsum(
        "rsc,dc->rsd", joint_rows, joint_weight, preferred_element_type=jnp.float32
    ).astype(jnp.bfloat16)
    joint_sums = jnp.sum(joint_rows, axis=(0, 1), dtype=jnp.float32)
    grad_ln1_bias = jnp.dot(
        joint_weight.astype(jnp.float32), joint_sums, precision=lax.Precision.HIGHEST
    )
    merged = lax.dynamic_update_slice(feed_buffer, normed_part, (0, 0, 0))
    both = lax.psum_scatter(merged, "tensor", scatter_dimension=0, tiled=True)
    summed = (
        halving_sum(grad_w_qkv * factor, 0).reshape(-1, 3, local_heads, head_size),
        halving_sum(weight_grad.reshape(local_heads, head_size, model_width) * factor, 2),
        summed_in,
        summed_out,
    )
    in_full = lax.dynamic_update_slice_in_dim(
        jnp.zeros((hidden * tensor_count,), jnp.float32), grad_b_in, tensor_rank * hidden, 0
    )
    joint_full = lax.dynamic_update_slice_in_dim(
        jnp.zeros((2, local_width * tensor_count), jnp.float32),
        grad_b_qv,
        tensor_rank * local_width,
        1,
    )
    early = reduce_vectors(
        (
            grad_ln1_bias,
            grad_b_o,
            grad_ln2_gain,
            grad_ln2_bias,
            grad_b_out,
            joint_full[0],
            joint_full[1],
            in_full,
        ),
        factor,
    )
    both, summed, early = lax.optimization_barrier((both, summed, early))
    both = both.astype(jnp.float32)
    normed_grad = both[:, :, :model_width]
    feed = both[:, :, model_width:] + b_out
    output = (middle + feed).astype(jnp.bfloat16)
    norm_one_back = jax.vjp(layer_norm, inputs, ln1_gain, ln1_bias)[1]
    input_part, grad_ln1_gain, _ = norm_one_back(normed_grad)
    input_grad = (middle_grad + input_part).astype(jnp.bfloat16)
    (late,) = reduce_vectors((grad_ln1_gain,), factor)
    return (
        output,
        input_grad,
        late,
        early[0],
        summed[0],
        jnp.stack((early[5], early[6])),
        summed[1],
        early[1],
        early[2],
        early[3],
        summed[2],
        early[7],
        summed[3],
        early[4],
    )


def reduce_vectors(vectors, factor):
    devices = lax.axis_size("group") * lax.axis_size("dp") * lax.axis_size("tensor")
    pieces = [(item * factor).reshape(devices, -1) for item in vectors]
    widths = [piece.shape[1] for piece in pieces]
    packed = jnp.concatenate(pieces, 1)
    packed = lax.all_to_all(packed, ("group", "dp", "tensor"), 0, 0, tiled=True)
    flat = jnp.sum(packed, axis=0)
    parts = []
    offset = 0
    for width in widths:
        parts.append(flat[offset : offset + width])
        offset += width
    return tuple(parts)


def half_columns(mine, other, core):
    return jnp.where(
        core == 0, jnp.concatenate([mine, other], 1), jnp.concatenate([other, mine], 1)
    )


def halving_steps(value, dim, steps, send_type=None):
    for axis, size, bit in steps:
        half = value.shape[dim] // 2
        low_half = lax.slice_in_dim(value, 0, half, axis=dim)
        high_half = lax.slice_in_dim(value, half, 2 * half, axis=dim)
        upper = (lax.axis_index(axis) // bit) % 2 == 1
        keep = jnp.where(upper, high_half, low_half)
        send = jnp.where(upper, low_half, high_half)
        if send_type is not None:
            send = send.astype(send_type)
        got = lax.ppermute(send, axis, [(i, i ^ bit) for i in range(size)])
        value = keep + got.astype(keep.dtype)
    return value


def halving_sum(value, dim):
    shape = value.shape
    groups = lax.axis_size("group")
    dps = lax.axis_size("dp")
    rest = shape[dim] // (groups * dps)
    value = value.reshape(shape[:dim] + (groups // 2, 2, dps * rest) + shape[dim + 1 :])
    value = jnp.swapaxes(value, dim, dim + 1)
    value = value.reshape(shape[:dim] + (groups * dps, rest) + shape[dim + 1 :])
    value = halving_steps(
        value, dim, [("group", groups, 1), ("group", groups, 2), ("dp", dps, 1)], jnp.bfloat16
    )
    return value.reshape(shape[:dim] + (shape[dim] // (groups * dps),) + shape[dim + 1 :])


def solution(mesh):
    in_specs = (
        P("tensor", ("group", "dp"), None),
        P("tensor", ("group", "dp"), None),
        P(),
        P(),
        P(),
        P(None, None, "tensor", None),
        P(None, "tensor"),
        P("tensor", None, None),
        P(),
        P(),
        P(),
        P(None, "tensor"),
        P("tensor"),
        P("tensor", None),
        P(),
    )
    out_specs = (
        P("tensor", ("group", "dp"), None),
        P("tensor", ("group", "dp"), None),
        P(("group", "dp", "tensor")),
        P(("group", "dp", "tensor")),
        P(("group", "dp"), None, "tensor", None),
        P(None, ("group", "dp", "tensor")),
        P("tensor", None, ("group", "dp")),
        P(("group", "dp", "tensor")),
        P(("group", "dp", "tensor")),
        P(("group", "dp", "tensor")),
        P(("group", "dp"), "tensor"),
        P(("group", "dp", "tensor")),
        P("tensor", ("group", "dp")),
        P(("group", "dp", "tensor")),
    )
    return jax.shard_map(shards, mesh=mesh, in_specs=in_specs, out_specs=out_specs, check_vma=False)
```

```python
from functools import partial
import math

import jax
import jax.numpy as jnp
from jax import lax
from jax.experimental import pallas as pl
from jax.experimental.pallas import tpu as pltpu
from jax.sharding import PartitionSpec as P

EPS = 1e-05
NEGATIVE = -1e30


def layer_norm(value, gain, shift):
    mean = jnp.mean(value, axis=-1, keepdims=True)
    centred = value - mean
    spread = jnp.mean(centred * centred, axis=-1, keepdims=True)
    return centred * lax.rsqrt(spread + EPS) * gain + shift


def gelu_tanh(value):
    return jax.nn.gelu(value, approximate=True)


def _valid(first_q, first_k, rows, cols, length):
    q_pos = first_q + lax.broadcasted_iota(jnp.int32, (rows, cols), 0)
    k_pos = first_k + lax.broadcasted_iota(jnp.int32, (rows, cols), 1)
    return (k_pos <= q_pos) & (k_pos < length)


def _key_blocks(i, block_q, block_k, length):
    causal = (i * block_q + block_q + block_k - 1) // block_k
    live = (length + block_k - 1) // block_k
    return jnp.minimum(causal, live)


def _attn_fwd_kernel(len_ref, q_ref, k_ref, v_ref, o_ref, lse_ref, s_buf, *, block_q, block_k, scale):
    i = pl.program_id(0)
    length = len_ref[0]
    count = _key_blocks(i, block_q, block_k, length)
    q = q_ref[...]

    def scores(j, m):
        first = pl.multiple_of(j * block_k, block_k)
        k = k_ref[pl.ds(first, block_k), :]
        s = lax.dot_general(q, k, (((1,), (1,)), ((), ())), preferred_element_type=jnp.float32) * scale
        edge = (first + block_k > i * block_q) | (first + block_k > length)
        s = lax.cond(
            edge,
            lambda v: jnp.where(_valid(i * block_q, first, block_q, block_k, length), v, NEGATIVE),
            lambda v: v,
            s,
        )
        s_buf[:, pl.ds(first, block_k)] = s
        return jnp.maximum(m, jnp.max(s, axis=1, keepdims=True))

    peak = lax.fori_loop(0, count, scores, jnp.full((block_q, 1), NEGATIVE, jnp.float32))

    def exps(j, total):
        first = pl.multiple_of(j * block_k, block_k)
        e = jnp.exp(s_buf[:, pl.ds(first, block_k)] - peak)
        s_buf[:, pl.ds(first, block_k)] = e
        return total + jnp.sum(e, axis=1, keepdims=True)

    total = lax.fori_loop(0, count, exps, jnp.zeros((block_q, 1), jnp.float32))

    inverse = 1.0 / total

    def mix(j, acc):
        first = pl.multiple_of(j * block_k, block_k)
        probs = (s_buf[:, pl.ds(first, block_k)] * inverse).astype(jnp.bfloat16)
        return acc + jnp.dot(probs, v_ref[pl.ds(first, block_k), :], preferred_element_type=jnp.float32)

    acc = lax.fori_loop(0, count, mix, jnp.zeros(o_ref.shape, jnp.float32))
    o_ref[...] = acc.astype(o_ref.dtype)
    lse_ref[...] = peak + jnp.log(total)


def attention_forward(q, k, v, length, *, block_q=512, block_k=512):
    n, d = q.shape
    scale = 1.0 / math.sqrt(d)
    kernel = partial(_attn_fwd_kernel, block_q=block_q, block_k=block_k, scale=scale)
    pairs = (n // block_q) * (n // block_k + 1) // 2
    return pl.pallas_call(
        kernel,
        out_shape=(jax.ShapeDtypeStruct((n, d), jnp.bfloat16), jax.ShapeDtypeStruct((n, 1), jnp.float32)),
        grid_spec=pltpu.PrefetchScalarGridSpec(
            num_scalar_prefetch=1,
            grid=(n // block_q,),
            in_specs=[
                pl.BlockSpec((block_q, d), lambda i, lens: (i, 0)),
                pl.BlockSpec((n, d), lambda i, lens: (0, 0)),
                pl.BlockSpec((n, d), lambda i, lens: (0, 0)),
            ],
            out_specs=[
                pl.BlockSpec((block_q, d), lambda i, lens: (i, 0)),
                pl.BlockSpec((block_q, 1), lambda i, lens: (i, 0)),
            ],
            scratch_shapes=[pltpu.VMEM((block_q, n), jnp.float32)],
        ),
        compiler_params=pltpu.CompilerParams(dimension_semantics=("arbitrary",)),
        cost_estimate=pl.CostEstimate(
            flops=4 * pairs * block_q * block_k * d,
            transcendentals=pairs * block_q * block_k,
            bytes_accessed=4 * n * d * 2,
        ),
    )(length, q, k, v)


def _attn_bwd_kernel(len_ref, q_ref, k_ref, v_ref, do_ref, lse_ref, dq_ref, dk_ref, dv_ref,
                     p_buf, dp_buf, dk_acc, dv_acc, *, block_q, block_k, scale):
    i = pl.program_id(0)
    length = len_ref[0]

    @pl.when(i == 0)
    def _():
        dk_acc[...] = jnp.zeros_like(dk_acc)
        dv_acc[...] = jnp.zeros_like(dv_acc)

    live = i * block_q < length

    @pl.when(live)
    def _():
        count = _key_blocks(i, block_q, block_k, length)
        q = q_ref[...]
        do = do_ref[...]
        lse = lse_ref[...]

        def first_pass(j, inner):
            first = pl.multiple_of(j * block_k, block_k)
            k = k_ref[pl.ds(first, block_k), :]
            v = v_ref[pl.ds(first, block_k), :]
            s = lax.dot_general(q, k, (((1,), (1,)), ((), ())), preferred_element_type=jnp.float32)
            edge = (first + block_k > i * block_q) | (first + block_k > length)
            p = lax.cond(
                edge,
                lambda v: jnp.where(
                    _valid(i * block_q, first, block_q, block_k, length),
                    jnp.exp(jnp.where(_valid(i * block_q, first, block_q, block_k, length), v, NEGATIVE) - lse),
                    0.0,
                ),
                lambda v: jnp.exp(v - lse),
                s * scale,
            )
            dp = lax.dot_general(do, v, (((1,), (1,)), ((), ())), preferred_element_type=jnp.float32)
            p_buf[:, pl.ds(first, block_k)] = p
            dp_buf[:, pl.ds(first, block_k)] = dp
            return inner + jnp.sum(p * dp, axis=1, keepdims=True)

        inner = lax.fori_loop(0, count, first_pass, jnp.zeros((block_q, 1), jnp.float32))

        def second_pass(j, dq):
            first = pl.multiple_of(j * block_k, block_k)
            p = p_buf[:, pl.ds(first, block_k)]
            dp = dp_buf[:, pl.ds(first, block_k)]
            ds = (p * (dp - inner)).astype(jnp.bfloat16)
            k = k_ref[pl.ds(first, block_k), :]
            dk_acc[pl.ds(first, block_k), :] += lax.dot_general(
                ds, q, (((0,), (0,)), ((), ())), preferred_element_type=jnp.float32)
            dv_acc[pl.ds(first, block_k), :] += lax.dot_general(
                p.astype(jnp.bfloat16), do, (((0,), (0,)), ((), ())), preferred_element_type=jnp.float32)
            return dq + jnp.dot(ds, k, preferred_element_type=jnp.float32)

        dq = lax.fori_loop(0, count, second_pass, jnp.zeros(dq_ref.shape, jnp.float32))
        dq_ref[...] = (dq * scale).astype(dq_ref.dtype)

    @pl.when(jnp.logical_not(live))
    def _():
        dq_ref[...] = jnp.zeros_like(dq_ref)

    @pl.when(i == pl.num_programs(0) - 1)
    def _():
        dk_ref[...] = (dk_acc[...] * scale).astype(dk_ref.dtype)
        dv_ref[...] = dv_acc[...].astype(dv_ref.dtype)


def attention_backward(q, k, v, do, lse, length, *, block_q=512, block_k=512):
    n, d = q.shape
    scale = 1.0 / math.sqrt(d)
    kernel = partial(_attn_bwd_kernel, block_q=block_q, block_k=block_k, scale=scale)
    pairs = (n // block_q) * (n // block_k + 1) // 2
    full = pl.BlockSpec((n, d), lambda i, lens: (0, 0))
    rows = pl.BlockSpec((block_q, d), lambda i, lens: (i, 0))
    return pl.pallas_call(
        kernel,
        out_shape=tuple(jax.ShapeDtypeStruct((n, d), jnp.bfloat16) for _ in range(3)),
        grid_spec=pltpu.PrefetchScalarGridSpec(
            num_scalar_prefetch=1,
            grid=(n // block_q,),
            in_specs=[rows, full, full, rows, pl.BlockSpec((block_q, 1), lambda i, lens: (i, 0))],
            out_specs=[rows, full, full],
            scratch_shapes=[
                pltpu.VMEM((block_q, n), jnp.float32),
                pltpu.VMEM((block_q, n), jnp.float32),
                pltpu.VMEM((n, d), jnp.float32),
                pltpu.VMEM((n, d), jnp.float32),
            ],
        ),
        compiler_params=pltpu.CompilerParams(dimension_semantics=("arbitrary",)),
        cost_estimate=pl.CostEstimate(
            flops=8 * pairs * block_q * block_k * d,
            transcendentals=pairs * block_q * block_k,
            bytes_accessed=8 * n * d * 2,
        ),
    )(length, q, k, v, do, lse)


def _attn_bwd1_kernel(len_ref, q_ref, k_ref, v_ref, do_ref, lse_ref, delta_ref, dq_ref, dk_ref, dv_ref,
                      dk_acc, dv_acc, *, block_q, block_k, scale):
    i = pl.program_id(0)
    length = len_ref[0]

    @pl.when(i == 0)
    def _():
        dk_acc[...] = jnp.zeros_like(dk_acc)
        dv_acc[...] = jnp.zeros_like(dv_acc)

    live = i * block_q < length

    @pl.when(live)
    def _():
        count = _key_blocks(i, block_q, block_k, length)
        q = q_ref[...]
        do = do_ref[...]
        lse = lse_ref[...]
        delta = delta_ref[...]

        def step(j, dq):
            first = pl.multiple_of(j * block_k, block_k)
            k = k_ref[pl.ds(first, block_k), :]
            v = v_ref[pl.ds(first, block_k), :]
            s = lax.dot_general(q, k, (((1,), (1,)), ((), ())), preferred_element_type=jnp.float32)
            edge = (first + block_k > i * block_q) | (first + block_k > length)
            p = lax.cond(
                edge,
                lambda w: jnp.where(
                    _valid(i * block_q, first, block_q, block_k, length),
                    jnp.exp(jnp.where(_valid(i * block_q, first, block_q, block_k, length), w, NEGATIVE) - lse),
                    0.0,
                ),
                lambda w: jnp.exp(w - lse),
                s * scale,
            )
            dp = lax.dot_general(do, v, (((1,), (1,)), ((), ())), preferred_element_type=jnp.float32)
            ds = (p * (dp - delta)).astype(jnp.bfloat16)
            dk_acc[pl.ds(first, block_k), :] += lax.dot_general(
                ds, q, (((0,), (0,)), ((), ())), preferred_element_type=jnp.float32)
            dv_acc[pl.ds(first, block_k), :] += lax.dot_general(
                p.astype(jnp.bfloat16), do, (((0,), (0,)), ((), ())), preferred_element_type=jnp.float32)
            return dq + jnp.dot(ds, k, preferred_element_type=jnp.float32)

        dq = lax.fori_loop(0, count, step, jnp.zeros(dq_ref.shape, jnp.float32))
        dq_ref[...] = (dq * scale).astype(dq_ref.dtype)

    @pl.when(jnp.logical_not(live))
    def _():
        dq_ref[...] = jnp.zeros_like(dq_ref)

    @pl.when(i == pl.num_programs(0) - 1)
    def _():
        dk_ref[...] = (dk_acc[...] * scale).astype(dk_ref.dtype)
        dv_ref[...] = dv_acc[...].astype(dv_ref.dtype)


def attention_backward1(q, k, v, do, lse, delta, length, *, block_q=512, block_k=512):
    n, d = q.shape
    scale = 1.0 / math.sqrt(d)
    kernel = partial(_attn_bwd1_kernel, block_q=block_q, block_k=block_k, scale=scale)
    pairs = (n // block_q) * (n // block_k + 1) // 2
    full = pl.BlockSpec((n, d), lambda i, lens: (0, 0))
    rows = pl.BlockSpec((block_q, d), lambda i, lens: (i, 0))
    col = pl.BlockSpec((block_q, 1), lambda i, lens: (i, 0))
    return pl.pallas_call(
        kernel,
        out_shape=tuple(jax.ShapeDtypeStruct((n, d), jnp.bfloat16) for _ in range(3)),
        grid_spec=pltpu.PrefetchScalarGridSpec(
            num_scalar_prefetch=1,
            grid=(n // block_q,),
            in_specs=[rows, full, full, rows, col, col],
            out_specs=[rows, full, full],
            scratch_shapes=[pltpu.VMEM((n, d), jnp.float32), pltpu.VMEM((n, d), jnp.float32)],
        ),
        compiler_params=pltpu.CompilerParams(dimension_semantics=("arbitrary",)),
        cost_estimate=pl.CostEstimate(
            flops=10 * pairs * block_q * block_k * d,
            transcendentals=pairs * block_q * block_k,
            bytes_accessed=8 * n * d * 2,
        ),
    )(length, q, k, v, do, lse, delta)


def shards(
    tokens,
    cotangent,
    lengths,
    ln1_gain,
    ln1_bias,
    w_qkv,
    b_qv,
    w_o,
    b_o,
    ln2_gain,
    ln2_bias,
    w_in,
    b_in,
    w_out,
    b_out,
):
    row_count, seq_count, model_width = tokens.shape
    tensor_count = lax.axis_size("tensor")
    tensor_rank = lax.axis_index("tensor")
    seq_total = row_count * tensor_count
    local_heads = w_qkv.shape[2]
    head_size = w_qkv.shape[3]
    local_width = local_heads * head_size
    hidden = w_in.shape[1]
    group_count = lax.axis_size("group")
    group_rank = lax.axis_index("group")
    member = group_rank * lax.axis_size("dp") + lax.axis_index("dp")
    seq_lengths = lax.dynamic_slice_in_dim(lengths, member * seq_count, seq_count, 0)
    group_totals = jnp.sum(lengths.reshape(group_count, -1), axis=1).astype(jnp.float32)
    factor = (
        group_count
        * lax.dynamic_index_in_dim(group_totals, group_rank, 0, keepdims=False)
        / jnp.sum(group_totals)
    )
    inputs = tokens.astype(jnp.float32)
    normed_low = layer_norm(inputs, ln1_gain, ln1_bias).astype(jnp.bfloat16)
    positions = tensor_rank * row_count + jnp.arange(row_count, dtype=jnp.int32)
    live = positions[:, None] < seq_lengths[None, :]
    upstream = jnp.where(live[:, :, None], cotangent, jnp.zeros_like(cotangent))
    core = group_rank % 2
    half_width = model_width // 2
    front = jnp.concatenate(
        [
            normed_low.reshape(row_count, seq_count * model_width),
            lax.dynamic_slice_in_dim(w_o.reshape(row_count, -1), core * half_width, half_width, 1),
        ],
        1,
    )
    front = lax.all_gather(front, "tensor", axis=0, tiled=True)
    wide = seq_count * model_width
    normed_full = front[:, :wide].reshape(seq_total, seq_count, model_width)
    out_mine = front[:, wide:]
    out_other = lax.ppermute(out_mine, "group", [(g, g ^ 1) for g in range(group_count)])
    upstream, front = lax.optimization_barrier((upstream, front))
    upstream_full = lax.all_gather(upstream, "tensor", axis=0, tiled=True)
    joint_weight = w_qkv.reshape(model_width, 3 * local_width)
    projected = jnp.dot(
        normed_full.reshape(seq_total * seq_count, model_width),
        joint_weight,
        preferred_element_type=jnp.float32,
    )
    projected = projected.reshape(seq_total, seq_count, 3, local_width)
    query = (projected[:, :, 0] + b_qv[0]).astype(jnp.bfloat16)
    keys = projected[:, :, 1].astype(jnp.bfloat16)
    values = (projected[:, :, 2] + b_qv[1]).astype(jnp.bfloat16)

    def item(array, s, h):
        return array[:, s, h * head_size : (h + 1) * head_size]

    def per_row(items):
        stacked = jnp.stack(items).reshape(seq_count, local_heads, seq_total, head_size)
        return jnp.transpose(stacked, (2, 0, 1, 3)).reshape(seq_total, seq_count, local_width)

    pairs = [(s, h) for s in range(seq_count) for h in range(local_heads)]
    forward_items = [
        attention_forward(
            item(query, s, h), item(keys, s, h), item(values, s, h), seq_lengths[s : s + 1]
        )
        for s, h in pairs
    ]
    attended = per_row([o for o, _ in forward_items])
    out_weight = w_o.reshape(local_width, model_width)
    own_rows = lax.all_to_all(
        jnp.transpose(attended, (1, 0, 2)).reshape(seq_count * seq_total, local_width),
        "tensor",
        0,
        1,
        tiled=True,
    )
    attention = (
        half_columns(
            jnp.dot(own_rows, out_mine, preferred_element_type=jnp.float32),
            jnp.dot(own_rows, out_other, preferred_element_type=jnp.float32),
            core,
        ).reshape(
            seq_count, row_count, model_width
        )
    )
    attention = jnp.transpose(attention, (1, 0, 2)) + b_o
    middle = inputs + attention
    act_grad = jnp.einsum("rsd,fd->rsf", upstream_full, w_out, preferred_element_type=jnp.float32)
    second_low = layer_norm(middle, ln2_gain, ln2_bias).astype(jnp.bfloat16)
    second_low, upstream_full = lax.optimization_barrier((second_low, upstream_full))
    second_full = lax.all_gather(second_low, "tensor", axis=0, tiled=True)
    second_full, act_grad = lax.optimization_barrier((second_full, act_grad))
    pre_act = (
        jnp.dot(
            second_full.reshape(seq_total * seq_count, model_width),
            w_in,
            preferred_element_type=jnp.float32,
        )
        + b_in
    )
    activated = gelu_tanh(pre_act).astype(jnp.bfloat16).reshape(seq_total, seq_count, hidden)
    piece = upstream_full
    grad_w_out = jnp.einsum("rsf,rsd->fd", activated, piece, preferred_element_type=jnp.float32)
    gelu_back = jax.vjp(gelu_tanh, pre_act)[1]
    pre_low = gelu_back(act_grad.reshape(seq_total * seq_count, hidden))[0].astype(jnp.bfloat16)
    grad_b_in = jnp.sum(pre_low, axis=0, dtype=jnp.float32)
    grad_w_in = jnp.einsum(
        "rd,rf->df",
        second_full.reshape(seq_total * seq_count, model_width),
        pre_low,
        preferred_element_type=jnp.float32,
    )
    pre_rows = pre_low.reshape(seq_total, seq_count, hidden)
    piece = pre_rows
    second_part = jnp.einsum("rsf,df->rsd", piece, w_in, preferred_element_type=jnp.float32)
    second_part = second_part.astype(jnp.bfloat16)
    feed_input, second_part = lax.optimization_barrier((activated, second_part))
    second_grad = lax.psum_scatter(
        second_part, "tensor", scatter_dimension=0, tiled=True
    ).astype(jnp.float32)
    feed_part = jnp.einsum(
        "rsf,fd->rsd", feed_input, w_out, preferred_element_type=jnp.float32
    ).astype(jnp.bfloat16)
    feed_buffer = lax.dynamic_update_slice(
        jnp.zeros(feed_part.shape[:2] + (2 * model_width,), feed_part.dtype),
        feed_part,
        (0, 0, model_width),
    )
    feed_buffer, second_grad = lax.optimization_barrier((feed_buffer, second_grad))
    norm_two_back = jax.vjp(layer_norm, middle, ln2_gain, ln2_bias)[1]
    middle_part, grad_ln2_gain, grad_ln2_bias = norm_two_back(second_grad)
    middle_grad = upstream.astype(jnp.float32) + middle_part
    branch_low = middle_grad.astype(jnp.bfloat16)
    grad_b_o = jnp.sum(branch_low, axis=(0, 1), dtype=jnp.float32)
    grad_b_out = jnp.sum(upstream, axis=(0, 1), dtype=jnp.float32)
    summed_in = halving_sum(grad_w_in * factor, 0)
    summed_out = halving_sum(grad_w_out * factor, 1)
    summed_in, summed_out, branch_low = lax.optimization_barrier(
        (summed_in, summed_out, branch_low)
    )
    piece = lax.all_gather(branch_low, "tensor", axis=0, tiled=True)
    weight_grad = jnp.einsum("rse,rsd->ed", attended, piece, preferred_element_type=jnp.float32)
    branch_rows = branch_low.reshape(row_count * seq_count, model_width)
    heads_grad = (
        jnp.dot(
            lax.dynamic_slice_in_dim(branch_rows, core * half_width, half_width, 1),
            out_mine.T,
            preferred_element_type=jnp.float32,
        )
        + jnp.dot(
            lax.dynamic_slice_in_dim(branch_rows, (1 - core) * half_width, half_width, 1),
            out_other.T,
            preferred_element_type=jnp.float32,
        )
    ).astype(jnp.bfloat16)
    attended_grad = lax.all_to_all(heads_grad, "tensor", 1, 0, tiled=True).reshape(
        seq_total, seq_count, local_width
    )
    backward_items = [
        attention_backward1(
            item(query, s, h),
            item(keys, s, h),
            item(values, s, h),
            item(attended_grad, s, h),
            lse,
            jnp.sum(
                item(attended_grad, s, h).astype(jnp.float32) * o.astype(jnp.float32),
                axis=1,
                keepdims=True,
            ),
            seq_lengths[s : s + 1],
        )
        for (s, h), (o, lse) in zip(pairs, forward_items)
    ]
    joint_grad = jnp.stack(
        [per_row([grads[kind] for grads in backward_items]) for kind in range(3)], axis=2
    )
    grad_b_qv = jnp.sum(joint_grad[:, :, 0::2], axis=(0, 1), dtype=jnp.float32)
    joint_rows = joint_grad.reshape(seq_total, seq_count, 3 * local_width)
    grad_w_qkv = jnp.einsum(
        "rd,rc->dc",
        normed_full.reshape(seq_total * seq_count, model_width),
        joint_rows.reshape(seq_total * seq_count, 3 * local_width),
        preferred_element_type=jnp.float32,
    )
    normed_part = jnp.einsum(
        "rsc,dc->rsd", joint_rows, joint_weight, preferred_element_type=jnp.float32
    ).astype(jnp.bfloat16)
    joint_sums = jnp.sum(joint_rows, axis=(0, 1), dtype=jnp.float32)
    grad_ln1_bias = jnp.dot(
        joint_weight.astype(jnp.float32), joint_sums, precision=lax.Precision.HIGHEST
    )
    merged = lax.dynamic_update_slice(feed_buffer, normed_part, (0, 0, 0))
    both = lax.psum_scatter(merged, "tensor", scatter_dimension=0, tiled=True)
    summed = (
        halving_sum(grad_w_qkv * factor, 0).reshape(-1, 3, local_heads, head_size),
        halving_sum(weight_grad.reshape(local_heads, head_size, model_width) * factor, 2),
        summed_in,
        summed_out,
    )
    in_full = lax.dynamic_update_slice_in_dim(
        jnp.zeros((hidden * tensor_count,), jnp.float32), grad_b_in, tensor_rank * hidden, 0
    )
    joint_full = lax.dynamic_update_slice_in_dim(
        jnp.zeros((2, local_width * tensor_count), jnp.float32),
        grad_b_qv,
        tensor_rank * local_width,
        1,
    )
    early = reduce_vectors(
        (
            grad_ln1_bias,
            grad_b_o,
            grad_ln2_gain,
            grad_ln2_bias,
            grad_b_out,
            joint_full[0],
            joint_full[1],
            in_full,
        ),
        factor,
    )
    both, summed, early = lax.optimization_barrier((both, summed, early))
    both = both.astype(jnp.float32)
    normed_grad = both[:, :, :model_width]
    feed = both[:, :, model_width:] + b_out
    output = (middle + feed).astype(jnp.bfloat16)
    norm_one_back = jax.vjp(layer_norm, inputs, ln1_gain, ln1_bias)[1]
    input_part, grad_ln1_gain, _ = norm_one_back(normed_grad)
    input_grad = (middle_grad + input_part).astype(jnp.bfloat16)
    (late,) = reduce_vectors((grad_ln1_gain,), factor)
    return (
        output,
        input_grad,
        late,
        early[0],
        summed[0],
        jnp.stack((early[5], early[6])),
        summed[1],
        early[1],
        early[2],
        early[3],
        summed[2],
        early[7],
        summed[3],
        early[4],
    )


def reduce_vectors(vectors, factor):
    devices = lax.axis_size("group") * lax.axis_size("dp") * lax.axis_size("tensor")
    pieces = [(item * factor).reshape(devices, -1) for item in vectors]
    widths = [piece.shape[1] for piece in pieces]
    packed = jnp.concatenate(pieces, 1)
    packed = lax.all_to_all(packed, ("group", "dp", "tensor"), 0, 0, tiled=True)
    flat = jnp.sum(packed, axis=0)
    parts = []
    offset = 0
    for width in widths:
        parts.append(flat[offset : offset + width])
        offset += width
    return tuple(parts)


def half_columns(mine, other, core):
    return jnp.where(
        core == 0, jnp.concatenate([mine, other], 1), jnp.concatenate([other, mine], 1)
    )


def halving_steps(value, dim, steps, send_type=None):
    for axis, size, bit in steps:
        half = value.shape[dim] // 2
        low_half = lax.slice_in_dim(value, 0, half, axis=dim)
        high_half = lax.slice_in_dim(value, half, 2 * half, axis=dim)
        upper = (lax.axis_index(axis) // bit) % 2 == 1
        keep = jnp.where(upper, high_half, low_half)
        send = jnp.where(upper, low_half, high_half)
        if send_type is not None:
            send = send.astype(send_type)
        got = lax.ppermute(send, axis, [(i, i ^ bit) for i in range(size)])
        value = keep + got.astype(keep.dtype)
    return value


def halving_sum(value, dim):
    shape = value.shape
    groups = lax.axis_size("group")
    dps = lax.axis_size("dp")
    rest = shape[dim] // (groups * dps)
    value = value.reshape(shape[:dim] + (groups // 2, 2, dps * rest) + shape[dim + 1 :])
    value = jnp.swapaxes(value, dim, dim + 1)
    value = value.reshape(shape[:dim] + (groups * dps, rest) + shape[dim + 1 :])
    value = halving_steps(
        value, dim, [("group", groups, 1), ("group", groups, 2), ("dp", dps, 1)], jnp.bfloat16
    )
    return value.reshape(shape[:dim] + (shape[dim] // (groups * dps),) + shape[dim + 1 :])


def solution(mesh):
    in_specs = (
        P("tensor", ("group", "dp"), None),
        P("tensor", ("group", "dp"), None),
        P(),
        P(),
        P(),
        P(None, None, "tensor", None),
        P(None, "tensor"),
        P("tensor", None, None),
        P(),
        P(),
        P(),
        P(None, "tensor"),
        P("tensor"),
        P("tensor", None),
        P(),
    )
    out_specs = (
        P("tensor", ("group", "dp"), None),
        P("tensor", ("group", "dp"), None),
        P(("group", "dp", "tensor")),
        P(("group", "dp", "tensor")),
        P(("group", "dp"), None, "tensor", None),
        P(None, ("group", "dp", "tensor")),
        P("tensor", None, ("group", "dp")),
        P(("group", "dp", "tensor")),
        P(("group", "dp", "tensor")),
        P(("group", "dp", "tensor")),
        P(("group", "dp"), "tensor"),
        P(("group", "dp", "tensor")),
        P("tensor", ("group", "dp")),
        P(("group", "dp", "tensor")),
    )
    return jax.shard_map(shards, mesh=mesh, in_specs=in_specs, out_specs=out_specs, check_vma=False)
```
